32 devices in a mesh: dp: 4 (over y, core), expert: 8 (over z, x).
Axes of the slice: x: 2, y: 2, z: 4, core: 2. Of those that a mesh axis runs over, the one named last changes fastest.
Arguments:
- images: bfloat16 [192, 197, 768], P(('dp', 'expert')), may hold values from -6 to 6
- first_gain: bfloat16 [768], P('dp'), may hold values from 0.5 to 1.5
- first_shift: bfloat16 [768], P('dp'), may hold values from -1.5 to 1.5
- attn_in: bfloat16 [768, 2304], P('dp'), may hold values from -0.21875 to 0.21875
- attn_out: bfloat16 [768, 768], P('dp'), may hold values from -2 to 2
- second_gain: bfloat16 [768], P('dp'), may hold values from 0.5 to 1.5
- second_shift: bfloat16 [768], P('dp'), may hold values from -1.5 to 1.5
- router: bfloat16 [768, 8], P('dp'), may hold values from -0.15625 to 0.15625
- expert_in: bfloat16 [8, 3072, 768], P('expert', 'dp'), may hold values from -0.21875 to 0.21875
- expert_bias: bfloat16 [8, 3072], P('expert', 'dp'), may hold values from -2.5 to 2.5
- expert_out: bfloat16 [8, 3072, 768], P('expert', 'dp'), may hold values from -0.625 to 0.625
- routes: int32 [192, 197, 2], P(('dp', 'expert')), may hold values from 0 to 7, all different within a row
- out_grad: bfloat16 [192, 197, 768], P(('dp', 'expert')), may hold values from -6 to 6
Outputs:
- block_out: bfloat16 [192, 197, 768], P(('dp', 'expert'))
- input_grad: float32 [192, 197, 768], P(('dp', 'expert'))
- grad_first_gain: float32 [768], P('dp')
- grad_first_shift: float32 [768], P('dp')
- grad_attn_in: float32 [768, 2304], P('dp')
- grad_attn_out: float32 [768, 768], P('dp')
- grad_second_gain: float32 [768], P('dp')
- grad_second_shift: float32 [768], P('dp')
- grad_router: float32 [768, 8], P('dp')
- grad_expert_in: float32 [8, 3072, 768], P('expert', 'dp')
- grad_expert_bias: float32 [8, 3072], P('expert', 'dp')
- grad_expert_out: float32 [8, 3072, 768], P('expert', 'dp')
The draws below stay inside these ranges and needn't reach their ends.
Inputs may be any that keep to these rules, and one draw needn't show every extreme that they name: `routes`: the 2 entries of a token name different experts; every expert is named by some token.
All inputs are finite; a program needn't handle non-finite values.
Results may differ from the reference program's by a relative error of at most 0.024.
Values may be sent and summed in bfloat16 or wider, within the bound.
A program may use at most 320 MiB of HBM per device.

```python
import jax
import jax.numpy as jnp
from jax import lax

D = 768
HEADS = 12
HEAD_DIM = 64
FF = 3072
TOP = 2
SEQ = 197
IMG_MB = 3
EXPERTS = 8
TOK_MB = 591
IMAGES = 192
CAP = 184


def block_scale(own_key, extent, cuts, least, top_value):
    level = 1.0
    for dim, blocks in cuts:
        steps = jax.random.uniform(jax.random.fold_in(jax.random.fold_in(own_key, 6), dim), (blocks,), jnp.float32, least / len(cuts), top_value / len(cuts))
        level = level * jnp.repeat(jnp.exp(steps), extent[dim] // blocks).reshape((-1,) + (1,) * (len(extent) - 1 - dim))
    return level


def distinct(rng, rows, number_of, top, lift):
    sequence = jax.random.permutation(jax.random.fold_in(rng, 1), number_of)
    pull = sequence
    for power in range(3):
        pull = pull * pull // number_of
    pull = pull * lift // number_of
    lots = jax.random.randint(jax.random.fold_in(rng, 2), (rows, number_of), 0, 4096) + pull
    holders = jax.random.permutation(jax.random.fold_in(rng, 3), rows)[jnp.arange(number_of) % rows]
    lots = jnp.where(jnp.arange(rows)[:, None] == holders[None, :], 1 << 14, lots)
    priority = lots * number_of + jnp.arange(number_of)
    return lax.top_k(priority.astype(jnp.int32), top)[1].astype(jnp.int32)


def scatter_about(key, shape, deviation, bound, pieces=(), kind=jnp.bfloat16):
    values = deviation * jax.random.normal(key, shape, jnp.float32)
    if pieces:
        values = values * block_scale(key, shape, pieces, -0.22, 0.18)
    return jnp.clip(values, -bound, bound).astype(kind)


def setup_inputs(seed: int = 0) -> dict:
    splits = jax.random.split(jax.random.key(seed), 14)
    return {
        "images": scatter_about(splits[0], (IMAGES, SEQ, D), 1.0, 6.0, ((0, 32),)),
        "first_gain": jnp.clip(1.0 + 0.1 * jax.random.normal(splits[1], (D,), jnp.float32), 0.5, 1.5).astype(jnp.bfloat16),
        "first_shift": scatter_about(splits[2], (D,), 0.3, 1.5, ((0, 4),)),
        "attn_in": scatter_about(splits[3], (D, 3 * D), D ** -0.5, 0.21875, ((0, 4),)),
        "attn_out": scatter_about(splits[4], (D, D), (max(1, D // 96)) ** -0.5, 2.0, ((0, 4),)),
        "second_gain": jnp.clip(1.0 + 0.1 * jax.random.normal(splits[5], (D,), jnp.float32), 0.5, 1.5).astype(jnp.bfloat16),
        "second_shift": scatter_about(splits[6], (D,), 0.3, 1.5, ((0, 4),)),
        "router": scatter_about(splits[7], (D, EXPERTS), (2 * D) ** -0.5, 0.15625, ((0, 4),)),
        "expert_in": scatter_about(splits[8], (EXPERTS, FF, D), D ** -0.5, 0.21875, ((0, 8), (1, 4))),
        "expert_bias": scatter_about(splits[9], (EXPERTS, FF), 0.5, 2.5, ((0, 8), (1, 4))),
        "expert_out": scatter_about(splits[10], (EXPERTS, FF, D), (max(1, 2 * FF // (EXPERTS * EXPERTS))) ** -0.5, 0.625, ((0, 8), (1, 4))),
        "routes": distinct(splits[11], IMAGES * SEQ, EXPERTS, TOP, 2048).reshape((IMAGES, SEQ, TOP)),
        "out_grad": scatter_about(splits[12], (IMAGES, SEQ, D), 1.0, 6.0, ((0, 32),)),
    }


@jax.custom_vjp
def low(v):
    return lax.optimization_barrier(v.astype(jnp.bfloat16)).astype(jnp.float32)

@jax.custom_vjp
def low_back(v):
    return v

def low_keep(v):
    return (low(v), None)

def low_pass(kept, grad):
    return (grad,)

def back_keep(v):
    return (v, None)

def back_low(kept, grad):
    return (low(grad),)
low.defvjp(low_keep, low_pass)
low_back.defvjp(back_keep, back_low)
epsilon = 1e-06
highest = lax.Precision.HIGHEST

def layer_norm(values, norm_gain, norm_shift):
    row_mean = lax.optimization_barrier(jnp.mean(values, axis=-1, keepdims=True))
    centred = values - row_mean
    row_var = lax.optimization_barrier(jnp.mean(centred * centred, axis=-1, keepdims=True))
    return centred * lax.rsqrt(row_var + epsilon) * norm_gain + norm_shift

def slot_tables(route_group):
    pair_order = route_group.T.reshape(-1)
    onehot = (pair_order[:, None] == jnp.arange(EXPERTS, dtype=jnp.int32)[None, :]).astype(jnp.int32)
    earlier = jnp.cumsum(onehot, axis=0) - onehot
    position = lax.optimization_barrier(jnp.sum(earlier * onehot, axis=1))
    kept_mask = position < CAP
    slot_index = jnp.where(kept_mask, pair_order * CAP + position, EXPERTS * CAP).astype(jnp.int32)
    token_ids = jnp.tile(jnp.arange(TOK_MB, dtype=jnp.int32), TOP)
    owners = jnp.full((EXPERTS * CAP + 1,), -1, jnp.int32).at[slot_index].set(token_ids)[:EXPERTS * CAP]
    return (slot_index, owners)

def gather_rows(hidden_rows, owners):
    return jnp.where((owners >= 0)[:, None], hidden_rows[jnp.maximum(owners, 0)], 0.0)

def attention_group(image_group, attn_in):
    projected = low_back(low(jnp.einsum('td,de->te', image_group, attn_in, precision=highest)))
    head_shape = (IMG_MB, SEQ, HEADS, HEAD_DIM)
    queries = projected[:, :D].reshape(head_shape)
    key_heads = projected[:, D:2 * D].reshape(head_shape)
    values = projected[:, 2 * D:].reshape(head_shape)
    scores = low_back(jnp.einsum('iqhc,ikhc->ihqk', queries, key_heads, precision=highest) * HEAD_DIM ** (-0.5))
    attn_probs = jax.nn.softmax(scores, axis=-1)
    mixed_heads = jnp.einsum('ihqk,ikhc->iqhc', low(attn_probs), values, precision=highest)
    return low_back(low(mixed_heads.reshape(TOK_MB, D)))

def expert_block(operands):
    slot_rows, weight_in, hidden_bias, weight_out = operands
    pre_act = low_back(jnp.einsum('rd,fd->rf', slot_rows, weight_in, precision=highest) + hidden_bias)
    activation = low(jax.nn.gelu(pre_act, approximate=False))
    return low_back(low(jnp.einsum('rf,fd->rd', activation, weight_out, precision=highest)))

def forward(images, first_gain, first_shift, attn_in, attn_out, second_gain, second_shift, router, expert_in, expert_bias, expert_out, routes):
    groups = images.shape[0] // IMG_MB
    flat_images = images.reshape(groups, TOK_MB, D)
    attn_input = low(layer_norm(flat_images, first_gain, first_shift))
    mixed_all = lax.map(jax.checkpoint(lambda image_group: attention_group(image_group, attn_in)), attn_input)
    residual = flat_images + low_back(jnp.einsum('gtd,de->gte', mixed_all, attn_out, precision=highest))
    hidden = low(layer_norm(residual, second_gain, second_shift))
    router_probs = jax.nn.softmax(jnp.einsum('gtd,de->gte', hidden, router, precision=highest), axis=-1)
    route_groups = routes.reshape(groups, TOK_MB, TOP)
    gate_values = jnp.take_along_axis(router_probs, route_groups, axis=2)
    slot_index, owners = jax.vmap(slot_tables)(route_groups)
    dispatched = low_back(jax.vmap(gather_rows)(hidden, owners))
    by_expert = dispatched.reshape(groups, EXPERTS, CAP, D).transpose(1, 0, 2, 3).reshape(EXPERTS, groups * CAP, D)
    expert_result = lax.map(jax.checkpoint(expert_block), (by_expert, expert_in, expert_bias, expert_out))
    returned = expert_result.reshape(EXPERTS, groups, CAP, D).transpose(1, 0, 2, 3).reshape(groups, EXPERTS * CAP, D)
    padded = jnp.concatenate([returned, jnp.zeros((groups, 1, D), jnp.float32)], axis=1)
    picked = jax.vmap(lambda row_table, row_index: row_table[row_index])(padded, slot_index).reshape(groups, TOP, TOK_MB, D)
    expert_mix = lax.optimization_barrier(jnp.sum(jnp.transpose(gate_values, (0, 2, 1))[:, :, :, None] * picked, axis=1))
    return (residual + expert_mix).reshape(images.shape)

def reference(images, first_gain, first_shift, attn_in, attn_out, second_gain, second_shift, router, expert_in, expert_bias, expert_out, routes, out_grad):
    floats = tuple((array.astype(jnp.float32) for array in (images, first_gain, first_shift, attn_in, attn_out, second_gain, second_shift, router, expert_in, expert_bias, expert_out)))
    result, pullback = jax.vjp(lambda *params: forward(*params, routes), *floats)
    gradients = pullback(out_grad.astype(jnp.float32))
    return (result.astype(jnp.bfloat16), gradients[0], gradients[1], gradients[2], gradients[3], gradients[4], gradients[5], gradients[6], gradients[7], gradients[8], gradients[9], gradients[10])
```

```python
import functools

import jax
import jax.numpy as jnp
from jax import lax
from jax.experimental import pallas as pl
from jax.experimental.pallas import tpu as pltpu
from jax.sharding import PartitionSpec as P

HEADS = 12
HEAD_DIM = 64
SEQ = 197
MICRO = 2
IMG_MB = 3
TOP = 2
LANES = 128
VMEM_LIMIT = 60 * 1024 * 1024

epsilon = 1e-06
f32 = jnp.float32
bf16 = jnp.bfloat16


def params(semantics, **more):
    return pltpu.CompilerParams(
        dimension_semantics=semantics, vmem_limit_bytes=VMEM_LIMIT, **more
    )


def dot(left, right):
    return lax.dot_general(
        left, right, (((1,), (0,)), ((), ())), preferred_element_type=f32
    )


def dot_t(left, right):
    return lax.dot_general(
        left, right, (((1,), (1,)), ((), ())), preferred_element_type=f32
    )


def t_dot(left, right):
    return lax.dot_general(
        left, right, (((0,), (0,)), ((), ())), preferred_element_type=f32
    )


def norm_forward(values):
    row_mean = jnp.mean(values, axis=-1, keepdims=True)
    centred = values - row_mean
    row_var = jnp.mean(centred * centred, axis=-1, keepdims=True)
    inverse = lax.rsqrt(row_var + epsilon)
    return centred * inverse, inverse


def norm_backward(grad_normed, normed, inverse):
    mean_grad = jnp.mean(grad_normed, axis=-1, keepdims=True)
    mean_cross = jnp.mean(grad_normed * normed, axis=-1, keepdims=True)
    return inverse * (grad_normed - mean_grad - normed * mean_cross)


def softmax_lanes(logits, count):
    lane = lax.broadcasted_iota(jnp.int32, logits.shape, 1)
    masked = jnp.where(lane < count, logits, -1e30)
    top = jnp.max(masked, axis=-1, keepdims=True)
    raised = jnp.where(lane < count, jnp.exp(masked - top), 0.0)
    return raised / jnp.sum(raised, axis=-1, keepdims=True)


def gelu_both(values):
    size = jnp.abs(values)
    bell = jnp.exp(values * values * -0.5)
    t = 1.0 / (1.0 + (0.3275911 * 0.7071067811865476) * size)
    tail = t * (
        0.5 * 0.254829592
        + t
        * (
            0.5 * -0.284496736
            + t * (0.5 * 1.421413741 + t * (0.5 * -1.453152027 + t * (0.5 * 1.061405429)))
        )
    )
    tail = tail * bell
    phi = jnp.where(values >= 0, 1.0 - tail, tail)
    return values * phi, phi + values * (0.3989422804014327 * bell)


def route_kernel(experts, capacity, routes_ref, slots_ref):
    seq = routes_ref.shape[1]
    row = lax.broadcasted_iota(jnp.int32, (seq, seq), 0)
    col = lax.broadcasted_iota(jnp.int32, (seq, seq), 1)
    earlier = (col < row).astype(f32).astype(bf16)
    lane = lax.broadcasted_iota(jnp.int32, (seq, LANES), 1)
    groups = routes_ref.shape[0] // IMG_MB
    for group in range(groups):
        base = jnp.zeros((1, LANES), f32)
        for choice in range(TOP):
            for image in range(IMG_MB):
                index = group * IMG_MB + image
                named = routes_ref[index][:, choice : choice + 1]
                onehot = (lane == named).astype(f32)
                count = dot(earlier, onehot.astype(bf16)) + base
                position = jnp.sum(onehot * count, axis=1, keepdims=True).astype(jnp.int32)
                base = base + jnp.sum(onehot, axis=0, keepdims=True)
                slot = jnp.where(position < capacity, named * capacity + position, -1)
                slots_ref[index, :, choice : choice + 1] = slot


def route(routes, experts, capacity):
    return pl.pallas_call(
        functools.partial(route_kernel, experts, capacity),
        out_shape=jax.ShapeDtypeStruct(routes.shape, jnp.int32),
        compiler_params=pltpu.CompilerParams(vmem_limit_bytes=VMEM_LIMIT),
        cost_estimate=pl.CostEstimate(
            flops=10**8, bytes_accessed=2 * 10**6, transcendentals=0
        ),
        name="route",
    )(routes)


def dispatch_kernel(capacity, slots_ref, rows_ref, out_ref):
    first = pl.program_id(0) * capacity
    seq = rows_ref.shape[1]
    column = lax.broadcasted_iota(jnp.int32, (seq, capacity), 1) + first
    acc = jnp.zeros((capacity, rows_ref.shape[2]), f32)
    for image in range(IMG_MB):
        slots = slots_ref[image]
        holds = (slots[:, 0:1] == column) | (slots[:, 1:2] == column)
        acc = acc + t_dot(holds.astype(f32).astype(bf16), rows_ref[image])
    out_ref[0] = acc.astype(bf16)


def dispatch(slots, rows, group, experts, capacity):
    seq, features = rows.shape[1:]
    return pl.pallas_call(
        functools.partial(dispatch_kernel, capacity),
        grid=(experts,),
        in_specs=[
            pl.BlockSpec((IMG_MB, seq, TOP), lambda e: (group, 0, 0)),
            pl.BlockSpec((IMG_MB, seq, features), lambda e: (group, 0, 0)),
        ],
        out_specs=pl.BlockSpec((1, capacity, features), lambda e: (e, 0, 0)),
        out_shape=jax.ShapeDtypeStruct((experts, capacity, features), bf16),
        compiler_params=params(("arbitrary",)),
        cost_estimate=pl.CostEstimate(
            flops=2 * experts * capacity * IMG_MB * seq * features,
            bytes_accessed=2 * features * (experts * capacity + IMG_MB * seq),
            transcendentals=0,
        ),
        name="dispatch",
    )(slots, rows)


def attend_kernel(
    experts, x_ref, routes_ref, win_ref, wout_ref, small_ref,
    proj_ref, mixed_ref, residual_ref, hidden_ref, gates_ref,
):
    features = x_ref.shape[2]
    image = x_ref[0].astype(f32)
    vectors = small_ref[...].astype(f32)
    normed, _ = norm_forward(image)
    attn_input = (
        normed * vectors[experts : experts + 1] + vectors[experts + 1 : experts + 2]
    ).astype(bf16)
    proj_ref[0] = dot(attn_input, win_ref[...]).astype(bf16)
    low_half = lax.broadcasted_iota(jnp.int32, (1, LANES), 1) < HEAD_DIM
    for pair in range(features // LANES):
        first = pair * LANES
        queries = proj_ref[0, :, first : first + LANES]
        keys = proj_ref[0, :, features + first : features + first + LANES]
        values = proj_ref[0, :, 2 * features + first : 2 * features + first + LANES]
        out = None
        for half in range(2):
            keep = low_half if half == 0 else jnp.logical_not(low_half)
            scores = dot_t(
                jnp.where(keep, queries * HEAD_DIM ** (-0.5), 0).astype(bf16), keys
            )
            top = jnp.max(scores, axis=-1, keepdims=True)
            raised = jnp.exp(scores - top)
            share = 1.0 / jnp.sum(raised, axis=-1, keepdims=True)
            weights = (raised * share).astype(bf16)
            part = dot(weights, jnp.where(keep, values, 0).astype(bf16))
            out = part if out is None else out + part
        mixed_ref[0, :, first : first + LANES] = out.astype(bf16)
    residual = image + dot(mixed_ref[0], wout_ref[...])
    residual_ref[0] = residual
    normed, _ = norm_forward(residual)
    hidden = (
        normed * vectors[experts + 2 : experts + 3] + vectors[experts + 3 : experts + 4]
    ).astype(bf16)
    hidden_ref[0] = hidden
    probs = softmax_lanes(dot_t(hidden, small_ref[...]), experts)
    lane = lax.broadcasted_iota(jnp.int32, probs.shape, 1)
    routes = routes_ref[0]
    for choice in range(TOP):
        gates_ref[0, :, choice : choice + 1] = jnp.sum(
            jnp.where(lane == routes[:, choice : choice + 1], probs, 0.0),
            axis=1,
            keepdims=True,
        )


def attend(images, routes, attn_in, attn_out, small, experts, group):
    seq, features = images.shape[1:]
    wide = attn_in.shape[1]
    first = group * IMG_MB

    def rows(width):
        return pl.BlockSpec((1, seq, width), lambda i: (i, 0, 0))

    def source(width):
        return pl.BlockSpec((1, seq, width), lambda i: (first + i, 0, 0))

    def whole(array):
        return pl.BlockSpec(array.shape, lambda i: (0, 0))

    def out(width, dtype):
        return jax.ShapeDtypeStruct((IMG_MB, seq, width), dtype)

    return pl.pallas_call(
        functools.partial(attend_kernel, experts),
        grid=(IMG_MB,),
        in_specs=[
            source(features),
            source(TOP),
            whole(attn_in),
            whole(attn_out),
            whole(small),
        ],
        out_specs=[rows(wide), rows(features), rows(features), rows(features), rows(TOP)],
        out_shape=[
            out(wide, bf16),
            out(features, bf16),
            out(features, f32),
            out(features, bf16),
            out(TOP, f32),
        ],
        compiler_params=params(("arbitrary",)),
        cost_estimate=pl.CostEstimate(
            flops=IMG_MB * seq * 16 * features * features,
            bytes_accessed=4 * features * (4 * features + IMG_MB * seq * 8),
            transcendentals=IMG_MB * HEADS * seq * seq,
        ),
        name="attend",
    )(images, routes, attn_in, attn_out, small)


def expert_kernel(
    experts, chunk, add, mine_ref, x_ref, g_ref, w1_ref, w2_ref, bias_ref, small_ref, *refs
):
    if add:
        old_w1_ref, old_w2_ref, old_bias_ref, old_router_ref = refs[:4]
        refs = refs[4:]
    (
        result_ref, dx_ref, dw1_ref, dw2_ref, dbias_ref, drouter_ref,
        result_acc, dx_acc, dr_ref, probs_ref, act_ref, pre_ref,
    ) = refs
    step = pl.program_id(0)
    last = pl.num_programs(0) - 1
    rows = x_ref.shape[0]
    mine = mine_ref[0]
    chunks = rows // chunk

    @pl.when(step == 0)
    def _():
        for index in range(chunks):
            at = pl.ds(index * chunk, chunk)
            probs = softmax_lanes(dot_t(x_ref[at, :], small_ref[...]), experts)
            lane = lax.broadcasted_iota(jnp.int32, probs.shape, 1)
            probs_ref[at, :] = probs
            gate = jnp.sum(jnp.where(lane == mine, probs, 0.0), axis=1, keepdims=True)
            dr_ref[at, :] = (gate * g_ref[at, :].astype(f32)).astype(bf16)
            result_acc[at, :] = jnp.zeros((chunk, x_ref.shape[1]), f32)
            dx_acc[at, :] = jnp.zeros((chunk, x_ref.shape[1]), f32)

    w1 = w1_ref[...]
    w2 = w2_ref[...]
    bias = bias_ref[...].astype(f32)
    dbias = jnp.zeros(bias.shape, f32)
    for index in range(chunks):
        at = pl.ds(index * chunk, chunk)
        act, slope = gelu_both(dot_t(x_ref[at, :], w1) + bias)
        act = act.astype(bf16)
        act_ref[at, :] = act
        result_acc[at, :] += dot(act, w2)
        grad_pre = (dot_t(dr_ref[at, :], w2) * slope).astype(bf16)
        pre_ref[at, :] = grad_pre
        dbias = dbias + jnp.sum(grad_pre.astype(f32), axis=0, keepdims=True)
        dx_acc[at, :] += dot(grad_pre, w1)
    dw1 = t_dot(pre_ref[...], x_ref[...])
    dw2 = t_dot(act_ref[...], dr_ref[...])
    if add:
        dw1 = dw1 + old_w1_ref[...]
        dw2 = dw2 + old_w2_ref[...]
        dbias = dbias + old_bias_ref[...]
    dw1_ref[...] = dw1.astype(dw1_ref.dtype)
    dw2_ref[...] = dw2.astype(dw2_ref.dtype)
    dbias_ref[...] = dbias

    @pl.when(step == last)
    def _():
        drouter = jnp.zeros(drouter_ref.shape, f32)
        if add:
            drouter = old_router_ref[...]
        for index in range(chunks):
            at = pl.ds(index * chunk, chunk)
            result = result_acc[at, :].astype(bf16)
            result_ref[at, :] = result
            grad_gate = jnp.sum(
                g_ref[at, :].astype(f32) * result.astype(f32), axis=1, keepdims=True
            )
            probs = probs_ref[at, :]
            lane = lax.broadcasted_iota(jnp.int32, probs.shape, 1)
            chosen = lane == mine
            gate = jnp.sum(jnp.where(chosen, probs, 0.0), axis=1, keepdims=True)
            logits = (grad_gate * gate) * (chosen.astype(f32) - probs)
            high = logits.astype(bf16)
            low = (logits - high.astype(f32)).astype(bf16)
            dx_ref[at, :] = (
                dx_acc[at, :] + dot(high, small_ref[...]) + dot(low, small_ref[...])
            ).astype(bf16)
            drouter = drouter + t_dot(high, x_ref[at, :]) + t_dot(low, x_ref[at, :])
        drouter_ref[...] = drouter


def row_chunk(rows):
    best = rows
    for size in range(16, 513, 16):
        if rows % size == 0:
            best = size
    return best


def expert_block(mine, x, g, w1, w2, bias, small, experts, old):
    rows, features = x.shape
    hidden_units = w1.shape[0]
    block = 256
    steps = hidden_units // block
    chunk = row_chunk(rows)
    add = old is not None
    out_type = bf16 if add else f32

    def whole(shape):
        return pl.BlockSpec(shape, lambda s: (0,) * len(shape))

    units = pl.BlockSpec((block, features), lambda s: (s, 0))
    unit_row = pl.BlockSpec((1, block), lambda s: (0, s))
    in_specs = [
        pl.BlockSpec(memory_space=pltpu.SMEM),
        whole(x.shape),
        whole(g.shape),
        units,
        units,
        unit_row,
        whole(small.shape),
    ]
    operands = [mine, x, g, w1, w2, bias, small]
    if add:
        in_specs += [units, units, unit_row, whole(small.shape)]
        operands += list(old)
    return pl.pallas_call(
        functools.partial(expert_kernel, experts, chunk, add),
        grid=(steps,),
        in_specs=in_specs,
        out_specs=[
            whole(x.shape), whole(x.shape), units, units, unit_row, whole(small.shape)
        ],
        out_shape=[
            jax.ShapeDtypeStruct(x.shape, bf16),
            jax.ShapeDtypeStruct(x.shape, bf16),
            jax.ShapeDtypeStruct(w1.shape, out_type),
            jax.ShapeDtypeStruct(w2.shape, out_type),
            jax.ShapeDtypeStruct((1, hidden_units), f32),
            jax.ShapeDtypeStruct(small.shape, f32),
        ],
        scratch_shapes=[
            pltpu.VMEM((rows, features), f32),
            pltpu.VMEM((rows, features), f32),
            pltpu.VMEM((rows, features), bf16),
            pltpu.VMEM((rows, small.shape[0]), f32),
            pltpu.VMEM((rows, block), bf16),
            pltpu.VMEM((rows, block), bf16),
        ],
        compiler_params=params(("arbitrary",)),
        cost_estimate=pl.CostEstimate(
            flops=12 * rows * features * hidden_units,
            bytes_accessed=(8 * rows + 12 * hidden_units) * features,
            transcendentals=rows * hidden_units,
        ),
        name="expert_block",
    )(*operands)


def combine_kernel(slots_ref, gates_ref, residual_ref, returned_ref, out_ref):
    seq = slots_ref.shape[1]
    total = returned_ref.shape[0]
    column = lax.broadcasted_iota(jnp.int32, (seq, total), 1)
    slots = slots_ref[0]
    gates = gates_ref[0]
    value = residual_ref[0]
    mix = None
    for choice in range(TOP):
        holds = slots[:, choice : choice + 1] == column
        picked = dot(holds.astype(f32).astype(bf16), returned_ref[...])
        part = gates[:, choice : choice + 1] * picked
        mix = part if mix is None else mix + part
    out_ref[0] = (value + mix).astype(bf16)


def combine(slots, gates, residual, returned, group):
    seq, features = residual.shape[1:]
    first = group * IMG_MB
    return pl.pallas_call(
        combine_kernel,
        grid=(IMG_MB,),
        in_specs=[
            pl.BlockSpec((1, seq, TOP), lambda i: (first + i, 0, 0)),
            pl.BlockSpec((1, seq, TOP), lambda i: (i, 0, 0)),
            pl.BlockSpec((1, seq, features), lambda i: (i, 0, 0)),
            pl.BlockSpec(returned.shape, lambda i: (0, 0)),
        ],
        out_specs=pl.BlockSpec((1, seq, features), lambda i: (i, 0, 0)),
        out_shape=jax.ShapeDtypeStruct(residual.shape, bf16),
        compiler_params=params(("arbitrary",)),
        cost_estimate=pl.CostEstimate(
            flops=4 * IMG_MB * seq * returned.shape[0] * features,
            bytes_accessed=2 * features * (returned.shape[0] + 3 * IMG_MB * seq),
            transcendentals=0,
        ),
        name="combine",
    )(slots, gates, residual, returned)


def attend_back_kernel(
    experts, add, x_ref, top_ref, slots_ref, sent_ref, proj_ref, mixed_ref, residual_ref,
    win_ref, wout_ref, small_ref, *refs
):
    if add:
        old_in_ref, old_out_ref, old_small_ref = refs[:3]
        refs = refs[3:]
    (grad_x_ref, dwin_ref, dwout_ref, dsmall_ref, acc_in, acc_out, acc_small, dproj_ref) = refs
    features = x_ref.shape[2]
    seq = x_ref.shape[1]
    step = pl.program_id(0)
    vectors = small_ref[...].astype(f32)

    @pl.when(step == 0)
    def _():
        if add:
            acc_in[...] = old_in_ref[...]
            acc_out[...] = old_out_ref[...]
            acc_small[...] = old_small_ref[...]
        else:
            acc_in[...] = jnp.zeros(acc_in.shape, f32)
            acc_out[...] = jnp.zeros(acc_out.shape, f32)
            acc_small[...] = jnp.zeros(acc_small.shape, f32)

    column = lax.broadcasted_iota(jnp.int32, (seq, sent_ref.shape[0]), 1)
    slots = slots_ref[0]
    holds = (slots[:, 0:1] == column) | (slots[:, 1:2] == column)
    grad_hidden = dot(holds.astype(f32).astype(bf16), sent_ref[...])
    normed_two, inverse_two = norm_forward(residual_ref[0])
    acc_small[2:3, :] += jnp.sum(grad_hidden * normed_two, axis=0, keepdims=True)
    acc_small[3:4, :] += jnp.sum(grad_hidden, axis=0, keepdims=True)
    grad_residual = top_ref[0].astype(f32) + norm_backward(
        grad_hidden * vectors[experts + 2 : experts + 3], normed_two, inverse_two
    )
    grad_branch = grad_residual.astype(bf16)
    acc_out[...] += t_dot(mixed_ref[0], grad_branch)
    grad_mixed = dot_t(grad_branch, wout_ref[...]).astype(bf16)
    low_half = lax.broadcasted_iota(jnp.int32, (1, LANES), 1) < HEAD_DIM
    scale = HEAD_DIM ** (-0.5)
    for pair in range(features // LANES):
        first = pair * LANES
        queries = proj_ref[0, :, first : first + LANES]
        keys = proj_ref[0, :, features + first : features + first + LANES]
        values = proj_ref[0, :, 2 * features + first : 2 * features + first + LANES]
        grad_out = grad_mixed[:, first : first + LANES]
        sums = [None, None, None]
        for half in range(2):
            keep = low_half if half == 0 else jnp.logical_not(low_half)
            head_queries = jnp.where(keep, queries * scale, 0).astype(bf16)
            head_keys = jnp.where(keep, keys, 0).astype(bf16)
            head_grad = jnp.where(keep, grad_out, 0).astype(bf16)
            scores = dot_t(keys, head_queries)
            top = jnp.max(scores, axis=0, keepdims=True)
            raised = jnp.exp(scores - top)
            probs = raised * (1.0 / jnp.sum(raised, axis=0, keepdims=True))
            grad_values = dot(probs.astype(bf16), head_grad)
            grad_weights = dot_t(values, head_grad)
            inner = jnp.sum(grad_weights * probs, axis=0, keepdims=True)
            grad_scores = (probs * (grad_weights - inner)).astype(bf16)
            grad_keys = dot(grad_scores, head_queries)
            grad_queries = t_dot(grad_scores, head_keys)
            for place, part in enumerate((grad_queries, grad_keys, grad_values)):
                sums[place] = part if half == 0 else sums[place] + part
        dproj_ref[:, first : first + LANES] = (sums[0] * scale).astype(bf16)
        dproj_ref[:, features + first : features + first + LANES] = sums[1].astype(bf16)
        dproj_ref[:, 2 * features + first : 2 * features + first + LANES] = sums[2].astype(bf16)
    normed_one, inverse_one = norm_forward(x_ref[0].astype(f32))
    attn_input = (
        normed_one * vectors[experts : experts + 1] + vectors[experts + 1 : experts + 2]
    ).astype(bf16)
    acc_in[...] += t_dot(attn_input, dproj_ref[...])
    grad_input = dot_t(dproj_ref[...], win_ref[...])
    acc_small[0:1, :] += jnp.sum(grad_input * normed_one, axis=0, keepdims=True)
    acc_small[1:2, :] += jnp.sum(grad_input, axis=0, keepdims=True)
    grad_x_ref[0] = grad_residual + norm_backward(
        grad_input * vectors[experts : experts + 1], normed_one, inverse_one
    )

    @pl.when(step == pl.num_programs(0) - 1)
    def _():
        dwin_ref[...] = acc_in[...].astype(dwin_ref.dtype)
        dwout_ref[...] = acc_out[...].astype(dwout_ref.dtype)
        dsmall_ref[...] = acc_small[...]


def attend_back(
    images, out_grad, slots, sent, proj, mixed, residual, attn_in, attn_out, small,
    experts, group, old,
):
    seq, features = images.shape[1:]
    wide = attn_in.shape[1]
    first = group * IMG_MB
    add = old is not None
    out_type = bf16 if add else f32

    def rows(width):
        return pl.BlockSpec((1, seq, width), lambda i: (i, 0, 0))

    def source(width):
        return pl.BlockSpec((1, seq, width), lambda i: (first + i, 0, 0))

    def whole(shape):
        return pl.BlockSpec(shape, lambda i: (0, 0))

    small_grads = (8, features)
    in_specs = [
        source(features), source(features), source(TOP), whole(sent.shape),
        rows(wide), rows(features), rows(features),
        whole(attn_in.shape), whole(attn_out.shape), whole(small.shape),
    ]
    operands = [
        images, out_grad, slots, sent, proj, mixed, residual, attn_in, attn_out, small
    ]
    if add:
        in_specs += [whole(attn_in.shape), whole(attn_out.shape), whole(small_grads)]
        operands += list(old)
    return pl.pallas_call(
        functools.partial(attend_back_kernel, experts, add),
        grid=(IMG_MB,),
        in_specs=in_specs,
        out_specs=[
            rows(features), whole(attn_in.shape), whole(attn_out.shape), whole(small_grads)
        ],
        out_shape=[
            jax.ShapeDtypeStruct((IMG_MB, seq, features), f32),
            jax.ShapeDtypeStruct(attn_in.shape, out_type),
            jax.ShapeDtypeStruct(attn_out.shape, out_type),
            jax.ShapeDtypeStruct(small_grads, f32),
        ],
        scratch_shapes=[
            pltpu.VMEM(attn_in.shape, f32),
            pltpu.VMEM(attn_out.shape, f32),
            pltpu.VMEM(small_grads, f32),
            pltpu.VMEM((seq, wide), bf16),
        ],
        compiler_params=params(("arbitrary",)),
        cost_estimate=pl.CostEstimate(
            flops=IMG_MB * seq * 40 * features * features,
            bytes_accessed=8 * features * (4 * features + IMG_MB * seq * 4),
            transcendentals=IMG_MB * HEADS * seq * seq,
        ),
        name="attend_back",
    )(*operands)


def per_device(
    images, first_gain, first_shift, attn_in, attn_out, second_gain, second_shift, router,
    expert_in, expert_bias, expert_out, routes, out_grad,
):
    features = images.shape[2]
    experts = router.shape[1]
    tok_mb = IMG_MB * SEQ
    capacity = max(2, (5 * TOP * tok_mb // (4 * experts) + 7) // 8 * 8)
    slot_rows = experts * capacity
    micro = images.shape[0] // IMG_MB
    small_rows = (experts + 4 + 15) // 16 * 16

    small = jnp.concatenate(
        [
            router.T,
            first_gain[None],
            first_shift[None],
            second_gain[None],
            second_shift[None],
            jnp.zeros((small_rows - experts - 4, router.shape[0]), bf16),
        ],
        axis=0,
    )
    small = lax.all_gather(small, "dp", axis=1, tiled=True)
    attn_in_full = lax.all_gather(attn_in, "dp", axis=0, tiled=True)
    attn_out_full = lax.all_gather(attn_out, "dp", axis=0, tiled=True)
    weight_in = lax.all_gather(expert_in[0], "dp", axis=0, tiled=True)
    weight_out = lax.all_gather(expert_out[0], "dp", axis=0, tiled=True)
    bias_row = lax.all_gather(expert_bias, "dp", axis=1, tiled=True)
    mine = lax.axis_index("expert").astype(jnp.int32)[None]

    def exchange(rows):
        return lax.all_to_all(
            rows.reshape(experts, capacity, features),
            "expert",
            split_axis=0,
            concat_axis=0,
            tiled=True,
        )

    slots = route(routes, experts, capacity)
    grads = [
        exchange(dispatch(slots, out_grad, group, experts, capacity)).reshape(slot_rows, features)
        for group in range(micro)
    ]
    saved = []
    received = []
    for group in range(micro):
        proj, mixed, residual, hidden, gates = attend(
            images, routes, attn_in_full, attn_out_full, small, experts, group
        )
        saved.append((proj, mixed, residual, gates))
        rows = dispatch(slots[group * IMG_MB : (group + 1) * IMG_MB], hidden, 0, experts, capacity)
        received.append(exchange(rows).reshape(slot_rows, features))
    old = None
    returned = []
    sent = []
    for group in range(micro):
        result, dx, *old = expert_block(
            mine, received[group], grads[group], weight_in, weight_out, bias_row, small,
            experts, old,
        )
        sent.append(exchange(dx).reshape(slot_rows, features))
        returned.append(exchange(result).reshape(slot_rows, features))
    dw1, dw2, dbias, drouter = old
    old = None
    grad_blocks = []
    out_blocks = []
    for group in range(micro):
        proj, mixed, residual, gates = saved[group]
        grad_x, *old = attend_back(
            images, out_grad, slots, sent[group], proj, mixed, residual, attn_in_full,
            attn_out_full, small, experts, group, old,
        )
        grad_blocks.append(grad_x)
        out_blocks.append(combine(slots, gates, residual, returned[group], group))
    dwin, dwout, dsmall = old

    def scatter(value, axis):
        return lax.psum_scatter(value, "dp", scatter_dimension=axis, tiled=True)

    grad_expert_in = scatter(dw1, 0).astype(f32)[None]
    grad_expert_out = scatter(dw2, 0).astype(f32)[None]
    grad_expert_bias = scatter(dbias.astype(bf16), 1).astype(f32)
    little = scatter(jnp.concatenate([dsmall, drouter], axis=0).astype(bf16), 1)
    grad_attn_in = lax.psum(scatter(dwin, 0), "expert").astype(f32)
    grad_attn_out = lax.psum(scatter(dwout, 0), "expert").astype(f32)
    little = lax.psum(little, "expert").astype(f32)
    return (
        jnp.concatenate(out_blocks, axis=0),
        jnp.concatenate(grad_blocks, axis=0),
        little[0],
        little[1],
        grad_attn_in,
        grad_attn_out,
        little[2],
        little[3],
        little[8 : 8 + experts].T,
        grad_expert_in,
        grad_expert_bias,
        grad_expert_out,
    )


def solution(mesh):
    return jax.shard_map(
        per_device,
        mesh=mesh,
        in_specs=(
            P(("dp", "expert"), None, None),
            P("dp"),
            P("dp"),
            P("dp", None),
            P("dp", None),
            P("dp"),
            P("dp"),
            P("dp", None),
            P("expert", "dp", None),
            P("expert", "dp"),
            P("expert", "dp", None),
            P(("dp", "expert"), None, None),
            P(("dp", "expert"), None, None),
        ),
        out_specs=(
            P(("dp", "expert"), None, None),
            P(("dp", "expert"), None, None),
            P("dp"),
            P("dp"),
            P("dp", None),
            P("dp", None),
            P("dp"),
            P("dp"),
            P("dp", None),
            P("expert", "dp", None),
            P("expert", "dp"),
            P("expert", "dp", None),
        ),
        check_vma=False,
    )
```

```python
import functools

import jax
import jax.numpy as jnp
from jax import lax
from jax.experimental import pallas as pl
from jax.experimental.pallas import tpu as pltpu
from jax.sharding import PartitionSpec as P

HEADS = 12
HEAD_DIM = 64
SEQ = 197
MICRO = 2
IMG_MB = 3
TOP = 2
LANES = 128
VMEM_LIMIT = 60 * 1024 * 1024

epsilon = 1e-06
f32 = jnp.float32
bf16 = jnp.bfloat16


def params(semantics, **more):
    return pltpu.CompilerParams(
        dimension_semantics=semantics, vmem_limit_bytes=VMEM_LIMIT, **more
    )


def dot(left, right):
    return lax.dot_general(
        left, right, (((1,), (0,)), ((), ())), preferred_element_type=f32
    )


def dot_t(left, right):
    return lax.dot_general(
        left, right, (((1,), (1,)), ((), ())), preferred_element_type=f32
    )


def t_dot(left, right):
    return lax.dot_general(
        left, right, (((0,), (0,)), ((), ())), preferred_element_type=f32
    )


def norm_forward(values):
    row_mean = jnp.mean(values, axis=-1, keepdims=True)
    centred = values - row_mean
    row_var = jnp.mean(centred * centred, axis=-1, keepdims=True)
    inverse = lax.rsqrt(row_var + epsilon)
    return centred * inverse, inverse


def norm_backward(grad_normed, normed, inverse):
    mean_grad = jnp.mean(grad_normed, axis=-1, keepdims=True)
    mean_cross = jnp.mean(grad_normed * normed, axis=-1, keepdims=True)
    return inverse * (grad_normed - mean_grad - normed * mean_cross)


def softmax_lanes(logits, count):
    lane = lax.broadcasted_iota(jnp.int32, logits.shape, 1)
    masked = jnp.where(lane < count, logits, -1e30)
    top = jnp.max(masked, axis=-1, keepdims=True)
    raised = jnp.where(lane < count, jnp.exp(masked - top), 0.0)
    return raised / jnp.sum(raised, axis=-1, keepdims=True)


def gelu_both(values):
    size = jnp.abs(values)
    bell = jnp.exp(values * values * -0.5)
    t = 1.0 / (1.0 + (0.3275911 * 0.7071067811865476) * size)
    tail = t * (
        0.5 * 0.254829592
        + t
        * (
            0.5 * -0.284496736
            + t * (0.5 * 1.421413741 + t * (0.5 * -1.453152027 + t * (0.5 * 1.061405429)))
        )
    )
    tail = tail * bell
    phi = jnp.where(values >= 0, 1.0 - tail, tail)
    return values * phi, phi + values * (0.3989422804014327 * bell)


class Rides:
    def __init__(self, arrays):
        self.arrays = list(arrays)
        self.parts = arrays[0].shape[0]
        self.in_specs = [pl.BlockSpec(memory_space=pl.ANY)] * len(arrays)
        self.out_shape = [jax.ShapeDtypeStruct(a.shape, a.dtype) for a in arrays]
        self.scratch = [
            pltpu.SemaphoreType.DMA((self.parts,)),
            pltpu.SemaphoreType.DMA((self.parts,)),
            pltpu.SemaphoreType.DMA,
        ] * len(arrays)

    def copies(self, refs, offset):
        me = lax.axis_index("expert")
        peer = lax.rem(me + offset, self.parts)
        sources, targets, sems = refs
        return [
            pltpu.make_async_remote_copy(
                src_ref=source.at[peer],
                dst_ref=target.at[me],
                send_sem=sems[3 * index].at[offset],
                recv_sem=sems[3 * index + 1].at[offset],
                device_id={"expert": peer},
                device_id_type=pl.DeviceIdType.MESH,
            )
            for index, (source, target) in enumerate(zip(sources, targets))
        ]

    def own(self, refs):
        me = lax.axis_index("expert")
        sources, targets, sems = refs
        return [
            pltpu.make_async_copy(source.at[me], target.at[me], sems[3 * index + 2])
            for index, (source, target) in enumerate(zip(sources, targets))
        ]

    def start(self, refs, more=()):
        me = lax.axis_index("expert")
        barrier = pltpu.get_barrier_semaphore()
        for peer in more:
            pl.semaphore_signal(
                barrier, inc=1, device_id=peer, device_id_type=pl.DeviceIdType.MESH
            )

        @pl.loop(1, self.parts)
        def _(offset):
            pl.semaphore_signal(
                barrier,
                inc=1,
                device_id={"expert": lax.rem(me + offset, self.parts)},
                device_id_type=pl.DeviceIdType.MESH,
            )

        pl.semaphore_wait(barrier, self.parts - 1 + len(more))

        @pl.loop(1, self.parts)
        def _(offset):
            for copy in self.copies(refs, offset):
                copy.start()

        for copy in self.own(refs):
            copy.start()

    def finish(self, refs):
        for copy in self.own(refs):
            copy.wait()

        @pl.loop(1, self.parts)
        def _(offset):
            for copy in self.copies(refs, offset):
                copy.wait()


def route_kernel(experts, capacity, routes_ref, slots_ref, lines_ref):
    seq = routes_ref.shape[1]
    row = lax.broadcasted_iota(jnp.int32, (seq, seq), 0)
    col = lax.broadcasted_iota(jnp.int32, (seq, seq), 1)
    earlier = (col < row).astype(f32).astype(bf16)
    lane = lax.broadcasted_iota(jnp.int32, (seq, LANES), 1)
    groups = routes_ref.shape[0] // IMG_MB
    for group in range(groups):
        base = jnp.zeros((1, LANES), f32)
        table = jnp.full((seq, LANES), -1.0, f32)
        for choice in range(TOP):
            for image in range(IMG_MB):
                index = group * IMG_MB + image
                named = routes_ref[index][:, choice : choice + 1]
                onehot = (lane == named).astype(f32)
                count = dot(earlier, onehot.astype(bf16)) + base
                position = jnp.sum(onehot * count, axis=1, keepdims=True).astype(jnp.int32)
                base = base + jnp.sum(onehot, axis=0, keepdims=True)
                slot = jnp.where(position < capacity, named * capacity + position, -1)
                slots_ref[index, :, choice : choice + 1] = slot
                table = jnp.where(lane == image * TOP + choice, slot.astype(f32), table)
        lines_ref[group] = table.T[: lines_ref.shape[1]].astype(jnp.int32)


def route(routes, experts, capacity):
    return pl.pallas_call(
        functools.partial(route_kernel, experts, capacity),
        out_shape=[
            jax.ShapeDtypeStruct(routes.shape, jnp.int32),
            jax.ShapeDtypeStruct((routes.shape[0] // IMG_MB, 8, routes.shape[1]), jnp.int32),
        ],
        compiler_params=pltpu.CompilerParams(vmem_limit_bytes=VMEM_LIMIT),
        cost_estimate=pl.CostEstimate(
            flops=10**8, bytes_accessed=2 * 10**6, transcendentals=0
        ),
        name="route",
    )(routes)


def dispatch_kernel(capacity, lines_ref, rows_ref, out_ref):
    first = pl.program_id(0) * capacity
    seq = rows_ref.shape[1]
    slot = lax.broadcasted_iota(jnp.int32, (capacity, seq), 0) + first
    lines = lines_ref[0]
    acc = jnp.zeros((capacity, rows_ref.shape[2]), f32)
    for image in range(IMG_MB):
        at = image * TOP
        holds = (lines[at : at + 1] == slot) | (lines[at + 1 : at + 2] == slot)
        acc = acc + dot(holds.astype(f32).astype(bf16), rows_ref[image])
    out_ref[0] = acc.astype(bf16)


def dispatch(lines, rows, group, experts, capacity):
    seq, features = rows.shape[1:]
    block = group if rows.shape[0] > IMG_MB else 0
    return pl.pallas_call(
        functools.partial(dispatch_kernel, capacity),
        grid=(experts,),
        in_specs=[
            pl.BlockSpec((1, 8, seq), lambda e: (group, 0, 0)),
            pl.BlockSpec((IMG_MB, seq, features), lambda e: (block, 0, 0)),
        ],
        out_specs=pl.BlockSpec((1, capacity, features), lambda e: (e, 0, 0)),
        out_shape=jax.ShapeDtypeStruct((experts, capacity, features), bf16),
        compiler_params=params(("arbitrary",)),
        cost_estimate=pl.CostEstimate(
            flops=2 * experts * capacity * IMG_MB * seq * features,
            bytes_accessed=2 * features * (experts * capacity + IMG_MB * seq),
            transcendentals=0,
        ),
        name="dispatch",
    )(lines, rows)


def attend_kernel(
    experts, x_ref, routes_ref, dense_ref, small_ref,
    proj_ref, mixed_ref, residual_ref, hidden_ref, gates_ref,
):
    features = x_ref.shape[2]
    image = x_ref[0].astype(f32)
    vectors = small_ref[...].astype(f32)
    normed, _ = norm_forward(image)
    attn_input = (
        normed * vectors[experts : experts + 1] + vectors[experts + 1 : experts + 2]
    ).astype(bf16)
    proj_ref[0] = dot(attn_input, dense_ref[:, : 3 * features]).astype(bf16)
    low_half = lax.broadcasted_iota(jnp.int32, (1, LANES), 1) < HEAD_DIM
    for pair in range(features // LANES):
        first = pair * LANES
        queries = proj_ref[0, :, first : first + LANES]
        keys = proj_ref[0, :, features + first : features + first + LANES]
        values = proj_ref[0, :, 2 * features + first : 2 * features + first + LANES]
        out = None
        for half in range(2):
            keep = low_half if half == 0 else jnp.logical_not(low_half)
            scores = dot_t(
                jnp.where(keep, queries * HEAD_DIM ** (-0.5), 0).astype(bf16), keys
            )
            top = jnp.max(scores, axis=-1, keepdims=True)
            raised = jnp.exp(scores - top)
            share = 1.0 / jnp.sum(raised, axis=-1, keepdims=True)
            weights = (raised * share).astype(bf16)
            part = dot(weights, jnp.where(keep, values, 0).astype(bf16))
            out = part if out is None else out + part
        mixed_ref[0, :, first : first + LANES] = out.astype(bf16)
    residual = image + dot(mixed_ref[0], dense_ref[:, 3 * features :])
    residual_ref[0] = residual
    normed, _ = norm_forward(residual)
    hidden = (
        normed * vectors[experts + 2 : experts + 3] + vectors[experts + 3 : experts + 4]
    ).astype(bf16)
    hidden_ref[0] = hidden
    probs = softmax_lanes(dot_t(hidden, small_ref[...]), experts)
    lane = lax.broadcasted_iota(jnp.int32, probs.shape, 1)
    routes = routes_ref[0]
    for choice in range(TOP):
        gates_ref[0, :, choice : choice + 1] = jnp.sum(
            jnp.where(lane == routes[:, choice : choice + 1], probs, 0.0),
            axis=1,
            keepdims=True,
        )


def attend(images, routes, dense, small, experts, group):
    seq, features = images.shape[1:]
    wide = 3 * features
    first = group * IMG_MB

    def rows(width):
        return pl.BlockSpec((1, seq, width), lambda i: (i, 0, 0))

    def source(width):
        return pl.BlockSpec((1, seq, width), lambda i: (first + i, 0, 0))

    def whole(array):
        return pl.BlockSpec(array.shape, lambda i: (0, 0))

    def out(width, dtype):
        return jax.ShapeDtypeStruct((IMG_MB, seq, width), dtype)

    return pl.pallas_call(
        functools.partial(attend_kernel, experts),
        grid=(IMG_MB,),
        in_specs=[
            source(features),
            source(TOP),
            whole(dense),
            whole(small),
        ],
        out_specs=[rows(wide), rows(features), rows(features), rows(features), rows(TOP)],
        out_shape=[
            out(wide, bf16),
            out(features, bf16),
            out(features, f32),
            out(features, bf16),
            out(TOP, f32),
        ],
        compiler_params=params(("arbitrary",)),
        cost_estimate=pl.CostEstimate(
            flops=IMG_MB * seq * 16 * features * features,
            bytes_accessed=4 * features * (4 * features + IMG_MB * seq * 8),
            transcendentals=IMG_MB * HEADS * seq * seq,
        ),
        name="attend",
    )(images, routes, dense, small)


def expert_kernel(
    experts, chunk, add, rides, x_ref, g_ref, w1_ref, w2_ref, bias_ref, small_ref, *refs
):
    if add:
        old_w_ref, old_router_ref = refs[:2]
        refs = refs[2:]
    count = len(rides.arrays)
    ride_refs = (refs[:count], refs[count + 4 : 2 * count + 4], refs[2 * count + 10 :])
    refs = refs[count : count + 4] + refs[2 * count + 4 : 2 * count + 10]
    (
        result_ref, dx_ref, dw_ref, drouter_ref,
        result_acc, dx_acc, dr_ref, probs_ref, act_ref, pre_ref,
    ) = refs
    step = pl.program_id(0)
    last = pl.num_programs(0) - 1
    rows = x_ref.shape[0]
    mine = lax.axis_index("expert")
    chunks = rows // chunk

    @pl.when(step == 0)
    def _():
        rides.start(ride_refs)

    @pl.when(step == 0)
    def _():
        for index in range(chunks):
            at = pl.ds(index * chunk, chunk)
            probs = softmax_lanes(dot_t(x_ref[at, :], small_ref[...]), experts)
            lane = lax.broadcasted_iota(jnp.int32, probs.shape, 1)
            probs_ref[at, :] = probs
            gate = jnp.sum(jnp.where(lane == mine, probs, 0.0), axis=1, keepdims=True)
            dr_ref[at, :] = (gate * g_ref[at, :].astype(f32)).astype(bf16)
            result_acc[at, :] = jnp.zeros((chunk, x_ref.shape[1]), f32)
            dx_acc[at, :] = jnp.zeros((chunk, x_ref.shape[1]), f32)

    w1 = w1_ref[...]
    w2 = w2_ref[...]
    bias = bias_ref[...].astype(f32)
    dbias = jnp.zeros(bias.shape, f32)
    for index in range(chunks):
        at = pl.ds(index * chunk, chunk)
        act, slope = gelu_both(dot_t(x_ref[at, :], w1) + bias)
        act = act.astype(bf16)
        act_ref[at, :] = act
        result_acc[at, :] += dot(act, w2)
        grad_pre = (dot_t(dr_ref[at, :], w2) * slope).astype(bf16)
        pre_ref[at, :] = grad_pre
        dbias = dbias + jnp.sum(grad_pre.astype(f32), axis=0, keepdims=True)
        dx_acc[at, :] += dot(grad_pre, w1)
    dw1 = t_dot(pre_ref[...], x_ref[...])
    dw2 = t_dot(act_ref[...], dr_ref[...])
    dbias = jnp.broadcast_to(dbias, (LANES, dbias.shape[1])).T
    first = 0
    for part in (dw1, dw2, dbias):
        at = pl.ds(first, part.shape[1])
        if add:
            part = part + old_w_ref[:, at]
        dw_ref[:, at] = part.astype(dw_ref.dtype)
        first += part.shape[1]

    @pl.when(step == last)
    def _():
        drouter = jnp.zeros(drouter_ref.shape, f32)
        if add:
            drouter = old_router_ref[...]
        for index in range(chunks):
            at = pl.ds(index * chunk, chunk)
            result = result_acc[at, :].astype(bf16)
            result_ref[at, :] = result
            grad_gate = jnp.sum(
                g_ref[at, :].astype(f32) * result.astype(f32), axis=1, keepdims=True
            )
            probs = probs_ref[at, :]
            lane = lax.broadcasted_iota(jnp.int32, probs.shape, 1)
            chosen = lane == mine
            gate = jnp.sum(jnp.where(chosen, probs, 0.0), axis=1, keepdims=True)
            logits = (grad_gate * gate) * (chosen.astype(f32) - probs)
            high = logits.astype(bf16)
            low = (logits - high.astype(f32)).astype(bf16)
            dx_ref[at, :] = (
                dx_acc[at, :] + dot(high, small_ref[...]) + dot(low, small_ref[...])
            ).astype(bf16)
            drouter = drouter + t_dot(high, x_ref[at, :]) + t_dot(low, x_ref[at, :])
        drouter_ref[...] = drouter
        rides.finish(ride_refs)


def row_chunk(rows):
    best = rows
    for size in range(16, 513, 16):
        if rows % size == 0:
            best = size
    return best


def expert_block(x, g, w1, w2, bias, small, experts, old, arrays, collective):
    rows, features = x.shape
    hidden_units = w1.shape[0]
    block = 512 if hidden_units % 512 == 0 else 256
    steps = hidden_units // block
    chunk = row_chunk(rows)
    add = old is not None
    out_type = bf16 if add else f32
    rides = Rides(arrays)

    def whole(shape):
        return pl.BlockSpec(
            shape, lambda s: (0,) * len(shape), pipeline_mode=pl.Buffered(1)
        )

    packed = 2 * features + LANES
    unit_grads = pl.BlockSpec((block, packed), lambda s: (s, 0))
    units = pl.BlockSpec((block, features), lambda s: (s, 0))
    unit_row = pl.BlockSpec((1, block), lambda s: (0, s))
    in_specs = [
        whole(x.shape),
        whole(g.shape),
        units,
        units,
        unit_row,
        whole(small.shape),
    ]
    operands = [x, g, w1, w2, bias, small]
    if add:
        in_specs += [unit_grads, whole(small.shape)]
        operands += list(old)
    return pl.pallas_call(
        functools.partial(expert_kernel, experts, chunk, add, rides),
        grid=(steps,),
        in_specs=in_specs + rides.in_specs,
        out_specs=[
            whole(x.shape), whole(x.shape), unit_grads, whole(small.shape)
        ]
        + rides.in_specs,
        out_shape=[
            jax.ShapeDtypeStruct(x.shape, bf16),
            jax.ShapeDtypeStruct(x.shape, bf16),
            jax.ShapeDtypeStruct((hidden_units, packed), out_type),
            jax.ShapeDtypeStruct(small.shape, f32),
        ]
        + rides.out_shape,
        scratch_shapes=[
            pltpu.VMEM((rows, features), f32),
            pltpu.VMEM((rows, features), f32),
            pltpu.VMEM((rows, features), bf16),
            pltpu.VMEM((rows, small.shape[0]), f32),
            pltpu.VMEM((rows, block), bf16),
            pltpu.VMEM((rows, block), bf16),
        ]
        + rides.scratch,
        compiler_params=params(
            ("arbitrary",), collective_id=collective, has_side_effects=True
        ),
        cost_estimate=pl.CostEstimate(
            flops=12 * rows * features * hidden_units,
            bytes_accessed=(8 * rows + 12 * hidden_units) * features,
            transcendentals=rows * hidden_units,
        ),
        name="expert_block",
    )(*operands, *rides.arrays)


def combine_kernel(slots_ref, gates_ref, residual_ref, returned_ref, out_ref):
    seq = slots_ref.shape[1]
    total = returned_ref.shape[0]
    column = lax.broadcasted_iota(jnp.int32, (seq, total), 1)
    slots = slots_ref[0]
    gates = gates_ref[0]
    value = residual_ref[0]
    mix = None
    for choice in range(TOP):
        holds = slots[:, choice : choice + 1] == column
        picked = dot(holds.astype(f32).astype(bf16), returned_ref[...])
        part = gates[:, choice : choice + 1] * picked
        mix = part if mix is None else mix + part
    out_ref[0] = (value + mix).astype(bf16)


def combine(slots, gates, residual, returned, group):
    seq, features = residual.shape[1:]
    first = group * IMG_MB
    return pl.pallas_call(
        combine_kernel,
        grid=(IMG_MB,),
        in_specs=[
            pl.BlockSpec((1, seq, TOP), lambda i: (first + i, 0, 0)),
            pl.BlockSpec((1, seq, TOP), lambda i: (i, 0, 0)),
            pl.BlockSpec((1, seq, features), lambda i: (i, 0, 0)),
            pl.BlockSpec(returned.shape, lambda i: (0, 0)),
        ],
        out_specs=pl.BlockSpec((1, seq, features), lambda i: (i, 0, 0)),
        out_shape=jax.ShapeDtypeStruct(residual.shape, bf16),
        compiler_params=params(("arbitrary",)),
        cost_estimate=pl.CostEstimate(
            flops=4 * IMG_MB * seq * returned.shape[0] * features,
            bytes_accessed=2 * features * (returned.shape[0] + 3 * IMG_MB * seq),
            transcendentals=0,
        ),
        name="combine",
    )(slots, gates, residual, returned)


def attend_back_kernel(
    experts, add, rides, ranks, x_ref, top_ref, slots_ref, sent_ref, proj_ref, mixed_ref, residual_ref,
    dense_ref, small_ref, *refs
):
    if add:
        old_dense_ref, old_small_ref, drouter_ref = refs[:3]
        refs = refs[3:]
    count = len(rides.arrays)
    outs = 2 if add else 3
    sources, refs = refs[:count], refs[count:]
    grad_x_ref, ddense_ref = refs[:2]
    if not add:
        dsmall_ref = refs[2]
    targets, refs = refs[outs : outs + count], refs[outs + count :]
    acc_in, acc_out, acc_small, dproj_ref = refs[:4]
    refs = refs[4:]
    more = ()
    if add:
        pack_ref, first_ref, second_ref, first_sems, second_sems = refs[:5]
        refs = refs[5:]
        rank = lax.axis_index("dp")
        core = lax.rem(rank, 2)
        pairs = ranks // 2
        partner = {"dp": rank + 1 - 2 * core}
        others = [{"dp": lax.rem(rank + 2 * hop, ranks)} for hop in range(1, pairs)]
        more = [partner] + others
    ride_refs = (sources, targets, refs)
    features = x_ref.shape[2]
    seq = x_ref.shape[1]
    step = pl.program_id(0)
    vectors = small_ref[...].astype(f32)

    @pl.when(step == 0)
    def _():
        rides.start(ride_refs, more)
        if add:
            acc_in[...] = old_dense_ref[:, : 3 * features]
            acc_out[...] = old_dense_ref[:, 3 * features :]
            acc_small[...] = old_small_ref[...]
        else:
            acc_in[...] = jnp.zeros(acc_in.shape, f32)
            acc_out[...] = jnp.zeros(acc_out.shape, f32)
            acc_small[...] = jnp.zeros(acc_small.shape, f32)

    column = lax.broadcasted_iota(jnp.int32, (seq, sent_ref.shape[0]), 1)
    slots = slots_ref[0]
    holds = (slots[:, 0:1] == column) | (slots[:, 1:2] == column)
    grad_hidden = dot(holds.astype(f32).astype(bf16), sent_ref[...])
    normed_two, inverse_two = norm_forward(residual_ref[0])
    acc_small[2:3, :] += jnp.sum(grad_hidden * normed_two, axis=0, keepdims=True)
    acc_small[3:4, :] += jnp.sum(grad_hidden, axis=0, keepdims=True)
    grad_residual = top_ref[0].astype(f32) + norm_backward(
        grad_hidden * vectors[experts + 2 : experts + 3], normed_two, inverse_two
    )
    grad_branch = grad_residual.astype(bf16)
    acc_out[...] += t_dot(mixed_ref[0], grad_branch)
    grad_mixed = dot_t(grad_branch, dense_ref[:, 3 * features :]).astype(bf16)
    low_half = lax.broadcasted_iota(jnp.int32, (1, LANES), 1) < HEAD_DIM
    scale = HEAD_DIM ** (-0.5)
    for pair in range(features // LANES):
        first = pair * LANES
        queries = proj_ref[0, :, first : first + LANES]
        keys = proj_ref[0, :, features + first : features + first + LANES]
        values = proj_ref[0, :, 2 * features + first : 2 * features + first + LANES]
        grad_out = grad_mixed[:, first : first + LANES]
        sums = [None, None, None]
        for half in range(2):
            keep = low_half if half == 0 else jnp.logical_not(low_half)
            head_queries = jnp.where(keep, queries * scale, 0).astype(bf16)
            head_keys = jnp.where(keep, keys, 0).astype(bf16)
            head_grad = jnp.where(keep, grad_out, 0).astype(bf16)
            scores = dot_t(keys, head_queries)
            top = jnp.max(scores, axis=0, keepdims=True)
            raised = jnp.exp(scores - top)
            probs = raised * (1.0 / jnp.sum(raised, axis=0, keepdims=True))
            grad_values = dot(probs.astype(bf16), head_grad)
            grad_weights = dot_t(values, head_grad)
            inner = jnp.sum(grad_weights * probs, axis=0, keepdims=True)
            grad_scores = (probs * (grad_weights - inner)).astype(bf16)
            grad_keys = dot(grad_scores, head_queries)
            grad_queries = t_dot(grad_scores, head_keys)
            for place, part in enumerate((grad_queries, grad_keys, grad_values)):
                sums[place] = part if half == 0 else sums[place] + part
        dproj_ref[:, first : first + LANES] = (sums[0] * scale).astype(bf16)
        dproj_ref[:, features + first : features + first + LANES] = sums[1].astype(bf16)
        dproj_ref[:, 2 * features + first : 2 * features + first + LANES] = sums[2].astype(bf16)
    normed_one, inverse_one = norm_forward(x_ref[0].astype(f32))
    attn_input = (
        normed_one * vectors[experts : experts + 1] + vectors[experts + 1 : experts + 2]
    ).astype(bf16)
    acc_in[...] += t_dot(attn_input, dproj_ref[...])
    grad_input = dot_t(dproj_ref[...], dense_ref[:, : 3 * features])
    acc_small[0:1, :] += jnp.sum(grad_input * normed_one, axis=0, keepdims=True)
    acc_small[1:2, :] += jnp.sum(grad_input, axis=0, keepdims=True)
    grad_x_ref[0] = grad_residual + norm_backward(
        grad_input * vectors[experts : experts + 1], normed_one, inverse_one
    )

    @pl.when(step == pl.num_programs(0) - 1)
    def _():
        if not add:
            ddense_ref[:, : 3 * features] = acc_in[...]
            ddense_ref[:, 3 * features :] = acc_out[...]
            dsmall_ref[...] = acc_small[...]
        else:
            used = acc_small.shape[0] + drouter_ref.shape[0]
            rest = jnp.zeros((LANES - used, features), f32)
            column = jnp.concatenate([acc_small[...], drouter_ref[...], rest], axis=0).T
            share = features // ranks
            for shard in range(ranks):
                at = slice(shard * share, (shard + 1) * share)
                place = (shard % 2, shard // 2)
                pack_ref[place[0], place[1], :, : 3 * features] = acc_in[at].astype(bf16)
                pack_ref[place[0], place[1], :, 3 * features : 4 * features] = acc_out[
                    at
                ].astype(bf16)
                pack_ref[place[0], place[1], :, 4 * features :] = column[at].astype(bf16)
            copy = pltpu.make_async_remote_copy(
                src_ref=pack_ref.at[1 - core],
                dst_ref=first_ref,
                send_sem=first_sems.at[0],
                recv_sem=first_sems.at[1],
                device_id=partner,
                device_id_type=pl.DeviceIdType.MESH,
            )
            copy.start()
            copy.wait()
            for pair in range(pairs):
                first_ref[pair] = (
                    first_ref[pair].astype(f32) + pack_ref[core, pair].astype(f32)
                ).astype(bf16)
            mine = rank // 2
            copies = [
                pltpu.make_async_remote_copy(
                    src_ref=first_ref.at[lax.rem(mine + hop, pairs)],
                    dst_ref=second_ref.at[hop - 1],
                    send_sem=second_sems.at[0, hop - 1],
                    recv_sem=second_sems.at[1, hop - 1],
                    device_id=others[hop - 1],
                    device_id_type=pl.DeviceIdType.MESH,
                )
                for hop in range(1, pairs)
            ]
            for copy in copies:
                copy.start()
            total = first_ref[mine].astype(f32)
            for copy in copies:
                copy.wait()
            for hop in range(1, pairs):
                total = total + second_ref[hop - 1].astype(f32)
            ddense_ref[...] = total.astype(bf16)
        rides.finish(ride_refs)


def attend_back(
    images, out_grad, slots, sent, proj, mixed, residual, dense, small, experts, group, old,
    arrays, collective, ranks,
):
    seq, features = images.shape[1:]
    wide = 3 * features
    first = group * IMG_MB
    add = old is not None
    rides = Rides(arrays)

    def rows(width):
        return pl.BlockSpec((1, seq, width), lambda i: (i, 0, 0))

    def source(width):
        return pl.BlockSpec((1, seq, width), lambda i: (first + i, 0, 0))

    def whole(shape):
        return pl.BlockSpec(shape, lambda i: (0, 0), pipeline_mode=pl.Buffered(1))

    small_grads = (8, features)
    in_specs = [
        source(features), source(features), source(TOP), whole(sent.shape),
        rows(wide), rows(features), rows(features),
        whole(dense.shape), whole(small.shape),
    ]
    operands = [images, out_grad, slots, sent, proj, mixed, residual, dense, small]
    out_specs = [rows(features), whole((features, 4 * features))]
    out_shape = [
        jax.ShapeDtypeStruct((IMG_MB, seq, features), f32),
        jax.ShapeDtypeStruct((features, 4 * features), f32),
    ]
    if add:
        in_specs += [whole(array.shape) for array in old]
        operands += list(old)
        shard = (features // ranks, 4 * features + LANES)
        out_specs[1] = whole(shard)
        out_shape[1] = jax.ShapeDtypeStruct(shard, bf16)
        reduce_scratch = [
            pltpu.VMEM((2, ranks // 2, *shard), bf16),
            pltpu.VMEM((ranks // 2, *shard), bf16),
            pltpu.VMEM((ranks // 2 - 1, *shard), bf16),
            pltpu.SemaphoreType.DMA((2,)),
            pltpu.SemaphoreType.DMA((2, ranks // 2 - 1)),
        ]
    else:
        out_specs.append(whole(small_grads))
        out_shape.append(jax.ShapeDtypeStruct(small_grads, f32))
        reduce_scratch = []
    return pl.pallas_call(
        functools.partial(attend_back_kernel, experts, add, rides, ranks),
        grid=(IMG_MB,),
        in_specs=in_specs + rides.in_specs,
        out_specs=out_specs + rides.in_specs,
        out_shape=out_shape + rides.out_shape,
        scratch_shapes=[
            pltpu.VMEM((features, 3 * features), f32),
            pltpu.VMEM((features, features), f32),
            pltpu.VMEM(small_grads, f32),
            pltpu.VMEM((seq, wide), bf16),
        ]
        + reduce_scratch
        + rides.scratch,
        compiler_params=params(
            ("arbitrary",), collective_id=collective, has_side_effects=True
        ),
        cost_estimate=pl.CostEstimate(
            flops=IMG_MB * seq * 40 * features * features,
            bytes_accessed=8 * features * (4 * features + IMG_MB * seq * 4),
            transcendentals=IMG_MB * HEADS * seq * seq,
        ),
        name="attend_back",
    )(*operands, *rides.arrays)


def per_device(
    images, first_gain, first_shift, attn_in, attn_out, second_gain, second_shift, router,
    expert_in, expert_bias, expert_out, routes, out_grad,
):
    features = images.shape[2]
    experts = router.shape[1]
    tok_mb = IMG_MB * SEQ
    capacity = max(2, (5 * TOP * tok_mb // (4 * experts) + 7) // 8 * 8)
    slot_rows = experts * capacity
    micro = images.shape[0] // IMG_MB
    small_rows = (experts + 4 + 15) // 16 * 16

    own = router.shape[0]
    ranks = features // own
    bias_rows = expert_bias.shape[1] // own
    small = jnp.concatenate(
        [
            router.T,
            first_gain[None],
            first_shift[None],
            second_gain[None],
            second_shift[None],
            jnp.zeros((small_rows - experts - 4, own), bf16),
            expert_bias.reshape(bias_rows, own),
        ],
        axis=0,
    )
    dense = lax.all_gather(
        jnp.concatenate([attn_in, attn_out], axis=1), "dp", axis=0, tiled=True
    )
    small = lax.all_gather(small, "dp", axis=1, tiled=True)
    bias_row = small[small_rows:].reshape(bias_rows, -1, own).transpose(1, 0, 2).reshape(1, -1)
    small = small[:small_rows]
    weight_in = lax.all_gather(expert_in[0], "dp", axis=0, tiled=True)
    weight_out = lax.all_gather(expert_out[0], "dp", axis=0, tiled=True)
    last = None

    def exchange(rows):
        nonlocal last
        if last is not None:
            rows, _ = lax.optimization_barrier((rows, last))
        last = lax.all_to_all(rows, "expert", split_axis=0, concat_axis=0, tiled=True)
        return last

    def flat(blocks):
        return blocks.reshape(slot_rows, features)

    def blocks(rows):
        return rows.reshape(experts, capacity, features)

    slots, lines = route(routes, experts, capacity)
    grad_rows = [dispatch(lines, out_grad, group, experts, capacity) for group in range(micro)]
    saved = []
    token_rows = []
    for group in range(micro):
        proj, mixed, residual, hidden, gates = attend(
            images, routes, dense, small, experts, group
        )
        saved.append((proj, mixed, residual, gates))
        token_rows.append(dispatch(lines, hidden, group, experts, capacity))
    grads = exchange(grad_rows[0])
    received = exchange(token_rows[0])
    result_0, dx_0, *old, grads_1, received_1 = expert_block(
        flat(received), flat(grads), weight_in, weight_out, bias_row, small, experts, None,
        [grad_rows[1], token_rows[1]], 0,
    )
    result_1, dx_1, dweights, drouter, sent = expert_block(
        flat(received_1), flat(grads_1), weight_in, weight_out, bias_row, small, experts, old,
        [blocks(dx_0)], 1,
    )
    dweights = lax.psum_scatter(dweights, "dp", scatter_dimension=0, tiled=True)
    proj, mixed, residual, _ = saved[0]
    grad_x_0, *old, sent_1 = attend_back(
        images, out_grad, slots, flat(sent), proj, mixed, residual, dense, small,
        experts, 0, None, [blocks(dx_1)], 2, ranks,
    )
    proj, mixed, residual, _ = saved[1]
    grad_x_1, ddense, returned_0, returned_1 = attend_back(
        images, out_grad, slots, flat(sent_1), proj, mixed, residual, dense, small,
        experts, 1, old + [drouter], [blocks(result_0), blocks(result_1)], 3, ranks,
    )
    grad_blocks = [grad_x_0, grad_x_1]
    out_blocks = [
        combine(slots, saved[group][3], saved[group][2], flat(returned), group)
        for group, returned in enumerate((returned_0, returned_1))
    ]
    share = ddense.shape[0] // experts
    shares = exchange(ddense.reshape(experts, share, ddense.shape[1]))
    total = jnp.sum(shares.astype(f32), axis=0, keepdims=True).astype(bf16)
    ddense = exchange(jnp.broadcast_to(total, shares.shape)).reshape(ddense.shape).astype(f32)
    little = ddense[:, 4 * features :].T
    dweights = dweights.astype(f32)
    return (
        jnp.concatenate(out_blocks, axis=0),
        jnp.concatenate(grad_blocks, axis=0),
        little[0],
        little[1],
        ddense[:, : 3 * features],
        ddense[:, 3 * features : 4 * features],
        little[2],
        little[3],
        little[8 : 8 + experts].T,
        dweights[None, :, :features],
        dweights[None, :, 2 * features],
        dweights[None, :, features : 2 * features],
    )


def solution(mesh):
    return jax.shard_map(
        per_device,
        mesh=mesh,
        in_specs=(
            P(("dp", "expert"), None, None),
            P("dp"),
            P("dp"),
            P("dp", None),
            P("dp", None),
            P("dp"),
            P("dp"),
            P("dp", None),
            P("expert", "dp", None),
            P("expert", "dp"),
            P("expert", "dp", None),
            P(("dp", "expert"), None, None),
            P(("dp", "expert"), None, None),
        ),
        out_specs=(
            P(("dp", "expert"), None, None),
            P(("dp", "expert"), None, None),
            P("dp"),
            P("dp"),
            P("dp", None),
            P("dp", None),
            P("dp"),
            P("dp"),
            P("dp", None),
            P("expert", "dp", None),
            P("expert", "dp"),
            P("expert", "dp", None),
        ),
        check_vma=False,
    )
```

```python
import functools

import jax
import jax.numpy as jnp
from jax import lax
from jax.experimental import pallas as pl
from jax.experimental.pallas import tpu as pltpu
from jax.sharding import PartitionSpec as P

HEADS = 12
HEAD_DIM = 64
SEQ = 197
MICRO = 2
IMG_MB = 3
TOP = 2
LANES = 128
VMEM_LIMIT = 60 * 1024 * 1024

epsilon = 1e-06
f32 = jnp.float32
bf16 = jnp.bfloat16


def params(semantics, **more):
    return pltpu.CompilerParams(
        dimension_semantics=semantics, vmem_limit_bytes=VMEM_LIMIT, **more
    )


def dot(left, right):
    return lax.dot_general(
        left, right, (((1,), (0,)), ((), ())), preferred_element_type=f32
    )


def dot_t(left, right):
    return lax.dot_general(
        left, right, (((1,), (1,)), ((), ())), preferred_element_type=f32
    )


def t_dot(left, right):
    return lax.dot_general(
        left, right, (((0,), (0,)), ((), ())), preferred_element_type=f32
    )


def norm_forward(values):
    row_mean = jnp.mean(values, axis=-1, keepdims=True)
    centred = values - row_mean
    row_var = jnp.mean(centred * centred, axis=-1, keepdims=True)
    inverse = lax.rsqrt(row_var + epsilon)
    return centred * inverse, inverse


def norm_backward(grad_normed, normed, inverse):
    mean_grad = jnp.mean(grad_normed, axis=-1, keepdims=True)
    mean_cross = jnp.mean(grad_normed * normed, axis=-1, keepdims=True)
    return inverse * (grad_normed - mean_grad - normed * mean_cross)


def softmax_lanes(logits, count):
    lane = lax.broadcasted_iota(jnp.int32, logits.shape, 1)
    masked = jnp.where(lane < count, logits, -1e30)
    top = jnp.max(masked, axis=-1, keepdims=True)
    raised = jnp.where(lane < count, jnp.exp(masked - top), 0.0)
    return raised / jnp.sum(raised, axis=-1, keepdims=True)


def gelu_both(values):
    size = jnp.abs(values)
    bell = jnp.exp(values * values * -0.5)
    t = 1.0 / (1.0 + (0.3275911 * 0.7071067811865476) * size)
    tail = t * (
        0.5 * 0.254829592
        + t
        * (
            0.5 * -0.284496736
            + t * (0.5 * 1.421413741 + t * (0.5 * -1.453152027 + t * (0.5 * 1.061405429)))
        )
    )
    tail = tail * bell
    phi = jnp.where(values >= 0, 1.0 - tail, tail)
    return values * phi, phi + values * (0.3989422804014327 * bell)


class Rides:
    def __init__(self, entries):
        self.arrays = [entry[0] for entry in entries]
        self.rows = [pl.ds(entry[1], entry[2] - entry[1]) for entry in entries]
        self.before = [entry[3] for entry in entries if entry[3] is not None]
        self.filled = [index for index, entry in enumerate(entries) if entry[3] is not None]
        arrays = self.arrays
        self.parts = arrays[0].shape[0]
        self.operands = self.arrays + self.before
        self.in_specs = [pl.BlockSpec(memory_space=pl.ANY)] * len(self.operands)
        self.out_specs = [pl.BlockSpec(memory_space=pl.ANY)] * len(arrays)
        self.out_shape = [jax.ShapeDtypeStruct(a.shape, a.dtype) for a in arrays]
        self.scratch = [
            pltpu.SemaphoreType.DMA((self.parts,)),
            pltpu.SemaphoreType.DMA((self.parts,)),
            pltpu.SemaphoreType.DMA,
        ] * len(arrays)

    def aliases(self, inputs, outputs):
        first = inputs + len(self.arrays)
        return {first + place: outputs + index for place, index in enumerate(self.filled)}

    def copy(self, refs, index, offset):
        me = lax.axis_index("expert")
        peer = lax.rem(me + offset, self.parts)
        sources, targets, sems = refs
        return pltpu.make_async_remote_copy(
            src_ref=sources[index].at[peer, self.rows[index]],
            dst_ref=targets[index].at[me, self.rows[index]],
            send_sem=sems[3 * index].at[offset],
            recv_sem=sems[3 * index + 1].at[offset],
            device_id={"expert": peer},
            device_id_type=pl.DeviceIdType.MESH,
        )

    def own(self, refs):
        me = lax.axis_index("expert")
        sources, targets, sems = refs
        return [
            pltpu.make_async_copy(
                sources[index].at[me, self.rows[index]],
                targets[index].at[me, self.rows[index]],
                sems[3 * index + 2],
            )
            for index in range(len(sources))
        ]

    def start(self, refs, more=()):
        me = lax.axis_index("expert")
        barrier = pltpu.get_barrier_semaphore()
        for peer in more:
            pl.semaphore_signal(
                barrier, inc=1, device_id=peer, device_id_type=pl.DeviceIdType.MESH
            )

        @pl.loop(1, self.parts)
        def _(offset):
            pl.semaphore_signal(
                barrier,
                inc=1,
                device_id={"expert": lax.rem(me + offset, self.parts)},
                device_id_type=pl.DeviceIdType.MESH,
            )

        pl.semaphore_wait(barrier, self.parts - 1 + len(more))
        for index in range(len(self.rows)):

            @pl.loop(1, self.parts)
            def _(offset):
                self.copy(refs, index, offset).start()

        for copy in self.own(refs):
            copy.start()

    def finish(self, refs):
        for copy in self.own(refs):
            copy.wait()
        for index in range(len(self.rows)):

            @pl.loop(1, self.parts)
            def _(offset):
                self.copy(refs, index, offset).wait()


def route_kernel(capacity, routes_ref, slots_ref, lines_ref):
    seq = routes_ref.shape[1]
    row = lax.broadcasted_iota(jnp.int32, (seq, seq), 0)
    col = lax.broadcasted_iota(jnp.int32, (seq, seq), 1)
    earlier = (col < row).astype(f32).astype(bf16)
    lane = lax.broadcasted_iota(jnp.int32, (seq, LANES), 1)
    base = jnp.zeros((1, LANES), f32)
    table = jnp.full((seq, LANES), -1.0, f32)
    for choice in range(TOP):
        for image in range(IMG_MB):
            named = routes_ref[image][:, choice : choice + 1]
            onehot = (lane == named).astype(f32)
            count = dot(earlier, onehot.astype(bf16)) + base
            position = jnp.sum(onehot * count, axis=1, keepdims=True).astype(jnp.int32)
            base = base + jnp.sum(onehot, axis=0, keepdims=True)
            slot = jnp.where(position < capacity, named * capacity + position, -1)
            slots_ref[image, :, choice : choice + 1] = slot
            table = jnp.where(lane == image * TOP + choice, slot.astype(f32), table)
    lines_ref[...] = table.T[: lines_ref.shape[0]].astype(jnp.int32)


def route(routes, group, capacity):
    seq = routes.shape[1]
    return pl.pallas_call(
        functools.partial(route_kernel, capacity),
        grid=(1,),
        in_specs=[pl.BlockSpec((IMG_MB, seq, TOP), lambda i: (group, 0, 0))],
        out_specs=[
            pl.BlockSpec((IMG_MB, seq, TOP), lambda i: (0, 0, 0)),
            pl.BlockSpec((8, seq), lambda i: (0, 0)),
        ],
        out_shape=[
            jax.ShapeDtypeStruct((IMG_MB, seq, TOP), jnp.int32),
            jax.ShapeDtypeStruct((8, seq), jnp.int32),
        ],
        compiler_params=params(("arbitrary",)),
        cost_estimate=pl.CostEstimate(
            flops=10**8, bytes_accessed=10**6, transcendentals=0
        ),
        name="route",
    )(routes)


def dispatch_kernel(capacity, lines_ref, rows_ref, out_ref):
    first = pl.program_id(0) * capacity
    seq = rows_ref.shape[1]
    slot = lax.broadcasted_iota(jnp.int32, (capacity, seq), 0) + first
    lines = lines_ref[...]
    acc = jnp.zeros((capacity, rows_ref.shape[2]), f32)
    for image in range(IMG_MB):
        at = image * TOP
        holds = (lines[at : at + 1] == slot) | (lines[at + 1 : at + 2] == slot)
        acc = acc + dot(holds.astype(f32).astype(bf16), rows_ref[image])
    out_ref[0] = acc.astype(bf16)


def dispatch(lines, rows, group, experts, capacity):
    seq, features = rows.shape[1:]
    return pl.pallas_call(
        functools.partial(dispatch_kernel, capacity),
        grid=(experts,),
        in_specs=[
            pl.BlockSpec((8, seq), lambda e: (0, 0)),
            pl.BlockSpec((IMG_MB, seq, features), lambda e: (group, 0, 0)),
        ],
        out_specs=pl.BlockSpec((1, capacity, features), lambda e: (e, 0, 0)),
        out_shape=jax.ShapeDtypeStruct((experts, capacity, features), bf16),
        compiler_params=params(("arbitrary",)),
        cost_estimate=pl.CostEstimate(
            flops=2 * experts * capacity * IMG_MB * seq * features,
            bytes_accessed=2 * features * (experts * capacity + IMG_MB * seq),
            transcendentals=0,
        ),
        name="dispatch",
    )(lines, rows)


def attend_kernel(
    experts, rides, x_ref, routes_ref, lines_ref, dense_ref, small_ref, *refs
):
    count = len(rides.arrays) if rides else 0
    sources, refs = refs[:count], refs[count:]
    proj_ref, mixed_ref, residual_ref, gates_ref, rows_ref = refs[:5]
    targets, (hidden_ref, *sems) = refs[5 : 5 + count], refs[5 + count :]
    step = pl.program_id(0)
    if rides:

        @pl.when(step == 0)
        def _():
            rides.start((sources, targets, sems))

    features = x_ref.shape[2]
    image = x_ref[0].astype(f32)
    vectors = small_ref[...].astype(f32)
    normed, _ = norm_forward(image)
    attn_input = (
        normed * vectors[experts : experts + 1] + vectors[experts + 1 : experts + 2]
    ).astype(bf16)
    proj_ref[0] = dot(attn_input, dense_ref[:, : 3 * features]).astype(bf16)
    low_half = lax.broadcasted_iota(jnp.int32, (1, LANES), 1) < HEAD_DIM
    for pair in range(features // LANES):
        first = pair * LANES
        queries = proj_ref[0, :, first : first + LANES]
        keys = proj_ref[0, :, features + first : features + first + LANES]
        values = proj_ref[0, :, 2 * features + first : 2 * features + first + LANES]
        out = None
        for half in range(2):
            keep = low_half if half == 0 else jnp.logical_not(low_half)
            scores = dot_t(
                jnp.where(keep, queries * HEAD_DIM ** (-0.5), 0).astype(bf16), keys
            )
            top = jnp.max(scores, axis=-1, keepdims=True)
            raised = jnp.exp(scores - top)
            share = 1.0 / jnp.sum(raised, axis=-1, keepdims=True)
            weights = (raised * share).astype(bf16)
            part = dot(weights, jnp.where(keep, values, 0).astype(bf16))
            out = part if out is None else out + part
        mixed_ref[0, :, first : first + LANES] = out.astype(bf16)
    residual = image + dot(mixed_ref[0], dense_ref[:, 3 * features :])
    residual_ref[0] = residual
    normed, _ = norm_forward(residual)
    hidden = (
        normed * vectors[experts + 2 : experts + 3] + vectors[experts + 3 : experts + 4]
    ).astype(bf16)
    hidden_ref[step] = hidden
    probs = softmax_lanes(dot_t(hidden, small_ref[...]), experts)
    lane = lax.broadcasted_iota(jnp.int32, probs.shape, 1)
    routes = routes_ref[0]
    for choice in range(TOP):
        gates_ref[0, :, choice : choice + 1] = jnp.sum(
            jnp.where(lane == routes[:, choice : choice + 1], probs, 0.0),
            axis=1,
            keepdims=True,
        )

    @pl.when(step == pl.num_programs(0) - 1)
    def _():
        seq = x_ref.shape[1]
        capacity = rows_ref.shape[1]
        lines = lines_ref[...]
        slot = lax.broadcasted_iota(jnp.int32, (capacity, seq), 0)

        @pl.loop(0, experts)
        def _(expert):
            here = slot + expert * capacity
            total = None
            for index in range(IMG_MB):
                at = index * TOP
                holds = (lines[at : at + 1] == here) | (lines[at + 1 : at + 2] == here)
                part = dot(holds.astype(f32).astype(bf16), hidden_ref[index])
                total = part if total is None else total + part
            rows_ref[expert] = total.astype(bf16)

        if rides:
            rides.finish((sources, targets, sems))


def attend(
    images, routes, lines, dense, small, experts, capacity, group, entries=(), collective=None
):
    seq, features = images.shape[1:]
    wide = 3 * features
    first = group * IMG_MB
    rides = Rides(entries) if entries else None
    more = {"collective_id": collective, "has_side_effects": True} if entries else {}
    slot_rows = (experts, capacity, features)

    def rows(width):
        return pl.BlockSpec((1, seq, width), lambda i: (i, 0, 0))

    def source(width):
        return pl.BlockSpec((1, seq, width), lambda i: (first + i, 0, 0))

    def whole(shape):
        return pl.BlockSpec(
            shape, lambda i: (0,) * len(shape), pipeline_mode=pl.Buffered(1)
        )

    def out(width, dtype):
        return jax.ShapeDtypeStruct((IMG_MB, seq, width), dtype)

    return pl.pallas_call(
        functools.partial(attend_kernel, experts, rides),
        grid=(IMG_MB,),
        in_specs=[
            source(features),
            source(TOP),
            whole(lines.shape),
            whole(dense.shape),
            whole(small.shape),
        ]
        + (rides.in_specs if rides else []),
        out_specs=[rows(wide), rows(features), rows(features), rows(TOP), whole(slot_rows)]
        + (rides.out_specs if rides else []),
        out_shape=[
            out(wide, bf16),
            out(features, bf16),
            out(features, f32),
            out(TOP, f32),
            jax.ShapeDtypeStruct(slot_rows, bf16),
        ]
        + (rides.out_shape if rides else []),
        scratch_shapes=[pltpu.VMEM((IMG_MB, seq, features), bf16)]
        + (rides.scratch if rides else []),
        compiler_params=params(("arbitrary",), **more),
        cost_estimate=pl.CostEstimate(
            flops=IMG_MB * seq * 16 * features * features,
            bytes_accessed=4 * features * (4 * features + IMG_MB * seq * 8),
            transcendentals=IMG_MB * HEADS * seq * seq,
        ),
        name="attend",
    )(images, routes, lines, dense, small, *(rides.operands if rides else []))


def expert_kernel(
    experts, chunk, add, rides, x_ref, g_ref, w1_ref, w2_ref, bias_ref, small_ref, *refs
):
    if add:
        old_w_ref, old_router_ref = refs[:2]
        refs = refs[2:]
    count = len(rides.arrays)
    sources, refs = refs[:count], refs[len(rides.operands) :]
    ride_refs = (sources, refs[4 : count + 4], refs[count + 10 :])
    refs = refs[:4] + refs[count + 4 : count + 10]
    (
        result_ref, dx_ref, dw_ref, drouter_ref,
        result_acc, dx_acc, dr_ref, probs_ref, act_ref, pre_ref,
    ) = refs
    step = pl.program_id(0)
    last = pl.num_programs(0) - 1
    rows = x_ref.shape[0]
    mine = lax.axis_index("expert")
    chunks = rows // chunk

    @pl.when(step == 0)
    def _():
        rides.start(ride_refs)

    @pl.when(step == 0)
    def _():
        for index in range(chunks):
            at = pl.ds(index * chunk, chunk)
            probs = softmax_lanes(dot_t(x_ref[at, :], small_ref[...]), experts)
            lane = lax.broadcasted_iota(jnp.int32, probs.shape, 1)
            probs_ref[at, :] = probs
            gate = jnp.sum(jnp.where(lane == mine, probs, 0.0), axis=1, keepdims=True)
            dr_ref[at, :] = (gate * g_ref[at, :].astype(f32)).astype(bf16)
            result_acc[at, :] = jnp.zeros((chunk, x_ref.shape[1]), f32)
            dx_acc[at, :] = jnp.zeros((chunk, x_ref.shape[1]), f32)

    w1 = w1_ref[...]
    w2 = w2_ref[...]
    bias = bias_ref[...].astype(f32)
    dbias = jnp.zeros(bias.shape, f32)
    for index in range(chunks):
        at = pl.ds(index * chunk, chunk)
        act, slope = gelu_both(dot_t(x_ref[at, :], w1) + bias)
        act = act.astype(bf16)
        act_ref[at, :] = act
        result_acc[at, :] += dot(act, w2)
        grad_pre = (dot_t(dr_ref[at, :], w2) * slope).astype(bf16)
        pre_ref[at, :] = grad_pre
        dbias = dbias + jnp.sum(grad_pre.astype(f32), axis=0, keepdims=True)
        dx_acc[at, :] += dot(grad_pre, w1)
    dw1 = t_dot(pre_ref[...], x_ref[...])
    dw2 = t_dot(act_ref[...], dr_ref[...])
    dbias = jnp.broadcast_to(dbias, (LANES, dbias.shape[1])).T
    first = 0
    for part in (dw1, dw2, dbias):
        at = pl.ds(first, part.shape[1])
        if add:
            part = part + old_w_ref[:, at]
        dw_ref[:, at] = part.astype(dw_ref.dtype)
        first += part.shape[1]

    @pl.when(step == last)
    def _():
        drouter = jnp.zeros(drouter_ref.shape, f32)
        if add:
            drouter = old_router_ref[...]
        for index in range(chunks):
            at = pl.ds(index * chunk, chunk)
            result = result_acc[at, :].astype(bf16)
            result_ref[at, :] = result
            grad_gate = jnp.sum(
                g_ref[at, :].astype(f32) * result.astype(f32), axis=1, keepdims=True
            )
            probs = probs_ref[at, :]
            lane = lax.broadcasted_iota(jnp.int32, probs.shape, 1)
            chosen = lane == mine
            gate = jnp.sum(jnp.where(chosen, probs, 0.0), axis=1, keepdims=True)
            logits = (grad_gate * gate) * (chosen.astype(f32) - probs)
            high = logits.astype(bf16)
            low = (logits - high.astype(f32)).astype(bf16)
            dx_ref[at, :] = (
                dx_acc[at, :] + dot(high, small_ref[...]) + dot(low, small_ref[...])
            ).astype(bf16)
            drouter = drouter + t_dot(high, x_ref[at, :]) + t_dot(low, x_ref[at, :])
        drouter_ref[...] = drouter
        rides.finish(ride_refs)


def row_chunk(rows):
    best = rows
    for size in range(16, 513, 16):
        if rows % size == 0:
            best = size
    return best


def expert_block(x, g, w1, w2, bias, small, experts, old, entries, collective):
    rows, features = x.shape
    hidden_units = w1.shape[0]
    block = 512 if hidden_units % 512 == 0 else 256
    steps = hidden_units // block
    chunk = row_chunk(rows)
    add = old is not None
    out_type = bf16 if add else f32
    rides = Rides(entries)

    def whole(shape):
        return pl.BlockSpec(
            shape, lambda s: (0,) * len(shape), pipeline_mode=pl.Buffered(1)
        )

    packed = 2 * features + LANES
    unit_grads = pl.BlockSpec((block, packed), lambda s: (s, 0))
    units = pl.BlockSpec((block, features), lambda s: (s, 0))
    unit_row = pl.BlockSpec((1, block), lambda s: (0, s))
    in_specs = [
        whole(x.shape),
        whole(g.shape),
        units,
        units,
        unit_row,
        whole(small.shape),
    ]
    operands = [x, g, w1, w2, bias, small]
    if add:
        in_specs += [unit_grads, whole(small.shape)]
        operands += list(old)
    return pl.pallas_call(
        functools.partial(expert_kernel, experts, chunk, add, rides),
        grid=(steps,),
        in_specs=in_specs + rides.in_specs,
        out_specs=[
            whole(x.shape), whole(x.shape), unit_grads, whole(small.shape)
        ]
        + rides.out_specs,
        out_shape=[
            jax.ShapeDtypeStruct(x.shape, bf16),
            jax.ShapeDtypeStruct(x.shape, bf16),
            jax.ShapeDtypeStruct((hidden_units, packed), out_type),
            jax.ShapeDtypeStruct(small.shape, f32),
        ]
        + rides.out_shape,
        scratch_shapes=[
            pltpu.VMEM((rows, features), f32),
            pltpu.VMEM((rows, features), f32),
            pltpu.VMEM((rows, features), bf16),
            pltpu.VMEM((rows, small.shape[0]), f32),
            pltpu.VMEM((rows, block), bf16),
            pltpu.VMEM((rows, block), bf16),
        ]
        + rides.scratch,
        compiler_params=params(
            ("arbitrary",), collective_id=collective, has_side_effects=True
        ),
        cost_estimate=pl.CostEstimate(
            flops=12 * rows * features * hidden_units,
            bytes_accessed=(8 * rows + 12 * hidden_units) * features,
            transcendentals=rows * hidden_units,
        ),
        name="expert_block",
    )(*operands, *rides.operands)


def inner_size(parts):
    size = 1
    while parts % (2 * size) == 0 and 4 * size * size <= parts:
        size *= 2
    return size


def finish_kernel(
    inner, outer, slots0_ref, slots1_ref, gates0_ref, gates1_ref, residual0_ref, residual1_ref,
    returned0_ref, returned1_ref, part_ref, out_ref, din_ref, dout_ref, little_ref,
    second_ref, full_ref, sems2, sems3, sems4,
):
    step = pl.program_id(0)
    seq = slots0_ref.shape[1]
    features = out_ref.shape[2]
    width = part_ref.shape[2]
    tiles = width // LANES
    chunks = 3
    edges = [LANES * (tiles * c // chunks) for c in range(chunks + 1)]
    cuts = [pl.ds(edges[c], edges[c + 1] - edges[c]) for c in range(chunks)]
    me = lax.axis_index("expert")
    row = lax.rem(me, inner)
    line = me // inner

    def row_peer(hop):
        return lax.rem(row + hop, inner)

    def line_peer(hop):
        return lax.rem(line + hop, outer)

    def copy(source, target, sems, chunk, hop, peer):
        return pltpu.make_async_remote_copy(
            src_ref=source,
            dst_ref=target,
            send_sem=sems.at[0, chunk, hop - 1],
            recv_sem=sems.at[1, chunk, hop - 1],
            device_id={"expert": peer},
            device_id_type=pl.DeviceIdType.MESH,
        )

    def reduce_lines(chunk):
        at = cuts[chunk]
        return [
            copy(
                part_ref.at[line_peer(hop), :, at], second_ref.at[hop - 1, :, at],
                sems2, chunk, hop, line_peer(hop) * inner + row,
            )
            for hop in range(1, outer)
        ]

    def gather_lines(chunk):
        at = cuts[chunk]
        return [
            copy(
                full_ref.at[row, line, :, at], full_ref.at[row, line, :, at],
                sems3, chunk, hop, line_peer(hop) * inner + row,
            )
            for hop in range(1, outer)
        ]

    def gather_rows(chunk):
        at = cuts[chunk]
        return [
            copy(
                full_ref.at[row, :, :, at], full_ref.at[row, :, :, at],
                sems4, chunk, hop, line * inner + row_peer(hop),
            )
            for hop in range(1, inner)
        ]

    def start(copies):
        for item in copies:
            item.start()

    def wait(copies):
        for item in copies:
            item.wait()

    @pl.when(step == 0)
    def _():
        barrier = pltpu.get_barrier_semaphore()
        peers = [line * inner + row_peer(hop) for hop in range(1, inner)]
        peers += [line_peer(hop) * inner + row for hop in range(1, outer)]
        for peer in peers:
            pl.semaphore_signal(
                barrier,
                inc=1,
                device_id={"expert": peer},
                device_id_type=pl.DeviceIdType.MESH,
            )
        pl.semaphore_wait(barrier, len(peers))
        for chunk in range(chunks):
            start(reduce_lines(chunk))

    column = lax.broadcasted_iota(jnp.int32, (seq, returned0_ref.shape[0]), 1)

    def mix(slots_ref, gates_ref, residual_ref, returned_ref):
        slots = slots_ref[0]
        gates = gates_ref[0]
        total = residual_ref[0]
        for choice in range(TOP):
            holds = slots[:, choice : choice + 1] == column
            picked = dot(holds.astype(f32).astype(bf16), returned_ref[...])
            total = total + gates[:, choice : choice + 1] * picked
        out_ref[0] = total.astype(bf16)

    @pl.when(step < IMG_MB)
    def _():
        mix(slots0_ref, gates0_ref, residual0_ref, returned0_ref)

    @pl.when(step >= IMG_MB)
    def _():
        mix(slots1_ref, gates1_ref, residual1_ref, returned1_ref)

    @pl.when(step == 1)
    def _():
        for chunk in range(chunks):
            at = cuts[chunk]
            wait(reduce_lines(chunk))
            total = part_ref[line, :, at].astype(f32)
            for hop in range(1, outer):
                total = total + second_ref[hop - 1, :, at].astype(f32)
            full_ref[row, line, :, at] = total.astype(bf16)
            start(gather_lines(chunk))

    @pl.when(step == 3)
    def _():
        for chunk in range(chunks):
            wait(gather_lines(chunk))
            start(gather_rows(chunk))

    @pl.when(step == 2 * IMG_MB - 1)
    def _():
        for chunk in range(chunks):
            wait(gather_rows(chunk))
        for part in range(inner):
            for place in range(outer):
                block = part * outer + place
                din_ref[block] = full_ref[part, place, :, : 3 * features].astype(f32)
                dout_ref[block] = full_ref[part, place, :, 3 * features : 4 * features].astype(
                    f32
                )
                little_ref[block] = full_ref[part, place, :, 4 * features :].astype(f32)


def finish(slots, gates, residuals, returned, part, parts, collective):
    outer, share, width = part.shape
    inner = inner_size(parts)
    seq = slots[0].shape[1]
    images = IMG_MB * len(slots)
    features = residuals[0].shape[2]
    chunks = 3

    def whole(shape):
        return pl.BlockSpec(
            shape, lambda i: (0,) * len(shape), pipeline_mode=pl.Buffered(1)
        )

    def early(width):
        return pl.BlockSpec((1, seq, width), lambda i: (jnp.minimum(i, IMG_MB - 1), 0, 0))

    def late(width):
        return pl.BlockSpec((1, seq, width), lambda i: (jnp.maximum(i - IMG_MB, 0), 0, 0))

    def each(width):
        return pl.BlockSpec((1, seq, width), lambda i: (i, 0, 0))

    outs = [3 * features, features, width - 4 * features]
    return pl.pallas_call(
        functools.partial(finish_kernel, inner, outer),
        grid=(images,),
        in_specs=[
            early(TOP), late(TOP), early(TOP), late(TOP), early(features), late(features),
            whole(returned[0].shape), whole(returned[1].shape),
            whole(part.shape),
        ],
        out_specs=[each(features)] + [whole((parts, share, size)) for size in outs],
        out_shape=[jax.ShapeDtypeStruct((images, seq, features), bf16)]
        + [jax.ShapeDtypeStruct((parts, share, size), f32) for size in outs],
        scratch_shapes=[
            pltpu.VMEM((outer - 1, share, width), bf16),
            pltpu.VMEM((inner, outer, share, width), bf16),
            pltpu.SemaphoreType.DMA((2, chunks, outer - 1)),
            pltpu.SemaphoreType.DMA((2, chunks, outer - 1)),
            pltpu.SemaphoreType.DMA((2, chunks, inner - 1)),
        ],
        compiler_params=params(
            ("arbitrary",), collective_id=collective, has_side_effects=True
        ),
        cost_estimate=pl.CostEstimate(
            flops=4 * images * seq * returned[0].shape[0] * features,
            bytes_accessed=2 * features * (2 * returned[0].shape[0] + 3 * images * seq),
            transcendentals=0,
        ),
        name="finish",
    )(*slots, *gates, *residuals, *returned, part)


def attend_back_kernel(
    experts, add, rides, ranks, x_ref, top_ref, slots_ref, sent_ref, proj_ref, mixed_ref, residual_ref,
    dense_ref, small_ref, *refs
):
    if add:
        old_dense_ref, old_small_ref, drouter_ref = refs[:3]
        refs = refs[3:]
    count = len(rides.arrays)
    outs = 2 if add else 3
    sources, refs = refs[:count], refs[len(rides.operands) :]
    grad_x_ref, ddense_ref = refs[:2]
    if not add:
        dsmall_ref = refs[2]
    targets, refs = refs[outs : outs + count], refs[outs + count :]
    acc_in, acc_out, acc_small, dproj_ref = refs[:4]
    refs = refs[4:]
    more = ()
    if add:
        pack_ref, first_ref, second_ref, part_ref, third_ref = refs[:5]
        first_sems, second_sems, third_sems = refs[5:8]
        refs = refs[8:]
        rank = lax.axis_index("dp")
        core = lax.rem(rank, 2)
        pairs = ranks // 2
        partner = {"dp": rank + 1 - 2 * core}
        others = [{"dp": lax.rem(rank + 2 * hop, ranks)} for hop in range(1, pairs)]
        more = [partner] + others
    ride_refs = (sources, targets, refs)
    features = x_ref.shape[2]
    seq = x_ref.shape[1]
    step = pl.program_id(0)
    vectors = small_ref[...].astype(f32)

    @pl.when(step == 0)
    def _():
        rides.start(ride_refs, more)
        if add:
            acc_in[...] = old_dense_ref[:, : 3 * features]
            acc_out[...] = old_dense_ref[:, 3 * features :]
            acc_small[...] = old_small_ref[...]
        else:
            acc_in[...] = jnp.zeros(acc_in.shape, f32)
            acc_out[...] = jnp.zeros(acc_out.shape, f32)
            acc_small[...] = jnp.zeros(acc_small.shape, f32)

    column = lax.broadcasted_iota(jnp.int32, (seq, sent_ref.shape[0]), 1)
    slots = slots_ref[0]
    holds = (slots[:, 0:1] == column) | (slots[:, 1:2] == column)
    grad_hidden = dot(holds.astype(f32).astype(bf16), sent_ref[...])
    normed_two, inverse_two = norm_forward(residual_ref[0])
    acc_small[2:3, :] += jnp.sum(grad_hidden * normed_two, axis=0, keepdims=True)
    acc_small[3:4, :] += jnp.sum(grad_hidden, axis=0, keepdims=True)
    grad_residual = top_ref[0].astype(f32) + norm_backward(
        grad_hidden * vectors[experts + 2 : experts + 3], normed_two, inverse_two
    )
    grad_branch = grad_residual.astype(bf16)
    acc_out[...] += t_dot(mixed_ref[0], grad_branch)
    grad_mixed = dot_t(grad_branch, dense_ref[:, 3 * features :]).astype(bf16)
    low_half = lax.broadcasted_iota(jnp.int32, (1, LANES), 1) < HEAD_DIM
    scale = HEAD_DIM ** (-0.5)
    for pair in range(features // LANES):
        first = pair * LANES
        queries = proj_ref[0, :, first : first + LANES]
        keys = proj_ref[0, :, features + first : features + first + LANES]
        values = proj_ref[0, :, 2 * features + first : 2 * features + first + LANES]
        grad_out = grad_mixed[:, first : first + LANES]
        sums = [None, None, None]
        for half in range(2):
            keep = low_half if half == 0 else jnp.logical_not(low_half)
            head_queries = jnp.where(keep, queries * scale, 0).astype(bf16)
            head_keys = jnp.where(keep, keys, 0).astype(bf16)
            head_grad = jnp.where(keep, grad_out, 0).astype(bf16)
            scores = dot_t(keys, head_queries)
            top = jnp.max(scores, axis=0, keepdims=True)
            raised = jnp.exp(scores - top)
            probs = raised * (1.0 / jnp.sum(raised, axis=0, keepdims=True))
            grad_values = dot(probs.astype(bf16), head_grad)
            grad_weights = dot_t(values, head_grad)
            inner = jnp.sum(grad_weights * probs, axis=0, keepdims=True)
            grad_scores = (probs * (grad_weights - inner)).astype(bf16)
            grad_keys = dot(grad_scores, head_queries)
            grad_queries = t_dot(grad_scores, head_keys)
            for place, part in enumerate((grad_queries, grad_keys, grad_values)):
                sums[place] = part if half == 0 else sums[place] + part
        dproj_ref[:, first : first + LANES] = (sums[0] * scale).astype(bf16)
        dproj_ref[:, features + first : features + first + LANES] = sums[1].astype(bf16)
        dproj_ref[:, 2 * features + first : 2 * features + first + LANES] = sums[2].astype(bf16)
    normed_one, inverse_one = norm_forward(x_ref[0].astype(f32))
    attn_input = (
        normed_one * vectors[experts : experts + 1] + vectors[experts + 1 : experts + 2]
    ).astype(bf16)
    acc_in[...] += t_dot(attn_input, dproj_ref[...])
    grad_input = dot_t(dproj_ref[...], dense_ref[:, : 3 * features])
    acc_small[0:1, :] += jnp.sum(grad_input * normed_one, axis=0, keepdims=True)
    acc_small[1:2, :] += jnp.sum(grad_input, axis=0, keepdims=True)
    grad_x_ref[0] = grad_residual + norm_backward(
        grad_input * vectors[experts : experts + 1], normed_one, inverse_one
    )

    @pl.when(step == pl.num_programs(0) - 1)
    def _():
        if not add:
            ddense_ref[:, : 3 * features] = acc_in[...]
            ddense_ref[:, 3 * features :] = acc_out[...]
            dsmall_ref[...] = acc_small[...]
        else:
            used = acc_small.shape[0] + drouter_ref.shape[0]
            rest = jnp.zeros((LANES - used, features), f32)
            column = jnp.concatenate([acc_small[...], drouter_ref[...], rest], axis=0).T
            share = features // ranks
            for shard in range(ranks):
                at = slice(shard * share, (shard + 1) * share)
                place = (shard % 2, shard // 2)
                pack_ref[place[0], place[1], :, : 3 * features] = acc_in[at].astype(bf16)
                pack_ref[place[0], place[1], :, 3 * features : 4 * features] = acc_out[
                    at
                ].astype(bf16)
                pack_ref[place[0], place[1], :, 4 * features :] = column[at].astype(bf16)
            copy = pltpu.make_async_remote_copy(
                src_ref=pack_ref.at[1 - core],
                dst_ref=first_ref,
                send_sem=first_sems.at[0],
                recv_sem=first_sems.at[1],
                device_id=partner,
                device_id_type=pl.DeviceIdType.MESH,
            )
            copy.start()
            copy.wait()
            for pair in range(pairs):
                first_ref[pair] = (
                    first_ref[pair].astype(f32) + pack_ref[core, pair].astype(f32)
                ).astype(bf16)
            mine = rank // 2
            copies = [
                pltpu.make_async_remote_copy(
                    src_ref=first_ref.at[lax.rem(mine + hop, pairs)],
                    dst_ref=second_ref.at[hop - 1],
                    send_sem=second_sems.at[0, hop - 1],
                    recv_sem=second_sems.at[1, hop - 1],
                    device_id=others[hop - 1],
                    device_id_type=pl.DeviceIdType.MESH,
                )
                for hop in range(1, pairs)
            ]
            for copy in copies:
                copy.start()
            total = first_ref[mine].astype(f32)
            for copy in copies:
                copy.wait()
            for hop in range(1, pairs):
                total = total + second_ref[hop - 1].astype(f32)
            total = total.astype(bf16)
            inner, outer, rows = part_ref.shape[:3]
            for block in range(inner * outer):
                part_ref[block // outer, block % outer] = total[block * rows : (block + 1) * rows]
            me = lax.axis_index("expert")
            row = lax.rem(me, inner)
            copies = []
            for hop in range(1, inner):
                peer = lax.rem(row + hop, inner)
                copies.append(
                    pltpu.make_async_remote_copy(
                        src_ref=part_ref.at[peer],
                        dst_ref=third_ref.at[hop - 1],
                        send_sem=third_sems.at[0, hop - 1],
                        recv_sem=third_sems.at[1, hop - 1],
                        device_id={"expert": me - row + peer},
                        device_id_type=pl.DeviceIdType.MESH,
                    )
                )
            for copy in copies:
                copy.start()
            for copy in copies:
                copy.wait()
            total = part_ref[row].astype(f32)
            for hop in range(1, inner):
                total = total + third_ref[hop - 1].astype(f32)
            ddense_ref[...] = total.astype(bf16)
        rides.finish(ride_refs)


def attend_back(
    images, out_grad, slots, sent, proj, mixed, residual, dense, small, experts, group, old,
    entries, collective, ranks,
):
    seq, features = images.shape[1:]
    wide = 3 * features
    first = group * IMG_MB
    add = old is not None
    rides = Rides(entries)

    def rows(width):
        return pl.BlockSpec((1, seq, width), lambda i: (i, 0, 0))

    def source(width):
        return pl.BlockSpec((1, seq, width), lambda i: (first + i, 0, 0))

    def whole(shape):
        return pl.BlockSpec(shape, lambda i: (0, 0), pipeline_mode=pl.Buffered(1))

    small_grads = (8, features)
    in_specs = [
        source(features), source(features), rows(TOP), whole(sent.shape),
        rows(wide), rows(features), rows(features),
        whole(dense.shape), whole(small.shape),
    ]
    operands = [images, out_grad, slots, sent, proj, mixed, residual, dense, small]
    out_specs = [rows(features), whole((features, 4 * features))]
    out_shape = [
        jax.ShapeDtypeStruct((IMG_MB, seq, features), f32),
        jax.ShapeDtypeStruct((features, 4 * features), f32),
    ]
    if add:
        in_specs += [whole(array.shape) for array in old]
        operands += list(old)
        shard = (features // ranks, 4 * features + LANES)
        inner = inner_size(experts)
        part = (experts // inner, shard[0] // experts, shard[1])
        out_specs[1] = pl.BlockSpec(
            part, lambda i: (0, 0, 0), pipeline_mode=pl.Buffered(1)
        )
        out_shape[1] = jax.ShapeDtypeStruct(part, bf16)
        reduce_scratch = [
            pltpu.VMEM((2, ranks // 2, *shard), bf16),
            pltpu.VMEM((ranks // 2, *shard), bf16),
            pltpu.VMEM((ranks // 2 - 1, *shard), bf16),
            pltpu.VMEM((inner, *part), bf16),
            pltpu.VMEM((inner - 1, *part), bf16),
            pltpu.SemaphoreType.DMA((2,)),
            pltpu.SemaphoreType.DMA((2, ranks // 2 - 1)),
            pltpu.SemaphoreType.DMA((2, inner - 1)),
        ]
    else:
        out_specs.append(whole(small_grads))
        out_shape.append(jax.ShapeDtypeStruct(small_grads, f32))
        reduce_scratch = []
    return pl.pallas_call(
        functools.partial(attend_back_kernel, experts, add, rides, ranks),
        grid=(IMG_MB,),
        in_specs=in_specs + rides.in_specs,
        out_specs=out_specs + rides.out_specs,
        out_shape=out_shape + rides.out_shape,
        scratch_shapes=[
            pltpu.VMEM((features, 3 * features), f32),
            pltpu.VMEM((features, features), f32),
            pltpu.VMEM(small_grads, f32),
            pltpu.VMEM((seq, wide), bf16),
        ]
        + reduce_scratch
        + rides.scratch,
        input_output_aliases=rides.aliases(len(operands), len(out_specs)),
        compiler_params=params(
            ("arbitrary",), collective_id=collective, has_side_effects=True
        ),
        cost_estimate=pl.CostEstimate(
            flops=IMG_MB * seq * 40 * features * features,
            bytes_accessed=8 * features * (4 * features + IMG_MB * seq * 4),
            transcendentals=IMG_MB * HEADS * seq * seq,
        ),
        name="attend_back",
    )(*operands, *rides.operands)


def per_device(
    images, first_gain, first_shift, attn_in, attn_out, second_gain, second_shift, router,
    expert_in, expert_bias, expert_out, routes, out_grad,
):
    features = images.shape[2]
    experts = router.shape[1]
    tok_mb = IMG_MB * SEQ
    capacity = max(2, (5 * TOP * tok_mb // (4 * experts) + 7) // 8 * 8)
    slot_rows = experts * capacity
    micro = images.shape[0] // IMG_MB
    small_rows = (experts + 4 + 15) // 16 * 16

    own = router.shape[0]
    ranks = features // own
    bias_rows = expert_bias.shape[1] // own
    small = jnp.concatenate(
        [
            router.T,
            first_gain[None],
            first_shift[None],
            second_gain[None],
            second_shift[None],
            jnp.zeros((small_rows - experts - 4, own), bf16),
            expert_bias.reshape(bias_rows, own),
        ],
        axis=0,
    )
    dense = lax.all_gather(
        jnp.concatenate([attn_in, attn_out], axis=1), "dp", axis=0, tiled=True
    )
    small = lax.all_gather(small, "dp", axis=1, tiled=True)
    bias_row = small[small_rows:].reshape(bias_rows, -1, own).transpose(1, 0, 2).reshape(1, -1)
    small = small[:small_rows]
    weight_in = lax.all_gather(expert_in[0], "dp", axis=0, tiled=True)
    weight_out = lax.all_gather(expert_out[0], "dp", axis=0, tiled=True)

    def flat(blocks):
        return blocks.reshape(slot_rows, features)

    def blocks(rows):
        return rows.reshape(experts, capacity, features)

    routed = [route(routes, group, capacity) for group in range(micro)]
    slots = [item[0] for item in routed]
    lines = [item[1] for item in routed]
    grad_rows = [
        dispatch(lines[group], out_grad, group, experts, capacity) for group in range(micro)
    ]
    grads_0 = lax.all_to_all(grad_rows[0], "expert", split_axis=0, concat_axis=0, tiled=True)
    *kept_0, token_rows_0 = attend(
        images, routes, lines[0], dense, small, experts, capacity, 0
    )
    *kept_1, token_rows_1, received_0 = attend(
        images, routes, lines[1], dense, small, experts, capacity, 1,
        [(token_rows_0, 0, capacity, None)], 5,
    )
    saved = [kept_0, kept_1]
    result_0, dx_0, *old, grads_1, received_1 = expert_block(
        flat(received_0), flat(grads_0), weight_in, weight_out, bias_row, small, experts, None,
        [(grad_rows[1], 0, capacity, None), (token_rows_1, 0, capacity, None)], 0,
    )
    early = max(8, capacity * 3 // 8 // 8 * 8)
    result_1, dx_1, dweights, drouter, sent_0, returned_0 = expert_block(
        flat(received_1), flat(grads_1), weight_in, weight_out, bias_row, small, experts, old,
        [(blocks(dx_0), 0, capacity, None), (blocks(result_0), 0, early, None)], 1,
    )
    dweights = lax.psum_scatter(dweights, "dp", scatter_dimension=0, tiled=True)
    proj, mixed, residual, _ = saved[0]
    grad_x_0, *old, sent_1 = attend_back(
        images, out_grad, slots[0], flat(sent_0), proj, mixed, residual, dense, small,
        experts, 0, None, [(blocks(dx_1), 0, capacity, None)], 2, ranks,
    )
    proj, mixed, residual, _ = saved[1]
    grad_x_1, ddense, returned_0, returned_1 = attend_back(
        images, out_grad, slots[1], flat(sent_1), proj, mixed, residual, dense, small,
        experts, 1, old + [drouter],
        [(blocks(result_0), early, capacity, returned_0), (blocks(result_1), 0, capacity, None)],
        3, ranks,
    )
    grad_blocks = [grad_x_0, grad_x_1]
    block_out, grad_attn_in, grad_attn_out, little = finish(
        slots, [item[3] for item in saved], [item[2] for item in saved],
        [flat(returned_0), flat(returned_1)],
        ddense, experts, 4,
    )
    little = little.reshape(own, -1).T
    dweights = dweights.astype(f32)
    return (
        block_out,
        jnp.concatenate(grad_blocks, axis=0),
        little[0],
        little[1],
        grad_attn_in.reshape(own, -1),
        grad_attn_out.reshape(own, -1),
        little[2],
        little[3],
        little[8 : 8 + experts].T,
        dweights[None, :, :features],
        dweights[None, :, 2 * features],
        dweights[None, :, features : 2 * features],
    )


def solution(mesh):
    return jax.shard_map(
        per_device,
        mesh=mesh,
        in_specs=(
            P(("dp", "expert"), None, None),
            P("dp"),
            P("dp"),
            P("dp", None),
            P("dp", None),
            P("dp"),
            P("dp"),
            P("dp", None),
            P("expert", "dp", None),
            P("expert", "dp"),
            P("expert", "dp", None),
            P(("dp", "expert"), None, None),
            P(("dp", "expert"), None, None),
        ),
        out_specs=(
            P(("dp", "expert"), None, None),
            P(("dp", "expert"), None, None),
            P("dp"),
            P("dp"),
            P("dp", None),
            P("dp", None),
            P("dp"),
            P("dp"),
            P("dp", None),
            P("expert", "dp", None),
            P("expert", "dp"),
            P("expert", "dp", None),
        ),
        check_vma=False,
    )
```

```python
import functools

import jax
import jax.numpy as jnp
from jax import lax
from jax.experimental import pallas as pl
from jax.experimental.pallas import tpu as pltpu
from jax.sharding import PartitionSpec as P

HEADS = 12
HEAD_DIM = 64
SEQ = 197
MICRO = 2
IMG_MB = 3
TOP = 2
LANES = 128
VMEM_LIMIT = 60 * 1024 * 1024

epsilon = 1e-06
f32 = jnp.float32
bf16 = jnp.bfloat16


def params(semantics, **more):
    return pltpu.CompilerParams(
        dimension_semantics=semantics, vmem_limit_bytes=VMEM_LIMIT, **more
    )


def dot(left, right):
    return lax.dot_general(
        left, right, (((1,), (0,)), ((), ())), preferred_element_type=f32
    )


def dot_t(left, right):
    return lax.dot_general(
        left, right, (((1,), (1,)), ((), ())), preferred_element_type=f32
    )


def t_dot(left, right):
    return lax.dot_general(
        left, right, (((0,), (0,)), ((), ())), preferred_element_type=f32
    )


def norm_forward(values):
    row_mean = jnp.mean(values, axis=-1, keepdims=True)
    centred = values - row_mean
    row_var = jnp.mean(centred * centred, axis=-1, keepdims=True)
    inverse = lax.rsqrt(row_var + epsilon)
    return centred * inverse, inverse


def norm_backward(grad_normed, normed, inverse):
    mean_grad = jnp.mean(grad_normed, axis=-1, keepdims=True)
    mean_cross = jnp.mean(grad_normed * normed, axis=-1, keepdims=True)
    return inverse * (grad_normed - mean_grad - normed * mean_cross)


def softmax_lanes(logits, count):
    lane = lax.broadcasted_iota(jnp.int32, logits.shape, 1)
    masked = jnp.where(lane < count, logits, -1e30)
    top = jnp.max(masked, axis=-1, keepdims=True)
    raised = jnp.where(lane < count, jnp.exp(masked - top), 0.0)
    return raised / jnp.sum(raised, axis=-1, keepdims=True)


def gelu_both(values):
    size = jnp.abs(values)
    bell = jnp.exp(values * values * -0.5)
    t = 1.0 / (1.0 + (0.3275911 * 0.7071067811865476) * size)
    tail = t * (
        0.5 * 0.254829592
        + t
        * (
            0.5 * -0.284496736
            + t * (0.5 * 1.421413741 + t * (0.5 * -1.453152027 + t * (0.5 * 1.061405429)))
        )
    )
    tail = tail * bell
    phi = jnp.where(values >= 0, 1.0 - tail, tail)
    return values * phi, phi + values * (0.3989422804014327 * bell)


class Rides:
    def __init__(self, entries):
        self.arrays = [entry[0] for entry in entries]
        self.rows = [pl.ds(entry[1], entry[2] - entry[1]) for entry in entries]
        self.before = [entry[3] for entry in entries if entry[3] is not None]
        self.filled = [index for index, entry in enumerate(entries) if entry[3] is not None]
        arrays = self.arrays
        self.parts = arrays[0].shape[0]
        self.operands = self.arrays + self.before
        self.in_specs = [pl.BlockSpec(memory_space=pl.ANY)] * len(self.operands)
        self.out_specs = [pl.BlockSpec(memory_space=pl.ANY)] * len(arrays)
        self.out_shape = [jax.ShapeDtypeStruct(a.shape, a.dtype) for a in arrays]
        self.scratch = [
            pltpu.SemaphoreType.DMA((self.parts,)),
            pltpu.SemaphoreType.DMA((self.parts,)),
            pltpu.SemaphoreType.DMA,
        ] * len(arrays)

    def aliases(self, inputs, outputs):
        first = inputs + len(self.arrays)
        return {first + place: outputs + index for place, index in enumerate(self.filled)}

    def copy(self, refs, index, offset):
        me = lax.axis_index("expert")
        peer = lax.rem(me + offset, self.parts)
        sources, targets, sems = refs
        return pltpu.make_async_remote_copy(
            src_ref=sources[index].at[peer, self.rows[index]],
            dst_ref=targets[index].at[me, self.rows[index]],
            send_sem=sems[3 * index].at[offset],
            recv_sem=sems[3 * index + 1].at[offset],
            device_id={"expert": peer},
            device_id_type=pl.DeviceIdType.MESH,
        )

    def own(self, refs):
        me = lax.axis_index("expert")
        sources, targets, sems = refs
        return [
            pltpu.make_async_copy(
                sources[index].at[me, self.rows[index]],
                targets[index].at[me, self.rows[index]],
                sems[3 * index + 2],
            )
            for index in range(len(sources))
        ]

    def start(self, refs, more=()):
        me = lax.axis_index("expert")
        barrier = pltpu.get_barrier_semaphore()
        for peer in more:
            pl.semaphore_signal(
                barrier, inc=1, device_id=peer, device_id_type=pl.DeviceIdType.MESH
            )

        @pl.loop(1, self.parts)
        def _(offset):
            pl.semaphore_signal(
                barrier,
                inc=1,
                device_id={"expert": lax.rem(me + offset, self.parts)},
                device_id_type=pl.DeviceIdType.MESH,
            )

        pl.semaphore_wait(barrier, self.parts - 1 + len(more))
        for index in range(len(self.rows)):

            @pl.loop(1, self.parts)
            def _(offset):
                self.copy(refs, index, offset).start()

        for copy in self.own(refs):
            copy.start()

    def finish(self, refs):
        for copy in self.own(refs):
            copy.wait()
        for index in range(len(self.rows)):

            @pl.loop(1, self.parts)
            def _(offset):
                self.copy(refs, index, offset).wait()


HBM = pl.BlockSpec(memory_space=pl.ANY)


def staged(*arrays):
    buffers = [pltpu.VMEM(array.shape, array.dtype) for array in arrays]
    return buffers + [pltpu.SemaphoreType.DMA((4,))]


def route_kernel(capacity, routes_ref, slots_ref, lines_ref):
    seq = routes_ref.shape[1]
    row = lax.broadcasted_iota(jnp.int32, (seq, seq), 0)
    col = lax.broadcasted_iota(jnp.int32, (seq, seq), 1)
    earlier = (col < row).astype(f32).astype(bf16)
    lane = lax.broadcasted_iota(jnp.int32, (seq, LANES), 1)
    base = jnp.zeros((1, LANES), f32)
    table = jnp.full((seq, LANES), -1.0, f32)
    for choice in range(TOP):
        for image in range(IMG_MB):
            named = routes_ref[image][:, choice : choice + 1]
            onehot = (lane == named).astype(f32)
            count = dot(earlier, onehot.astype(bf16)) + base
            position = jnp.sum(onehot * count, axis=1, keepdims=True).astype(jnp.int32)
            base = base + jnp.sum(onehot, axis=0, keepdims=True)
            slot = jnp.where(position < capacity, named * capacity + position, -1)
            slots_ref[image, :, choice : choice + 1] = slot
            table = jnp.where(lane == image * TOP + choice, slot.astype(f32), table)
    lines_ref[...] = table.T[: lines_ref.shape[0]].astype(jnp.int32)


def route(routes, group, capacity):
    seq = routes.shape[1]
    return pl.pallas_call(
        functools.partial(route_kernel, capacity),
        grid=(1,),
        in_specs=[pl.BlockSpec((IMG_MB, seq, TOP), lambda i: (group, 0, 0))],
        out_specs=[
            pl.BlockSpec((IMG_MB, seq, TOP), lambda i: (0, 0, 0)),
            pl.BlockSpec((8, seq), lambda i: (0, 0)),
        ],
        out_shape=[
            jax.ShapeDtypeStruct((IMG_MB, seq, TOP), jnp.int32),
            jax.ShapeDtypeStruct((8, seq), jnp.int32),
        ],
        compiler_params=params(("arbitrary",)),
        cost_estimate=pl.CostEstimate(
            flops=10**8, bytes_accessed=10**6, transcendentals=0
        ),
        name="route",
    )(routes)


def dispatch_kernel(capacity, lines_ref, rows_ref, out_ref):
    first = pl.program_id(0) * capacity
    seq = rows_ref.shape[1]
    slot = lax.broadcasted_iota(jnp.int32, (capacity, seq), 0) + first
    lines = lines_ref[...]
    acc = jnp.zeros((capacity, rows_ref.shape[2]), f32)
    for image in range(IMG_MB):
        at = image * TOP
        holds = (lines[at : at + 1] == slot) | (lines[at + 1 : at + 2] == slot)
        acc = acc + dot(holds.astype(f32).astype(bf16), rows_ref[image])
    out_ref[0] = acc.astype(bf16)


def dispatch(lines, rows, group, experts, capacity):
    seq, features = rows.shape[1:]
    return pl.pallas_call(
        functools.partial(dispatch_kernel, capacity),
        grid=(experts,),
        in_specs=[
            pl.BlockSpec((8, seq), lambda e: (0, 0)),
            pl.BlockSpec((IMG_MB, seq, features), lambda e: (group, 0, 0)),
        ],
        out_specs=pl.BlockSpec((1, capacity, features), lambda e: (e, 0, 0)),
        out_shape=jax.ShapeDtypeStruct((experts, capacity, features), bf16),
        compiler_params=params(("arbitrary",)),
        cost_estimate=pl.CostEstimate(
            flops=2 * experts * capacity * IMG_MB * seq * features,
            bytes_accessed=2 * features * (experts * capacity + IMG_MB * seq),
            transcendentals=0,
        ),
        name="dispatch",
    )(lines, rows)


def attend_kernel(
    experts, rides, x_ref, routes_ref, lines_ref, dense_hbm, small_ref, *refs
):
    count = len(rides.arrays) if rides else 0
    sources, refs = refs[:count], refs[count:]
    proj_ref, mixed_ref, residual_ref, gates_ref, rows_ref = refs[:5]
    targets, (hidden_ref, dense_ref, load_sem, *sems) = refs[5 : 5 + count], refs[5 + count :]
    step = pl.program_id(0)
    load = pltpu.make_async_copy(dense_hbm, dense_ref, load_sem.at[0])

    @pl.when(step == 0)
    def _():
        if rides:
            rides.start((sources, targets, sems))
        load.start()
        load.wait()

    features = x_ref.shape[2]
    image = x_ref[0].astype(f32)
    vectors = small_ref[...].astype(f32)
    normed, _ = norm_forward(image)
    attn_input = (
        normed * vectors[experts : experts + 1] + vectors[experts + 1 : experts + 2]
    ).astype(bf16)
    proj_ref[0] = dot(attn_input, dense_ref[:, : 3 * features]).astype(bf16)
    low_half = lax.broadcasted_iota(jnp.int32, (1, LANES), 1) < HEAD_DIM
    for pair in range(features // LANES):
        first = pair * LANES
        queries = proj_ref[0, :, first : first + LANES]
        keys = proj_ref[0, :, features + first : features + first + LANES]
        values = proj_ref[0, :, 2 * features + first : 2 * features + first + LANES]
        out = None
        for half in range(2):
            keep = low_half if half == 0 else jnp.logical_not(low_half)
            scores = dot_t(
                jnp.where(keep, queries * HEAD_DIM ** (-0.5), 0).astype(bf16), keys
            )
            top = jnp.max(scores, axis=-1, keepdims=True)
            raised = jnp.exp(scores - top)
            share = 1.0 / jnp.sum(raised, axis=-1, keepdims=True)
            weights = (raised * share).astype(bf16)
            part = dot(weights, jnp.where(keep, values, 0).astype(bf16))
            out = part if out is None else out + part
        mixed_ref[0, :, first : first + LANES] = out.astype(bf16)
    residual = image + dot(mixed_ref[0], dense_ref[:, 3 * features :])
    residual_ref[0] = residual
    normed, _ = norm_forward(residual)
    hidden = (
        normed * vectors[experts + 2 : experts + 3] + vectors[experts + 3 : experts + 4]
    ).astype(bf16)
    hidden_ref[step] = hidden
    probs = softmax_lanes(dot_t(hidden, small_ref[...]), experts)
    lane = lax.broadcasted_iota(jnp.int32, probs.shape, 1)
    routes = routes_ref[0]
    for choice in range(TOP):
        gates_ref[0, :, choice : choice + 1] = jnp.sum(
            jnp.where(lane == routes[:, choice : choice + 1], probs, 0.0),
            axis=1,
            keepdims=True,
        )

    @pl.when(step == pl.num_programs(0) - 1)
    def _():
        seq = x_ref.shape[1]
        capacity = rows_ref.shape[1]
        lines = lines_ref[...]
        slot = lax.broadcasted_iota(jnp.int32, (capacity, seq), 0)

        @pl.loop(0, experts)
        def _(expert):
            here = slot + expert * capacity
            total = None
            for index in range(IMG_MB):
                at = index * TOP
                holds = (lines[at : at + 1] == here) | (lines[at + 1 : at + 2] == here)
                part = dot(holds.astype(f32).astype(bf16), hidden_ref[index])
                total = part if total is None else total + part
            rows_ref[expert] = total.astype(bf16)

        if rides:
            rides.finish((sources, targets, sems))


def attend(
    images, routes, lines, dense, small, experts, capacity, group, entries=(), collective=None
):
    seq, features = images.shape[1:]
    wide = 3 * features
    first = group * IMG_MB
    rides = Rides(entries) if entries else None
    more = {"collective_id": collective, "has_side_effects": True} if entries else {}
    slot_rows = (experts, capacity, features)

    def rows(width):
        return pl.BlockSpec((1, seq, width), lambda i: (i, 0, 0))

    def source(width):
        return pl.BlockSpec((1, seq, width), lambda i: (first + i, 0, 0))

    def whole(shape):
        return pl.BlockSpec(
            shape, lambda i: (0,) * len(shape), pipeline_mode=pl.Buffered(1)
        )

    def out(width, dtype):
        return jax.ShapeDtypeStruct((IMG_MB, seq, width), dtype)

    return pl.pallas_call(
        functools.partial(attend_kernel, experts, rides),
        grid=(IMG_MB,),
        in_specs=[
            source(features),
            source(TOP),
            whole(lines.shape),
            HBM,
            whole(small.shape),
        ]
        + (rides.in_specs if rides else []),
        out_specs=[rows(wide), rows(features), rows(features), rows(TOP), whole(slot_rows)]
        + (rides.out_specs if rides else []),
        out_shape=[
            out(wide, bf16),
            out(features, bf16),
            out(features, f32),
            out(TOP, f32),
            jax.ShapeDtypeStruct(slot_rows, bf16),
        ]
        + (rides.out_shape if rides else []),
        scratch_shapes=[pltpu.VMEM((IMG_MB, seq, features), bf16), *staged(dense)]
        + (rides.scratch if rides else []),
        compiler_params=params(("arbitrary",), **more),
        cost_estimate=pl.CostEstimate(
            flops=IMG_MB * seq * 16 * features * features,
            bytes_accessed=4 * features * (4 * features + IMG_MB * seq * 8),
            transcendentals=IMG_MB * HEADS * seq * seq,
        ),
        name="attend",
    )(images, routes, lines, dense, small, *(rides.operands if rides else []))


def expert_kernel(
    experts, chunk, add, rides, x_hbm, g_hbm, w1_ref, w2_ref, bias_ref, small_ref, *refs
):
    if add:
        old_w_ref, old_router_ref = refs[:2]
        refs = refs[2:]
    count = len(rides.arrays)
    sources, refs = refs[:count], refs[len(rides.operands) :]
    ride_refs = (sources, refs[4 : count + 4], refs[count + 15 :])
    refs = refs[:4] + refs[count + 4 : count + 15]
    (
        result_hbm, dx_hbm, dw_ref, drouter_ref,
        result_acc, dx_acc, dr_ref, probs_ref, act_ref, pre_ref,
        x_ref, g_ref, result_ref, dx_ref, copy_sems,
    ) = refs
    loads = [
        pltpu.make_async_copy(x_hbm, x_ref, copy_sems.at[0]),
        pltpu.make_async_copy(g_hbm, g_ref, copy_sems.at[1]),
    ]
    stores = [
        pltpu.make_async_copy(result_ref, result_hbm, copy_sems.at[2]),
        pltpu.make_async_copy(dx_ref, dx_hbm, copy_sems.at[3]),
    ]
    step = pl.program_id(0)
    last = pl.num_programs(0) - 1
    rows = x_ref.shape[0]
    mine = lax.axis_index("expert")
    chunks = rows // chunk

    @pl.when(step == 0)
    def _():
        rides.start(ride_refs)
        for load in loads:
            load.start()
        for load in loads:
            load.wait()
        for index in range(chunks):
            at = pl.ds(index * chunk, chunk)
            probs = softmax_lanes(dot_t(x_ref[at, :], small_ref[...]), experts)
            lane = lax.broadcasted_iota(jnp.int32, probs.shape, 1)
            probs_ref[at, :] = probs
            gate = jnp.sum(jnp.where(lane == mine, probs, 0.0), axis=1, keepdims=True)
            dr_ref[at, :] = (gate * g_ref[at, :].astype(f32)).astype(bf16)
            result_acc[at, :] = jnp.zeros((chunk, x_ref.shape[1]), f32)
            dx_acc[at, :] = jnp.zeros((chunk, x_ref.shape[1]), f32)

    w1 = w1_ref[...]
    w2 = w2_ref[...]
    bias = bias_ref[...].astype(f32)
    dbias = jnp.zeros(bias.shape, f32)
    for index in range(chunks):
        at = pl.ds(index * chunk, chunk)
        act, slope = gelu_both(dot_t(x_ref[at, :], w1) + bias)
        act = act.astype(bf16)
        act_ref[at, :] = act
        result_acc[at, :] += dot(act, w2)
        grad_pre = (dot_t(dr_ref[at, :], w2) * slope).astype(bf16)
        pre_ref[at, :] = grad_pre
        dbias = dbias + jnp.sum(grad_pre.astype(f32), axis=0, keepdims=True)
        dx_acc[at, :] += dot(grad_pre, w1)
    dw1 = t_dot(pre_ref[...], x_ref[...])
    dw2 = t_dot(act_ref[...], dr_ref[...])
    dbias = jnp.broadcast_to(dbias, (LANES, dbias.shape[1])).T
    first = 0
    for part in (dw1, dw2, dbias):
        at = pl.ds(first, part.shape[1])
        if add:
            part = part + old_w_ref[:, at]
        dw_ref[:, at] = part.astype(dw_ref.dtype)
        first += part.shape[1]

    @pl.when(step == last)
    def _():
        drouter = jnp.zeros(drouter_ref.shape, f32)
        if add:
            drouter = old_router_ref[...]
        for index in range(chunks):
            at = pl.ds(index * chunk, chunk)
            result = result_acc[at, :].astype(bf16)
            result_ref[at, :] = result
            grad_gate = jnp.sum(
                g_ref[at, :].astype(f32) * result.astype(f32), axis=1, keepdims=True
            )
            probs = probs_ref[at, :]
            lane = lax.broadcasted_iota(jnp.int32, probs.shape, 1)
            chosen = lane == mine
            gate = jnp.sum(jnp.where(chosen, probs, 0.0), axis=1, keepdims=True)
            logits = (grad_gate * gate) * (chosen.astype(f32) - probs)
            high = logits.astype(bf16)
            low = (logits - high.astype(f32)).astype(bf16)
            dx_ref[at, :] = (
                dx_acc[at, :] + dot(high, small_ref[...]) + dot(low, small_ref[...])
            ).astype(bf16)
            drouter = drouter + t_dot(high, x_ref[at, :]) + t_dot(low, x_ref[at, :])
        drouter_ref[...] = drouter
        for store in stores:
            store.start()
        rides.finish(ride_refs)
        for store in stores:
            store.wait()


def row_chunk(rows):
    best = rows
    for size in range(16, 513, 16):
        if rows % size == 0:
            best = size
    return best


def expert_block(x, g, w1, w2, bias, small, experts, old, entries, collective):
    rows, features = x.shape
    hidden_units = w1.shape[0]
    block = 512 if hidden_units % 512 == 0 else 256
    steps = hidden_units // block
    chunk = row_chunk(rows)
    add = old is not None
    out_type = bf16 if add else f32
    rides = Rides(entries)

    def whole(shape):
        return pl.BlockSpec(
            shape, lambda s: (0,) * len(shape), pipeline_mode=pl.Buffered(1)
        )

    packed = 2 * features + LANES
    unit_grads = pl.BlockSpec((block, packed), lambda s: (s, 0))
    units = pl.BlockSpec((block, features), lambda s: (s, 0))
    unit_row = pl.BlockSpec((1, block), lambda s: (0, s))
    in_specs = [
        HBM,
        HBM,
        units,
        units,
        unit_row,
        whole(small.shape),
    ]
    operands = [x, g, w1, w2, bias, small]
    if add:
        in_specs += [unit_grads, whole(small.shape)]
        operands += list(old)
    return pl.pallas_call(
        functools.partial(expert_kernel, experts, chunk, add, rides),
        grid=(steps,),
        in_specs=in_specs + rides.in_specs,
        out_specs=[
            HBM, HBM, unit_grads, whole(small.shape)
        ]
        + rides.out_specs,
        out_shape=[
            jax.ShapeDtypeStruct(x.shape, bf16),
            jax.ShapeDtypeStruct(x.shape, bf16),
            jax.ShapeDtypeStruct((hidden_units, packed), out_type),
            jax.ShapeDtypeStruct(small.shape, f32),
        ]
        + rides.out_shape,
        scratch_shapes=[
            pltpu.VMEM((rows, features), f32),
            pltpu.VMEM((rows, features), f32),
            pltpu.VMEM((rows, features), bf16),
            pltpu.VMEM((rows, small.shape[0]), f32),
            pltpu.VMEM((rows, block), bf16),
            pltpu.VMEM((rows, block), bf16),
            *staged(x, g, x, x),
        ]
        + rides.scratch,
        compiler_params=params(
            ("arbitrary",), collective_id=collective, has_side_effects=True
        ),
        cost_estimate=pl.CostEstimate(
            flops=12 * rows * features * hidden_units,
            bytes_accessed=(8 * rows + 12 * hidden_units) * features,
            transcendentals=rows * hidden_units,
        ),
        name="expert_block",
    )(*operands, *rides.operands)


def inner_size(parts):
    size = 1
    while parts % (2 * size) == 0 and 4 * size * size <= parts:
        size *= 2
    return size


def finish_kernel(
    inner, outer, slots0_ref, slots1_ref, gates0_ref, gates1_ref, residual0_ref, residual1_ref,
    returned0_hbm, returned1_hbm, part_ref, out_ref, din_ref, dout_ref, little_ref,
    returned0_ref, returned1_ref, load_sems, second_ref, full_ref, sems2, sems3, sems4,
):
    step = pl.program_id(0)
    seq = slots0_ref.shape[1]
    features = out_ref.shape[2]
    width = part_ref.shape[2]
    tiles = width // LANES
    chunks = 3
    edges = [LANES * (tiles * c // chunks) for c in range(chunks + 1)]
    cuts = [pl.ds(edges[c], edges[c + 1] - edges[c]) for c in range(chunks)]
    me = lax.axis_index("expert")
    row = lax.rem(me, inner)
    line = me // inner

    def row_peer(hop):
        return lax.rem(row + hop, inner)

    def line_peer(hop):
        return lax.rem(line + hop, outer)

    def copy(source, target, sems, chunk, hop, peer):
        return pltpu.make_async_remote_copy(
            src_ref=source,
            dst_ref=target,
            send_sem=sems.at[0, chunk, hop - 1],
            recv_sem=sems.at[1, chunk, hop - 1],
            device_id={"expert": peer},
            device_id_type=pl.DeviceIdType.MESH,
        )

    def reduce_lines(chunk):
        at = cuts[chunk]
        return [
            copy(
                part_ref.at[line_peer(hop), :, at], second_ref.at[hop - 1, :, at],
                sems2, chunk, hop, line_peer(hop) * inner + row,
            )
            for hop in range(1, outer)
        ]

    def gather_lines(chunk):
        at = cuts[chunk]
        return [
            copy(
                full_ref.at[row, line, :, at], full_ref.at[row, line, :, at],
                sems3, chunk, hop, line_peer(hop) * inner + row,
            )
            for hop in range(1, outer)
        ]

    def gather_rows(chunk):
        at = cuts[chunk]
        return [
            copy(
                full_ref.at[row, :, :, at], full_ref.at[row, :, :, at],
                sems4, chunk, hop, line * inner + row_peer(hop),
            )
            for hop in range(1, inner)
        ]

    loads = [
        pltpu.make_async_copy(returned0_hbm, returned0_ref, load_sems.at[0]),
        pltpu.make_async_copy(returned1_hbm, returned1_ref, load_sems.at[1]),
    ]

    def start(copies):
        for item in copies:
            item.start()

    def wait(copies):
        for item in copies:
            item.wait()

    @pl.when(step == 0)
    def _():
        barrier = pltpu.get_barrier_semaphore()
        peers = [line * inner + row_peer(hop) for hop in range(1, inner)]
        peers += [line_peer(hop) * inner + row for hop in range(1, outer)]
        for peer in peers:
            pl.semaphore_signal(
                barrier,
                inc=1,
                device_id={"expert": peer},
                device_id_type=pl.DeviceIdType.MESH,
            )
        pl.semaphore_wait(barrier, len(peers))
        for chunk in range(chunks):
            start(reduce_lines(chunk))
        start(loads)
        wait(loads[:1])

    @pl.when(step == IMG_MB)
    def _():
        wait(loads[1:])

    column = lax.broadcasted_iota(jnp.int32, (seq, returned0_ref.shape[0]), 1)

    def mix(slots_ref, gates_ref, residual_ref, returned_ref):
        slots = slots_ref[0]
        gates = gates_ref[0]
        total = residual_ref[0]
        for choice in range(TOP):
            holds = slots[:, choice : choice + 1] == column
            picked = dot(holds.astype(f32).astype(bf16), returned_ref[...])
            total = total + gates[:, choice : choice + 1] * picked
        out_ref[0] = total.astype(bf16)

    @pl.when(step < IMG_MB)
    def _():
        mix(slots0_ref, gates0_ref, residual0_ref, returned0_ref)

    @pl.when(step >= IMG_MB)
    def _():
        mix(slots1_ref, gates1_ref, residual1_ref, returned1_ref)

    @pl.when(step == 1)
    def _():
        for chunk in range(chunks):
            at = cuts[chunk]
            wait(reduce_lines(chunk))
            total = part_ref[line, :, at].astype(f32)
            for hop in range(1, outer):
                total = total + second_ref[hop - 1, :, at].astype(f32)
            full_ref[row, line, :, at] = total.astype(bf16)
            start(gather_lines(chunk))

    @pl.when(step == 3)
    def _():
        for chunk in range(chunks):
            wait(gather_lines(chunk))
            start(gather_rows(chunk))

    @pl.when(step == 2 * IMG_MB - 1)
    def _():
        for chunk in range(chunks):
            wait(gather_rows(chunk))
        for part in range(inner):
            for place in range(outer):
                block = part * outer + place
                din_ref[block] = full_ref[part, place, :, : 3 * features].astype(f32)
                dout_ref[block] = full_ref[part, place, :, 3 * features : 4 * features].astype(
                    f32
                )
                little_ref[block] = full_ref[part, place, :, 4 * features :].astype(f32)


def finish(slots, gates, residuals, returned, part, parts, collective):
    outer, share, width = part.shape
    inner = inner_size(parts)
    seq = slots[0].shape[1]
    images = IMG_MB * len(slots)
    features = residuals[0].shape[2]
    chunks = 3

    def whole(shape):
        return pl.BlockSpec(
            shape, lambda i: (0,) * len(shape), pipeline_mode=pl.Buffered(1)
        )

    def early(width):
        return pl.BlockSpec((1, seq, width), lambda i: (jnp.minimum(i, IMG_MB - 1), 0, 0))

    def late(width):
        return pl.BlockSpec((1, seq, width), lambda i: (jnp.maximum(i - IMG_MB, 0), 0, 0))

    def each(width):
        return pl.BlockSpec((1, seq, width), lambda i: (i, 0, 0))

    outs = [3 * features, features, width - 4 * features]
    return pl.pallas_call(
        functools.partial(finish_kernel, inner, outer),
        grid=(images,),
        in_specs=[
            early(TOP), late(TOP), early(TOP), late(TOP), early(features), late(features),
            HBM, HBM, whole(part.shape),
        ],
        out_specs=[each(features)] + [whole((parts, share, size)) for size in outs],
        out_shape=[jax.ShapeDtypeStruct((images, seq, features), bf16)]
        + [jax.ShapeDtypeStruct((parts, share, size), f32) for size in outs],
        scratch_shapes=[
            *staged(*returned),
            pltpu.VMEM((outer - 1, share, width), bf16),
            pltpu.VMEM((inner, outer, share, width), bf16),
            pltpu.SemaphoreType.DMA((2, chunks, outer - 1)),
            pltpu.SemaphoreType.DMA((2, chunks, outer - 1)),
            pltpu.SemaphoreType.DMA((2, chunks, inner - 1)),
        ],
        compiler_params=params(
            ("arbitrary",), collective_id=collective, has_side_effects=True
        ),
        cost_estimate=pl.CostEstimate(
            flops=4 * images * seq * returned[0].shape[0] * features,
            bytes_accessed=2 * features * (2 * returned[0].shape[0] + 3 * images * seq),
            transcendentals=0,
        ),
        name="finish",
    )(*slots, *gates, *residuals, *returned, part)


def attend_back_kernel(
    experts, add, rides, ranks, x_ref, top_ref, slots_ref, sent_hbm, proj_ref, mixed_ref, residual_ref,
    dense_hbm, small_ref, *refs
):
    if add:
        old_dense_ref, old_small_ref, drouter_ref = refs[:3]
        refs = refs[3:]
    count = len(rides.arrays)
    outs = 2 if add else 3
    sources, refs = refs[:count], refs[len(rides.operands) :]
    grad_x_ref, ddense_ref = refs[:2]
    if not add:
        dsmall_ref = refs[2]
    targets, refs = refs[outs : outs + count], refs[outs + count :]
    acc_in, acc_out, acc_small, dproj_ref = refs[:4]
    sent_ref, dense_ref, copy_sems = refs[4:7]
    refs = refs[7:]
    more = ()
    if add:
        pack_ref, first_ref, second_ref, part_ref, third_ref = refs[:5]
        first_sems, second_sems, third_sems = refs[5:8]
        refs = refs[8:]
        rank = lax.axis_index("dp")
        core = lax.rem(rank, 2)
        pairs = ranks // 2
        partner = {"dp": rank + 1 - 2 * core}
        others = [{"dp": lax.rem(rank + 2 * hop, ranks)} for hop in range(1, pairs)]
        more = [partner] + others
    ride_refs = (sources, targets, refs)
    features = x_ref.shape[2]
    seq = x_ref.shape[1]
    step = pl.program_id(0)
    vectors = small_ref[...].astype(f32)
    loads = [
        pltpu.make_async_copy(sent_hbm, sent_ref, copy_sems.at[0]),
        pltpu.make_async_copy(dense_hbm, dense_ref, copy_sems.at[1]),
    ]
    sums_hbm = old_dense_ref if add else ddense_ref
    halves = [
        (acc_in, sums_hbm.at[:, pl.ds(0, 3 * features)], copy_sems.at[2]),
        (acc_out, sums_hbm.at[:, pl.ds(3 * features, features)], copy_sems.at[3]),
    ]
    if add:
        moves = [pltpu.make_async_copy(far, near, sem) for near, far, sem in halves]
    else:
        moves = [pltpu.make_async_copy(near, far, sem) for near, far, sem in halves]

    @pl.when(step == 0)
    def _():
        rides.start(ride_refs, more)
        for load in loads:
            load.start()
        if add:
            for move in moves:
                move.start()
            acc_small[...] = old_small_ref[...]
        else:
            acc_in[...] = jnp.zeros(acc_in.shape, f32)
            acc_out[...] = jnp.zeros(acc_out.shape, f32)
            acc_small[...] = jnp.zeros(acc_small.shape, f32)
        for load in loads:
            load.wait()

    column = lax.broadcasted_iota(jnp.int32, (seq, sent_ref.shape[0]), 1)
    slots = slots_ref[0]
    holds = (slots[:, 0:1] == column) | (slots[:, 1:2] == column)
    grad_hidden = dot(holds.astype(f32).astype(bf16), sent_ref[...])
    normed_two, inverse_two = norm_forward(residual_ref[0])
    acc_small[2:3, :] += jnp.sum(grad_hidden * normed_two, axis=0, keepdims=True)
    acc_small[3:4, :] += jnp.sum(grad_hidden, axis=0, keepdims=True)
    grad_residual = top_ref[0].astype(f32) + norm_backward(
        grad_hidden * vectors[experts + 2 : experts + 3], normed_two, inverse_two
    )
    grad_branch = grad_residual.astype(bf16)
    grad_mixed = dot_t(grad_branch, dense_ref[:, 3 * features :]).astype(bf16)
    low_half = lax.broadcasted_iota(jnp.int32, (1, LANES), 1) < HEAD_DIM
    scale = HEAD_DIM ** (-0.5)
    for pair in range(features // LANES):
        first = pair * LANES
        queries = proj_ref[0, :, first : first + LANES]
        keys = proj_ref[0, :, features + first : features + first + LANES]
        values = proj_ref[0, :, 2 * features + first : 2 * features + first + LANES]
        grad_out = grad_mixed[:, first : first + LANES]
        sums = [None, None, None]
        for half in range(2):
            keep = low_half if half == 0 else jnp.logical_not(low_half)
            head_queries = jnp.where(keep, queries * scale, 0).astype(bf16)
            head_keys = jnp.where(keep, keys, 0).astype(bf16)
            head_grad = jnp.where(keep, grad_out, 0).astype(bf16)
            scores = dot_t(keys, head_queries)
            top = jnp.max(scores, axis=0, keepdims=True)
            raised = jnp.exp(scores - top)
            probs = raised * (1.0 / jnp.sum(raised, axis=0, keepdims=True))
            grad_values = dot(probs.astype(bf16), head_grad)
            grad_weights = dot_t(values, head_grad)
            inner = jnp.sum(grad_weights * probs, axis=0, keepdims=True)
            grad_scores = (probs * (grad_weights - inner)).astype(bf16)
            grad_keys = dot(grad_scores, head_queries)
            grad_queries = t_dot(grad_scores, head_keys)
            for place, part in enumerate((grad_queries, grad_keys, grad_values)):
                sums[place] = part if half == 0 else sums[place] + part
        dproj_ref[:, first : first + LANES] = (sums[0] * scale).astype(bf16)
        dproj_ref[:, features + first : features + first + LANES] = sums[1].astype(bf16)
        dproj_ref[:, 2 * features + first : 2 * features + first + LANES] = sums[2].astype(bf16)
    normed_one, inverse_one = norm_forward(x_ref[0].astype(f32))
    attn_input = (
        normed_one * vectors[experts : experts + 1] + vectors[experts + 1 : experts + 2]
    ).astype(bf16)
    if add:

        @pl.when(step == 0)
        def _():
            for move in moves:
                move.wait()

    acc_out[...] += t_dot(mixed_ref[0], grad_branch)
    acc_in[...] += t_dot(attn_input, dproj_ref[...])
    grad_input = dot_t(dproj_ref[...], dense_ref[:, : 3 * features])
    acc_small[0:1, :] += jnp.sum(grad_input * normed_one, axis=0, keepdims=True)
    acc_small[1:2, :] += jnp.sum(grad_input, axis=0, keepdims=True)
    grad_x_ref[0] = grad_residual + norm_backward(
        grad_input * vectors[experts : experts + 1], normed_one, inverse_one
    )

    @pl.when(step == pl.num_programs(0) - 1)
    def _():
        if not add:
            for move in moves:
                move.start()
            dsmall_ref[...] = acc_small[...]
        else:
            used = acc_small.shape[0] + drouter_ref.shape[0]
            rest = jnp.zeros((LANES - used, features), f32)
            column = jnp.concatenate([acc_small[...], drouter_ref[...], rest], axis=0).T
            share = features // ranks
            for shard in range(ranks):
                at = slice(shard * share, (shard + 1) * share)
                place = (shard % 2, shard // 2)
                pack_ref[place[0], place[1], :, : 3 * features] = acc_in[at].astype(bf16)
                pack_ref[place[0], place[1], :, 3 * features : 4 * features] = acc_out[
                    at
                ].astype(bf16)
                pack_ref[place[0], place[1], :, 4 * features :] = column[at].astype(bf16)
            copy = pltpu.make_async_remote_copy(
                src_ref=pack_ref.at[1 - core],
                dst_ref=first_ref,
                send_sem=first_sems.at[0],
                recv_sem=first_sems.at[1],
                device_id=partner,
                device_id_type=pl.DeviceIdType.MESH,
            )
            copy.start()
            copy.wait()
            for pair in range(pairs):
                first_ref[pair] = (
                    first_ref[pair].astype(f32) + pack_ref[core, pair].astype(f32)
                ).astype(bf16)
            mine = rank // 2
            copies = [
                pltpu.make_async_remote_copy(
                    src_ref=first_ref.at[lax.rem(mine + hop, pairs)],
                    dst_ref=second_ref.at[hop - 1],
                    send_sem=second_sems.at[0, hop - 1],
                    recv_sem=second_sems.at[1, hop - 1],
                    device_id=others[hop - 1],
                    device_id_type=pl.DeviceIdType.MESH,
                )
                for hop in range(1, pairs)
            ]
            for copy in copies:
                copy.start()
            total = first_ref[mine].astype(f32)
            for copy in copies:
                copy.wait()
            for hop in range(1, pairs):
                total = total + second_ref[hop - 1].astype(f32)
            total = total.astype(bf16)
            inner, outer, rows = part_ref.shape[:3]
            for block in range(inner * outer):
                part_ref[block // outer, block % outer] = total[block * rows : (block + 1) * rows]
            me = lax.axis_index("expert")
            row = lax.rem(me, inner)
            copies = []
            for hop in range(1, inner):
                peer = lax.rem(row + hop, inner)
                copies.append(
                    pltpu.make_async_remote_copy(
                        src_ref=part_ref.at[peer],
                        dst_ref=third_ref.at[hop - 1],
                        send_sem=third_sems.at[0, hop - 1],
                        recv_sem=third_sems.at[1, hop - 1],
                        device_id={"expert": me - row + peer},
                        device_id_type=pl.DeviceIdType.MESH,
                    )
                )
            for copy in copies:
                copy.start()
            for copy in copies:
                copy.wait()
            total = part_ref[row].astype(f32)
            for hop in range(1, inner):
                total = total + third_ref[hop - 1].astype(f32)
            ddense_ref[...] = total.astype(bf16)
        rides.finish(ride_refs)
        if not add:
            for move in moves:
                move.wait()


def attend_back(
    images, out_grad, slots, sent, proj, mixed, residual, dense, small, experts, group, old,
    entries, collective, ranks,
):
    seq, features = images.shape[1:]
    wide = 3 * features
    first = group * IMG_MB
    add = old is not None
    rides = Rides(entries)

    def rows(width):
        return pl.BlockSpec((1, seq, width), lambda i: (i, 0, 0))

    def source(width):
        return pl.BlockSpec((1, seq, width), lambda i: (first + i, 0, 0))

    def whole(shape):
        return pl.BlockSpec(shape, lambda i: (0, 0), pipeline_mode=pl.Buffered(1))

    small_grads = (8, features)
    in_specs = [
        source(features), source(features), rows(TOP), HBM,
        rows(wide), rows(features), rows(features),
        HBM, whole(small.shape),
    ]
    operands = [images, out_grad, slots, sent, proj, mixed, residual, dense, small]
    out_specs = [rows(features), HBM]
    out_shape = [
        jax.ShapeDtypeStruct((IMG_MB, seq, features), f32),
        jax.ShapeDtypeStruct((features, 4 * features), f32),
    ]
    if add:
        in_specs += [HBM] + [whole(array.shape) for array in old[1:]]
        operands += list(old)
        shard = (features // ranks, 4 * features + LANES)
        inner = inner_size(experts)
        part = (experts // inner, shard[0] // experts, shard[1])
        out_specs[1] = pl.BlockSpec(
            part, lambda i: (0, 0, 0), pipeline_mode=pl.Buffered(1)
        )
        out_shape[1] = jax.ShapeDtypeStruct(part, bf16)
        reduce_scratch = [
            pltpu.VMEM((2, ranks // 2, *shard), bf16),
            pltpu.VMEM((ranks // 2, *shard), bf16),
            pltpu.VMEM((ranks // 2 - 1, *shard), bf16),
            pltpu.VMEM((inner, *part), bf16),
            pltpu.VMEM((inner - 1, *part), bf16),
            pltpu.SemaphoreType.DMA((2,)),
            pltpu.SemaphoreType.DMA((2, ranks // 2 - 1)),
            pltpu.SemaphoreType.DMA((2, inner - 1)),
        ]
    else:
        out_specs.append(whole(small_grads))
        out_shape.append(jax.ShapeDtypeStruct(small_grads, f32))
        reduce_scratch = []
    return pl.pallas_call(
        functools.partial(attend_back_kernel, experts, add, rides, ranks),
        grid=(IMG_MB,),
        in_specs=in_specs + rides.in_specs,
        out_specs=out_specs + rides.out_specs,
        out_shape=out_shape + rides.out_shape,
        scratch_shapes=[
            pltpu.VMEM((features, 3 * features), f32),
            pltpu.VMEM((features, features), f32),
            pltpu.VMEM(small_grads, f32),
            pltpu.VMEM((seq, wide), bf16),
            *staged(sent, dense),
        ]
        + reduce_scratch
        + rides.scratch,
        input_output_aliases=rides.aliases(len(operands), len(out_specs)),
        compiler_params=params(
            ("arbitrary",), collective_id=collective, has_side_effects=True
        ),
        cost_estimate=pl.CostEstimate(
            flops=IMG_MB * seq * 40 * features * features,
            bytes_accessed=8 * features * (4 * features + IMG_MB * seq * 4),
            transcendentals=IMG_MB * HEADS * seq * seq,
        ),
        name="attend_back",
    )(*operands, *rides.operands)


def per_device(
    images, first_gain, first_shift, attn_in, attn_out, second_gain, second_shift, router,
    expert_in, expert_bias, expert_out, routes, out_grad,
):
    features = images.shape[2]
    experts = router.shape[1]
    tok_mb = IMG_MB * SEQ
    capacity = max(2, (5 * TOP * tok_mb // (4 * experts) + 7) // 8 * 8)
    slot_rows = experts * capacity
    micro = images.shape[0] // IMG_MB
    small_rows = (experts + 4 + 15) // 16 * 16

    own = router.shape[0]
    ranks = features // own
    bias_rows = expert_bias.shape[1] // own
    small = jnp.concatenate(
        [
            router.T,
            first_gain[None],
            first_shift[None],
            second_gain[None],
            second_shift[None],
            jnp.zeros((small_rows - experts - 4, own), bf16),
            expert_bias.reshape(bias_rows, own),
        ],
        axis=0,
    )
    dense = lax.all_gather(
        jnp.concatenate([attn_in, attn_out], axis=1), "dp", axis=0, tiled=True
    )
    small = lax.all_gather(small, "dp", axis=1, tiled=True)
    bias_row = small[small_rows:].reshape(bias_rows, -1, own).transpose(1, 0, 2).reshape(1, -1)
    small = small[:small_rows]
    weight_in = lax.all_gather(expert_in[0], "dp", axis=0, tiled=True)
    weight_out = lax.all_gather(expert_out[0], "dp", axis=0, tiled=True)

    def flat(blocks):
        return blocks.reshape(slot_rows, features)

    def blocks(rows):
        return rows.reshape(experts, capacity, features)

    routed = [route(routes, group, capacity) for group in range(micro)]
    slots = [item[0] for item in routed]
    lines = [item[1] for item in routed]
    grad_rows = [
        dispatch(lines[group], out_grad, group, experts, capacity) for group in range(micro)
    ]
    grads_0 = lax.all_to_all(grad_rows[0], "expert", split_axis=0, concat_axis=0, tiled=True)
    *kept_0, token_rows_0 = attend(
        images, routes, lines[0], dense, small, experts, capacity, 0
    )
    *kept_1, token_rows_1, received_0 = attend(
        images, routes, lines[1], dense, small, experts, capacity, 1,
        [(token_rows_0, 0, capacity, None)], 5,
    )
    saved = [kept_0, kept_1]
    result_0, dx_0, *old, grads_1, received_1 = expert_block(
        flat(received_0), flat(grads_0), weight_in, weight_out, bias_row, small, experts, None,
        [(grad_rows[1], 0, capacity, None), (token_rows_1, 0, capacity, None)], 0,
    )
    early = max(8, capacity * 3 // 8 // 8 * 8)
    result_1, dx_1, dweights, drouter, sent_0, returned_0 = expert_block(
        flat(received_1), flat(grads_1), weight_in, weight_out, bias_row, small, experts, old,
        [(blocks(dx_0), 0, capacity, None), (blocks(result_0), 0, early, None)], 1,
    )
    dweights = lax.psum_scatter(dweights, "dp", scatter_dimension=0, tiled=True)
    proj, mixed, residual, _ = saved[0]
    grad_x_0, *old, sent_1 = attend_back(
        images, out_grad, slots[0], flat(sent_0), proj, mixed, residual, dense, small,
        experts, 0, None, [(blocks(dx_1), 0, capacity, None)], 2, ranks,
    )
    proj, mixed, residual, _ = saved[1]
    grad_x_1, ddense, returned_0, returned_1 = attend_back(
        images, out_grad, slots[1], flat(sent_1), proj, mixed, residual, dense, small,
        experts, 1, old + [drouter],
        [(blocks(result_0), early, capacity, returned_0), (blocks(result_1), 0, capacity, None)],
        3, ranks,
    )
    grad_blocks = [grad_x_0, grad_x_1]
    block_out, grad_attn_in, grad_attn_out, little = finish(
        slots, [item[3] for item in saved], [item[2] for item in saved],
        [flat(returned_0), flat(returned_1)],
        ddense, experts, 4,
    )
    little = little.reshape(own, -1).T
    dweights = dweights.astype(f32)
    return (
        block_out,
        jnp.concatenate(grad_blocks, axis=0),
        little[0],
        little[1],
        grad_attn_in.reshape(own, -1),
        grad_attn_out.reshape(own, -1),
        little[2],
        little[3],
        little[8 : 8 + experts].T,
        dweights[None, :, :features],
        dweights[None, :, 2 * features],
        dweights[None, :, features : 2 * features],
    )


def solution(mesh):
    return jax.shard_map(
        per_device,
        mesh=mesh,
        in_specs=(
            P(("dp", "expert"), None, None),
            P("dp"),
            P("dp"),
            P("dp", None),
            P("dp", None),
            P("dp"),
            P("dp"),
            P("dp", None),
            P("expert", "dp", None),
            P("expert", "dp"),
            P("expert", "dp", None),
            P(("dp", "expert"), None, None),
            P(("dp", "expert"), None, None),
        ),
        out_specs=(
            P(("dp", "expert"), None, None),
            P(("dp", "expert"), None, None),
            P("dp"),
            P("dp"),
            P("dp", None),
            P("dp", None),
            P("dp"),
            P("dp"),
            P("dp", None),
            P("expert", "dp", None),
            P("expert", "dp"),
            P("expert", "dp", None),
        ),
        check_vma=False,
    )
```

```python
import functools

import jax
import jax.numpy as jnp
from jax import lax
from jax.experimental import pallas as pl
from jax.experimental.pallas import tpu as pltpu
from jax.sharding import PartitionSpec as P

HEADS = 12
HEAD_DIM = 64
SEQ = 197
MICRO = 2
IMG_MB = 3
TOP = 2
LANES = 128
VMEM_LIMIT = 60 * 1024 * 1024

epsilon = 1e-06
f32 = jnp.float32
bf16 = jnp.bfloat16


def params(semantics, **more):
    return pltpu.CompilerParams(
        dimension_semantics=semantics, vmem_limit_bytes=VMEM_LIMIT, **more
    )


def dot(left, right):
    return lax.dot_general(
        left, right, (((1,), (0,)), ((), ())), preferred_element_type=f32
    )


def dot_t(left, right):
    return lax.dot_general(
        left, right, (((1,), (1,)), ((), ())), preferred_element_type=f32
    )


def t_dot(left, right):
    return lax.dot_general(
        left, right, (((0,), (0,)), ((), ())), preferred_element_type=f32
    )


def norm_forward(values):
    row_mean = jnp.mean(values, axis=-1, keepdims=True)
    centred = values - row_mean
    row_var = jnp.mean(centred * centred, axis=-1, keepdims=True)
    inverse = lax.rsqrt(row_var + epsilon)
    return centred * inverse, inverse


def norm_backward(grad_normed, normed, inverse):
    mean_grad = jnp.mean(grad_normed, axis=-1, keepdims=True)
    mean_cross = jnp.mean(grad_normed * normed, axis=-1, keepdims=True)
    return inverse * (grad_normed - mean_grad - normed * mean_cross)


def softmax_lanes(logits, count):
    lane = lax.broadcasted_iota(jnp.int32, logits.shape, 1)
    masked = jnp.where(lane < count, logits, -1e30)
    top = jnp.max(masked, axis=-1, keepdims=True)
    raised = jnp.where(lane < count, jnp.exp(masked - top), 0.0)
    return raised / jnp.sum(raised, axis=-1, keepdims=True)


def gelu_both(values):
    size = jnp.abs(values)
    bell = jnp.exp(values * values * -0.5)
    t = 1.0 / (1.0 + (0.3275911 * 0.7071067811865476) * size)
    tail = t * (
        0.5 * 0.254829592
        + t
        * (
            0.5 * -0.284496736
            + t * (0.5 * 1.421413741 + t * (0.5 * -1.453152027 + t * (0.5 * 1.061405429)))
        )
    )
    tail = tail * bell
    phi = jnp.where(values >= 0, 1.0 - tail, tail)
    return values * phi, phi + values * (0.3989422804014327 * bell)


class Rides:
    def __init__(self, entries):
        self.arrays = [entry[0] for entry in entries]
        self.rows = [pl.ds(entry[1], entry[2] - entry[1]) for entry in entries]
        self.before = [entry[3] for entry in entries if entry[3] is not None]
        self.filled = [index for index, entry in enumerate(entries) if entry[3] is not None]
        arrays = self.arrays
        self.parts = arrays[0].shape[0]
        self.operands = self.arrays + self.before
        self.in_specs = [pl.BlockSpec(memory_space=pl.ANY)] * len(self.operands)
        self.out_specs = [pl.BlockSpec(memory_space=pl.ANY)] * len(arrays)
        self.out_shape = [jax.ShapeDtypeStruct(a.shape, a.dtype) for a in arrays]
        self.scratch = [
            pltpu.SemaphoreType.DMA((self.parts,)),
            pltpu.SemaphoreType.DMA((self.parts,)),
            pltpu.SemaphoreType.DMA,
        ] * len(arrays)

    def aliases(self, inputs, outputs):
        first = inputs + len(self.arrays)
        return {first + place: outputs + index for place, index in enumerate(self.filled)}

    def copy(self, refs, index, offset):
        me = lax.axis_index("expert")
        peer = lax.rem(me + offset, self.parts)
        sources, targets, sems = refs
        return pltpu.make_async_remote_copy(
            src_ref=sources[index].at[peer, self.rows[index]],
            dst_ref=targets[index].at[me, self.rows[index]],
            send_sem=sems[3 * index].at[offset],
            recv_sem=sems[3 * index + 1].at[offset],
            device_id={"expert": peer},
            device_id_type=pl.DeviceIdType.MESH,
        )

    def own(self, refs):
        me = lax.axis_index("expert")
        sources, targets, sems = refs
        return [
            pltpu.make_async_copy(
                sources[index].at[me, self.rows[index]],
                targets[index].at[me, self.rows[index]],
                sems[3 * index + 2],
            )
            for index in range(len(sources))
        ]

    def start(self, refs, more=()):
        self.greet(more)
        self.send(refs)

    def greet(self, more):
        me = lax.axis_index("expert")
        barrier = pltpu.get_barrier_semaphore()
        for peer in more:
            pl.semaphore_signal(
                barrier, inc=1, device_id=peer, device_id_type=pl.DeviceIdType.MESH
            )

        @pl.loop(1, self.parts)
        def _(offset):
            pl.semaphore_signal(
                barrier,
                inc=1,
                device_id={"expert": lax.rem(me + offset, self.parts)},
                device_id_type=pl.DeviceIdType.MESH,
            )

        pl.semaphore_wait(barrier, self.parts - 1 + len(more))

    def send(self, refs):
        for index in range(len(self.rows)):

            @pl.loop(1, self.parts)
            def _(offset):
                self.copy(refs, index, offset).start()

        for copy in self.own(refs):
            copy.start()

    def finish(self, refs):
        for copy in self.own(refs):
            copy.wait()
        for index in range(len(self.rows)):

            @pl.loop(1, self.parts)
            def _(offset):
                self.copy(refs, index, offset).wait()


class Gather:
    def __init__(self, rows, ranks):
        self.rows = rows
        self.pairs = ranks // 2
        self.ranks = ranks
        sems = pltpu.SemaphoreType.DMA((2, self.pairs))
        self.scratch = [sems, sems, pltpu.SemaphoreType.DMA]

    def place(self, full, rank):
        return full.at[pl.ds(pl.multiple_of(rank * self.rows, self.rows), self.rows)]

    def copy(self, source, target, sems, hop, peer):
        return pltpu.make_async_remote_copy(
            src_ref=source,
            dst_ref=target,
            send_sem=sems.at[0, hop],
            recv_sem=sems.at[1, hop],
            device_id={"dp": peer},
            device_id_type=pl.DeviceIdType.MESH,
        )

    def first(self, refs, hop):
        shard, full, sems = refs
        target = self.place(full, lax.axis_index("dp"))
        source = target if shard is None else shard
        return self.copy(source, target, sems[0], hop, dp_peers(self.ranks)[hop])

    def second(self, refs, hop):
        _, full, sems = refs
        rank = lax.axis_index("dp")
        held = self.place(full, lax.rem(rank + self.ranks - 2 * hop, self.ranks))
        return self.copy(held, held, sems[1], hop, dp_peers(self.ranks)[0])

    def own(self, refs):
        shard, full, sems = refs
        target = self.place(full, lax.axis_index("dp"))
        return pltpu.make_async_copy(shard, target, sems[2])

    def start(self, refs):
        for hop in range(self.pairs):
            self.first(refs, hop).start()
        if refs[0] is not None:
            self.own(refs).start()

    def forward(self, refs):
        for hop in range(1, self.pairs):
            self.first(refs, hop).wait()
            self.second(refs, hop).start()

    def finish(self, refs):
        if refs[0] is not None:
            self.own(refs).wait()
        self.first(refs, 0).wait()
        for hop in range(1, self.pairs):
            self.second(refs, hop).wait()


def dp_peers(ranks):
    rank = lax.axis_index("dp")
    partner = rank + 1 - 2 * lax.rem(rank, 2)
    return [partner] + [lax.rem(rank + 2 * hop, ranks) for hop in range(1, ranks // 2)]


HBM = pl.BlockSpec(memory_space=pl.ANY)


def staged(*arrays):
    buffers = [pltpu.VMEM(array.shape, array.dtype) for array in arrays]
    return buffers + [pltpu.SemaphoreType.DMA((4,))]


def route_group(capacity, routes_ref, slots_ref, first):
    seq = routes_ref.shape[1]
    row = lax.broadcasted_iota(jnp.int32, (seq, seq), 0)
    col = lax.broadcasted_iota(jnp.int32, (seq, seq), 1)
    earlier = (col < row).astype(f32).astype(bf16)
    lane = lax.broadcasted_iota(jnp.int32, (seq, LANES), 1)
    base = jnp.zeros((1, LANES), f32)
    table = jnp.full((seq, LANES), -1.0, f32)
    for choice in range(TOP):
        for image in range(IMG_MB):
            named = routes_ref[first + image][:, choice : choice + 1]
            onehot = (lane == named).astype(f32)
            count = dot(earlier, onehot.astype(bf16)) + base
            position = jnp.sum(onehot * count, axis=1, keepdims=True).astype(jnp.int32)
            base = base + jnp.sum(onehot, axis=0, keepdims=True)
            slot = jnp.where(position < capacity, named * capacity + position, -1)
            slots_ref[first + image, :, choice : choice + 1] = slot
            table = jnp.where(lane == image * TOP + choice, slot.astype(f32), table)
    return table.T[:8].astype(jnp.int32)


def dispatch(lines, rows_ref, first, out_ref):
    experts, capacity = out_ref.shape[:2]
    seq = rows_ref.shape[1]
    slot = lax.broadcasted_iota(jnp.int32, (capacity, seq), 0)

    @pl.loop(0, experts)
    def _(expert):
        here = slot + expert * capacity
        total = None
        for index in range(IMG_MB):
            at = index * TOP
            holds = (lines[at : at + 1] == here) | (lines[at + 1 : at + 2] == here)
            part = dot(holds.astype(f32).astype(bf16), rows_ref[first + index])
            total = part if total is None else total + part
        out_ref[expert] = total.astype(bf16)


def front_kernel(
    experts, capacity, ranks, rides, gathers,
    x_ref, routes_ref, top_ref, router_ref, vectors_ref, in_hbm, out_hbm, w1_hbm, w2_hbm,
    proj_ref, mixed_ref, residual_ref, gates_ref, slots_ref, small_ref, bias_ref,
    dense_hbm, w1_full, w2_full, grad_rows_hbm, token_rows_hbm, grads_hbm, received_hbm,
    dense_ref, rows_a, rows_b, hidden_ref, lines_ref, sems, *more,
):
    step = pl.program_id(0)
    features = x_ref.shape[2]
    ride_a = ([rows_a], [grads_hbm], more[:3])
    ride_b = ([rows_b], [received_hbm], more[3:6])
    dense_part = (None, dense_ref, more[6:9])
    w1_part = (w1_hbm, w1_full, more[9:12])
    w2_part = (w2_hbm, w2_full, more[12:15])
    gather_dense, gather_units = gathers
    keep_dense = pltpu.make_async_copy(dense_ref, dense_hbm, sems.at[0])
    keep_grads = pltpu.make_async_copy(rows_b, grad_rows_hbm, sems.at[1])
    keep_tokens = pltpu.make_async_copy(rows_a, token_rows_hbm, sems.at[2])

    @pl.when(step == 0)
    def _():
        own = features // ranks
        rank = lax.axis_index("dp")
        mine = pl.ds(pl.multiple_of(rank * own, own), own)
        fills = [
            pltpu.make_async_copy(
                in_hbm, dense_ref.at[mine, pl.ds(0, 3 * features)], sems.at[2]
            ),
            pltpu.make_async_copy(
                out_hbm, dense_ref.at[mine, pl.ds(3 * features, features)], sems.at[3]
            ),
        ]
        for fill in fills:
            fill.start()
        given = vectors_ref.shape[0]
        columns = jnp.concatenate(
            [
                router_ref[...].astype(f32),
                vectors_ref[...].astype(f32).T,
                jnp.zeros((own, LANES - experts - given), f32),
            ],
            axis=1,
        )
        dense_ref[mine, 4 * features :] = columns.astype(bf16)
        rides.greet([{"dp": peer} for peer in dp_peers(ranks)])
        for fill in fills:
            fill.wait()
        gather_dense.start(dense_part)
        lines = route_group(capacity, routes_ref, slots_ref, 0)
        lines_ref[0] = lines
        dispatch(lines, top_ref, 0, rows_a)
        rides.send(ride_a)
        lines = route_group(capacity, routes_ref, slots_ref, IMG_MB)
        lines_ref[1] = lines
        dispatch(lines, top_ref, IMG_MB, rows_b)
        keep_grads.start()
        gather_dense.forward(dense_part)
        gather_units.start(w1_part)
        gather_units.start(w2_part)
        gather_dense.finish(dense_part)
        keep_dense.start()
        small = dense_ref[:, 4 * features :].astype(f32).T
        small_ref[...] = small[: small_ref.shape[0]].astype(bf16)
        for line in range(given - 4):
            at = experts + 4 + line
            for place in range(ranks):
                first = (place * (given - 4) + line) * own
                bias_ref[:, first : first + own] = small[
                    at : at + 1, place * own : (place + 1) * own
                ].astype(bf16)
        keep_grads.wait()

    image = x_ref[0].astype(f32)
    vectors = small_ref[...].astype(f32)
    normed, _ = norm_forward(image)
    attn_input = (
        normed * vectors[experts : experts + 1] + vectors[experts + 1 : experts + 2]
    ).astype(bf16)
    proj_ref[0] = dot(attn_input, dense_ref[:, : 3 * features]).astype(bf16)
    low_half = lax.broadcasted_iota(jnp.int32, (1, LANES), 1) < HEAD_DIM
    for pair in range(features // LANES):
        first = pair * LANES
        queries = proj_ref[0, :, first : first + LANES]
        keys = proj_ref[0, :, features + first : features + first + LANES]
        values = proj_ref[0, :, 2 * features + first : 2 * features + first + LANES]
        out = None
        for half in range(2):
            keep = low_half if half == 0 else jnp.logical_not(low_half)
            scores = dot_t(
                jnp.where(keep, queries * HEAD_DIM ** (-0.5), 0).astype(bf16), keys
            )
            top = jnp.max(scores, axis=-1, keepdims=True)
            raised = jnp.exp(scores - top)
            share = 1.0 / jnp.sum(raised, axis=-1, keepdims=True)
            weights = (raised * share).astype(bf16)
            part = dot(weights, jnp.where(keep, values, 0).astype(bf16))
            out = part if out is None else out + part
        mixed_ref[0, :, first : first + LANES] = out.astype(bf16)
    residual = image + dot(mixed_ref[0], dense_ref[:, 3 * features : 4 * features])
    residual_ref[0] = residual
    normed, _ = norm_forward(residual)
    hidden = (
        normed * vectors[experts + 2 : experts + 3] + vectors[experts + 3 : experts + 4]
    ).astype(bf16)
    hidden_ref[lax.rem(step, IMG_MB)] = hidden
    probs = softmax_lanes(dot_t(hidden, small_ref[...]), experts)
    lane = lax.broadcasted_iota(jnp.int32, probs.shape, 1)
    routes = routes_ref[step]
    for choice in range(TOP):
        gates_ref[0, :, choice : choice + 1] = jnp.sum(
            jnp.where(lane == routes[:, choice : choice + 1], probs, 0.0),
            axis=1,
            keepdims=True,
        )

    @pl.when(step == IMG_MB - 1)
    def _():
        dispatch(lines_ref[0], hidden_ref, 0, rows_b)
        rides.send(ride_b)

    @pl.when(step == pl.num_programs(0) - 1)
    def _():
        rides.finish(ride_a)
        dispatch(lines_ref[1], hidden_ref, 0, rows_a)
        keep_tokens.start()
        gather_units.forward(w1_part)
        gather_units.forward(w2_part)
        gather_units.finish(w1_part)
        gather_units.finish(w2_part)
        keep_dense.wait()
        rides.finish(ride_b)
        keep_tokens.wait()


def front(
    images, routes, out_grad, router, vectors, attn_in, attn_out, w1, w2, experts, capacity,
    ranks, small_rows, collective,
):
    count, seq, features = images.shape
    width = 4 * features + LANES
    slot_rows = jax.ShapeDtypeStruct((experts, capacity, features), bf16)
    rides = Rides([(slot_rows, 0, capacity, None)])
    gathers = (Gather(router.shape[0], ranks), Gather(w1.shape[0], ranks))

    def rows(width):
        return pl.BlockSpec((1, seq, width), lambda i: (i, 0, 0))

    def whole(shape):
        return pl.BlockSpec(
            shape, lambda i: (0,) * len(shape), pipeline_mode=pl.Buffered(1)
        )

    def out(width, dtype):
        return jax.ShapeDtypeStruct((count, seq, width), dtype)

    units = jax.ShapeDtypeStruct((ranks * w1.shape[0], features), bf16)
    return pl.pallas_call(
        functools.partial(front_kernel, experts, capacity, ranks, rides, gathers),
        grid=(count,),
        in_specs=[
            rows(features), whole(routes.shape), whole(out_grad.shape), whole(router.shape),
            whole(vectors.shape), HBM, HBM, HBM, HBM,
        ],
        out_specs=[
            rows(3 * features), rows(features), rows(features), rows(TOP),
            whole(routes.shape), whole((small_rows, features)), whole((1, ranks * w1.shape[0])),
        ]
        + [HBM] * 7,
        out_shape=[
            out(3 * features, bf16),
            out(features, bf16),
            out(features, f32),
            out(TOP, f32),
            jax.ShapeDtypeStruct(routes.shape, jnp.int32),
            jax.ShapeDtypeStruct((small_rows, features), bf16),
            jax.ShapeDtypeStruct((1, ranks * w1.shape[0]), bf16),
            jax.ShapeDtypeStruct((features, width), bf16),
            units,
            units,
            slot_rows,
            slot_rows,
            slot_rows,
            slot_rows,
        ],
        scratch_shapes=[
            pltpu.VMEM((features, width), bf16),
            pltpu.VMEM(slot_rows.shape, bf16),
            pltpu.VMEM(slot_rows.shape, bf16),
            pltpu.VMEM((IMG_MB, seq, features), bf16),
            pltpu.VMEM((count // IMG_MB, 8, seq), jnp.int32),
            pltpu.SemaphoreType.DMA((4,)),
        ]
        + rides.scratch
        + rides.scratch
        + gathers[0].scratch
        + gathers[1].scratch
        + gathers[1].scratch,
        compiler_params=params(
            ("arbitrary",), collective_id=collective, has_side_effects=True
        ),
        cost_estimate=pl.CostEstimate(
            flops=count * seq * 16 * features * features,
            bytes_accessed=4 * features * (4 * features + count * seq * 8),
            transcendentals=count * HEADS * seq * seq,
        ),
        name="front",
    )(images, routes, out_grad, router, vectors, attn_in, attn_out, w1, w2)


def expert_kernel(
    experts, chunk, add, rides, x_hbm, g_hbm, w1_ref, w2_ref, bias_ref, small_ref, *refs
):
    if add:
        old_w_ref, old_router_ref = refs[:2]
        refs = refs[2:]
    count = len(rides.arrays)
    sources, refs = refs[:count], refs[len(rides.operands) :]
    ride_refs = (sources, refs[4 : count + 4], refs[count + 15 :])
    refs = refs[:4] + refs[count + 4 : count + 15]
    (
        result_hbm, dx_hbm, dw_ref, drouter_ref,
        result_acc, dx_acc, dr_ref, probs_ref, act_ref, pre_ref,
        x_ref, g_ref, result_ref, dx_ref, copy_sems,
    ) = refs
    loads = [
        pltpu.make_async_copy(x_hbm, x_ref, copy_sems.at[0]),
        pltpu.make_async_copy(g_hbm, g_ref, copy_sems.at[1]),
    ]
    stores = [
        pltpu.make_async_copy(result_ref, result_hbm, copy_sems.at[2]),
        pltpu.make_async_copy(dx_ref, dx_hbm, copy_sems.at[3]),
    ]
    step = pl.program_id(0)
    last = pl.num_programs(0) - 1
    rows = x_ref.shape[0]
    mine = lax.axis_index("expert")
    chunks = rows // chunk

    @pl.when(step == 0)
    def _():
        rides.start(ride_refs)
        for load in loads:
            load.start()
        for load in loads:
            load.wait()
        for index in range(chunks):
            at = pl.ds(index * chunk, chunk)
            probs = softmax_lanes(dot_t(x_ref[at, :], small_ref[...]), experts)
            lane = lax.broadcasted_iota(jnp.int32, probs.shape, 1)
            probs_ref[at, :] = probs
            gate = jnp.sum(jnp.where(lane == mine, probs, 0.0), axis=1, keepdims=True)
            dr_ref[at, :] = (gate * g_ref[at, :].astype(f32)).astype(bf16)
            result_acc[at, :] = jnp.zeros((chunk, x_ref.shape[1]), f32)
            dx_acc[at, :] = jnp.zeros((chunk, x_ref.shape[1]), f32)

    w1 = w1_ref[...]
    w2 = w2_ref[...]
    bias = bias_ref[...].astype(f32)
    dbias = jnp.zeros(bias.shape, f32)
    for index in range(chunks):
        at = pl.ds(index * chunk, chunk)
        act, slope = gelu_both(dot_t(x_ref[at, :], w1) + bias)
        act = act.astype(bf16)
        act_ref[at, :] = act
        result_acc[at, :] += dot(act, w2)
        grad_pre = (dot_t(dr_ref[at, :], w2) * slope).astype(bf16)
        pre_ref[at, :] = grad_pre
        dbias = dbias + jnp.sum(grad_pre.astype(f32), axis=0, keepdims=True)
        dx_acc[at, :] += dot(grad_pre, w1)
    dw1 = t_dot(pre_ref[...], x_ref[...])
    dw2 = t_dot(act_ref[...], dr_ref[...])
    dbias = jnp.broadcast_to(dbias, (LANES, dbias.shape[1])).T
    first = 0
    for part in (dw1, dw2, dbias):
        at = pl.ds(first, part.shape[1])
        if add:
            part = part + old_w_ref[:, at]
        dw_ref[:, at] = part.astype(dw_ref.dtype)
        first += part.shape[1]

    @pl.when(step == last)
    def _():
        drouter = jnp.zeros(drouter_ref.shape, f32)
        if add:
            drouter = old_router_ref[...]
        for index in range(chunks):
            at = pl.ds(index * chunk, chunk)
            result = result_acc[at, :].astype(bf16)
            result_ref[at, :] = result
            grad_gate = jnp.sum(
                g_ref[at, :].astype(f32) * result.astype(f32), axis=1, keepdims=True
            )
            probs = probs_ref[at, :]
            lane = lax.broadcasted_iota(jnp.int32, probs.shape, 1)
            chosen = lane == mine
            gate = jnp.sum(jnp.where(chosen, probs, 0.0), axis=1, keepdims=True)
            logits = (grad_gate * gate) * (chosen.astype(f32) - probs)
            high = logits.astype(bf16)
            low = (logits - high.astype(f32)).astype(bf16)
            dx_ref[at, :] = (
                dx_acc[at, :] + dot(high, small_ref[...]) + dot(low, small_ref[...])
            ).astype(bf16)
            drouter = drouter + t_dot(high, x_ref[at, :]) + t_dot(low, x_ref[at, :])
        drouter_ref[...] = drouter
        for store in stores:
            store.start()
        rides.finish(ride_refs)
        for store in stores:
            store.wait()


def row_chunk(rows):
    best = rows
    for size in range(16, 513, 16):
        if rows % size == 0:
            best = size
    return best


def expert_block(x, g, w1, w2, bias, small, experts, old, entries, collective):
    rows, features = x.shape
    hidden_units = w1.shape[0]
    block = 512 if hidden_units % 512 == 0 else 256
    steps = hidden_units // block
    chunk = row_chunk(rows)
    add = old is not None
    out_type = bf16 if add else f32
    rides = Rides(entries)

    def whole(shape):
        return pl.BlockSpec(
            shape, lambda s: (0,) * len(shape), pipeline_mode=pl.Buffered(1)
        )

    packed = 2 * features + LANES
    unit_grads = pl.BlockSpec((block, packed), lambda s: (s, 0))
    units = pl.BlockSpec((block, features), lambda s: (s, 0))
    unit_row = pl.BlockSpec((1, block), lambda s: (0, s))
    in_specs = [
        HBM,
        HBM,
        units,
        units,
        unit_row,
        whole(small.shape),
    ]
    operands = [x, g, w1, w2, bias, small]
    if add:
        in_specs += [unit_grads, whole(small.shape)]
        operands += list(old)
    return pl.pallas_call(
        functools.partial(expert_kernel, experts, chunk, add, rides),
        grid=(steps,),
        in_specs=in_specs + rides.in_specs,
        out_specs=[
            HBM, HBM, unit_grads, whole(small.shape)
        ]
        + rides.out_specs,
        out_shape=[
            jax.ShapeDtypeStruct(x.shape, bf16),
            jax.ShapeDtypeStruct(x.shape, bf16),
            jax.ShapeDtypeStruct((hidden_units, packed), out_type),
            jax.ShapeDtypeStruct(small.shape, f32),
        ]
        + rides.out_shape,
        scratch_shapes=[
            pltpu.VMEM((rows, features), f32),
            pltpu.VMEM((rows, features), f32),
            pltpu.VMEM((rows, features), bf16),
            pltpu.VMEM((rows, small.shape[0]), f32),
            pltpu.VMEM((rows, block), bf16),
            pltpu.VMEM((rows, block), bf16),
            *staged(x, g, x, x),
        ]
        + rides.scratch,
        compiler_params=params(
            ("arbitrary",), collective_id=collective, has_side_effects=True
        ),
        cost_estimate=pl.CostEstimate(
            flops=12 * rows * features * hidden_units,
            bytes_accessed=(8 * rows + 12 * hidden_units) * features,
            transcendentals=rows * hidden_units,
        ),
        name="expert_block",
    )(*operands, *rides.operands)


def inner_size(parts):
    size = 1
    while parts % (2 * size) == 0 and 4 * size * size <= parts:
        size *= 2
    return size


def finish_kernel(
    inner, outer, slots_ref, gates_ref, residual_ref,
    returned0_hbm, returned1_hbm, part_ref, out_ref, din_ref, dout_ref, little_ref,
    returned0_ref, returned1_ref, load_sems, second_ref, full_ref, sems2, sems3, sems4,
):
    step = pl.program_id(0)
    seq = slots_ref.shape[1]
    features = out_ref.shape[2]
    width = part_ref.shape[2]
    tiles = width // LANES
    chunks = 3
    edges = [LANES * (tiles * c // chunks) for c in range(chunks + 1)]
    cuts = [pl.ds(edges[c], edges[c + 1] - edges[c]) for c in range(chunks)]
    me = lax.axis_index("expert")
    row = lax.rem(me, inner)
    line = me // inner

    def row_peer(hop):
        return lax.rem(row + hop, inner)

    def line_peer(hop):
        return lax.rem(line + hop, outer)

    def copy(source, target, sems, chunk, hop, peer):
        return pltpu.make_async_remote_copy(
            src_ref=source,
            dst_ref=target,
            send_sem=sems.at[0, chunk, hop - 1],
            recv_sem=sems.at[1, chunk, hop - 1],
            device_id={"expert": peer},
            device_id_type=pl.DeviceIdType.MESH,
        )

    def reduce_lines(chunk):
        at = cuts[chunk]
        return [
            copy(
                part_ref.at[line_peer(hop), :, at], second_ref.at[hop - 1, :, at],
                sems2, chunk, hop, line_peer(hop) * inner + row,
            )
            for hop in range(1, outer)
        ]

    def gather_lines(chunk):
        at = cuts[chunk]
        return [
            copy(
                full_ref.at[row, line, :, at], full_ref.at[row, line, :, at],
                sems3, chunk, hop, line_peer(hop) * inner + row,
            )
            for hop in range(1, outer)
        ]

    def gather_rows(chunk):
        at = cuts[chunk]
        return [
            copy(
                full_ref.at[row, :, :, at], full_ref.at[row, :, :, at],
                sems4, chunk, hop, line * inner + row_peer(hop),
            )
            for hop in range(1, inner)
        ]

    loads = [
        pltpu.make_async_copy(returned0_hbm, returned0_ref, load_sems.at[0]),
        pltpu.make_async_copy(returned1_hbm, returned1_ref, load_sems.at[1]),
    ]

    def start(copies):
        for item in copies:
            item.start()

    def wait(copies):
        for item in copies:
            item.wait()

    @pl.when(step == 0)
    def _():
        barrier = pltpu.get_barrier_semaphore()
        peers = [line * inner + row_peer(hop) for hop in range(1, inner)]
        peers += [line_peer(hop) * inner + row for hop in range(1, outer)]
        for peer in peers:
            pl.semaphore_signal(
                barrier,
                inc=1,
                device_id={"expert": peer},
                device_id_type=pl.DeviceIdType.MESH,
            )
        pl.semaphore_wait(barrier, len(peers))
        for chunk in range(chunks):
            start(reduce_lines(chunk))
        start(loads)
        wait(loads[:1])

    @pl.when(step == IMG_MB)
    def _():
        wait(loads[1:])

    column = lax.broadcasted_iota(jnp.int32, (seq, returned0_ref.shape[0]), 1)

    def mix(returned_ref):
        slots = slots_ref[0]
        gates = gates_ref[0]
        total = residual_ref[0]
        for choice in range(TOP):
            holds = slots[:, choice : choice + 1] == column
            picked = dot(holds.astype(f32).astype(bf16), returned_ref[...])
            total = total + gates[:, choice : choice + 1] * picked
        out_ref[0] = total.astype(bf16)

    @pl.when(step < IMG_MB)
    def _():
        mix(returned0_ref)

    @pl.when(step >= IMG_MB)
    def _():
        mix(returned1_ref)

    @pl.when(step == 1)
    def _():
        for chunk in range(chunks):
            at = cuts[chunk]
            wait(reduce_lines(chunk))
            total = part_ref[line, :, at].astype(f32)
            for hop in range(1, outer):
                total = total + second_ref[hop - 1, :, at].astype(f32)
            full_ref[row, line, :, at] = total.astype(bf16)
            start(gather_lines(chunk))

    @pl.when(step == 3)
    def _():
        for chunk in range(chunks):
            wait(gather_lines(chunk))
            start(gather_rows(chunk))

    @pl.when(step == 2 * IMG_MB - 1)
    def _():
        for chunk in range(chunks):
            wait(gather_rows(chunk))
        for part in range(inner):
            for place in range(outer):
                block = part * outer + place
                din_ref[block] = full_ref[part, place, :, : 3 * features].astype(f32)
                dout_ref[block] = full_ref[part, place, :, 3 * features : 4 * features].astype(
                    f32
                )
                little_ref[block] = full_ref[part, place, :, 4 * features :].astype(f32)


def finish(slots, gates, residual, returned, part, parts, collective):
    outer, share, width = part.shape
    inner = inner_size(parts)
    images, seq, features = residual.shape
    chunks = 3

    def whole(shape):
        return pl.BlockSpec(
            shape, lambda i: (0,) * len(shape), pipeline_mode=pl.Buffered(1)
        )

    def each(width):
        return pl.BlockSpec((1, seq, width), lambda i: (i, 0, 0))

    outs = [3 * features, features, width - 4 * features]
    return pl.pallas_call(
        functools.partial(finish_kernel, inner, outer),
        grid=(images,),
        in_specs=[
            each(TOP), each(TOP), each(features),
            HBM, HBM, whole(part.shape),
        ],
        out_specs=[each(features)] + [whole((parts, share, size)) for size in outs],
        out_shape=[jax.ShapeDtypeStruct((images, seq, features), bf16)]
        + [jax.ShapeDtypeStruct((parts, share, size), f32) for size in outs],
        scratch_shapes=[
            *staged(*returned),
            pltpu.VMEM((outer - 1, share, width), bf16),
            pltpu.VMEM((inner, outer, share, width), bf16),
            pltpu.SemaphoreType.DMA((2, chunks, outer - 1)),
            pltpu.SemaphoreType.DMA((2, chunks, outer - 1)),
            pltpu.SemaphoreType.DMA((2, chunks, inner - 1)),
        ],
        compiler_params=params(
            ("arbitrary",), collective_id=collective, has_side_effects=True
        ),
        cost_estimate=pl.CostEstimate(
            flops=4 * images * seq * returned[0].shape[0] * features,
            bytes_accessed=2 * features * (2 * returned[0].shape[0] + 3 * images * seq),
            transcendentals=0,
        ),
        name="finish",
    )(slots, gates, residual, *returned, part)


def attend_back_kernel(
    experts, add, rides, ranks, x_ref, top_ref, slots_ref, sent_hbm, proj_ref, mixed_ref, residual_ref,
    dense_hbm, small_ref, *refs
):
    if add:
        old_dense_ref, old_small_ref, drouter_ref, sums_b_hbm = refs[:4]
        refs = refs[4:]
    else:
        dweights_hbm, refs = refs[0], refs[1:]
    count = len(rides.arrays)
    outs = 4 if add else 5
    sources, refs = refs[:count], refs[len(rides.operands) :]
    grad_x_ref, ddense_ref = refs[:2]
    if add:
        grad_b_ref, bias_b_ref = refs[2:4]
    else:
        dsmall_ref, sums_b_hbm, grad_a_ref = refs[2:5]
    targets, refs = refs[outs : outs + count], refs[outs + count :]
    acc_in, acc_out, acc_small, dproj_ref = refs[:4]
    sent_ref, dense_ref, copy_sems = refs[4:7]
    refs = refs[7:]
    rank = lax.axis_index("dp")
    core = lax.rem(rank, 2)
    mine = rank // 2
    pairs = ranks // 2
    partner, *others = [{"dp": peer} for peer in dp_peers(ranks)]
    more = [partner] + others

    def remote(source, target, sems, index, peer):
        return pltpu.make_async_remote_copy(
            src_ref=source,
            dst_ref=target,
            send_sem=sems.at[0, index],
            recv_sem=sems.at[1, index],
            device_id=peer,
            device_id_type=pl.DeviceIdType.MESH,
        )

    if add:
        pack_ref, first_ref, second_ref, part_ref, third_ref = refs[:5]
        first_sems, second_sems, third_sems = refs[5:8]
        own_b_ref, other_b_ref, own_b_sem, other_b_sems = refs[8:12]
        refs = refs[12:]
    else:
        own_w_ref, other_w_ref, other_a_ref = refs[:3]
        own_w_sems, other_w_sems, other_a_sems, keep_b_sem = refs[3:7]
        refs = refs[7:]

    def core_swap(pair):
        rows = other_w_ref.shape[1]
        at = pl.multiple_of((2 * pair + 1 - core) * rows, rows)
        source = dweights_hbm.at[pl.ds(at, rows)]
        return remote(source, other_w_ref.at[pair], other_w_sems, pair, partner)

    def core_own(pair):
        rows = own_w_ref.shape[1]
        at = pl.multiple_of((2 * pair + core) * rows, rows)
        return pltpu.make_async_copy(
            dweights_hbm.at[pl.ds(at, rows)], own_w_ref.at[pair], own_w_sems.at[pair]
        )

    def send_a(hop):
        at = pl.ds(0, x_ref.shape[2])
        source = own_w_ref.at[lax.rem(mine + hop, pairs), :, at]
        return remote(source, other_a_ref.at[hop - 1], other_a_sems, hop - 1, others[hop - 1])

    def keep_b():
        at = pl.ds(x_ref.shape[2], sums_b_hbm.shape[2])
        return pltpu.make_async_copy(own_w_ref.at[:, :, at], sums_b_hbm, keep_b_sem.at[0])

    def send_b(hop):
        source = sums_b_hbm.at[lax.rem(mine + hop, pairs)]
        return remote(source, other_b_ref.at[hop - 1], other_b_sems, hop - 1, others[hop - 1])

    def own_b():
        return pltpu.make_async_copy(sums_b_hbm.at[mine], own_b_ref, own_b_sem.at[0])

    ride_refs = (sources, targets, refs)
    features = x_ref.shape[2]
    seq = x_ref.shape[1]
    step = pl.program_id(0)
    vectors = small_ref[...].astype(f32)
    loads = [
        pltpu.make_async_copy(sent_hbm, sent_ref, copy_sems.at[0]),
        pltpu.make_async_copy(dense_hbm, dense_ref, copy_sems.at[1]),
    ]
    sums_hbm = old_dense_ref if add else ddense_ref
    halves = [
        (acc_in, sums_hbm.at[:, pl.ds(0, 3 * features)], copy_sems.at[2]),
        (acc_out, sums_hbm.at[:, pl.ds(3 * features, features)], copy_sems.at[3]),
    ]
    if add:
        moves = [pltpu.make_async_copy(far, near, sem) for near, far, sem in halves]
    else:
        moves = [pltpu.make_async_copy(near, far, sem) for near, far, sem in halves]

    @pl.when(step == 0)
    def _():
        rides.start(ride_refs, more)
        for load in loads:
            load.start()
        if add:
            own_b().start()
            for hop in range(1, pairs):
                send_b(hop).start()
        else:
            for pair in range(pairs):
                core_swap(pair).start()
                core_own(pair).start()
        if add:
            for move in moves:
                move.start()
            acc_small[...] = old_small_ref[...]
        else:
            acc_in[...] = jnp.zeros(acc_in.shape, f32)
            acc_out[...] = jnp.zeros(acc_out.shape, f32)
            acc_small[...] = jnp.zeros(acc_small.shape, f32)
        for load in loads:
            load.wait()

    if not add:

        @pl.when(step == 1)
        def _():
            for pair in range(pairs):
                core_swap(pair).wait()
                core_own(pair).wait()
                total = own_w_ref[pair].astype(f32) + other_w_ref[pair].astype(f32)
                own_w_ref[pair] = total.astype(bf16)
            for hop in range(1, pairs):
                send_a(hop).start()
            keep_b().start()

    column = lax.broadcasted_iota(jnp.int32, (seq, sent_ref.shape[0]), 1)
    slots = slots_ref[0]
    holds = (slots[:, 0:1] == column) | (slots[:, 1:2] == column)
    grad_hidden = dot(holds.astype(f32).astype(bf16), sent_ref[...])
    normed_two, inverse_two = norm_forward(residual_ref[0])
    acc_small[2:3, :] += jnp.sum(grad_hidden * normed_two, axis=0, keepdims=True)
    acc_small[3:4, :] += jnp.sum(grad_hidden, axis=0, keepdims=True)
    grad_residual = top_ref[0].astype(f32) + norm_backward(
        grad_hidden * vectors[experts + 2 : experts + 3], normed_two, inverse_two
    )
    grad_branch = grad_residual.astype(bf16)
    grad_mixed = dot_t(grad_branch, dense_ref[:, 3 * features : 4 * features]).astype(bf16)
    low_half = lax.broadcasted_iota(jnp.int32, (1, LANES), 1) < HEAD_DIM
    scale = HEAD_DIM ** (-0.5)
    for pair in range(features // LANES):
        first = pair * LANES
        queries = proj_ref[0, :, first : first + LANES]
        keys = proj_ref[0, :, features + first : features + first + LANES]
        values = proj_ref[0, :, 2 * features + first : 2 * features + first + LANES]
        grad_out = grad_mixed[:, first : first + LANES]
        sums = [None, None, None]
        for half in range(2):
            keep = low_half if half == 0 else jnp.logical_not(low_half)
            head_queries = jnp.where(keep, queries * scale, 0).astype(bf16)
            head_keys = jnp.where(keep, keys, 0).astype(bf16)
            head_grad = jnp.where(keep, grad_out, 0).astype(bf16)
            scores = dot_t(keys, head_queries)
            top = jnp.max(scores, axis=0, keepdims=True)
            raised = jnp.exp(scores - top)
            probs = raised * (1.0 / jnp.sum(raised, axis=0, keepdims=True))
            grad_values = dot(probs.astype(bf16), head_grad)
            grad_weights = dot_t(values, head_grad)
            inner = jnp.sum(grad_weights * probs, axis=0, keepdims=True)
            grad_scores = (probs * (grad_weights - inner)).astype(bf16)
            grad_keys = dot(grad_scores, head_queries)
            grad_queries = t_dot(grad_scores, head_keys)
            for place, part in enumerate((grad_queries, grad_keys, grad_values)):
                sums[place] = part if half == 0 else sums[place] + part
        dproj_ref[:, first : first + LANES] = (sums[0] * scale).astype(bf16)
        dproj_ref[:, features + first : features + first + LANES] = sums[1].astype(bf16)
        dproj_ref[:, 2 * features + first : 2 * features + first + LANES] = sums[2].astype(bf16)
    normed_one, inverse_one = norm_forward(x_ref[0].astype(f32))
    attn_input = (
        normed_one * vectors[experts : experts + 1] + vectors[experts + 1 : experts + 2]
    ).astype(bf16)
    if add:

        @pl.when(step == 0)
        def _():
            for move in moves:
                move.wait()

    acc_out[...] += t_dot(mixed_ref[0], grad_branch)
    acc_in[...] += t_dot(attn_input, dproj_ref[...])
    grad_input = dot_t(dproj_ref[...], dense_ref[:, : 3 * features])
    acc_small[0:1, :] += jnp.sum(grad_input * normed_one, axis=0, keepdims=True)
    acc_small[1:2, :] += jnp.sum(grad_input, axis=0, keepdims=True)
    grad_x_ref[0] = grad_residual + norm_backward(
        grad_input * vectors[experts : experts + 1], normed_one, inverse_one
    )

    @pl.when(step == pl.num_programs(0) - 1)
    def _():
        if not add:
            for move in moves:
                move.start()
            dsmall_ref[...] = acc_small[...]
            total = own_w_ref[mine, :, :features].astype(f32)
            for hop in range(1, pairs):
                send_a(hop).wait()
                total = total + other_a_ref[hop - 1].astype(f32)
            grad_a_ref[...] = total
            keep_b().wait()
        else:
            used = acc_small.shape[0] + drouter_ref.shape[0]
            rest = jnp.zeros((LANES - used, features), f32)
            column = jnp.concatenate([acc_small[...], drouter_ref[...], rest], axis=0).T
            share = features // ranks
            for shard in range(ranks):
                at = slice(shard * share, (shard + 1) * share)
                place = (shard % 2, shard // 2)
                pack_ref[place[0], place[1], :, : 3 * features] = acc_in[at].astype(bf16)
                pack_ref[place[0], place[1], :, 3 * features : 4 * features] = acc_out[
                    at
                ].astype(bf16)
                pack_ref[place[0], place[1], :, 4 * features :] = column[at].astype(bf16)
            copy = remote(pack_ref.at[1 - core], first_ref, first_sems, 0, partner)
            copy.start()
            copy.wait()
            for pair in range(pairs):
                first_ref[pair] = (
                    first_ref[pair].astype(f32) + pack_ref[core, pair].astype(f32)
                ).astype(bf16)
            copies = [
                remote(
                    first_ref.at[lax.rem(mine + hop, pairs)], second_ref.at[hop - 1],
                    second_sems, hop - 1, others[hop - 1],
                )
                for hop in range(1, pairs)
            ]
            for copy in copies:
                copy.start()
            own_b().wait()
            total = own_b_ref[...].astype(f32)
            for hop in range(1, pairs):
                send_b(hop).wait()
                total = total + other_b_ref[hop - 1].astype(f32)
            grad_b_ref[...] = total[:, :features]
            bias_b_ref[...] = total[:, features:]
            total = first_ref[mine].astype(f32)
            for copy in copies:
                copy.wait()
            for hop in range(1, pairs):
                total = total + second_ref[hop - 1].astype(f32)
            total = total.astype(bf16)
            inner, outer, rows = part_ref.shape[:3]
            for block in range(inner * outer):
                part_ref[block // outer, block % outer] = total[block * rows : (block + 1) * rows]
            me = lax.axis_index("expert")
            row = lax.rem(me, inner)
            copies = []
            for hop in range(1, inner):
                peer = lax.rem(row + hop, inner)
                copies.append(
                    remote(
                        part_ref.at[peer], third_ref.at[hop - 1], third_sems, hop - 1,
                        {"expert": me - row + peer},
                    )
                )
            for copy in copies:
                copy.start()
            for copy in copies:
                copy.wait()
            total = part_ref[row].astype(f32)
            for hop in range(1, inner):
                total = total + third_ref[hop - 1].astype(f32)
            ddense_ref[...] = total.astype(bf16)
        rides.finish(ride_refs)
        if not add:
            for move in moves:
                move.wait()


def attend_back(
    images, out_grad, slots, sent, proj, mixed, residual, dense, small, experts, group, old,
    entries, collective, ranks, dweights=None, sums_b=None,
):
    seq, features = images.shape[1:]
    wide = 3 * features
    first = group * IMG_MB
    add = old is not None
    rides = Rides(entries)

    def rows(width):
        return pl.BlockSpec((1, seq, width), lambda i: (i, 0, 0))

    def source(width):
        return pl.BlockSpec((1, seq, width), lambda i: (first + i, 0, 0))

    def whole(shape):
        return pl.BlockSpec(shape, lambda i: (0, 0), pipeline_mode=pl.Buffered(1))

    small_grads = (8, features)
    in_specs = [
        source(features), source(features), source(TOP), HBM,
        source(wide), source(features), source(features),
        HBM, whole(small.shape),
    ]
    operands = [images, out_grad, slots, sent, proj, mixed, residual, dense, small]
    out_specs = [rows(features), HBM]
    out_shape = [
        jax.ShapeDtypeStruct((IMG_MB, seq, features), f32),
        jax.ShapeDtypeStruct((features, 4 * features), f32),
    ]
    if add:
        in_specs += [HBM] + [whole(array.shape) for array in old[1:]] + [HBM]
        operands += list(old) + [sums_b]
        out_specs += [whole((sums_b.shape[1], features)), whole((sums_b.shape[1], LANES))]
        out_shape += [
            jax.ShapeDtypeStruct((sums_b.shape[1], features), f32),
            jax.ShapeDtypeStruct((sums_b.shape[1], LANES), f32),
        ]
        shard = (features // ranks, 4 * features + LANES)
        inner = inner_size(experts)
        part = (experts // inner, shard[0] // experts, shard[1])
        out_specs[1] = pl.BlockSpec(
            part, lambda i: (0, 0, 0), pipeline_mode=pl.Buffered(1)
        )
        out_shape[1] = jax.ShapeDtypeStruct(part, bf16)
        reduce_scratch = [
            pltpu.VMEM((2, ranks // 2, *shard), bf16),
            pltpu.VMEM((ranks // 2, *shard), bf16),
            pltpu.VMEM((ranks // 2 - 1, *shard), bf16),
            pltpu.VMEM((inner, *part), bf16),
            pltpu.VMEM((inner - 1, *part), bf16),
            pltpu.SemaphoreType.DMA((2, 1)),
            pltpu.SemaphoreType.DMA((2, ranks // 2 - 1)),
            pltpu.SemaphoreType.DMA((2, inner - 1)),
            pltpu.VMEM(sums_b.shape[1:], bf16),
            pltpu.VMEM((ranks // 2 - 1, *sums_b.shape[1:]), bf16),
            pltpu.SemaphoreType.DMA((1,)),
            pltpu.SemaphoreType.DMA((2, ranks // 2 - 1)),
        ]
    else:
        out_specs.append(whole(small_grads))
        out_shape.append(jax.ShapeDtypeStruct(small_grads, f32))
        in_specs.append(HBM)
        operands.append(dweights)
        units = dweights.shape[0] // ranks
        rest = dweights.shape[1] - features
        out_specs += [HBM, whole((units, features))]
        out_shape += [
            jax.ShapeDtypeStruct((ranks // 2, units, rest), bf16),
            jax.ShapeDtypeStruct((units, features), f32),
        ]
        reduce_scratch = [
            pltpu.VMEM((ranks // 2, units, dweights.shape[1]), bf16),
            pltpu.VMEM((ranks // 2, units, dweights.shape[1]), bf16),
            pltpu.VMEM((ranks // 2 - 1, units, features), bf16),
            pltpu.SemaphoreType.DMA((ranks // 2,)),
            pltpu.SemaphoreType.DMA((2, ranks // 2)),
            pltpu.SemaphoreType.DMA((2, ranks // 2 - 1)),
            pltpu.SemaphoreType.DMA((1,)),
        ]
    return pl.pallas_call(
        functools.partial(attend_back_kernel, experts, add, rides, ranks),
        grid=(IMG_MB,),
        in_specs=in_specs + rides.in_specs,
        out_specs=out_specs + rides.out_specs,
        out_shape=out_shape + rides.out_shape,
        scratch_shapes=[
            pltpu.VMEM((features, 3 * features), f32),
            pltpu.VMEM((features, features), f32),
            pltpu.VMEM(small_grads, f32),
            pltpu.VMEM((seq, wide), bf16),
            *staged(sent, dense),
        ]
        + reduce_scratch
        + rides.scratch,
        input_output_aliases=rides.aliases(len(operands), len(out_specs)),
        compiler_params=params(
            ("arbitrary",), collective_id=collective, has_side_effects=True
        ),
        cost_estimate=pl.CostEstimate(
            flops=IMG_MB * seq * 40 * features * features,
            bytes_accessed=8 * features * (4 * features + IMG_MB * seq * 4),
            transcendentals=IMG_MB * HEADS * seq * seq,
        ),
        name="attend_back",
    )(*operands, *rides.operands)


def per_device(
    images, first_gain, first_shift, attn_in, attn_out, second_gain, second_shift, router,
    expert_in, expert_bias, expert_out, routes, out_grad,
):
    features = images.shape[2]
    experts = router.shape[1]
    tok_mb = IMG_MB * SEQ
    capacity = max(2, (5 * TOP * tok_mb // (4 * experts) + 7) // 8 * 8)
    slot_rows = experts * capacity
    own = router.shape[0]
    ranks = features // own
    bias_rows = expert_bias.shape[1] // own
    used = experts + 4 + bias_rows
    small_rows = (used + 15) // 16 * 16
    vectors = jnp.concatenate(
        [first_gain, first_shift, second_gain, second_shift, expert_bias.reshape(-1)]
    ).reshape(4 + bias_rows, own)

    def flat(blocks):
        return blocks.reshape(slot_rows, features)

    def blocks(rows):
        return rows.reshape(experts, capacity, features)

    (
        proj, mixed, residual, gates, slots, small, bias_row, dense, weight_in, weight_out,
        grad_rows_1, token_rows_1, grads_0, received_0,
    ) = front(
        images, routes, out_grad, router, vectors, attn_in, attn_out, expert_in[0],
        expert_out[0], experts, capacity, ranks, small_rows, 5,
    )
    result_0, dx_0, *old, grads_1, received_1 = expert_block(
        flat(received_0), flat(grads_0), weight_in, weight_out, bias_row, small, experts, None,
        [(grad_rows_1, 0, capacity, None), (token_rows_1, 0, capacity, None)], 0,
    )
    early = max(8, capacity * 3 // 8 // 8 * 8)
    result_1, dx_1, dweights, drouter, sent_0, returned_0 = expert_block(
        flat(received_1), flat(grads_1), weight_in, weight_out, bias_row, small, experts, old,
        [(blocks(dx_0), 0, capacity, None), (blocks(result_0), 0, early, None)], 1,
    )
    grad_x_0, *old, sums_b, grad_expert_in, sent_1 = attend_back(
        images, out_grad, slots, flat(sent_0), proj, mixed, residual, dense, small,
        experts, 0, None, [(blocks(dx_1), 0, capacity, None)], 2, ranks, dweights,
    )
    grad_x_1, ddense, grad_expert_out, grad_bias, returned_0, returned_1 = attend_back(
        images, out_grad, slots, flat(sent_1), proj, mixed, residual, dense, small,
        experts, 1, old + [drouter],
        [(blocks(result_0), early, capacity, returned_0), (blocks(result_1), 0, capacity, None)],
        3, ranks, None, sums_b,
    )
    grad_blocks = [grad_x_0, grad_x_1]
    block_out, grad_attn_in, grad_attn_out, little = finish(
        slots, gates, residual, [flat(returned_0), flat(returned_1)], ddense, experts, 4
    )
    little = little.reshape(own, -1).T
    return (
        block_out,
        jnp.concatenate(grad_blocks, axis=0),
        little[0],
        little[1],
        grad_attn_in.reshape(own, -1),
        grad_attn_out.reshape(own, -1),
        little[2],
        little[3],
        little[8 : 8 + experts].T,
        grad_expert_in[None],
        grad_bias[None, :, 0],
        grad_expert_out[None],
    )


def solution(mesh):
    return jax.shard_map(
        per_device,
        mesh=mesh,
        in_specs=(
            P(("dp", "expert"), None, None),
            P("dp"),
            P("dp"),
            P("dp", None),
            P("dp", None),
            P("dp"),
            P("dp"),
            P("dp", None),
            P("expert", "dp", None),
            P("expert", "dp"),
            P("expert", "dp", None),
            P(("dp", "expert"), None, None),
            P(("dp", "expert"), None, None),
        ),
        out_specs=(
            P(("dp", "expert"), None, None),
            P(("dp", "expert"), None, None),
            P("dp"),
            P("dp"),
            P("dp", None),
            P("dp", None),
            P("dp"),
            P("dp"),
            P("dp", None),
            P("expert", "dp", None),
            P("expert", "dp"),
            P("expert", "dp", None),
        ),
        check_vma=False,
    )
```

```python
import functools

import jax
import jax.numpy as jnp
from jax import lax
from jax.experimental import pallas as pl
from jax.experimental.pallas import tpu as pltpu
from jax.sharding import PartitionSpec as P

HEADS = 12
HEAD_DIM = 64
SEQ = 197
MICRO = 2
IMG_MB = 3
TOP = 2
LANES = 128
VMEM_LIMIT = 60 * 1024 * 1024

epsilon = 1e-06
f32 = jnp.float32
bf16 = jnp.bfloat16


def params(semantics, **more):
    return pltpu.CompilerParams(
        dimension_semantics=semantics, vmem_limit_bytes=VMEM_LIMIT, **more
    )


def dot(left, right):
    return lax.dot_general(
        left, right, (((1,), (0,)), ((), ())), preferred_element_type=f32
    )


def dot_t(left, right):
    return lax.dot_general(
        left, right, (((1,), (1,)), ((), ())), preferred_element_type=f32
    )


def t_dot(left, right):
    return lax.dot_general(
        left, right, (((0,), (0,)), ((), ())), preferred_element_type=f32
    )


def norm_forward(values):
    row_mean = jnp.mean(values, axis=-1, keepdims=True)
    centred = values - row_mean
    row_var = jnp.mean(centred * centred, axis=-1, keepdims=True)
    inverse = lax.rsqrt(row_var + epsilon)
    return centred * inverse, inverse


def norm_backward(grad_normed, normed, inverse):
    mean_grad = jnp.mean(grad_normed, axis=-1, keepdims=True)
    mean_cross = jnp.mean(grad_normed * normed, axis=-1, keepdims=True)
    return inverse * (grad_normed - mean_grad - normed * mean_cross)


def softmax_lanes(logits, count):
    lane = lax.broadcasted_iota(jnp.int32, logits.shape, 1)
    masked = jnp.where(lane < count, logits, -1e30)
    top = jnp.max(masked, axis=-1, keepdims=True)
    raised = jnp.where(lane < count, jnp.exp(masked - top), 0.0)
    return raised / jnp.sum(raised, axis=-1, keepdims=True)


def gelu_both(values):
    size = jnp.abs(values)
    bell = jnp.exp(values * values * -0.5)
    t = 1.0 / (1.0 + (0.3275911 * 0.7071067811865476) * size)
    tail = t * (
        0.5 * 0.254829592
        + t
        * (
            0.5 * -0.284496736
            + t * (0.5 * 1.421413741 + t * (0.5 * -1.453152027 + t * (0.5 * 1.061405429)))
        )
    )
    tail = tail * bell
    phi = jnp.where(values >= 0, 1.0 - tail, tail)
    return values * phi, phi + values * (0.3989422804014327 * bell)


class Rides:
    def __init__(self, entries):
        self.arrays = [entry[0] for entry in entries]
        self.rows = [pl.ds(entry[1], entry[2] - entry[1]) for entry in entries]
        self.before = [entry[3] for entry in entries if entry[3] is not None]
        self.filled = [index for index, entry in enumerate(entries) if entry[3] is not None]
        arrays = self.arrays
        self.parts = arrays[0].shape[0]
        self.operands = self.arrays + self.before
        self.in_specs = [pl.BlockSpec(memory_space=pl.ANY)] * len(self.operands)
        self.out_specs = [pl.BlockSpec(memory_space=pl.ANY)] * len(arrays)
        self.out_shape = [jax.ShapeDtypeStruct(a.shape, a.dtype) for a in arrays]
        self.scratch = [
            pltpu.SemaphoreType.DMA((self.parts,)),
            pltpu.SemaphoreType.DMA((self.parts,)),
            pltpu.SemaphoreType.DMA,
        ] * len(arrays)

    def aliases(self, inputs, outputs):
        first = inputs + len(self.arrays)
        return {first + place: outputs + index for place, index in enumerate(self.filled)}

    def copy(self, refs, index, offset):
        me = lax.axis_index("expert")
        peer = lax.rem(me + offset, self.parts)
        sources, targets, sems = refs
        return pltpu.make_async_remote_copy(
            src_ref=sources[index].at[peer, self.rows[index]],
            dst_ref=targets[index].at[me, self.rows[index]],
            send_sem=sems[3 * index].at[offset],
            recv_sem=sems[3 * index + 1].at[offset],
            device_id={"expert": peer},
            device_id_type=pl.DeviceIdType.MESH,
        )

    def own(self, refs):
        me = lax.axis_index("expert")
        sources, targets, sems = refs
        return [
            pltpu.make_async_copy(
                sources[index].at[me, self.rows[index]],
                targets[index].at[me, self.rows[index]],
                sems[3 * index + 2],
            )
            for index in range(len(sources))
        ]

    def start(self, refs, more=()):
        self.greet(more)
        self.send(refs)

    def greet(self, more):
        me = lax.axis_index("expert")
        barrier = pltpu.get_barrier_semaphore()
        for peer in more:
            pl.semaphore_signal(
                barrier, inc=1, device_id=peer, device_id_type=pl.DeviceIdType.MESH
            )

        @pl.loop(1, self.parts)
        def _(offset):
            pl.semaphore_signal(
                barrier,
                inc=1,
                device_id={"expert": lax.rem(me + offset, self.parts)},
                device_id_type=pl.DeviceIdType.MESH,
            )

        pl.semaphore_wait(barrier, self.parts - 1 + len(more))

    def send_hop(self, refs, hop):
        for index in range(len(self.rows)):
            self.copy(refs, index, hop).start()

    def send_own(self, refs):
        for copy in self.own(refs):
            copy.start()

    def send(self, refs):
        for index in range(len(self.rows)):

            @pl.loop(1, self.parts)
            def _(offset):
                self.copy(refs, index, offset).start()

        for copy in self.own(refs):
            copy.start()

    def finish(self, refs):
        for copy in self.own(refs):
            copy.wait()
        for index in range(len(self.rows)):

            @pl.loop(1, self.parts)
            def _(offset):
                self.copy(refs, index, offset).wait()


class Gather:
    def __init__(self, rows, ranks):
        self.rows = rows
        self.pairs = ranks // 2
        self.ranks = ranks
        sems = pltpu.SemaphoreType.DMA((2, self.pairs))
        self.scratch = [sems, sems, pltpu.SemaphoreType.DMA]

    def place(self, full, rank):
        return full.at[pl.ds(pl.multiple_of(rank * self.rows, self.rows), self.rows)]

    def copy(self, source, target, sems, hop, peer):
        return pltpu.make_async_remote_copy(
            src_ref=source,
            dst_ref=target,
            send_sem=sems.at[0, hop],
            recv_sem=sems.at[1, hop],
            device_id={"dp": peer},
            device_id_type=pl.DeviceIdType.MESH,
        )

    def first(self, refs, hop):
        shard, full, sems = refs
        target = self.place(full, lax.axis_index("dp"))
        source = target if shard is None else shard
        return self.copy(source, target, sems[0], hop, dp_peers(self.ranks)[hop])

    def second(self, refs, hop):
        _, full, sems = refs
        rank = lax.axis_index("dp")
        held = self.place(full, lax.rem(rank + self.ranks - 2 * hop, self.ranks))
        return self.copy(held, held, sems[1], hop, dp_peers(self.ranks)[0])

    def own(self, refs):
        shard, full, sems = refs
        target = self.place(full, lax.axis_index("dp"))
        return pltpu.make_async_copy(shard, target, sems[2])

    def start(self, refs):
        for hop in range(self.pairs):
            self.first(refs, hop).start()
        if refs[0] is not None:
            self.own(refs).start()

    def forward(self, refs):
        for hop in range(1, self.pairs):
            self.first(refs, hop).wait()
            self.second(refs, hop).start()

    def finish(self, refs):
        if refs[0] is not None:
            self.own(refs).wait()
        self.first(refs, 0).wait()
        for hop in range(1, self.pairs):
            self.second(refs, hop).wait()


def dp_peers(ranks):
    rank = lax.axis_index("dp")
    partner = rank + 1 - 2 * lax.rem(rank, 2)
    return [partner] + [lax.rem(rank + 2 * hop, ranks) for hop in range(1, ranks // 2)]


HBM = pl.BlockSpec(memory_space=pl.ANY)


def staged(*arrays):
    buffers = [pltpu.VMEM(array.shape, array.dtype) for array in arrays]
    return buffers + [pltpu.SemaphoreType.DMA((4,))]


def route_group(capacity, routes_ref, slots_ref, first):
    seq = routes_ref.shape[1]
    row = lax.broadcasted_iota(jnp.int32, (seq, seq), 0)
    col = lax.broadcasted_iota(jnp.int32, (seq, seq), 1)
    earlier = (col < row).astype(f32).astype(bf16)
    lane = lax.broadcasted_iota(jnp.int32, (seq, LANES), 1)
    base = jnp.zeros((1, LANES), f32)
    table = jnp.full((seq, LANES), -1.0, f32)
    for choice in range(TOP):
        for image in range(IMG_MB):
            named = routes_ref[first + image][:, choice : choice + 1]
            onehot = (lane == named).astype(f32)
            count = dot(earlier, onehot.astype(bf16)) + base
            position = jnp.sum(onehot * count, axis=1, keepdims=True).astype(jnp.int32)
            base = base + jnp.sum(onehot, axis=0, keepdims=True)
            slot = jnp.where(position < capacity, named * capacity + position, -1)
            slots_ref[first + image, :, choice : choice + 1] = slot
            table = jnp.where(lane == image * TOP + choice, slot.astype(f32), table)
    return table.T[:8].astype(jnp.int32)


def dispatch(lines, rows_ref, first, out_ref, send=None):
    experts, capacity = out_ref.shape[:2]
    seq = rows_ref.shape[1]
    slot = lax.broadcasted_iota(jnp.int32, (capacity, seq), 0)

    me = lax.axis_index("expert")

    def fill(hop):
        expert = lax.rem(me + hop, experts)
        here = slot + expert * capacity
        total = None
        for index in range(IMG_MB):
            at = index * TOP
            holds = (lines[at : at + 1] == here) | (lines[at + 1 : at + 2] == here)
            part = dot(holds.astype(f32).astype(bf16), rows_ref[first + index])
            total = part if total is None else total + part
        out_ref[expert] = total.astype(bf16)

    @pl.loop(1, experts)
    def _(hop):
        fill(hop)
        if send is not None:
            send(hop)

    fill(0)


def front_kernel(
    experts, capacity, ranks, rides, gathers,
    x_ref, named_ref, top_ref, router_ref, gains_ref, own_bias_ref, in_hbm, out_hbm, w1_hbm, w2_hbm,
    proj_ref, mixed_ref, residual_ref, gates_ref, slots_ref, small_ref, bias_ref,
    dense_hbm, w1_full, w2_full, grad_rows_hbm, token_rows_hbm, grads_hbm, received_hbm,
    dense_ref, rows_a, rows_b, hidden_ref, lines_ref, routes_ref, sems, *more,
):
    step = pl.program_id(0)
    features = x_ref.shape[2]
    ride_a = ([rows_a], [grads_hbm], more[:3])
    ride_b = ([rows_b], [received_hbm], more[3:6])
    dense_part = (None, dense_ref, more[6:9])
    w1_part = (w1_hbm, w1_full, more[9:12])
    w2_part = (w2_hbm, w2_full, more[12:15])
    gather_dense, gather_units = gathers
    keep_dense = pltpu.make_async_copy(dense_ref, dense_hbm, sems.at[0])
    keep_grads = pltpu.make_async_copy(rows_b, grad_rows_hbm, sems.at[1])
    keep_tokens = pltpu.make_async_copy(rows_a, token_rows_hbm, sems.at[2])

    @pl.when(step == 0)
    def _():
        own = features // ranks
        rank = lax.axis_index("dp")
        mine = pl.ds(pl.multiple_of(rank * own, own), own)
        fills = [
            pltpu.make_async_copy(
                in_hbm, dense_ref.at[mine, pl.ds(0, 3 * features)], sems.at[2]
            ),
            pltpu.make_async_copy(
                out_hbm, dense_ref.at[mine, pl.ds(3 * features, features)], sems.at[3]
            ),
        ]
        for fill in fills:
            fill.start()
        pieces = own_bias_ref.shape[1] // own
        own_bias = own_bias_ref[...].astype(f32)
        columns = jnp.concatenate(
            [router_ref[...].astype(f32), gains_ref[...].astype(f32)]
            + [own_bias[:, piece * own : (piece + 1) * own] for piece in range(pieces)]
            + [jnp.zeros((LANES - experts - 4 - pieces, own), f32)],
            axis=0,
        )
        dense_ref[mine, 4 * features :] = columns.T.astype(bf16)
        rides.greet([{"dp": peer} for peer in dp_peers(ranks)])
        for fill in fills:
            fill.wait()
        gather_dense.start(dense_part)
        images = named_ref.shape[0]
        named = [named_ref[index].astype(f32) for index in range(images)]
        rest = jnp.zeros((LANES - TOP * images, named_ref.shape[2]), f32)
        named = jnp.concatenate(named + [rest], axis=0).T.astype(jnp.int32)
        for index in range(images):
            routes_ref[index] = named[:, TOP * index : TOP * (index + 1)]
        lines = route_group(capacity, routes_ref, slots_ref, 0)
        lines_ref[0] = lines
        dispatch(lines, top_ref, 0, rows_a, lambda hop: rides.send_hop(ride_a, hop))
        rides.send_own(ride_a)
        lines = route_group(capacity, routes_ref, slots_ref, IMG_MB)
        lines_ref[1] = lines
        dispatch(lines, top_ref, IMG_MB, rows_b)
        keep_grads.start()
        gather_dense.forward(dense_part)
        gather_units.start(w1_part)
        gather_units.start(w2_part)
        gather_dense.finish(dense_part)
        keep_dense.start()
        small = dense_ref[:, 4 * features :].astype(f32).T
        small_ref[...] = small[: small_ref.shape[0]].astype(bf16)
        for line in range(pieces):
            at = experts + 4 + line
            for place in range(ranks):
                first = (place * pieces + line) * own
                bias_ref[:, first : first + own] = small[
                    at : at + 1, place * own : (place + 1) * own
                ].astype(bf16)
        keep_grads.wait()

    image = x_ref[0].astype(f32)
    vectors = small_ref[...].astype(f32)
    normed, _ = norm_forward(image)
    attn_input = (
        normed * vectors[experts : experts + 1] + vectors[experts + 1 : experts + 2]
    ).astype(bf16)
    proj_ref[0] = dot(attn_input, dense_ref[:, : 3 * features]).astype(bf16)
    low_half = lax.broadcasted_iota(jnp.int32, (1, LANES), 1) < HEAD_DIM
    for pair in range(features // LANES):
        first = pair * LANES
        queries = proj_ref[0, :, first : first + LANES]
        keys = proj_ref[0, :, features + first : features + first + LANES]
        values = proj_ref[0, :, 2 * features + first : 2 * features + first + LANES]
        out = None
        for half in range(2):
            keep = low_half if half == 0 else jnp.logical_not(low_half)
            scores = dot_t(
                jnp.where(keep, queries * HEAD_DIM ** (-0.5), 0).astype(bf16), keys
            )
            top = jnp.max(scores, axis=-1, keepdims=True)
            raised = jnp.exp(scores - top)
            share = 1.0 / jnp.sum(raised, axis=-1, keepdims=True)
            weights = (raised * share).astype(bf16)
            part = dot(weights, jnp.where(keep, values, 0).astype(bf16))
            out = part if out is None else out + part
        mixed_ref[0, :, first : first + LANES] = out.astype(bf16)
    residual = image + dot(mixed_ref[0], dense_ref[:, 3 * features : 4 * features])
    residual_ref[0] = residual
    normed, _ = norm_forward(residual)
    hidden = (
        normed * vectors[experts + 2 : experts + 3] + vectors[experts + 3 : experts + 4]
    ).astype(bf16)
    hidden_ref[lax.rem(step, IMG_MB)] = hidden
    probs = softmax_lanes(dot_t(hidden, small_ref[...]), experts)
    lane = lax.broadcasted_iota(jnp.int32, probs.shape, 1)
    routes = routes_ref[step]
    for choice in range(TOP):
        gates_ref[0, :, choice : choice + 1] = jnp.sum(
            jnp.where(lane == routes[:, choice : choice + 1], probs, 0.0),
            axis=1,
            keepdims=True,
        )

    @pl.when(step == IMG_MB - 1)
    def _():
        dispatch(lines_ref[0], hidden_ref, 0, rows_b, lambda hop: rides.send_hop(ride_b, hop))
        rides.send_own(ride_b)

    @pl.when(step == pl.num_programs(0) - 1)
    def _():
        rides.finish(ride_a)
        dispatch(lines_ref[1], hidden_ref, 0, rows_a)
        keep_tokens.start()
        gather_units.forward(w1_part)
        gather_units.forward(w2_part)
        gather_units.finish(w1_part)
        gather_units.finish(w2_part)
        keep_dense.wait()
        rides.finish(ride_b)
        keep_tokens.wait()


def front(
    images, named, out_grad, router, gains, bias, attn_in, attn_out, w1, w2, experts, capacity,
    ranks, small_rows, collective,
):
    count, seq, features = images.shape
    width = 4 * features + LANES
    slot_rows = jax.ShapeDtypeStruct((experts, capacity, features), bf16)
    rides = Rides([(slot_rows, 0, capacity, None)])
    gathers = (Gather(router.shape[1], ranks), Gather(w1.shape[0], ranks))

    def rows(width):
        return pl.BlockSpec((1, seq, width), lambda i: (i, 0, 0))

    def whole(shape):
        return pl.BlockSpec(
            shape, lambda i: (0,) * len(shape), pipeline_mode=pl.Buffered(1)
        )

    def out(width, dtype):
        return jax.ShapeDtypeStruct((count, seq, width), dtype)

    units = jax.ShapeDtypeStruct((ranks * w1.shape[0], features), bf16)
    return pl.pallas_call(
        functools.partial(front_kernel, experts, capacity, ranks, rides, gathers),
        grid=(count,),
        in_specs=[
            rows(features), whole(named.shape), whole(out_grad.shape), whole(router.shape),
            whole(gains.shape), whole(bias.shape), HBM, HBM, HBM, HBM,
        ],
        out_specs=[
            rows(3 * features), rows(features), rows(features), rows(TOP),
            whole((count, seq, TOP)), whole((small_rows, features)), whole((1, ranks * w1.shape[0])),
        ]
        + [HBM] * 7,
        out_shape=[
            out(3 * features, bf16),
            out(features, bf16),
            out(features, f32),
            out(TOP, f32),
            jax.ShapeDtypeStruct((count, seq, TOP), jnp.int32),
            jax.ShapeDtypeStruct((small_rows, features), bf16),
            jax.ShapeDtypeStruct((1, ranks * w1.shape[0]), bf16),
            jax.ShapeDtypeStruct((features, width), bf16),
            units,
            units,
            slot_rows,
            slot_rows,
            slot_rows,
            slot_rows,
        ],
        scratch_shapes=[
            pltpu.VMEM((features, width), bf16),
            pltpu.VMEM(slot_rows.shape, bf16),
            pltpu.VMEM(slot_rows.shape, bf16),
            pltpu.VMEM((IMG_MB, seq, features), bf16),
            pltpu.VMEM((count // IMG_MB, 8, seq), jnp.int32),
            pltpu.VMEM((count, seq, TOP), jnp.int32),
            pltpu.SemaphoreType.DMA((4,)),
        ]
        + rides.scratch
        + rides.scratch
        + gathers[0].scratch
        + gathers[1].scratch
        + gathers[1].scratch,
        compiler_params=params(
            ("arbitrary",), collective_id=collective, has_side_effects=True
        ),
        cost_estimate=pl.CostEstimate(
            flops=count * seq * 16 * features * features,
            bytes_accessed=4 * features * (4 * features + count * seq * 8),
            transcendentals=count * HEADS * seq * seq,
        ),
        name="front",
    )(images, named, out_grad, router, gains, bias, attn_in, attn_out, w1, w2)


def expert_kernel(
    experts, chunk, add, rides, x_hbm, g_hbm, w1_ref, w2_ref, bias_ref, small_ref, *refs
):
    if add:
        old_w_ref, old_router_ref = refs[:2]
        refs = refs[2:]
    count = len(rides.arrays)
    sources, refs = refs[:count], refs[len(rides.operands) :]
    ride_refs = (sources, refs[4 : count + 4], refs[count + 15 :])
    refs = refs[:4] + refs[count + 4 : count + 15]
    (
        result_hbm, dx_hbm, dw_ref, drouter_ref,
        result_acc, dx_acc, dr_ref, probs_ref, act_ref, pre_ref,
        x_ref, g_ref, result_ref, dx_ref, copy_sems,
    ) = refs
    loads = [
        pltpu.make_async_copy(x_hbm, x_ref, copy_sems.at[0]),
        pltpu.make_async_copy(g_hbm, g_ref, copy_sems.at[1]),
    ]
    stores = [
        pltpu.make_async_copy(result_ref, result_hbm, copy_sems.at[2]),
        pltpu.make_async_copy(dx_ref, dx_hbm, copy_sems.at[3]),
    ]
    step = pl.program_id(0)
    last = pl.num_programs(0) - 1
    rows = x_ref.shape[0]
    mine = lax.axis_index("expert")
    chunks = rows // chunk

    @pl.when(step == 0)
    def _():
        rides.start(ride_refs)
        for load in loads:
            load.start()
        for load in loads:
            load.wait()
        for index in range(chunks):
            at = pl.ds(index * chunk, chunk)
            probs = softmax_lanes(dot_t(x_ref[at, :], small_ref[...]), experts)
            lane = lax.broadcasted_iota(jnp.int32, probs.shape, 1)
            probs_ref[at, :] = probs
            gate = jnp.sum(jnp.where(lane == mine, probs, 0.0), axis=1, keepdims=True)
            dr_ref[at, :] = (gate * g_ref[at, :].astype(f32)).astype(bf16)
            result_acc[at, :] = jnp.zeros((chunk, x_ref.shape[1]), f32)
            dx_acc[at, :] = jnp.zeros((chunk, x_ref.shape[1]), f32)

    w1 = w1_ref[...]
    w2 = w2_ref[...]
    bias = bias_ref[...].astype(f32)
    dbias = jnp.zeros(bias.shape, f32)
    for index in range(chunks):
        at = pl.ds(index * chunk, chunk)
        act, slope = gelu_both(dot_t(x_ref[at, :], w1) + bias)
        act = act.astype(bf16)
        act_ref[at, :] = act
        result_acc[at, :] += dot(act, w2)
        grad_pre = (dot_t(dr_ref[at, :], w2) * slope).astype(bf16)
        pre_ref[at, :] = grad_pre
        dbias = dbias + jnp.sum(grad_pre.astype(f32), axis=0, keepdims=True)
        dx_acc[at, :] += dot(grad_pre, w1)
    dw1 = t_dot(pre_ref[...], x_ref[...])
    dw2 = t_dot(act_ref[...], dr_ref[...])
    dbias = jnp.broadcast_to(dbias, (LANES, dbias.shape[1])).T
    first = 0
    for part in (dw1, dw2, dbias):
        at = pl.ds(first, part.shape[1])
        if add:
            part = part + old_w_ref[:, at]
        dw_ref[:, at] = part.astype(dw_ref.dtype)
        first += part.shape[1]

    @pl.when(step == last)
    def _():
        drouter = jnp.zeros(drouter_ref.shape, f32)
        if add:
            drouter = old_router_ref[...]
        for index in range(chunks):
            at = pl.ds(index * chunk, chunk)
            result = result_acc[at, :].astype(bf16)
            result_ref[at, :] = result
            grad_gate = jnp.sum(
                g_ref[at, :].astype(f32) * result.astype(f32), axis=1, keepdims=True
            )
            probs = probs_ref[at, :]
            lane = lax.broadcasted_iota(jnp.int32, probs.shape, 1)
            chosen = lane == mine
            gate = jnp.sum(jnp.where(chosen, probs, 0.0), axis=1, keepdims=True)
            logits = (grad_gate * gate) * (chosen.astype(f32) - probs)
            high = logits.astype(bf16)
            low = (logits - high.astype(f32)).astype(bf16)
            dx_ref[at, :] = (
                dx_acc[at, :] + dot(high, small_ref[...]) + dot(low, small_ref[...])
            ).astype(bf16)
            drouter = drouter + t_dot(high, x_ref[at, :]) + t_dot(low, x_ref[at, :])
        drouter_ref[...] = drouter
        for store in stores:
            store.start()
        rides.finish(ride_refs)
        for store in stores:
            store.wait()


def row_chunk(rows):
    best = rows
    for size in range(16, 513, 16):
        if rows % size == 0:
            best = size
    return best


def expert_block(x, g, w1, w2, bias, small, experts, old, entries, collective):
    rows, features = x.shape
    hidden_units = w1.shape[0]
    block = 512 if hidden_units % 512 == 0 else 256
    steps = hidden_units // block
    chunk = row_chunk(rows)
    add = old is not None
    out_type = bf16 if add else f32
    rides = Rides(entries)

    def whole(shape):
        return pl.BlockSpec(
            shape, lambda s: (0,) * len(shape), pipeline_mode=pl.Buffered(1)
        )

    packed = 2 * features + LANES
    unit_grads = pl.BlockSpec((block, packed), lambda s: (s, 0))
    units = pl.BlockSpec((block, features), lambda s: (s, 0))
    unit_row = pl.BlockSpec((1, block), lambda s: (0, s))
    in_specs = [
        HBM,
        HBM,
        units,
        units,
        unit_row,
        whole(small.shape),
    ]
    operands = [x, g, w1, w2, bias, small]
    if add:
        in_specs += [unit_grads, whole(small.shape)]
        operands += list(old)
    return pl.pallas_call(
        functools.partial(expert_kernel, experts, chunk, add, rides),
        grid=(steps,),
        in_specs=in_specs + rides.in_specs,
        out_specs=[
            HBM, HBM, unit_grads, whole(small.shape)
        ]
        + rides.out_specs,
        out_shape=[
            jax.ShapeDtypeStruct(x.shape, bf16),
            jax.ShapeDtypeStruct(x.shape, bf16),
            jax.ShapeDtypeStruct((hidden_units, packed), out_type),
            jax.ShapeDtypeStruct(small.shape, f32),
        ]
        + rides.out_shape,
        scratch_shapes=[
            pltpu.VMEM((rows, features), f32),
            pltpu.VMEM((rows, features), f32),
            pltpu.VMEM((rows, features), bf16),
            pltpu.VMEM((rows, small.shape[0]), f32),
            pltpu.VMEM((rows, block), bf16),
            pltpu.VMEM((rows, block), bf16),
            *staged(x, g, x, x),
        ]
        + rides.scratch,
        compiler_params=params(
            ("arbitrary",), collective_id=collective, has_side_effects=True
        ),
        cost_estimate=pl.CostEstimate(
            flops=12 * rows * features * hidden_units,
            bytes_accessed=(8 * rows + 12 * hidden_units) * features,
            transcendentals=rows * hidden_units,
        ),
        name="expert_block",
    )(*operands, *rides.operands)


def inner_size(parts):
    size = 1
    while parts % (2 * size) == 0 and 4 * size * size <= parts:
        size *= 2
    return size


def finish_kernel(
    inner, outer, slots_ref, gates_ref, residual_ref,
    returned0_hbm, returned1_hbm, part_ref, out_ref, din_ref, dout_ref, little_ref,
    returned0_ref, returned1_ref, load_sems, flat_ref, second_ref, full_ref, sems2, sems3, sems4,
):
    step = pl.program_id(0)
    seq = slots_ref.shape[1]
    features = out_ref.shape[2]
    width = part_ref.shape[2]
    tiles = width // LANES
    chunks = 5
    edges = [LANES * (tiles * c // chunks) for c in range(chunks + 1)]
    cuts = [pl.ds(edges[c], edges[c + 1] - edges[c]) for c in range(chunks)]
    me = lax.axis_index("expert")
    row = lax.rem(me, inner)
    line = me // inner

    def row_peer(hop):
        return lax.rem(row + hop, inner)

    def line_peer(hop):
        return lax.rem(line + hop, outer)

    def copy(source, target, sems, chunk, hop, peer):
        return pltpu.make_async_remote_copy(
            src_ref=source,
            dst_ref=target,
            send_sem=sems.at[0, chunk, hop - 1],
            recv_sem=sems.at[1, chunk, hop - 1],
            device_id={"expert": peer},
            device_id_type=pl.DeviceIdType.MESH,
        )

    def reduce_lines(chunk):
        at = cuts[chunk]
        return [
            copy(
                part_ref.at[line_peer(hop), :, at], second_ref.at[hop - 1, :, at],
                sems2, chunk, hop, line_peer(hop) * inner + row,
            )
            for hop in range(1, outer)
        ]

    def gather_lines(chunk):
        at = cuts[chunk]
        return [
            copy(
                full_ref.at[row, line, :, at], full_ref.at[row, line, :, at],
                sems3, chunk, hop, line_peer(hop) * inner + row,
            )
            for hop in range(1, outer)
        ]

    def gather_rows(chunk):
        at = cuts[chunk]
        return [
            copy(
                full_ref.at[row, :, :, at], full_ref.at[row, :, :, at],
                sems4, chunk, hop, line * inner + row_peer(hop),
            )
            for hop in range(1, inner)
        ]

    loads = [
        pltpu.make_async_copy(returned0_hbm, returned0_ref, load_sems.at[0]),
        pltpu.make_async_copy(returned1_hbm, returned1_ref, load_sems.at[1]),
    ]

    def start(copies):
        for item in copies:
            item.start()

    def wait(copies):
        for item in copies:
            item.wait()

    @pl.when(step == 0)
    def _():
        barrier = pltpu.get_barrier_semaphore()
        peers = [line * inner + row_peer(hop) for hop in range(1, inner)]
        peers += [line_peer(hop) * inner + row for hop in range(1, outer)]
        for peer in peers:
            pl.semaphore_signal(
                barrier,
                inc=1,
                device_id={"expert": peer},
                device_id_type=pl.DeviceIdType.MESH,
            )
        pl.semaphore_wait(barrier, len(peers))
        for chunk in range(chunks):
            start(reduce_lines(chunk))
        start(loads)
        wait(loads[:1])

    @pl.when(step == IMG_MB)
    def _():
        wait(loads[1:])

    column = lax.broadcasted_iota(jnp.int32, (seq, returned0_ref.shape[0]), 1)

    def mix(returned_ref):
        slots = slots_ref[0]
        gates = gates_ref[0]
        total = residual_ref[0]
        for choice in range(TOP):
            holds = slots[:, choice : choice + 1] == column
            picked = dot(holds.astype(f32).astype(bf16), returned_ref[...])
            total = total + gates[:, choice : choice + 1] * picked
        out_ref[0] = total.astype(bf16)

    @pl.when(step < IMG_MB)
    def _():
        mix(returned0_ref)

    @pl.when(step >= IMG_MB)
    def _():
        mix(returned1_ref)

    @pl.when(step == 1)
    def _():
        for chunk in range(chunks):
            at = cuts[chunk]
            wait(reduce_lines(chunk))
            total = part_ref[line, :, at].astype(f32)
            for hop in range(1, outer):
                total = total + second_ref[hop - 1, :, at].astype(f32)
            full_ref[row, line, :, at] = total.astype(bf16)
            start(gather_lines(chunk))

    @pl.when(step == 3)
    def _():
        for chunk in range(chunks):
            wait(gather_lines(chunk))
            start(gather_rows(chunk))

    @pl.when(step == 2 * IMG_MB - 1)
    def _():
        for chunk in range(chunks):
            wait(gather_rows(chunk))
        for part in range(inner):
            for place in range(outer):
                block = part * outer + place
                din_ref[block] = full_ref[part, place, :, : 3 * features].astype(f32)
                dout_ref[block] = full_ref[part, place, :, 3 * features : 4 * features].astype(
                    f32
                )
                share = full_ref.shape[2]
                flat_ref[block * share : (block + 1) * share] = full_ref[
                    part, place, :, 4 * features :
                ].astype(f32)
        little_ref[...] = flat_ref[...].T[: little_ref.shape[0]]


def finish(slots, gates, residual, returned, part, parts, lines, collective):
    outer, share, width = part.shape
    inner = inner_size(parts)
    images, seq, features = residual.shape
    chunks = 5

    def whole(shape):
        return pl.BlockSpec(
            shape, lambda i: (0,) * len(shape), pipeline_mode=pl.Buffered(1)
        )

    def each(width):
        return pl.BlockSpec((1, seq, width), lambda i: (i, 0, 0))

    outs = [3 * features, features]
    little = (lines, parts * share)
    return pl.pallas_call(
        functools.partial(finish_kernel, inner, outer),
        grid=(images,),
        in_specs=[
            each(TOP), each(TOP), each(features),
            HBM, HBM, whole(part.shape),
        ],
        out_specs=[each(features)] + [whole((parts, share, size)) for size in outs]
        + [whole(little)],
        out_shape=[jax.ShapeDtypeStruct((images, seq, features), bf16)]
        + [jax.ShapeDtypeStruct((parts, share, size), f32) for size in outs]
        + [jax.ShapeDtypeStruct(little, f32)],
        scratch_shapes=[
            *staged(*returned),
            pltpu.VMEM((parts * share, LANES), f32),
            pltpu.VMEM((outer - 1, share, width), bf16),
            pltpu.VMEM((inner, outer, share, width), bf16),
            pltpu.SemaphoreType.DMA((2, chunks, outer - 1)),
            pltpu.SemaphoreType.DMA((2, chunks, outer - 1)),
            pltpu.SemaphoreType.DMA((2, chunks, inner - 1)),
        ],
        compiler_params=params(
            ("arbitrary",), collective_id=collective, has_side_effects=True
        ),
        cost_estimate=pl.CostEstimate(
            flops=4 * images * seq * returned[0].shape[0] * features,
            bytes_accessed=2 * features * (2 * returned[0].shape[0] + 3 * images * seq),
            transcendentals=0,
        ),
        name="finish",
    )(slots, gates, residual, *returned, part)


def attend_back_kernel(
    experts, add, rides, ranks, x_ref, top_ref, slots_ref, sent_hbm, proj_ref, mixed_ref, residual_ref,
    dense_hbm, small_ref, *refs
):
    if add:
        old_dense_ref, old_small_ref, drouter_ref, sums_b_hbm = refs[:4]
        refs = refs[4:]
    else:
        dweights_hbm, refs = refs[0], refs[1:]
    count = len(rides.arrays)
    outs = 4 if add else 5
    sources, refs = refs[:count], refs[len(rides.operands) :]
    grad_x_ref, ddense_ref = refs[:2]
    if add:
        grad_b_ref, bias_b_ref = refs[2:4]
    else:
        dsmall_ref, sums_b_hbm, grad_a_ref = refs[2:5]
    targets, refs = refs[outs : outs + count], refs[outs + count :]
    acc_in, acc_out, acc_small, dproj_ref = refs[:4]
    sent_ref, dense_ref, copy_sems = refs[4:7]
    refs = refs[7:]
    rank = lax.axis_index("dp")
    core = lax.rem(rank, 2)
    mine = rank // 2
    pairs = ranks // 2
    partner, *others = [{"dp": peer} for peer in dp_peers(ranks)]
    more = [partner] + others

    def remote(source, target, sems, index, peer):
        return pltpu.make_async_remote_copy(
            src_ref=source,
            dst_ref=target,
            send_sem=sems.at[0, index],
            recv_sem=sems.at[1, index],
            device_id=peer,
            device_id_type=pl.DeviceIdType.MESH,
        )

    if add:
        pack_ref, first_ref, second_ref, part_ref, third_ref = refs[:5]
        first_sems, second_sems, third_sems = refs[5:8]
        own_b_ref, other_b_ref, own_b_sem, other_b_sems = refs[8:12]
        refs = refs[12:]
    else:
        own_w_ref, other_w_ref, other_a_ref = refs[:3]
        own_w_sems, other_w_sems, other_a_sems, keep_b_sem = refs[3:7]
        refs = refs[7:]

    def core_swap(pair):
        rows = other_w_ref.shape[1]
        at = pl.multiple_of((2 * pair + 1 - core) * rows, rows)
        source = dweights_hbm.at[pl.ds(at, rows)]
        return remote(source, other_w_ref.at[pair], other_w_sems, pair, partner)

    def core_own(pair):
        rows = own_w_ref.shape[1]
        at = pl.multiple_of((2 * pair + core) * rows, rows)
        return pltpu.make_async_copy(
            dweights_hbm.at[pl.ds(at, rows)], own_w_ref.at[pair], own_w_sems.at[pair]
        )

    def send_a(hop):
        at = pl.ds(0, x_ref.shape[2])
        source = own_w_ref.at[lax.rem(mine + hop, pairs), :, at]
        return remote(source, other_a_ref.at[hop - 1], other_a_sems, hop - 1, others[hop - 1])

    def keep_b():
        at = pl.ds(x_ref.shape[2], sums_b_hbm.shape[2])
        return pltpu.make_async_copy(own_w_ref.at[:, :, at], sums_b_hbm, keep_b_sem.at[0])

    def send_b(hop):
        source = sums_b_hbm.at[lax.rem(mine + hop, pairs)]
        return remote(source, other_b_ref.at[hop - 1], other_b_sems, hop - 1, others[hop - 1])

    def own_b():
        return pltpu.make_async_copy(sums_b_hbm.at[mine], own_b_ref, own_b_sem.at[0])

    ride_refs = (sources, targets, refs)
    features = x_ref.shape[2]
    seq = x_ref.shape[1]
    step = pl.program_id(0)
    vectors = small_ref[...].astype(f32)
    loads = [
        pltpu.make_async_copy(sent_hbm, sent_ref, copy_sems.at[0]),
        pltpu.make_async_copy(dense_hbm, dense_ref, copy_sems.at[1]),
    ]
    sums_hbm = old_dense_ref if add else ddense_ref
    halves = [
        (acc_in, sums_hbm.at[:, pl.ds(0, 3 * features)], copy_sems.at[2]),
        (acc_out, sums_hbm.at[:, pl.ds(3 * features, features)], copy_sems.at[3]),
    ]
    if add:
        moves = [pltpu.make_async_copy(far, near, sem) for near, far, sem in halves]
    else:
        moves = [pltpu.make_async_copy(near, far, sem) for near, far, sem in halves]

    @pl.when(step == 0)
    def _():
        rides.start(ride_refs, more)
        for load in loads:
            load.start()
        if add:
            own_b().start()
            for hop in range(1, pairs):
                send_b(hop).start()
        else:
            for pair in range(pairs):
                core_swap(pair).start()
                core_own(pair).start()
        if add:
            for move in moves:
                move.start()
            acc_small[...] = old_small_ref[...]
        else:
            acc_in[...] = jnp.zeros(acc_in.shape, f32)
            acc_out[...] = jnp.zeros(acc_out.shape, f32)
            acc_small[...] = jnp.zeros(acc_small.shape, f32)
        for load in loads:
            load.wait()

    if not add:

        @pl.when(step == 1)
        def _():
            for pair in range(pairs):
                core_swap(pair).wait()
                core_own(pair).wait()
                total = own_w_ref[pair].astype(f32) + other_w_ref[pair].astype(f32)
                own_w_ref[pair] = total.astype(bf16)
            for hop in range(1, pairs):
                send_a(hop).start()
            keep_b().start()

    column = lax.broadcasted_iota(jnp.int32, (seq, sent_ref.shape[0]), 1)
    slots = slots_ref[0]
    holds = (slots[:, 0:1] == column) | (slots[:, 1:2] == column)
    grad_hidden = dot(holds.astype(f32).astype(bf16), sent_ref[...])
    normed_two, inverse_two = norm_forward(residual_ref[0])
    acc_small[2:3, :] += jnp.sum(grad_hidden * normed_two, axis=0, keepdims=True)
    acc_small[3:4, :] += jnp.sum(grad_hidden, axis=0, keepdims=True)
    grad_residual = top_ref[0].astype(f32) + norm_backward(
        grad_hidden * vectors[experts + 2 : experts + 3], normed_two, inverse_two
    )
    grad_branch = grad_residual.astype(bf16)
    grad_mixed = dot_t(grad_branch, dense_ref[:, 3 * features : 4 * features]).astype(bf16)
    low_half = lax.broadcasted_iota(jnp.int32, (1, LANES), 1) < HEAD_DIM
    scale = HEAD_DIM ** (-0.5)
    for pair in range(features // LANES):
        first = pair * LANES
        queries = proj_ref[0, :, first : first + LANES]
        keys = proj_ref[0, :, features + first : features + first + LANES]
        values = proj_ref[0, :, 2 * features + first : 2 * features + first + LANES]
        grad_out = grad_mixed[:, first : first + LANES]
        sums = [None, None, None]
        for half in range(2):
            keep = low_half if half == 0 else jnp.logical_not(low_half)
            head_queries = jnp.where(keep, queries * scale, 0).astype(bf16)
            head_keys = jnp.where(keep, keys, 0).astype(bf16)
            head_grad = jnp.where(keep, grad_out, 0).astype(bf16)
            scores = dot_t(keys, head_queries)
            top = jnp.max(scores, axis=0, keepdims=True)
            raised = jnp.exp(scores - top)
            probs = raised * (1.0 / jnp.sum(raised, axis=0, keepdims=True))
            grad_values = dot(probs.astype(bf16), head_grad)
            grad_weights = dot_t(values, head_grad)
            inner = jnp.sum(grad_weights * probs, axis=0, keepdims=True)
            grad_scores = (probs * (grad_weights - inner)).astype(bf16)
            grad_keys = dot(grad_scores, head_queries)
            grad_queries = t_dot(grad_scores, head_keys)
            for place, part in enumerate((grad_queries, grad_keys, grad_values)):
                sums[place] = part if half == 0 else sums[place] + part
        dproj_ref[:, first : first + LANES] = (sums[0] * scale).astype(bf16)
        dproj_ref[:, features + first : features + first + LANES] = sums[1].astype(bf16)
        dproj_ref[:, 2 * features + first : 2 * features + first + LANES] = sums[2].astype(bf16)
    normed_one, inverse_one = norm_forward(x_ref[0].astype(f32))
    attn_input = (
        normed_one * vectors[experts : experts + 1] + vectors[experts + 1 : experts + 2]
    ).astype(bf16)
    if add:

        @pl.when(step == 0)
        def _():
            for move in moves:
                move.wait()

    acc_out[...] += t_dot(mixed_ref[0], grad_branch)
    acc_in[...] += t_dot(attn_input, dproj_ref[...])
    grad_input = dot_t(dproj_ref[...], dense_ref[:, : 3 * features])
    acc_small[0:1, :] += jnp.sum(grad_input * normed_one, axis=0, keepdims=True)
    acc_small[1:2, :] += jnp.sum(grad_input, axis=0, keepdims=True)
    grad_x_ref[0] = grad_residual + norm_backward(
        grad_input * vectors[experts : experts + 1], normed_one, inverse_one
    )

    @pl.when(step == pl.num_programs(0) - 1)
    def _():
        if not add:
            for move in moves:
                move.start()
            dsmall_ref[...] = acc_small[...]
            total = own_w_ref[mine, :, :features].astype(f32)
            for hop in range(1, pairs):
                send_a(hop).wait()
                total = total + other_a_ref[hop - 1].astype(f32)
            grad_a_ref[...] = total
            keep_b().wait()
        else:
            used = acc_small.shape[0] + drouter_ref.shape[0]
            rest = jnp.zeros((LANES - used, features), f32)
            column = jnp.concatenate([acc_small[...], drouter_ref[...], rest], axis=0).T
            share = features // ranks
            for shard in range(ranks):
                at = slice(shard * share, (shard + 1) * share)
                place = (shard % 2, shard // 2)
                pack_ref[place[0], place[1], :, : 3 * features] = acc_in[at].astype(bf16)
                pack_ref[place[0], place[1], :, 3 * features : 4 * features] = acc_out[
                    at
                ].astype(bf16)
                pack_ref[place[0], place[1], :, 4 * features :] = column[at].astype(bf16)
            copy = remote(pack_ref.at[1 - core], first_ref, first_sems, 0, partner)
            copy.start()
            copy.wait()
            for pair in range(pairs):
                first_ref[pair] = (
                    first_ref[pair].astype(f32) + pack_ref[core, pair].astype(f32)
                ).astype(bf16)
            copies = [
                remote(
                    first_ref.at[lax.rem(mine + hop, pairs)], second_ref.at[hop - 1],
                    second_sems, hop - 1, others[hop - 1],
                )
                for hop in range(1, pairs)
            ]
            for copy in copies:
                copy.start()
            own_b().wait()
            total = own_b_ref[...].astype(f32)
            for hop in range(1, pairs):
                send_b(hop).wait()
                total = total + other_b_ref[hop - 1].astype(f32)
            grad_b_ref[...] = total[:, :features]
            bias_b_ref[...] = total[:, features:]
            total = first_ref[mine].astype(f32)
            for copy in copies:
                copy.wait()
            for hop in range(1, pairs):
                total = total + second_ref[hop - 1].astype(f32)
            total = total.astype(bf16)
            inner, outer, rows = part_ref.shape[:3]
            for block in range(inner * outer):
                part_ref[block // outer, block % outer] = total[block * rows : (block + 1) * rows]
            me = lax.axis_index("expert")
            row = lax.rem(me, inner)
            copies = []
            for hop in range(1, inner):
                peer = lax.rem(row + hop, inner)
                copies.append(
                    remote(
                        part_ref.at[peer], third_ref.at[hop - 1], third_sems, hop - 1,
                        {"expert": me - row + peer},
                    )
                )
            for copy in copies:
                copy.start()
            for copy in copies:
                copy.wait()
            total = part_ref[row].astype(f32)
            for hop in range(1, inner):
                total = total + third_ref[hop - 1].astype(f32)
            ddense_ref[...] = total.astype(bf16)
        rides.finish(ride_refs)
        if not add:
            for move in moves:
                move.wait()


def attend_back(
    images, out_grad, slots, sent, proj, mixed, residual, dense, small, experts, group, old,
    entries, collective, ranks, dweights=None, sums_b=None,
):
    seq, features = images.shape[1:]
    wide = 3 * features
    first = group * IMG_MB
    add = old is not None
    rides = Rides(entries)

    def rows(width):
        return pl.BlockSpec((1, seq, width), lambda i: (i, 0, 0))

    def source(width):
        return pl.BlockSpec((1, seq, width), lambda i: (first + i, 0, 0))

    def whole(shape):
        return pl.BlockSpec(shape, lambda i: (0, 0), pipeline_mode=pl.Buffered(1))

    small_grads = (8, features)
    in_specs = [
        source(features), source(features), source(TOP), HBM,
        source(wide), source(features), source(features),
        HBM, whole(small.shape),
    ]
    operands = [images, out_grad, slots, sent, proj, mixed, residual, dense, small]
    out_specs = [rows(features), HBM]
    out_shape = [
        jax.ShapeDtypeStruct((IMG_MB, seq, features), f32),
        jax.ShapeDtypeStruct((features, 4 * features), f32),
    ]
    if add:
        in_specs += [HBM] + [whole(array.shape) for array in old[1:]] + [HBM]
        operands += list(old) + [sums_b]
        out_specs += [whole((sums_b.shape[1], features)), whole((sums_b.shape[1], LANES))]
        out_shape += [
            jax.ShapeDtypeStruct((sums_b.shape[1], features), f32),
            jax.ShapeDtypeStruct((sums_b.shape[1], LANES), f32),
        ]
        shard = (features // ranks, 4 * features + LANES)
        inner = inner_size(experts)
        part = (experts // inner, shard[0] // experts, shard[1])
        out_specs[1] = pl.BlockSpec(
            part, lambda i: (0, 0, 0), pipeline_mode=pl.Buffered(1)
        )
        out_shape[1] = jax.ShapeDtypeStruct(part, bf16)
        reduce_scratch = [
            pltpu.VMEM((2, ranks // 2, *shard), bf16),
            pltpu.VMEM((ranks // 2, *shard), bf16),
            pltpu.VMEM((ranks // 2 - 1, *shard), bf16),
            pltpu.VMEM((inner, *part), bf16),
            pltpu.VMEM((inner - 1, *part), bf16),
            pltpu.SemaphoreType.DMA((2, 1)),
            pltpu.SemaphoreType.DMA((2, ranks // 2 - 1)),
            pltpu.SemaphoreType.DMA((2, inner - 1)),
            pltpu.VMEM(sums_b.shape[1:], bf16),
            pltpu.VMEM((ranks // 2 - 1, *sums_b.shape[1:]), bf16),
            pltpu.SemaphoreType.DMA((1,)),
            pltpu.SemaphoreType.DMA((2, ranks // 2 - 1)),
        ]
    else:
        out_specs.append(whole(small_grads))
        out_shape.append(jax.ShapeDtypeStruct(small_grads, f32))
        in_specs.append(HBM)
        operands.append(dweights)
        units = dweights.shape[0] // ranks
        rest = dweights.shape[1] - features
        out_specs += [HBM, whole((units, features))]
        out_shape += [
            jax.ShapeDtypeStruct((ranks // 2, units, rest), bf16),
            jax.ShapeDtypeStruct((units, features), f32),
        ]
        reduce_scratch = [
            pltpu.VMEM((ranks // 2, units, dweights.shape[1]), bf16),
            pltpu.VMEM((ranks // 2, units, dweights.shape[1]), bf16),
            pltpu.VMEM((ranks // 2 - 1, units, features), bf16),
            pltpu.SemaphoreType.DMA((ranks // 2,)),
            pltpu.SemaphoreType.DMA((2, ranks // 2)),
            pltpu.SemaphoreType.DMA((2, ranks // 2 - 1)),
            pltpu.SemaphoreType.DMA((1,)),
        ]
    return pl.pallas_call(
        functools.partial(attend_back_kernel, experts, add, rides, ranks),
        grid=(IMG_MB,),
        in_specs=in_specs + rides.in_specs,
        out_specs=out_specs + rides.out_specs,
        out_shape=out_shape + rides.out_shape,
        scratch_shapes=[
            pltpu.VMEM((features, 3 * features), f32),
            pltpu.VMEM((features, features), f32),
            pltpu.VMEM(small_grads, f32),
            pltpu.VMEM((seq, wide), bf16),
            *staged(sent, dense),
        ]
        + reduce_scratch
        + rides.scratch,
        input_output_aliases=rides.aliases(len(operands), len(out_specs)),
        compiler_params=params(
            ("arbitrary",), collective_id=collective, has_side_effects=True
        ),
        cost_estimate=pl.CostEstimate(
            flops=IMG_MB * seq * 40 * features * features,
            bytes_accessed=8 * features * (4 * features + IMG_MB * seq * 4),
            transcendentals=IMG_MB * HEADS * seq * seq,
        ),
        name="attend_back",
    )(*operands, *rides.operands)


def per_device(
    images, first_gain, first_shift, attn_in, attn_out, second_gain, second_shift, router,
    expert_in, expert_bias, expert_out, routes, out_grad,
):
    features = images.shape[2]
    experts = router.shape[1]
    tok_mb = IMG_MB * SEQ
    capacity = max(2, (5 * TOP * tok_mb // (4 * experts) + 7) // 8 * 8)
    slot_rows = experts * capacity
    own = router.shape[0]
    ranks = features // own
    bias_rows = expert_bias.shape[1] // own
    used = experts + 4 + bias_rows
    small_rows = (used + 15) // 16 * 16
    line = lax.broadcasted_iota(jnp.int32, (4, own), 0)
    gains = jnp.where(
        line < 2,
        jnp.where(line == 0, first_gain[None], first_shift[None]),
        jnp.where(line == 2, second_gain[None], second_shift[None]),
    )

    def flat(blocks):
        return blocks.reshape(slot_rows, features)

    def blocks(rows):
        return rows.reshape(experts, capacity, features)

    (
        proj, mixed, residual, gates, slots, small, bias_row, dense, weight_in, weight_out,
        grad_rows_1, token_rows_1, grads_0, received_0,
    ) = front(
        images, routes.transpose(0, 2, 1), out_grad, router.T, gains, expert_bias, attn_in,
        attn_out, expert_in[0],
        expert_out[0], experts, capacity, ranks, small_rows, 5,
    )
    result_0, dx_0, *old, grads_1, received_1 = expert_block(
        flat(received_0), flat(grads_0), weight_in, weight_out, bias_row, small, experts, None,
        [(grad_rows_1, 0, capacity, None), (token_rows_1, 0, capacity, None)], 0,
    )
    early = max(8, capacity * 3 // 8 // 8 * 8)
    result_1, dx_1, dweights, drouter, sent_0, returned_0 = expert_block(
        flat(received_1), flat(grads_1), weight_in, weight_out, bias_row, small, experts, old,
        [(blocks(dx_0), 0, capacity, None), (blocks(result_0), 0, early, None)], 1,
    )
    grad_x_0, *old, sums_b, grad_expert_in, sent_1 = attend_back(
        images, out_grad, slots, flat(sent_0), proj, mixed, residual, dense, small,
        experts, 0, None, [(blocks(dx_1), 0, capacity, None)], 2, ranks, dweights,
    )
    grad_x_1, ddense, grad_expert_out, grad_bias, returned_0, returned_1 = attend_back(
        images, out_grad, slots, flat(sent_1), proj, mixed, residual, dense, small,
        experts, 1, old + [drouter],
        [(blocks(result_0), early, capacity, returned_0), (blocks(result_1), 0, capacity, None)],
        3, ranks, None, sums_b,
    )
    grad_blocks = [grad_x_0, grad_x_1]
    block_out, grad_attn_in, grad_attn_out, little = finish(
        slots, gates, residual, [flat(returned_0), flat(returned_1)], ddense, experts,
        8 + small_rows, 4,
    )
    return (
        block_out,
        jnp.concatenate(grad_blocks, axis=0),
        little[0],
        little[1],
        grad_attn_in.reshape(own, -1),
        grad_attn_out.reshape(own, -1),
        little[2],
        little[3],
        little[8 : 8 + experts].T,
        grad_expert_in[None],
        grad_bias[None, :, 0],
        grad_expert_out[None],
    )


def solution(mesh):
    return jax.shard_map(
        per_device,
        mesh=mesh,
        in_specs=(
            P(("dp", "expert"), None, None),
            P("dp"),
            P("dp"),
            P("dp", None),
            P("dp", None),
            P("dp"),
            P("dp"),
            P("dp", None),
            P("expert", "dp", None),
            P("expert", "dp"),
            P("expert", "dp", None),
            P(("dp", "expert"), None, None),
            P(("dp", "expert"), None, None),
        ),
        out_specs=(
            P(("dp", "expert"), None, None),
            P(("dp", "expert"), None, None),
            P("dp"),
            P("dp"),
            P("dp", None),
            P("dp", None),
            P("dp"),
            P("dp"),
            P("dp", None),
            P("expert", "dp", None),
            P("expert", "dp"),
            P("expert", "dp", None),
        ),
        check_vma=False,
    )
```

```python
import functools

import jax
import jax.numpy as jnp
from jax import lax
from jax.experimental import pallas as pl
from jax.experimental.pallas import tpu as pltpu
from jax.sharding import PartitionSpec as P

HEADS = 12
HEAD_DIM = 64
SEQ = 197
MICRO = 2
IMG_MB = 3
TOP = 2
LANES = 128
VMEM_LIMIT = 60 * 1024 * 1024

epsilon = 1e-06
f32 = jnp.float32
bf16 = jnp.bfloat16


def params(semantics, **more):
    return pltpu.CompilerParams(
        dimension_semantics=semantics, vmem_limit_bytes=VMEM_LIMIT, **more
    )


def dot(left, right):
    return lax.dot_general(
        left, right, (((1,), (0,)), ((), ())), preferred_element_type=f32
    )


def dot_t(left, right):
    return lax.dot_general(
        left, right, (((1,), (1,)), ((), ())), preferred_element_type=f32
    )


def t_dot(left, right):
    return lax.dot_general(
        left, right, (((0,), (0,)), ((), ())), preferred_element_type=f32
    )


def norm_forward(values):
    row_mean = jnp.mean(values, axis=-1, keepdims=True)
    centred = values - row_mean
    row_var = jnp.mean(centred * centred, axis=-1, keepdims=True)
    inverse = lax.rsqrt(row_var + epsilon)
    return centred * inverse, inverse


def norm_backward(grad_normed, normed, inverse):
    mean_grad = jnp.mean(grad_normed, axis=-1, keepdims=True)
    mean_cross = jnp.mean(grad_normed * normed, axis=-1, keepdims=True)
    return inverse * (grad_normed - mean_grad - normed * mean_cross)


def softmax_lanes(logits, count):
    lane = lax.broadcasted_iota(jnp.int32, logits.shape, 1)
    masked = jnp.where(lane < count, logits, -1e30)
    top = jnp.max(masked, axis=-1, keepdims=True)
    raised = jnp.where(lane < count, jnp.exp(masked - top), 0.0)
    return raised / jnp.sum(raised, axis=-1, keepdims=True)


def gelu_both(values):
    size = jnp.abs(values)
    bell = jnp.exp(values * values * -0.5)
    t = 1.0 / (1.0 + (0.3275911 * 0.7071067811865476) * size)
    tail = t * (
        0.5 * 0.254829592
        + t
        * (
            0.5 * -0.284496736
            + t * (0.5 * 1.421413741 + t * (0.5 * -1.453152027 + t * (0.5 * 1.061405429)))
        )
    )
    tail = tail * bell
    phi = jnp.where(values >= 0, 1.0 - tail, tail)
    return values * phi, phi + values * (0.3989422804014327 * bell)


class Rides:
    def __init__(self, entries):
        self.arrays = [entry[0] for entry in entries]
        self.rows = [pl.ds(entry[1], entry[2] - entry[1]) for entry in entries]
        self.before = [entry[3] for entry in entries if entry[3] is not None]
        self.filled = [index for index, entry in enumerate(entries) if entry[3] is not None]
        arrays = self.arrays
        self.parts = arrays[0].shape[0]
        self.operands = self.arrays + self.before
        self.in_specs = [pl.BlockSpec(memory_space=pl.ANY)] * len(self.operands)
        self.out_specs = [pl.BlockSpec(memory_space=pl.ANY)] * len(arrays)
        self.out_shape = [jax.ShapeDtypeStruct(a.shape, a.dtype) for a in arrays]
        self.scratch = [
            pltpu.SemaphoreType.DMA((self.parts,)),
            pltpu.SemaphoreType.DMA((self.parts,)),
            pltpu.SemaphoreType.DMA,
        ] * len(arrays)

    def aliases(self, inputs, outputs):
        first = inputs + len(self.arrays)
        return {first + place: outputs + index for place, index in enumerate(self.filled)}

    def copy(self, refs, index, offset):
        me = lax.axis_index("expert")
        peer = lax.rem(me + offset, self.parts)
        sources, targets, sems = refs
        return pltpu.make_async_remote_copy(
            src_ref=sources[index].at[peer, self.rows[index]],
            dst_ref=targets[index].at[me, self.rows[index]],
            send_sem=sems[3 * index].at[offset],
            recv_sem=sems[3 * index + 1].at[offset],
            device_id={"expert": peer},
            device_id_type=pl.DeviceIdType.MESH,
        )

    def own(self, refs):
        me = lax.axis_index("expert")
        sources, targets, sems = refs
        return [
            pltpu.make_async_copy(
                sources[index].at[me, self.rows[index]],
                targets[index].at[me, self.rows[index]],
                sems[3 * index + 2],
            )
            for index in range(len(sources))
        ]

    def start(self, refs, more=()):
        self.greet(more)
        self.send(refs)

    def greet(self, more):
        me = lax.axis_index("expert")
        barrier = pltpu.get_barrier_semaphore()
        for peer in more:
            pl.semaphore_signal(
                barrier, inc=1, device_id=peer, device_id_type=pl.DeviceIdType.MESH
            )

        @pl.loop(1, self.parts)
        def _(offset):
            pl.semaphore_signal(
                barrier,
                inc=1,
                device_id={"expert": lax.rem(me + offset, self.parts)},
                device_id_type=pl.DeviceIdType.MESH,
            )

        pl.semaphore_wait(barrier, self.parts - 1 + len(more))

    def send_hop(self, refs, hop):
        for index in range(len(self.rows)):
            self.copy(refs, index, hop).start()

    def send_own(self, refs):
        for copy in self.own(refs):
            copy.start()

    def send(self, refs):
        for index in range(len(self.rows)):

            @pl.loop(1, self.parts)
            def _(offset):
                self.copy(refs, index, offset).start()

        for copy in self.own(refs):
            copy.start()

    def finish(self, refs):
        for copy in self.own(refs):
            copy.wait()
        for index in range(len(self.rows)):

            @pl.loop(1, self.parts)
            def _(offset):
                self.copy(refs, index, offset).wait()


class Gather:
    def __init__(self, rows, ranks):
        self.rows = rows
        self.pairs = ranks // 2
        self.ranks = ranks
        sems = pltpu.SemaphoreType.DMA((2, self.pairs))
        self.scratch = [sems, sems, pltpu.SemaphoreType.DMA]

    def place(self, full, rank):
        return full.at[pl.ds(pl.multiple_of(rank * self.rows, self.rows), self.rows)]

    def copy(self, source, target, sems, hop, peer):
        return pltpu.make_async_remote_copy(
            src_ref=source,
            dst_ref=target,
            send_sem=sems.at[0, hop],
            recv_sem=sems.at[1, hop],
            device_id={"dp": peer},
            device_id_type=pl.DeviceIdType.MESH,
        )

    def first(self, refs, hop):
        shard, full, sems = refs
        target = self.place(full, lax.axis_index("dp"))
        source = target if shard is None else shard
        return self.copy(source, target, sems[0], hop, dp_peers(self.ranks)[hop])

    def second(self, refs, hop):
        _, full, sems = refs
        rank = lax.axis_index("dp")
        held = self.place(full, lax.rem(rank + self.ranks - 2 * hop, self.ranks))
        return self.copy(held, held, sems[1], hop, dp_peers(self.ranks)[0])

    def own(self, refs):
        shard, full, sems = refs
        target = self.place(full, lax.axis_index("dp"))
        return pltpu.make_async_copy(shard, target, sems[2])

    def start(self, refs):
        for hop in range(self.pairs):
            self.first(refs, hop).start()
        if refs[0] is not None:
            self.own(refs).start()

    def forward(self, refs):
        for hop in range(1, self.pairs):
            self.first(refs, hop).wait()
            self.second(refs, hop).start()

    def finish(self, refs):
        if refs[0] is not None:
            self.own(refs).wait()
        self.first(refs, 0).wait()
        for hop in range(1, self.pairs):
            self.second(refs, hop).wait()


def dp_peers(ranks):
    rank = lax.axis_index("dp")
    partner = rank + 1 - 2 * lax.rem(rank, 2)
    return [partner] + [lax.rem(rank + 2 * hop, ranks) for hop in range(1, ranks // 2)]


HBM = pl.BlockSpec(memory_space=pl.ANY)


def staged(*arrays):
    buffers = [pltpu.VMEM(array.shape, array.dtype) for array in arrays]
    return buffers + [pltpu.SemaphoreType.DMA((4,))]


def route_group(capacity, routes_ref, slots_ref, first):
    seq = routes_ref.shape[1]
    row = lax.broadcasted_iota(jnp.int32, (seq, seq), 0)
    col = lax.broadcasted_iota(jnp.int32, (seq, seq), 1)
    earlier = (col < row).astype(f32).astype(bf16)
    lane = lax.broadcasted_iota(jnp.int32, (seq, LANES), 1)
    base = jnp.zeros((1, LANES), f32)
    table = jnp.full((seq, LANES), -1.0, f32)
    for choice in range(TOP):
        for image in range(IMG_MB):
            named = routes_ref[first + image][:, choice : choice + 1]
            onehot = (lane == named).astype(f32)
            count = dot(earlier, onehot.astype(bf16)) + base
            position = jnp.sum(onehot * count, axis=1, keepdims=True).astype(jnp.int32)
            base = base + jnp.sum(onehot, axis=0, keepdims=True)
            slot = jnp.where(position < capacity, named * capacity + position, -1)
            slots_ref[first + image, :, choice : choice + 1] = slot
            table = jnp.where(lane == image * TOP + choice, slot.astype(f32), table)
    return table.T[:8].astype(jnp.int32)


def dispatch(lines, rows_ref, first, out_ref, send=None):
    experts, capacity = out_ref.shape[:2]
    seq = rows_ref.shape[1]
    slot = lax.broadcasted_iota(jnp.int32, (capacity, seq), 0)

    me = lax.axis_index("expert")

    def fill(hop):
        expert = lax.rem(me + hop, experts)
        here = slot + expert * capacity
        total = None
        for index in range(IMG_MB):
            at = index * TOP
            holds = (lines[at : at + 1] == here) | (lines[at + 1 : at + 2] == here)
            part = dot(holds.astype(f32).astype(bf16), rows_ref[first + index])
            total = part if total is None else total + part
        out_ref[expert] = total.astype(bf16)

    @pl.loop(1, experts)
    def _(hop):
        fill(hop)
        if send is not None:
            send(hop)

    fill(0)


def front_kernel(
    experts, capacity, ranks, rides, gathers,
    x_ref, named_ref, top_ref, router_ref, gains_ref, own_bias_ref, in_hbm, out_hbm, w1_hbm, w2_hbm,
    proj_ref, mixed_ref, residual_ref, gates_ref, slots_ref, small_ref, bias_ref,
    dense_hbm, w1_full, w2_full, grad_rows_hbm, token_rows_hbm, grads_hbm, received_hbm,
    dense_ref, rows_a, rows_b, hidden_ref, lines_ref, routes_ref, sems, *more,
):
    step = pl.program_id(0)
    features = x_ref.shape[2]
    ride_a = ([rows_a], [grads_hbm], more[:3])
    ride_b = ([rows_b], [received_hbm], more[3:6])
    dense_part = (None, dense_ref, more[6:9])
    w1_part = (w1_hbm, w1_full, more[9:12])
    w2_part = (w2_hbm, w2_full, more[12:15])
    gather_dense, gather_units = gathers
    keep_dense = pltpu.make_async_copy(dense_ref, dense_hbm, sems.at[0])
    keep_grads = pltpu.make_async_copy(rows_b, grad_rows_hbm, sems.at[1])
    keep_tokens = pltpu.make_async_copy(rows_a, token_rows_hbm, sems.at[2])

    @pl.when(step == 0)
    def _():
        own = features // ranks
        rank = lax.axis_index("dp")
        mine = pl.ds(pl.multiple_of(rank * own, own), own)
        fills = [
            pltpu.make_async_copy(
                in_hbm, dense_ref.at[mine, pl.ds(0, 3 * features)], sems.at[2]
            ),
            pltpu.make_async_copy(
                out_hbm, dense_ref.at[mine, pl.ds(3 * features, features)], sems.at[3]
            ),
        ]
        for fill in fills:
            fill.start()
        pieces = own_bias_ref.shape[1] // own
        own_bias = own_bias_ref[...].astype(f32)
        columns = jnp.concatenate(
            [router_ref[...].astype(f32), gains_ref[...].astype(f32)]
            + [own_bias[:, piece * own : (piece + 1) * own] for piece in range(pieces)]
            + [jnp.zeros((LANES - experts - 4 - pieces, own), f32)],
            axis=0,
        )
        dense_ref[mine, 4 * features :] = columns.T.astype(bf16)
        rides.greet([{"dp": peer} for peer in dp_peers(ranks)])
        for fill in fills:
            fill.wait()
        gather_dense.start(dense_part)
        images = named_ref.shape[0]
        named = [named_ref[index].astype(f32) for index in range(images)]
        rest = jnp.zeros((LANES - TOP * images, named_ref.shape[2]), f32)
        named = jnp.concatenate(named + [rest], axis=0).T.astype(jnp.int32)
        for index in range(images):
            routes_ref[index] = named[:, TOP * index : TOP * (index + 1)]
        lines = route_group(capacity, routes_ref, slots_ref, 0)
        lines_ref[0] = lines
        dispatch(lines, top_ref, 0, rows_a, lambda hop: rides.send_hop(ride_a, hop))
        rides.send_own(ride_a)
        lines = route_group(capacity, routes_ref, slots_ref, IMG_MB)
        lines_ref[1] = lines
        dispatch(lines, top_ref, IMG_MB, rows_b)
        keep_grads.start()
        gather_dense.forward(dense_part)
        gather_units.start(w1_part)
        gather_units.start(w2_part)
        gather_dense.finish(dense_part)
        keep_dense.start()
        small = dense_ref[:, 4 * features :].astype(f32).T
        small_ref[...] = small[: small_ref.shape[0]].astype(bf16)
        for line in range(pieces):
            at = experts + 4 + line
            for place in range(ranks):
                first = (place * pieces + line) * own
                bias_ref[:, first : first + own] = small[
                    at : at + 1, place * own : (place + 1) * own
                ].astype(bf16)
        keep_grads.wait()

    image = x_ref[0].astype(f32)
    vectors = small_ref[...].astype(f32)
    normed, _ = norm_forward(image)
    attn_input = (
        normed * vectors[experts : experts + 1] + vectors[experts + 1 : experts + 2]
    ).astype(bf16)
    proj_ref[0] = dot(attn_input, dense_ref[:, : 3 * features]).astype(bf16)
    low_half = lax.broadcasted_iota(jnp.int32, (1, LANES), 1) < HEAD_DIM
    for pair in range(features // LANES):
        first = pair * LANES
        queries = proj_ref[0, :, first : first + LANES]
        keys = proj_ref[0, :, features + first : features + first + LANES]
        values = proj_ref[0, :, 2 * features + first : 2 * features + first + LANES]
        out = None
        for half in range(2):
            keep = low_half if half == 0 else jnp.logical_not(low_half)
            scores = dot_t(
                jnp.where(keep, queries * HEAD_DIM ** (-0.5), 0).astype(bf16), keys
            )
            top = jnp.max(scores, axis=-1, keepdims=True)
            raised = jnp.exp(scores - top)
            share = 1.0 / jnp.sum(raised, axis=-1, keepdims=True)
            weights = (raised * share).astype(bf16)
            part = dot(weights, jnp.where(keep, values, 0).astype(bf16))
            out = part if out is None else out + part
        mixed_ref[0, :, first : first + LANES] = out.astype(bf16)
    residual = image + dot(mixed_ref[0], dense_ref[:, 3 * features : 4 * features])
    residual_ref[0] = residual
    normed, _ = norm_forward(residual)
    hidden = (
        normed * vectors[experts + 2 : experts + 3] + vectors[experts + 3 : experts + 4]
    ).astype(bf16)
    hidden_ref[lax.rem(step, IMG_MB)] = hidden
    probs = softmax_lanes(dot_t(hidden, small_ref[...]), experts)
    lane = lax.broadcasted_iota(jnp.int32, probs.shape, 1)
    routes = routes_ref[step]
    for choice in range(TOP):
        gates_ref[0, :, choice : choice + 1] = jnp.sum(
            jnp.where(lane == routes[:, choice : choice + 1], probs, 0.0),
            axis=1,
            keepdims=True,
        )

    @pl.when(step == IMG_MB - 1)
    def _():
        dispatch(lines_ref[0], hidden_ref, 0, rows_b, lambda hop: rides.send_hop(ride_b, hop))
        rides.send_own(ride_b)

    @pl.when(step == pl.num_programs(0) - 1)
    def _():
        rides.finish(ride_a)
        dispatch(lines_ref[1], hidden_ref, 0, rows_a)
        keep_tokens.start()
        gather_units.forward(w1_part)
        gather_units.forward(w2_part)
        gather_units.finish(w1_part)
        gather_units.finish(w2_part)
        keep_dense.wait()
        rides.finish(ride_b)
        keep_tokens.wait()


def front(
    images, named, out_grad, router, gains, bias, attn_in, attn_out, w1, w2, experts, capacity,
    ranks, small_rows, collective,
):
    count, seq, features = images.shape
    width = 4 * features + LANES
    slot_rows = jax.ShapeDtypeStruct((experts, capacity, features), bf16)
    rides = Rides([(slot_rows, 0, capacity, None)])
    gathers = (Gather(router.shape[1], ranks), Gather(w1.shape[0], ranks))

    def rows(width):
        return pl.BlockSpec((1, seq, width), lambda i: (i, 0, 0))

    def whole(shape):
        return pl.BlockSpec(
            shape, lambda i: (0,) * len(shape), pipeline_mode=pl.Buffered(1)
        )

    def out(width, dtype):
        return jax.ShapeDtypeStruct((count, seq, width), dtype)

    units = jax.ShapeDtypeStruct((ranks * w1.shape[0], features), bf16)
    return pl.pallas_call(
        functools.partial(front_kernel, experts, capacity, ranks, rides, gathers),
        grid=(count,),
        in_specs=[
            rows(features), whole(named.shape), whole(out_grad.shape), whole(router.shape),
            whole(gains.shape), whole(bias.shape), HBM, HBM, HBM, HBM,
        ],
        out_specs=[
            rows(3 * features), rows(features), rows(features), rows(TOP),
            whole((count, seq, TOP)), whole((small_rows, features)), whole((1, ranks * w1.shape[0])),
        ]
        + [HBM] * 7,
        out_shape=[
            out(3 * features, bf16),
            out(features, bf16),
            out(features, f32),
            out(TOP, f32),
            jax.ShapeDtypeStruct((count, seq, TOP), jnp.int32),
            jax.ShapeDtypeStruct((small_rows, features), bf16),
            jax.ShapeDtypeStruct((1, ranks * w1.shape[0]), bf16),
            jax.ShapeDtypeStruct((features, width), bf16),
            units,
            units,
            slot_rows,
            slot_rows,
            slot_rows,
            slot_rows,
        ],
        scratch_shapes=[
            pltpu.VMEM((features, width), bf16),
            pltpu.VMEM(slot_rows.shape, bf16),
            pltpu.VMEM(slot_rows.shape, bf16),
            pltpu.VMEM((IMG_MB, seq, features), bf16),
            pltpu.VMEM((count // IMG_MB, 8, seq), jnp.int32),
            pltpu.VMEM((count, seq, TOP), jnp.int32),
            pltpu.SemaphoreType.DMA((4,)),
        ]
        + rides.scratch
        + rides.scratch
        + gathers[0].scratch
        + gathers[1].scratch
        + gathers[1].scratch,
        compiler_params=params(
            ("arbitrary",), collective_id=collective, has_side_effects=True
        ),
        cost_estimate=pl.CostEstimate(
            flops=count * seq * 16 * features * features,
            bytes_accessed=4 * features * (4 * features + count * seq * 8),
            transcendentals=count * HEADS * seq * seq,
        ),
        name="front",
    )(images, named, out_grad, router, gains, bias, attn_in, attn_out, w1, w2)


def expert_kernel(
    experts, chunk, add, rides, x_hbm, g_hbm, w1_ref, w2_ref, bias_ref, small_ref, *refs
):
    if add:
        old_w_ref, old_router_ref = refs[:2]
        refs = refs[2:]
    count = len(rides.arrays)
    sources, refs = refs[:count], refs[len(rides.operands) :]
    ride_refs = (sources, refs[4 : count + 4], refs[count + 15 :])
    refs = refs[:4] + refs[count + 4 : count + 15]
    (
        result_hbm, dx_hbm, dw_ref, drouter_ref,
        result_acc, dx_acc, dr_ref, probs_ref, act_ref, pre_ref,
        x_ref, g_ref, result_ref, dx_ref, copy_sems,
    ) = refs
    loads = [
        pltpu.make_async_copy(x_hbm, x_ref, copy_sems.at[0]),
        pltpu.make_async_copy(g_hbm, g_ref, copy_sems.at[1]),
    ]
    stores = [
        pltpu.make_async_copy(result_ref, result_hbm, copy_sems.at[2]),
        pltpu.make_async_copy(dx_ref, dx_hbm, copy_sems.at[3]),
    ]
    step = pl.program_id(0)
    last = pl.num_programs(0) - 1
    rows = x_ref.shape[0]
    mine = lax.axis_index("expert")
    chunks = rows // chunk

    def each_chunk(body):
        for index in range(chunks):
            body(pl.ds(index * chunk, chunk))

    @pl.when(step == 0)
    def _():
        rides.start(ride_refs)
        for load in loads:
            load.start()
        for load in loads:
            load.wait()

        @each_chunk
        def _(at):
            probs = softmax_lanes(dot_t(x_ref[at, :], small_ref[...]), experts)
            lane = lax.broadcasted_iota(jnp.int32, probs.shape, 1)
            probs_ref[at, :] = probs
            gate = jnp.sum(jnp.where(lane == mine, probs, 0.0), axis=1, keepdims=True)
            dr_ref[at, :] = (gate * g_ref[at, :].astype(f32)).astype(bf16)
            result_acc[at, :] = jnp.zeros((chunk, x_ref.shape[1]), f32)
            dx_acc[at, :] = jnp.zeros((chunk, x_ref.shape[1]), f32)

    w1 = w1_ref[...]
    w2 = w2_ref[...]
    bias = bias_ref[...].astype(f32)

    def rows_step(index, dbias):
        at = pl.ds(index * chunk, chunk)
        act, slope = gelu_both(dot_t(x_ref[at, :], w1) + bias)
        act = act.astype(bf16)
        act_ref[at, :] = act
        result_acc[at, :] += dot(act, w2)
        grad_pre = (dot_t(dr_ref[at, :], w2) * slope).astype(bf16)
        pre_ref[at, :] = grad_pre
        dx_acc[at, :] += dot(grad_pre, w1)
        return dbias + jnp.sum(grad_pre.astype(f32), axis=0, keepdims=True)

    dbias = jnp.zeros(bias.shape, f32)
    for index in range(chunks):
        dbias = rows_step(index, dbias)
    dw1 = t_dot(pre_ref[...], x_ref[...])
    dw2 = t_dot(act_ref[...], dr_ref[...])
    dbias = jnp.broadcast_to(dbias, (LANES, dbias.shape[1])).T
    first = 0
    for part in (dw1, dw2, dbias):
        at = pl.ds(first, part.shape[1])
        if add:
            part = part + old_w_ref[:, at]
        dw_ref[:, at] = part.astype(dw_ref.dtype)
        first += part.shape[1]

    @pl.when(step == last)
    def _():
        if add:
            drouter_ref[...] = old_router_ref[...]
        else:
            drouter_ref[...] = jnp.zeros(drouter_ref.shape, f32)

        @each_chunk
        def _(at):
            result = result_acc[at, :].astype(bf16)
            result_ref[at, :] = result
            grad_gate = jnp.sum(
                g_ref[at, :].astype(f32) * result.astype(f32), axis=1, keepdims=True
            )
            probs = probs_ref[at, :]
            lane = lax.broadcasted_iota(jnp.int32, probs.shape, 1)
            chosen = lane == mine
            gate = jnp.sum(jnp.where(chosen, probs, 0.0), axis=1, keepdims=True)
            logits = (grad_gate * gate) * (chosen.astype(f32) - probs)
            high = logits.astype(bf16)
            low = (logits - high.astype(f32)).astype(bf16)
            dx_ref[at, :] = (
                dx_acc[at, :] + dot(high, small_ref[...]) + dot(low, small_ref[...])
            ).astype(bf16)
            drouter_ref[...] += t_dot(high, x_ref[at, :]) + t_dot(low, x_ref[at, :])

        for store in stores:
            store.start()
        rides.finish(ride_refs)
        for store in stores:
            store.wait()


def row_chunk(rows):
    best = rows
    for size in range(16, 513, 16):
        if rows % size == 0:
            best = size
    return best


def expert_block(x, g, w1, w2, bias, small, experts, old, entries, collective):
    rows, features = x.shape
    hidden_units = w1.shape[0]
    block = 512 if hidden_units % 512 == 0 else 256
    steps = hidden_units // block
    chunk = row_chunk(rows)
    add = old is not None
    out_type = bf16 if add else f32
    rides = Rides(entries)

    def whole(shape):
        return pl.BlockSpec(
            shape, lambda s: (0,) * len(shape), pipeline_mode=pl.Buffered(1)
        )

    packed = 2 * features + LANES
    unit_grads = pl.BlockSpec((block, packed), lambda s: (s, 0))
    units = pl.BlockSpec((block, features), lambda s: (s, 0))
    unit_row = pl.BlockSpec((1, block), lambda s: (0, s))
    in_specs = [
        HBM,
        HBM,
        units,
        units,
        unit_row,
        whole(small.shape),
    ]
    operands = [x, g, w1, w2, bias, small]
    if add:
        in_specs += [unit_grads, whole(small.shape)]
        operands += list(old)
    return pl.pallas_call(
        functools.partial(expert_kernel, experts, chunk, add, rides),
        grid=(steps,),
        in_specs=in_specs + rides.in_specs,
        out_specs=[
            HBM, HBM, unit_grads, whole(small.shape)
        ]
        + rides.out_specs,
        out_shape=[
            jax.ShapeDtypeStruct(x.shape, bf16),
            jax.ShapeDtypeStruct(x.shape, bf16),
            jax.ShapeDtypeStruct((hidden_units, packed), out_type),
            jax.ShapeDtypeStruct(small.shape, f32),
        ]
        + rides.out_shape,
        scratch_shapes=[
            pltpu.VMEM((rows, features), f32),
            pltpu.VMEM((rows, features), f32),
            pltpu.VMEM((rows, features), bf16),
            pltpu.VMEM((rows, small.shape[0]), f32),
            pltpu.VMEM((rows, block), bf16),
            pltpu.VMEM((rows, block), bf16),
            *staged(x, g, x, x),
        ]
        + rides.scratch,
        compiler_params=params(
            ("arbitrary",), collective_id=collective, has_side_effects=True
        ),
        cost_estimate=pl.CostEstimate(
            flops=12 * rows * features * hidden_units,
            bytes_accessed=(8 * rows + 12 * hidden_units) * features,
            transcendentals=rows * hidden_units,
        ),
        name="expert_block",
    )(*operands, *rides.operands)


def inner_size(parts):
    size = 1
    while parts % (2 * size) == 0 and 4 * size * size <= parts:
        size *= 2
    return size


def finish_kernel(
    inner, outer, bits, slots_ref, gates_ref, residual_ref,
    returned0_hbm, returned1_hbm, part_ref, out_ref, din_ref, dout_ref, little_ref,
    returned0_ref, returned1_ref, load_sems, flat_ref, sum_ref, second_ref, full_ref, sems2, sems3, sems4,
):
    step = pl.program_id(0)
    seq = slots_ref.shape[1]
    features = out_ref.shape[2]
    width = part_ref.shape[2]
    tiles = width // LANES
    chunks = 4
    edges = [LANES * (tiles * c // chunks) for c in range(chunks + 1)]
    cuts = [pl.ds(edges[c], edges[c + 1] - edges[c]) for c in range(chunks)]
    me = lax.axis_index("expert")
    row = lax.rem(me, inner)
    line = me // inner

    def row_peer(hop):
        return lax.rem(row + hop, inner)

    def copy(source, target, sems, chunk, hop, peer):
        return pltpu.make_async_remote_copy(
            src_ref=source,
            dst_ref=target,
            send_sem=sems.at[0, chunk, hop - 1],
            recv_sem=sems.at[1, chunk, hop - 1],
            device_id={"expert": peer},
            device_id_type=pl.DeviceIdType.MESH,
        )

    def flip(bit):
        size = 2**bit
        return line + size * (1 - 2 * lax.rem(line // size, 2))

    def held(bit, side):
        size = 2**bit
        mine = lax.rem(line // size, 2)
        first = lax.rem(line, size) + size * (mine if side else 1 - mine)
        return [first + 2 * size * place for place in range(outer // (2 * size))]

    def slot(bit, place):
        return sum(outer // 2 ** (lower + 1) for lower in range(bit)) + place

    def reduce_lines(bit, chunk):
        at = cuts[chunk]
        source = part_ref if bit == 0 else sum_ref
        return [
            copy(
                source.at[block, :, at], second_ref.at[slot(bit, place), :, at],
                sems2, chunk, 1 + slot(bit, place), flip(bit) * inner + row,
            )
            for place, block in enumerate(held(bit, False))
        ]

    def add_lines(bit, chunk):
        at = cuts[chunk]
        source = part_ref if bit == 0 else sum_ref
        for place, block in enumerate(held(bit, True)):
            total = source[block, :, at].astype(f32) + second_ref[
                slot(bit, place), :, at
            ].astype(f32)
            if bit == bits - 1:
                full_ref[row, block, :, at] = total.astype(bf16)
            else:
                sum_ref[block, :, at] = total.astype(bf16)

    def gather_lines(bit, chunk):
        at = cuts[chunk]
        return [
            copy(
                full_ref.at[row, block, :, at], full_ref.at[row, block, :, at],
                sems3, chunk, 1 + slot(bit, place), flip(bit) * inner + row,
            )
            for place, block in enumerate(held(bit, True))
        ]

    def gather_rows(chunk):
        at = cuts[chunk]
        return [
            copy(
                full_ref.at[row, :, :, at], full_ref.at[row, :, :, at],
                sems4, chunk, hop, line * inner + row_peer(hop),
            )
            for hop in range(1, inner)
        ]

    loads = [
        pltpu.make_async_copy(returned0_hbm, returned0_ref, load_sems.at[0]),
        pltpu.make_async_copy(returned1_hbm, returned1_ref, load_sems.at[1]),
    ]

    def start(copies):
        for item in copies:
            item.start()

    def wait(copies):
        for item in copies:
            item.wait()

    @pl.when(step == 0)
    def _():
        barrier = pltpu.get_barrier_semaphore()
        peers = [line * inner + row_peer(hop) for hop in range(1, inner)]
        peers += [flip(bit) * inner + row for bit in range(bits)]
        for peer in peers:
            pl.semaphore_signal(
                barrier,
                inc=1,
                device_id={"expert": peer},
                device_id_type=pl.DeviceIdType.MESH,
            )
        pl.semaphore_wait(barrier, len(peers))
        for chunk in range(chunks):
            start(reduce_lines(0, chunk))
        start(loads)
        wait(loads[:1])

    @pl.when(step == IMG_MB)
    def _():
        wait(loads[1:])

    column = lax.broadcasted_iota(jnp.int32, (seq, returned0_ref.shape[0]), 1)

    def mix(returned_ref):
        slots = slots_ref[0]
        gates = gates_ref[0]
        total = residual_ref[0]
        for choice in range(TOP):
            holds = slots[:, choice : choice + 1] == column
            picked = dot(holds.astype(f32).astype(bf16), returned_ref[...])
            total = total + gates[:, choice : choice + 1] * picked
        out_ref[0] = total.astype(bf16)

    @pl.when(step < IMG_MB)
    def _():
        mix(returned0_ref)

    @pl.when(step >= IMG_MB)
    def _():
        mix(returned1_ref)

    def reduced(bit, chunk):
        wait(reduce_lines(bit, chunk))
        add_lines(bit, chunk)
        if bit < bits - 1:
            start(reduce_lines(bit + 1, chunk))
        else:
            start(gather_lines(bit, chunk))

    def gathered(bit, chunk):
        wait(gather_lines(bit, chunk))
        if bit > 0:
            start(gather_lines(bit - 1, chunk))
        else:
            start(gather_rows(chunk))

    stages = [functools.partial(reduced, bit) for bit in range(bits)]
    stages += [functools.partial(gathered, bit) for bit in reversed(range(bits))]
    for place, stage in enumerate(stages):

        @pl.when(step == min(place + 1, 2 * IMG_MB - 1))
        def _():
            for chunk in range(chunks):
                stage(chunk)

    @pl.when(step == 2 * IMG_MB - 1)
    def _():
        for chunk in range(chunks):
            wait(gather_rows(chunk))
        for part in range(inner):
            for place in range(outer):
                block = part * outer + place
                din_ref[block] = full_ref[part, place, :, : 3 * features].astype(f32)
                dout_ref[block] = full_ref[part, place, :, 3 * features : 4 * features].astype(
                    f32
                )
                share = full_ref.shape[2]
                flat_ref[block * share : (block + 1) * share] = full_ref[
                    part, place, :, 4 * features :
                ].astype(f32)
        little_ref[...] = flat_ref[...].T[: little_ref.shape[0]]


def finish(slots, gates, residual, returned, part, parts, lines, collective):
    outer, share, width = part.shape
    inner = inner_size(parts)
    bits = outer.bit_length() - 1
    images, seq, features = residual.shape
    chunks = 4

    def whole(shape):
        return pl.BlockSpec(
            shape, lambda i: (0,) * len(shape), pipeline_mode=pl.Buffered(1)
        )

    def each(width):
        return pl.BlockSpec((1, seq, width), lambda i: (i, 0, 0))

    outs = [3 * features, features]
    little = (lines, parts * share)
    return pl.pallas_call(
        functools.partial(finish_kernel, inner, outer, bits),
        grid=(images,),
        in_specs=[
            each(TOP), each(TOP), each(features),
            HBM, HBM, whole(part.shape),
        ],
        out_specs=[each(features)] + [whole((parts, share, size)) for size in outs]
        + [whole(little)],
        out_shape=[jax.ShapeDtypeStruct((images, seq, features), bf16)]
        + [jax.ShapeDtypeStruct((parts, share, size), f32) for size in outs]
        + [jax.ShapeDtypeStruct(little, f32)],
        scratch_shapes=[
            *staged(*returned),
            pltpu.VMEM((parts * share, LANES), f32),
            pltpu.VMEM((outer, share, width), bf16),
            pltpu.VMEM((outer - 1, share, width), bf16),
            pltpu.VMEM((inner, outer, share, width), bf16),
            pltpu.SemaphoreType.DMA((2, chunks, outer - 1)),
            pltpu.SemaphoreType.DMA((2, chunks, outer - 1)),
            pltpu.SemaphoreType.DMA((2, chunks, inner - 1)),
        ],
        compiler_params=params(
            ("arbitrary",), collective_id=collective, has_side_effects=True
        ),
        cost_estimate=pl.CostEstimate(
            flops=4 * images * seq * returned[0].shape[0] * features,
            bytes_accessed=2 * features * (2 * returned[0].shape[0] + 3 * images * seq),
            transcendentals=0,
        ),
        name="finish",
    )(slots, gates, residual, *returned, part)


def attend_back_kernel(
    experts, add, rides, ranks, x_ref, top_ref, slots_ref, sent_hbm, proj_ref, mixed_ref, residual_ref,
    dense_hbm, small_ref, *refs
):
    if add:
        old_dense_ref, old_small_ref, drouter_ref, sums_b_hbm = refs[:4]
        refs = refs[4:]
    else:
        dweights_hbm, refs = refs[0], refs[1:]
    count = len(rides.arrays)
    outs = 4 if add else 5
    sources, refs = refs[:count], refs[len(rides.operands) :]
    grad_x_ref, ddense_ref = refs[:2]
    if add:
        grad_b_ref, bias_b_ref = refs[2:4]
    else:
        dsmall_ref, sums_b_hbm, grad_a_ref = refs[2:5]
    targets, refs = refs[outs : outs + count], refs[outs + count :]
    acc_in, acc_out, acc_small, dproj_ref, grad_mixed_ref = refs[:5]
    sent_ref, dense_ref, copy_sems = refs[5:8]
    refs = refs[8:]
    rank = lax.axis_index("dp")
    core = lax.rem(rank, 2)
    mine = rank // 2
    pairs = ranks // 2
    partner, *others = [{"dp": peer} for peer in dp_peers(ranks)]
    more = [partner] + others

    def remote(source, target, sems, index, peer):
        return pltpu.make_async_remote_copy(
            src_ref=source,
            dst_ref=target,
            send_sem=sems.at[0, index],
            recv_sem=sems.at[1, index],
            device_id=peer,
            device_id_type=pl.DeviceIdType.MESH,
        )

    if add:
        pack_ref, first_ref, second_ref, part_ref, third_ref = refs[:5]
        first_sems, second_sems, third_sems = refs[5:8]
        own_b_ref, other_b_ref, own_b_sem, other_b_sems = refs[8:12]
        refs = refs[12:]
    else:
        own_w_ref, other_w_ref, other_a_ref = refs[:3]
        own_w_sems, other_w_sems, other_a_sems, keep_b_sem = refs[3:7]
        refs = refs[7:]

    def core_swap(pair):
        rows = other_w_ref.shape[1]
        at = pl.multiple_of((2 * pair + 1 - core) * rows, rows)
        source = dweights_hbm.at[pl.ds(at, rows)]
        return remote(source, other_w_ref.at[pair], other_w_sems, pair, partner)

    def core_own(pair):
        rows = own_w_ref.shape[1]
        at = pl.multiple_of((2 * pair + core) * rows, rows)
        return pltpu.make_async_copy(
            dweights_hbm.at[pl.ds(at, rows)], own_w_ref.at[pair], own_w_sems.at[pair]
        )

    def send_a(hop):
        at = pl.ds(0, x_ref.shape[2])
        source = own_w_ref.at[lax.rem(mine + hop, pairs), :, at]
        return remote(source, other_a_ref.at[hop - 1], other_a_sems, hop - 1, others[hop - 1])

    def keep_b():
        at = pl.ds(x_ref.shape[2], sums_b_hbm.shape[2])
        return pltpu.make_async_copy(own_w_ref.at[:, :, at], sums_b_hbm, keep_b_sem.at[0])

    def send_b(hop):
        source = sums_b_hbm.at[lax.rem(mine + hop, pairs)]
        return remote(source, other_b_ref.at[hop - 1], other_b_sems, hop - 1, others[hop - 1])

    def own_b():
        return pltpu.make_async_copy(sums_b_hbm.at[mine], own_b_ref, own_b_sem.at[0])

    ride_refs = (sources, targets, refs)
    features = x_ref.shape[2]
    seq = x_ref.shape[1]
    step = pl.program_id(0)
    vectors = small_ref[...].astype(f32)
    loads = [
        pltpu.make_async_copy(sent_hbm, sent_ref, copy_sems.at[0]),
        pltpu.make_async_copy(dense_hbm, dense_ref, copy_sems.at[1]),
    ]
    sums_hbm = old_dense_ref if add else ddense_ref
    halves = [
        (acc_in, sums_hbm.at[:, pl.ds(0, 3 * features)], copy_sems.at[2]),
        (acc_out, sums_hbm.at[:, pl.ds(3 * features, features)], copy_sems.at[3]),
    ]
    if add:
        moves = [pltpu.make_async_copy(far, near, sem) for near, far, sem in halves]
    else:
        moves = [pltpu.make_async_copy(near, far, sem) for near, far, sem in halves]

    @pl.when(step == 0)
    def _():
        rides.start(ride_refs, more)
        for load in loads:
            load.start()
        if add:
            own_b().start()
            for hop in range(1, pairs):
                send_b(hop).start()
        else:
            for pair in range(pairs):
                core_swap(pair).start()
                core_own(pair).start()
        if add:
            for move in moves:
                move.start()
            acc_small[...] = old_small_ref[...]
        else:
            acc_in[...] = jnp.zeros(acc_in.shape, f32)
            acc_out[...] = jnp.zeros(acc_out.shape, f32)
            acc_small[...] = jnp.zeros(acc_small.shape, f32)
        for load in loads:
            load.wait()

    if not add:

        @pl.when(step == 1)
        def _():
            for pair in range(pairs):
                core_swap(pair).wait()
                core_own(pair).wait()
                total = own_w_ref[pair].astype(f32) + other_w_ref[pair].astype(f32)
                own_w_ref[pair] = total.astype(bf16)
            for hop in range(1, pairs):
                send_a(hop).start()
            keep_b().start()

    column = lax.broadcasted_iota(jnp.int32, (seq, sent_ref.shape[0]), 1)
    slots = slots_ref[0]
    holds = (slots[:, 0:1] == column) | (slots[:, 1:2] == column)
    grad_hidden = dot(holds.astype(f32).astype(bf16), sent_ref[...])
    normed_two, inverse_two = norm_forward(residual_ref[0])
    acc_small[2:3, :] += jnp.sum(grad_hidden * normed_two, axis=0, keepdims=True)
    acc_small[3:4, :] += jnp.sum(grad_hidden, axis=0, keepdims=True)
    grad_residual = top_ref[0].astype(f32) + norm_backward(
        grad_hidden * vectors[experts + 2 : experts + 3], normed_two, inverse_two
    )
    grad_branch = grad_residual.astype(bf16)
    grad_mixed_ref[...] = dot_t(grad_branch, dense_ref[:, 3 * features : 4 * features]).astype(
        bf16
    )
    low_half = lax.broadcasted_iota(jnp.int32, (1, LANES), 1) < HEAD_DIM
    scale = HEAD_DIM ** (-0.5)
    def head_pair(first):
        queries = proj_ref[0, :, pl.ds(first, LANES)]
        keys = proj_ref[0, :, pl.ds(features + first, LANES)]
        values = proj_ref[0, :, pl.ds(2 * features + first, LANES)]
        grad_out = grad_mixed_ref[:, pl.ds(first, LANES)]
        sums = [None, None, None]
        for half in range(2):
            keep = low_half if half == 0 else jnp.logical_not(low_half)
            head_queries = jnp.where(keep, queries * scale, 0).astype(bf16)
            head_keys = jnp.where(keep, keys, 0).astype(bf16)
            head_grad = jnp.where(keep, grad_out, 0).astype(bf16)
            scores = dot_t(keys, head_queries)
            top = jnp.max(scores, axis=0, keepdims=True)
            raised = jnp.exp(scores - top)
            probs = raised * (1.0 / jnp.sum(raised, axis=0, keepdims=True))
            grad_values = dot(probs.astype(bf16), head_grad)
            grad_weights = dot_t(values, head_grad)
            inner = jnp.sum(grad_weights * probs, axis=0, keepdims=True)
            grad_scores = (probs * (grad_weights - inner)).astype(bf16)
            grad_keys = dot(grad_scores, head_queries)
            grad_queries = t_dot(grad_scores, head_keys)
            for place, part in enumerate((grad_queries, grad_keys, grad_values)):
                sums[place] = part if half == 0 else sums[place] + part
        dproj_ref[:, pl.ds(first, LANES)] = (sums[0] * scale).astype(bf16)
        dproj_ref[:, pl.ds(features + first, LANES)] = sums[1].astype(bf16)
        dproj_ref[:, pl.ds(2 * features + first, LANES)] = sums[2].astype(bf16)
    for pair in range(features // LANES):
        head_pair(pair * LANES)
    normed_one, inverse_one = norm_forward(x_ref[0].astype(f32))
    attn_input = (
        normed_one * vectors[experts : experts + 1] + vectors[experts + 1 : experts + 2]
    ).astype(bf16)
    if add:

        @pl.when(step == 0)
        def _():
            for move in moves:
                move.wait()

    acc_out[...] += t_dot(mixed_ref[0], grad_branch)
    acc_in[...] += t_dot(attn_input, dproj_ref[...])
    grad_input = dot_t(dproj_ref[...], dense_ref[:, : 3 * features])
    acc_small[0:1, :] += jnp.sum(grad_input * normed_one, axis=0, keepdims=True)
    acc_small[1:2, :] += jnp.sum(grad_input, axis=0, keepdims=True)
    grad_x_ref[0] = grad_residual + norm_backward(
        grad_input * vectors[experts : experts + 1], normed_one, inverse_one
    )

    @pl.when(step == pl.num_programs(0) - 1)
    def _():
        if not add:
            for move in moves:
                move.start()
            dsmall_ref[...] = acc_small[...]
            total = own_w_ref[mine, :, :features].astype(f32)
            for hop in range(1, pairs):
                send_a(hop).wait()
                total = total + other_a_ref[hop - 1].astype(f32)
            grad_a_ref[...] = total
            keep_b().wait()
        else:
            used = acc_small.shape[0] + drouter_ref.shape[0]
            rest = jnp.zeros((LANES - used, features), f32)
            column = jnp.concatenate([acc_small[...], drouter_ref[...], rest], axis=0).T
            share = features // ranks
            for shard in range(ranks):
                at = slice(shard * share, (shard + 1) * share)
                place = (shard % 2, shard // 2)
                pack_ref[place[0], place[1], :, : 3 * features] = acc_in[at].astype(bf16)
                pack_ref[place[0], place[1], :, 3 * features : 4 * features] = acc_out[
                    at
                ].astype(bf16)
                pack_ref[place[0], place[1], :, 4 * features :] = column[at].astype(bf16)
            copy = remote(pack_ref.at[1 - core], first_ref, first_sems, 0, partner)
            copy.start()
            copy.wait()
            for pair in range(pairs):
                first_ref[pair] = (
                    first_ref[pair].astype(f32) + pack_ref[core, pair].astype(f32)
                ).astype(bf16)
            copies = [
                remote(
                    first_ref.at[lax.rem(mine + hop, pairs)], second_ref.at[hop - 1],
                    second_sems, hop - 1, others[hop - 1],
                )
                for hop in range(1, pairs)
            ]
            for copy in copies:
                copy.start()
            own_b().wait()
            total = own_b_ref[...].astype(f32)
            for hop in range(1, pairs):
                send_b(hop).wait()
                total = total + other_b_ref[hop - 1].astype(f32)
            grad_b_ref[...] = total[:, :features]
            bias_b_ref[...] = total[:, features:]
            total = first_ref[mine].astype(f32)
            for copy in copies:
                copy.wait()
            for hop in range(1, pairs):
                total = total + second_ref[hop - 1].astype(f32)
            total = total.astype(bf16)
            inner, outer, rows = part_ref.shape[:3]
            for block in range(inner * outer):
                part_ref[block // outer, block % outer] = total[block * rows : (block + 1) * rows]
            me = lax.axis_index("expert")
            row = lax.rem(me, inner)
            copies = []
            for hop in range(1, inner):
                peer = lax.rem(row + hop, inner)
                copies.append(
                    remote(
                        part_ref.at[peer], third_ref.at[hop - 1], third_sems, hop - 1,
                        {"expert": me - row + peer},
                    )
                )
            for copy in copies:
                copy.start()
            for copy in copies:
                copy.wait()
            total = part_ref[row].astype(f32)
            for hop in range(1, inner):
                total = total + third_ref[hop - 1].astype(f32)
            ddense_ref[...] = total.astype(bf16)
        rides.finish(ride_refs)
        if not add:
            for move in moves:
                move.wait()


def attend_back(
    images, out_grad, slots, sent, proj, mixed, residual, dense, small, experts, group, old,
    entries, collective, ranks, dweights=None, sums_b=None,
):
    seq, features = images.shape[1:]
    wide = 3 * features
    first = group * IMG_MB
    add = old is not None
    rides = Rides(entries)

    def rows(width):
        return pl.BlockSpec((1, seq, width), lambda i: (i, 0, 0))

    def source(width):
        return pl.BlockSpec((1, seq, width), lambda i: (first + i, 0, 0))

    def whole(shape):
        return pl.BlockSpec(shape, lambda i: (0, 0), pipeline_mode=pl.Buffered(1))

    small_grads = (8, features)
    in_specs = [
        source(features), source(features), source(TOP), HBM,
        source(wide), source(features), source(features),
        HBM, whole(small.shape),
    ]
    operands = [images, out_grad, slots, sent, proj, mixed, residual, dense, small]
    out_specs = [rows(features), HBM]
    out_shape = [
        jax.ShapeDtypeStruct((IMG_MB, seq, features), f32),
        jax.ShapeDtypeStruct((features, 4 * features), f32),
    ]
    if add:
        in_specs += [HBM] + [whole(array.shape) for array in old[1:]] + [HBM]
        operands += list(old) + [sums_b]
        out_specs += [whole((sums_b.shape[1], features)), whole((sums_b.shape[1], LANES))]
        out_shape += [
            jax.ShapeDtypeStruct((sums_b.shape[1], features), f32),
            jax.ShapeDtypeStruct((sums_b.shape[1], LANES), f32),
        ]
        shard = (features // ranks, 4 * features + LANES)
        inner = inner_size(experts)
        part = (experts // inner, shard[0] // experts, shard[1])
        out_specs[1] = pl.BlockSpec(
            part, lambda i: (0, 0, 0), pipeline_mode=pl.Buffered(1)
        )
        out_shape[1] = jax.ShapeDtypeStruct(part, bf16)
        reduce_scratch = [
            pltpu.VMEM((2, ranks // 2, *shard), bf16),
            pltpu.VMEM((ranks // 2, *shard), bf16),
            pltpu.VMEM((ranks // 2 - 1, *shard), bf16),
            pltpu.VMEM((inner, *part), bf16),
            pltpu.VMEM((inner - 1, *part), bf16),
            pltpu.SemaphoreType.DMA((2, 1)),
            pltpu.SemaphoreType.DMA((2, ranks // 2 - 1)),
            pltpu.SemaphoreType.DMA((2, inner - 1)),
            pltpu.VMEM(sums_b.shape[1:], bf16),
            pltpu.VMEM((ranks // 2 - 1, *sums_b.shape[1:]), bf16),
            pltpu.SemaphoreType.DMA((1,)),
            pltpu.SemaphoreType.DMA((2, ranks // 2 - 1)),
        ]
    else:
        out_specs.append(whole(small_grads))
        out_shape.append(jax.ShapeDtypeStruct(small_grads, f32))
        in_specs.append(HBM)
        operands.append(dweights)
        units = dweights.shape[0] // ranks
        rest = dweights.shape[1] - features
        out_specs += [HBM, whole((units, features))]
        out_shape += [
            jax.ShapeDtypeStruct((ranks // 2, units, rest), bf16),
            jax.ShapeDtypeStruct((units, features), f32),
        ]
        reduce_scratch = [
            pltpu.VMEM((ranks // 2, units, dweights.shape[1]), bf16),
            pltpu.VMEM((ranks // 2, units, dweights.shape[1]), bf16),
            pltpu.VMEM((ranks // 2 - 1, units, features), bf16),
            pltpu.SemaphoreType.DMA((ranks // 2,)),
            pltpu.SemaphoreType.DMA((2, ranks // 2)),
            pltpu.SemaphoreType.DMA((2, ranks // 2 - 1)),
            pltpu.SemaphoreType.DMA((1,)),
        ]
    return pl.pallas_call(
        functools.partial(attend_back_kernel, experts, add, rides, ranks),
        grid=(IMG_MB,),
        in_specs=in_specs + rides.in_specs,
        out_specs=out_specs + rides.out_specs,
        out_shape=out_shape + rides.out_shape,
        scratch_shapes=[
            pltpu.VMEM((features, 3 * features), f32),
            pltpu.VMEM((features, features), f32),
            pltpu.VMEM(small_grads, f32),
            pltpu.VMEM((seq, wide), bf16),
            pltpu.VMEM((seq, features), bf16),
            *staged(sent, dense),
        ]
        + reduce_scratch
        + rides.scratch,
        input_output_aliases=rides.aliases(len(operands), len(out_specs)),
        compiler_params=params(
            ("arbitrary",), collective_id=collective, has_side_effects=True
        ),
        cost_estimate=pl.CostEstimate(
            flops=IMG_MB * seq * 40 * features * features,
            bytes_accessed=8 * features * (4 * features + IMG_MB * seq * 4),
            transcendentals=IMG_MB * HEADS * seq * seq,
        ),
        name="attend_back",
    )(*operands, *rides.operands)


def per_device(
    images, first_gain, first_shift, attn_in, attn_out, second_gain, second_shift, router,
    expert_in, expert_bias, expert_out, routes, out_grad,
):
    features = images.shape[2]
    experts = router.shape[1]
    tok_mb = IMG_MB * SEQ
    capacity = max(2, (5 * TOP * tok_mb // (4 * experts) + 7) // 8 * 8)
    slot_rows = experts * capacity
    own = router.shape[0]
    ranks = features // own
    bias_rows = expert_bias.shape[1] // own
    used = experts + 4 + bias_rows
    small_rows = (used + 15) // 16 * 16
    line = lax.broadcasted_iota(jnp.int32, (4, own), 0)
    gains = jnp.where(
        line < 2,
        jnp.where(line == 0, first_gain[None], first_shift[None]),
        jnp.where(line == 2, second_gain[None], second_shift[None]),
    )

    def flat(blocks):
        return blocks.reshape(slot_rows, features)

    def blocks(rows):
        return rows.reshape(experts, capacity, features)

    (
        proj, mixed, residual, gates, slots, small, bias_row, dense, weight_in, weight_out,
        grad_rows_1, token_rows_1, grads_0, received_0,
    ) = front(
        images, routes.transpose(0, 2, 1), out_grad, router.T, gains, expert_bias, attn_in,
        attn_out, expert_in[0],
        expert_out[0], experts, capacity, ranks, small_rows, 5,
    )
    result_0, dx_0, *old, grads_1, received_1 = expert_block(
        flat(received_0), flat(grads_0), weight_in, weight_out, bias_row, small, experts, None,
        [(grad_rows_1, 0, capacity, None), (token_rows_1, 0, capacity, None)], 0,
    )
    early = max(8, capacity * 3 // 8 // 8 * 8)
    result_1, dx_1, dweights, drouter, sent_0, returned_0 = expert_block(
        flat(received_1), flat(grads_1), weight_in, weight_out, bias_row, small, experts, old,
        [(blocks(dx_0), 0, capacity, None), (blocks(result_0), 0, early, None)], 1,
    )
    grad_x_0, *old, sums_b, grad_expert_in, sent_1 = attend_back(
        images, out_grad, slots, flat(sent_0), proj, mixed, residual, dense, small,
        experts, 0, None, [(blocks(dx_1), 0, capacity, None)], 2, ranks, dweights,
    )
    grad_x_1, ddense, grad_expert_out, grad_bias, returned_0, returned_1 = attend_back(
        images, out_grad, slots, flat(sent_1), proj, mixed, residual, dense, small,
        experts, 1, old + [drouter],
        [(blocks(result_0), early, capacity, returned_0), (blocks(result_1), 0, capacity, None)],
        3, ranks, None, sums_b,
    )
    grad_blocks = [grad_x_0, grad_x_1]
    block_out, grad_attn_in, grad_attn_out, little = finish(
        slots, gates, residual, [flat(returned_0), flat(returned_1)], ddense, experts,
        8 + small_rows, 4,
    )
    return (
        block_out,
        jnp.concatenate(grad_blocks, axis=0),
        little[0],
        little[1],
        grad_attn_in.reshape(own, -1),
        grad_attn_out.reshape(own, -1),
        little[2],
        little[3],
        little[8 : 8 + experts].T,
        grad_expert_in[None],
        grad_bias[None, :, 0],
        grad_expert_out[None],
    )


def solution(mesh):
    return jax.shard_map(
        per_device,
        mesh=mesh,
        in_specs=(
            P(("dp", "expert"), None, None),
            P("dp"),
            P("dp"),
            P("dp", None),
            P("dp", None),
            P("dp"),
            P("dp"),
            P("dp", None),
            P("expert", "dp", None),
            P("expert", "dp"),
            P("expert", "dp", None),
            P(("dp", "expert"), None, None),
            P(("dp", "expert"), None, None),
        ),
        out_specs=(
            P(("dp", "expert"), None, None),
            P(("dp", "expert"), None, None),
            P("dp"),
            P("dp"),
            P("dp", None),
            P("dp", None),
            P("dp"),
            P("dp"),
            P("dp", None),
            P("expert", "dp", None),
            P("expert", "dp"),
            P("expert", "dp", None),
        ),
        check_vma=False,
    )
```

```python
import functools

import jax
import jax.numpy as jnp
from jax import lax
from jax.experimental import pallas as pl
from jax.experimental.pallas import tpu as pltpu
from jax.sharding import PartitionSpec as P

HEADS = 12
HEAD_DIM = 64
SEQ = 197
MICRO = 2
IMG_MB = 3
TOP = 2
LANES = 128
VMEM_LIMIT = 60 * 1024 * 1024

epsilon = 1e-06
f32 = jnp.float32
bf16 = jnp.bfloat16


def params(semantics, **more):
    return pltpu.CompilerParams(
        dimension_semantics=semantics, vmem_limit_bytes=VMEM_LIMIT, **more
    )


def dot(left, right):
    return lax.dot_general(
        left, right, (((1,), (0,)), ((), ())), preferred_element_type=f32
    )


def dot_t(left, right):
    return lax.dot_general(
        left, right, (((1,), (1,)), ((), ())), preferred_element_type=f32
    )


def t_dot(left, right):
    return lax.dot_general(
        left, right, (((0,), (0,)), ((), ())), preferred_element_type=f32
    )


def norm_forward(values):
    row_mean = jnp.mean(values, axis=-1, keepdims=True)
    centred = values - row_mean
    row_var = jnp.mean(centred * centred, axis=-1, keepdims=True)
    inverse = lax.rsqrt(row_var + epsilon)
    return centred * inverse, inverse


def norm_backward(grad_normed, normed, inverse):
    mean_grad = jnp.mean(grad_normed, axis=-1, keepdims=True)
    mean_cross = jnp.mean(grad_normed * normed, axis=-1, keepdims=True)
    return inverse * (grad_normed - mean_grad - normed * mean_cross)


def softmax_lanes(logits, count):
    lane = lax.broadcasted_iota(jnp.int32, logits.shape, 1)
    masked = jnp.where(lane < count, logits, -1e30)
    top = jnp.max(masked, axis=-1, keepdims=True)
    raised = jnp.where(lane < count, jnp.exp(masked - top), 0.0)
    return raised / jnp.sum(raised, axis=-1, keepdims=True)


def gelu_both(values):
    size = jnp.abs(values)
    bell = jnp.exp(values * values * -0.5)
    t = 1.0 / (1.0 + (0.3275911 * 0.7071067811865476) * size)
    tail = t * (
        0.5 * 0.254829592
        + t
        * (
            0.5 * -0.284496736
            + t * (0.5 * 1.421413741 + t * (0.5 * -1.453152027 + t * (0.5 * 1.061405429)))
        )
    )
    tail = tail * bell
    phi = jnp.where(values >= 0, 1.0 - tail, tail)
    return values * phi, phi + values * (0.3989422804014327 * bell)


class Rides:
    def __init__(self, entries):
        self.arrays = [entry[0] for entry in entries]
        self.rows = [pl.ds(entry[1], entry[2] - entry[1]) for entry in entries]
        self.before = [entry[3] for entry in entries if entry[3] is not None]
        self.filled = [index for index, entry in enumerate(entries) if entry[3] is not None]
        arrays = self.arrays
        self.parts = arrays[0].shape[0]
        self.operands = self.arrays + self.before
        self.in_specs = [pl.BlockSpec(memory_space=pl.ANY)] * len(self.operands)
        self.out_specs = [pl.BlockSpec(memory_space=pl.ANY)] * len(arrays)
        self.out_shape = [jax.ShapeDtypeStruct(a.shape, a.dtype) for a in arrays]
        self.scratch = [
            pltpu.SemaphoreType.DMA((self.parts,)),
            pltpu.SemaphoreType.DMA((self.parts,)),
            pltpu.SemaphoreType.DMA,
        ] * len(arrays)

    def aliases(self, inputs, outputs):
        first = inputs + len(self.arrays)
        return {first + place: outputs + index for place, index in enumerate(self.filled)}

    def copy(self, refs, index, offset):
        me = lax.axis_index("expert")
        peer = lax.rem(me + offset, self.parts)
        sources, targets, sems = refs
        return pltpu.make_async_remote_copy(
            src_ref=sources[index].at[peer, self.rows[index]],
            dst_ref=targets[index].at[me, self.rows[index]],
            send_sem=sems[3 * index].at[offset],
            recv_sem=sems[3 * index + 1].at[offset],
            device_id={"expert": peer},
            device_id_type=pl.DeviceIdType.MESH,
        )

    def own(self, refs):
        me = lax.axis_index("expert")
        sources, targets, sems = refs
        return [
            pltpu.make_async_copy(
                sources[index].at[me, self.rows[index]],
                targets[index].at[me, self.rows[index]],
                sems[3 * index + 2],
            )
            for index in range(len(sources))
        ]

    def start(self, refs, more=()):
        self.greet(more)
        self.send(refs)

    def greet(self, more):
        me = lax.axis_index("expert")
        barrier = pltpu.get_barrier_semaphore()
        for peer in more:
            pl.semaphore_signal(
                barrier, inc=1, device_id=peer, device_id_type=pl.DeviceIdType.MESH
            )

        @pl.loop(1, self.parts)
        def _(offset):
            pl.semaphore_signal(
                barrier,
                inc=1,
                device_id={"expert": lax.rem(me + offset, self.parts)},
                device_id_type=pl.DeviceIdType.MESH,
            )

        pl.semaphore_wait(barrier, self.parts - 1 + len(more))

    def send_hop(self, refs, hop):
        for index in range(len(self.rows)):
            self.copy(refs, index, hop).start()

    def send_own(self, refs):
        for copy in self.own(refs):
            copy.start()

    def send(self, refs):
        for index in range(len(self.rows)):

            @pl.loop(1, self.parts)
            def _(offset):
                self.copy(refs, index, offset).start()

        for copy in self.own(refs):
            copy.start()

    def finish(self, refs):
        for copy in self.own(refs):
            copy.wait()
        for index in range(len(self.rows)):

            @pl.loop(1, self.parts)
            def _(offset):
                self.copy(refs, index, offset).wait()


class Gather:
    def __init__(self, rows, ranks):
        self.rows = rows
        self.pairs = ranks // 2
        self.ranks = ranks
        sems = pltpu.SemaphoreType.DMA((2, self.pairs))
        self.scratch = [sems, sems, pltpu.SemaphoreType.DMA]

    def place(self, full, rank):
        return full.at[pl.ds(pl.multiple_of(rank * self.rows, self.rows), self.rows)]

    def copy(self, source, target, sems, hop, peer):
        return pltpu.make_async_remote_copy(
            src_ref=source,
            dst_ref=target,
            send_sem=sems.at[0, hop],
            recv_sem=sems.at[1, hop],
            device_id={"dp": peer},
            device_id_type=pl.DeviceIdType.MESH,
        )

    def first(self, refs, hop):
        shard, full, sems = refs
        target = self.place(full, lax.axis_index("dp"))
        source = target if shard is None else shard
        return self.copy(source, target, sems[0], hop, dp_peers(self.ranks)[hop])

    def second(self, refs, hop):
        _, full, sems = refs
        rank = lax.axis_index("dp")
        held = self.place(full, lax.rem(rank + self.ranks - 2 * hop, self.ranks))
        return self.copy(held, held, sems[1], hop, dp_peers(self.ranks)[0])

    def own(self, refs):
        shard, full, sems = refs
        target = self.place(full, lax.axis_index("dp"))
        return pltpu.make_async_copy(shard, target, sems[2])

    def start(self, refs):
        for hop in range(self.pairs):
            self.first(refs, hop).start()
        if refs[0] is not None:
            self.own(refs).start()

    def forward(self, refs):
        for hop in range(1, self.pairs):
            self.first(refs, hop).wait()
            self.second(refs, hop).start()

    def finish(self, refs):
        if refs[0] is not None:
            self.own(refs).wait()
        self.first(refs, 0).wait()
        for hop in range(1, self.pairs):
            self.second(refs, hop).wait()


def dp_peers(ranks):
    rank = lax.axis_index("dp")
    partner = rank + 1 - 2 * lax.rem(rank, 2)
    return [partner] + [lax.rem(rank + 2 * hop, ranks) for hop in range(1, ranks // 2)]


HBM = pl.BlockSpec(memory_space=pl.ANY)


def staged(*arrays):
    buffers = [pltpu.VMEM(array.shape, array.dtype) for array in arrays]
    return buffers + [pltpu.SemaphoreType.DMA((4,))]


def route_group(capacity, routes_ref, slots_ref, first):
    seq = routes_ref.shape[1]
    row = lax.broadcasted_iota(jnp.int32, (seq, seq), 0)
    col = lax.broadcasted_iota(jnp.int32, (seq, seq), 1)
    earlier = (col < row).astype(f32).astype(bf16)
    lane = lax.broadcasted_iota(jnp.int32, (seq, LANES), 1)
    base = jnp.zeros((1, LANES), f32)
    table = jnp.full((seq, LANES), -1.0, f32)
    for choice in range(TOP):
        for image in range(IMG_MB):
            named = routes_ref[first + image][:, choice : choice + 1]
            onehot = (lane == named).astype(f32)
            count = dot(earlier, onehot.astype(bf16)) + base
            position = jnp.sum(onehot * count, axis=1, keepdims=True).astype(jnp.int32)
            base = base + jnp.sum(onehot, axis=0, keepdims=True)
            slot = jnp.where(position < capacity, named * capacity + position, -1)
            slots_ref[first + image, :, choice : choice + 1] = slot
            table = jnp.where(lane == image * TOP + choice, slot.astype(f32), table)
    return table.T[:8].astype(jnp.int32)


def dispatch(lines, rows_ref, first, out_ref, send=None):
    experts, capacity = out_ref.shape[:2]
    seq = rows_ref.shape[1]
    slot = lax.broadcasted_iota(jnp.int32, (capacity, seq), 0)

    me = lax.axis_index("expert")

    def fill(hop):
        expert = lax.rem(me + hop, experts)
        here = slot + expert * capacity
        total = None
        for index in range(IMG_MB):
            at = index * TOP
            holds = (lines[at : at + 1] == here) | (lines[at + 1 : at + 2] == here)
            part = dot(holds.astype(f32).astype(bf16), rows_ref[first + index])
            total = part if total is None else total + part
        out_ref[expert] = total.astype(bf16)

    @pl.loop(1, experts)
    def _(hop):
        fill(hop)
        if send is not None:
            send(hop)

    fill(0)


def front_kernel(
    experts, capacity, ranks, rides, gathers,
    x_ref, named_ref, top_ref, router_ref, gains_ref, own_bias_ref, in_hbm, out_hbm, w1_hbm, w2_hbm,
    proj_ref, mixed_ref, residual_ref, gates_ref, slots_ref, small_ref, bias_ref,
    dense_hbm, w1_full, w2_full, grad_rows_hbm, token_rows_hbm, grads_hbm, received_hbm,
    dense_ref, rows_a, rows_b, hidden_ref, lines_ref, routes_ref, sems, *more,
):
    step = pl.program_id(0)
    features = x_ref.shape[2]
    ride_a = ([rows_a], [grads_hbm], more[:3])
    ride_b = ([rows_b], [received_hbm], more[3:6])
    dense_part = (None, dense_ref, more[6:9])
    w1_part = (w1_hbm, w1_full, more[9:12])
    w2_part = (w2_hbm, w2_full, more[12:15])
    gather_dense, gather_units = gathers
    keep_dense = pltpu.make_async_copy(dense_ref, dense_hbm, sems.at[0])
    keep_grads = pltpu.make_async_copy(rows_b, grad_rows_hbm, sems.at[1])
    keep_tokens = pltpu.make_async_copy(rows_a, token_rows_hbm, sems.at[2])

    @pl.when(step == 0)
    def _():
        own = features // ranks
        rank = lax.axis_index("dp")
        mine = pl.ds(pl.multiple_of(rank * own, own), own)
        fills = [
            pltpu.make_async_copy(
                in_hbm, dense_ref.at[mine, pl.ds(0, 3 * features)], sems.at[2]
            ),
            pltpu.make_async_copy(
                out_hbm, dense_ref.at[mine, pl.ds(3 * features, features)], sems.at[3]
            ),
        ]
        for fill in fills:
            fill.start()
        pieces = own_bias_ref.shape[1] // own
        own_bias = own_bias_ref[...].astype(f32)
        columns = jnp.concatenate(
            [router_ref[...].astype(f32), gains_ref[...].astype(f32)]
            + [own_bias[:, piece * own : (piece + 1) * own] for piece in range(pieces)]
            + [jnp.zeros((LANES - experts - 4 - pieces, own), f32)],
            axis=0,
        )
        dense_ref[mine, 4 * features :] = columns.T.astype(bf16)
        rides.greet([{"dp": peer} for peer in dp_peers(ranks)])
        for fill in fills:
            fill.wait()
        gather_dense.start(dense_part)
        images = named_ref.shape[0]
        named = [named_ref[index].astype(f32) for index in range(images)]
        rest = jnp.zeros((LANES - TOP * images, named_ref.shape[2]), f32)
        named = jnp.concatenate(named + [rest], axis=0).T.astype(jnp.int32)
        for index in range(images):
            routes_ref[index] = named[:, TOP * index : TOP * (index + 1)]
        lines = route_group(capacity, routes_ref, slots_ref, 0)
        lines_ref[0] = lines
        dispatch(lines, top_ref, 0, rows_a, lambda hop: rides.send_hop(ride_a, hop))
        rides.send_own(ride_a)
        lines = route_group(capacity, routes_ref, slots_ref, IMG_MB)
        lines_ref[1] = lines
        dispatch(lines, top_ref, IMG_MB, rows_b)
        keep_grads.start()
        gather_dense.forward(dense_part)
        gather_units.start(w1_part)
        gather_units.start(w2_part)
        gather_dense.finish(dense_part)
        keep_dense.start()
        small = dense_ref[:, 4 * features :].astype(f32).T
        small_ref[...] = small[: small_ref.shape[0]].astype(bf16)
        for line in range(pieces):
            at = experts + 4 + line
            for place in range(ranks):
                first = (place * pieces + line) * own
                bias_ref[:, first : first + own] = small[
                    at : at + 1, place * own : (place + 1) * own
                ].astype(bf16)
        keep_grads.wait()

    image = x_ref[0].astype(f32)
    vectors = small_ref[...].astype(f32)
    normed, _ = norm_forward(image)
    attn_input = (
        normed * vectors[experts : experts + 1] + vectors[experts + 1 : experts + 2]
    ).astype(bf16)
    proj_ref[0] = dot(attn_input, dense_ref[:, : 3 * features]).astype(bf16)
    low_half = lax.broadcasted_iota(jnp.int32, (1, LANES), 1) < HEAD_DIM
    for pair in range(features // LANES):
        first = pair * LANES
        queries = proj_ref[0, :, first : first + LANES]
        keys = proj_ref[0, :, features + first : features + first + LANES]
        values = proj_ref[0, :, 2 * features + first : 2 * features + first + LANES]
        out = None
        for half in range(2):
            keep = low_half if half == 0 else jnp.logical_not(low_half)
            scores = dot_t(
                jnp.where(keep, queries * HEAD_DIM ** (-0.5), 0).astype(bf16), keys
            )
            top = jnp.max(scores, axis=-1, keepdims=True)
            raised = jnp.exp(scores - top)
            share = 1.0 / jnp.sum(raised, axis=-1, keepdims=True)
            weights = (raised * share).astype(bf16)
            part = dot(weights, jnp.where(keep, values, 0).astype(bf16))
            out = part if out is None else out + part
        mixed_ref[0, :, first : first + LANES] = out.astype(bf16)
    residual = image + dot(mixed_ref[0], dense_ref[:, 3 * features : 4 * features])
    residual_ref[0] = residual
    normed, _ = norm_forward(residual)
    hidden = (
        normed * vectors[experts + 2 : experts + 3] + vectors[experts + 3 : experts + 4]
    ).astype(bf16)
    hidden_ref[lax.rem(step, IMG_MB)] = hidden
    probs = softmax_lanes(dot_t(hidden, small_ref[...]), experts)
    lane = lax.broadcasted_iota(jnp.int32, probs.shape, 1)
    routes = routes_ref[step]
    for choice in range(TOP):
        gates_ref[0, :, choice : choice + 1] = jnp.sum(
            jnp.where(lane == routes[:, choice : choice + 1], probs, 0.0),
            axis=1,
            keepdims=True,
        )

    @pl.when(step == IMG_MB - 1)
    def _():
        dispatch(lines_ref[0], hidden_ref, 0, rows_b, lambda hop: rides.send_hop(ride_b, hop))
        rides.send_own(ride_b)

    @pl.when(step == pl.num_programs(0) - 1)
    def _():
        rides.finish(ride_a)
        dispatch(lines_ref[1], hidden_ref, 0, rows_a)
        keep_tokens.start()
        gather_units.forward(w1_part)
        gather_units.forward(w2_part)
        gather_units.finish(w1_part)
        gather_units.finish(w2_part)
        keep_dense.wait()
        rides.finish(ride_b)
        keep_tokens.wait()


def front(
    images, named, out_grad, router, gains, bias, attn_in, attn_out, w1, w2, experts, capacity,
    ranks, small_rows, collective,
):
    count, seq, features = images.shape
    width = 4 * features + LANES
    slot_rows = jax.ShapeDtypeStruct((experts, capacity, features), bf16)
    rides = Rides([(slot_rows, 0, capacity, None)])
    gathers = (Gather(router.shape[1], ranks), Gather(w1.shape[0], ranks))

    def rows(width):
        return pl.BlockSpec((1, seq, width), lambda i: (i, 0, 0))

    def whole(shape):
        return pl.BlockSpec(
            shape, lambda i: (0,) * len(shape), pipeline_mode=pl.Buffered(1)
        )

    def out(width, dtype):
        return jax.ShapeDtypeStruct((count, seq, width), dtype)

    units = jax.ShapeDtypeStruct((ranks * w1.shape[0], features), bf16)
    return pl.pallas_call(
        functools.partial(front_kernel, experts, capacity, ranks, rides, gathers),
        grid=(count,),
        in_specs=[
            rows(features), whole(named.shape), whole(out_grad.shape), whole(router.shape),
            whole(gains.shape), whole(bias.shape), HBM, HBM, HBM, HBM,
        ],
        out_specs=[
            rows(3 * features), rows(features), rows(features), rows(TOP),
            whole((count, seq, TOP)), whole((small_rows, features)), whole((1, ranks * w1.shape[0])),
        ]
        + [HBM] * 7,
        out_shape=[
            out(3 * features, bf16),
            out(features, bf16),
            out(features, f32),
            out(TOP, f32),
            jax.ShapeDtypeStruct((count, seq, TOP), jnp.int32),
            jax.ShapeDtypeStruct((small_rows, features), bf16),
            jax.ShapeDtypeStruct((1, ranks * w1.shape[0]), bf16),
            jax.ShapeDtypeStruct((features, width), bf16),
            units,
            units,
            slot_rows,
            slot_rows,
            slot_rows,
            slot_rows,
        ],
        scratch_shapes=[
            pltpu.VMEM((features, width), bf16),
            pltpu.VMEM(slot_rows.shape, bf16),
            pltpu.VMEM(slot_rows.shape, bf16),
            pltpu.VMEM((IMG_MB, seq, features), bf16),
            pltpu.VMEM((count // IMG_MB, 8, seq), jnp.int32),
            pltpu.VMEM((count, seq, TOP), jnp.int32),
            pltpu.SemaphoreType.DMA((4,)),
        ]
        + rides.scratch
        + rides.scratch
        + gathers[0].scratch
        + gathers[1].scratch
        + gathers[1].scratch,
        compiler_params=params(
            ("arbitrary",), collective_id=collective, has_side_effects=True
        ),
        cost_estimate=pl.CostEstimate(
            flops=count * seq * 16 * features * features,
            bytes_accessed=4 * features * (4 * features + count * seq * 8),
            transcendentals=count * HEADS * seq * seq,
        ),
        name="front",
    )(images, named, out_grad, router, gains, bias, attn_in, attn_out, w1, w2)


def expert_kernel(
    experts, chunk, add, rides, x_hbm, g_hbm, w1_ref, w2_ref, bias_ref, small_ref, *refs
):
    if add:
        old_w_ref, old_router_ref = refs[:2]
        refs = refs[2:]
    count = len(rides.arrays)
    sources, refs = refs[:count], refs[len(rides.operands) :]
    ride_refs = (sources, refs[4 : count + 4], refs[count + 15 :])
    refs = refs[:4] + refs[count + 4 : count + 15]
    (
        result_hbm, dx_hbm, dw_ref, drouter_ref,
        result_acc, dx_acc, dr_ref, probs_ref, act_ref, pre_ref,
        x_ref, g_ref, result_ref, dx_ref, copy_sems,
    ) = refs
    loads = [
        pltpu.make_async_copy(x_hbm, x_ref, copy_sems.at[0]),
        pltpu.make_async_copy(g_hbm, g_ref, copy_sems.at[1]),
    ]
    stores = [
        pltpu.make_async_copy(result_ref, result_hbm, copy_sems.at[2]),
        pltpu.make_async_copy(dx_ref, dx_hbm, copy_sems.at[3]),
    ]
    step = pl.program_id(0)
    last = pl.num_programs(0) - 1
    rows = x_ref.shape[0]
    mine = lax.axis_index("expert")
    chunks = rows // chunk

    def each_chunk(body):
        for index in range(chunks):
            body(pl.ds(index * chunk, chunk))

    @pl.when(step == 0)
    def _():
        rides.start(ride_refs)
        for load in loads:
            load.start()
        for load in loads:
            load.wait()

        @each_chunk
        def _(at):
            probs = softmax_lanes(dot_t(x_ref[at, :], small_ref[...]), experts)
            lane = lax.broadcasted_iota(jnp.int32, probs.shape, 1)
            probs_ref[at, :] = probs
            gate = jnp.sum(jnp.where(lane == mine, probs, 0.0), axis=1, keepdims=True)
            dr_ref[at, :] = (gate * g_ref[at, :].astype(f32)).astype(bf16)
            result_acc[at, :] = jnp.zeros((chunk, x_ref.shape[1]), f32)
            dx_acc[at, :] = jnp.zeros((chunk, x_ref.shape[1]), f32)

    w1 = w1_ref[...]
    w2 = w2_ref[...]
    bias = bias_ref[...].astype(f32)

    def rows_step(index, dbias):
        at = pl.ds(index * chunk, chunk)
        act, slope = gelu_both(dot_t(x_ref[at, :], w1) + bias)
        act = act.astype(bf16)
        act_ref[at, :] = act
        result_acc[at, :] += dot(act, w2)
        grad_pre = (dot_t(dr_ref[at, :], w2) * slope).astype(bf16)
        pre_ref[at, :] = grad_pre
        dx_acc[at, :] += dot(grad_pre, w1)
        return dbias + jnp.sum(grad_pre.astype(f32), axis=0, keepdims=True)

    dbias = jnp.zeros(bias.shape, f32)
    for index in range(chunks):
        dbias = rows_step(index, dbias)
    dw1 = t_dot(pre_ref[...], x_ref[...])
    dw2 = t_dot(act_ref[...], dr_ref[...])
    dbias = jnp.broadcast_to(dbias, (LANES, dbias.shape[1])).T
    first = 0
    for part in (dw1, dw2, dbias):
        at = pl.ds(first, part.shape[1])
        if add:
            part = part + old_w_ref[:, at].astype(f32)
        dw_ref[:, at] = part.astype(dw_ref.dtype)
        first += part.shape[1]

    @pl.when(step == last)
    def _():
        if add:
            drouter_ref[...] = old_router_ref[...]
        else:
            drouter_ref[...] = jnp.zeros(drouter_ref.shape, f32)

        @each_chunk
        def _(at):
            result = result_acc[at, :].astype(bf16)
            result_ref[at, :] = result
            grad_gate = jnp.sum(
                g_ref[at, :].astype(f32) * result.astype(f32), axis=1, keepdims=True
            )
            probs = probs_ref[at, :]
            lane = lax.broadcasted_iota(jnp.int32, probs.shape, 1)
            chosen = lane == mine
            gate = jnp.sum(jnp.where(chosen, probs, 0.0), axis=1, keepdims=True)
            logits = (grad_gate * gate) * (chosen.astype(f32) - probs)
            high = logits.astype(bf16)
            low = (logits - high.astype(f32)).astype(bf16)
            dx_ref[at, :] = (
                dx_acc[at, :] + dot(high, small_ref[...]) + dot(low, small_ref[...])
            ).astype(bf16)
            drouter_ref[...] += t_dot(high, x_ref[at, :]) + t_dot(low, x_ref[at, :])

        for store in stores:
            store.start()
        rides.finish(ride_refs)
        for store in stores:
            store.wait()


def row_chunk(rows):
    best = rows
    for size in range(16, 513, 16):
        if rows % size == 0:
            best = size
    return best


def expert_block(x, g, w1, w2, bias, small, experts, old, entries, collective):
    rows, features = x.shape
    hidden_units = w1.shape[0]
    block = 512 if hidden_units % 512 == 0 else 256
    steps = hidden_units // block
    chunk = row_chunk(rows)
    add = old is not None
    out_type = bf16
    rides = Rides(entries)

    def whole(shape):
        return pl.BlockSpec(
            shape, lambda s: (0,) * len(shape), pipeline_mode=pl.Buffered(1)
        )

    packed = 2 * features + LANES
    unit_grads = pl.BlockSpec((block, packed), lambda s: (s, 0))
    units = pl.BlockSpec((block, features), lambda s: (s, 0))
    unit_row = pl.BlockSpec((1, block), lambda s: (0, s))
    in_specs = [
        HBM,
        HBM,
        units,
        units,
        unit_row,
        whole(small.shape),
    ]
    operands = [x, g, w1, w2, bias, small]
    if add:
        in_specs += [unit_grads, whole(small.shape)]
        operands += list(old)
    return pl.pallas_call(
        functools.partial(expert_kernel, experts, chunk, add, rides),
        grid=(steps,),
        in_specs=in_specs + rides.in_specs,
        out_specs=[
            HBM, HBM, unit_grads, whole(small.shape)
        ]
        + rides.out_specs,
        out_shape=[
            jax.ShapeDtypeStruct(x.shape, bf16),
            jax.ShapeDtypeStruct(x.shape, bf16),
            jax.ShapeDtypeStruct((hidden_units, packed), out_type),
            jax.ShapeDtypeStruct(small.shape, f32),
        ]
        + rides.out_shape,
        scratch_shapes=[
            pltpu.VMEM((rows, features), f32),
            pltpu.VMEM((rows, features), f32),
            pltpu.VMEM((rows, features), bf16),
            pltpu.VMEM((rows, small.shape[0]), f32),
            pltpu.VMEM((rows, block), bf16),
            pltpu.VMEM((rows, block), bf16),
            *staged(x, g, x, x),
        ]
        + rides.scratch,
        compiler_params=params(
            ("arbitrary",), collective_id=collective, has_side_effects=True
        ),
        cost_estimate=pl.CostEstimate(
            flops=12 * rows * features * hidden_units,
            bytes_accessed=(8 * rows + 12 * hidden_units) * features,
            transcendentals=rows * hidden_units,
        ),
        name="expert_block",
    )(*operands, *rides.operands)


def inner_size(parts):
    size = 1
    while parts % (2 * size) == 0 and 4 * size * size <= parts:
        size *= 2
    return size


def finish_kernel(
    inner, outer, bits, slots_ref, gates_ref, residual_ref,
    returned0_hbm, returned1_hbm, part_ref, out_ref, din_ref, dout_ref, little_ref,
    returned0_ref, returned1_ref, load_sems, flat_ref, sum_ref, second_ref, full_ref, sems2, sems3, sems4,
):
    step = pl.program_id(0)
    seq = slots_ref.shape[1]
    features = out_ref.shape[2]
    width = part_ref.shape[2]
    tiles = width // LANES
    chunks = 4
    edges = [LANES * (tiles * c // chunks) for c in range(chunks + 1)]
    cuts = [pl.ds(edges[c], edges[c + 1] - edges[c]) for c in range(chunks)]
    me = lax.axis_index("expert")
    row = lax.rem(me, inner)
    line = me // inner

    def row_peer(hop):
        return lax.rem(row + hop, inner)

    def copy(source, target, sems, chunk, hop, peer):
        return pltpu.make_async_remote_copy(
            src_ref=source,
            dst_ref=target,
            send_sem=sems.at[0, chunk, hop - 1],
            recv_sem=sems.at[1, chunk, hop - 1],
            device_id={"expert": peer},
            device_id_type=pl.DeviceIdType.MESH,
        )

    def flip(bit):
        size = 2**bit
        return line + size * (1 - 2 * lax.rem(line // size, 2))

    def held(bit, side):
        size = 2**bit
        mine = lax.rem(line // size, 2)
        first = lax.rem(line, size) + size * (mine if side else 1 - mine)
        return [first + 2 * size * place for place in range(outer // (2 * size))]

    def slot(bit, place):
        return sum(outer // 2 ** (lower + 1) for lower in range(bit)) + place

    def reduce_lines(bit, chunk):
        at = cuts[chunk]
        source = part_ref if bit == 0 else sum_ref
        return [
            copy(
                source.at[block, :, at], second_ref.at[slot(bit, place), :, at],
                sems2, chunk, 1 + slot(bit, place), flip(bit) * inner + row,
            )
            for place, block in enumerate(held(bit, False))
        ]

    def add_lines(bit, chunk):
        at = cuts[chunk]
        source = part_ref if bit == 0 else sum_ref
        for place, block in enumerate(held(bit, True)):
            total = source[block, :, at].astype(f32) + second_ref[
                slot(bit, place), :, at
            ].astype(f32)
            if bit == bits - 1:
                full_ref[row, block, :, at] = total.astype(bf16)
            else:
                sum_ref[block, :, at] = total.astype(bf16)

    def gather_lines(bit, chunk):
        at = cuts[chunk]
        return [
            copy(
                full_ref.at[row, block, :, at], full_ref.at[row, block, :, at],
                sems3, chunk, 1 + slot(bit, place), flip(bit) * inner + row,
            )
            for place, block in enumerate(held(bit, True))
        ]

    def gather_rows(chunk):
        at = cuts[chunk]
        return [
            copy(
                full_ref.at[row, :, :, at], full_ref.at[row, :, :, at],
                sems4, chunk, hop, line * inner + row_peer(hop),
            )
            for hop in range(1, inner)
        ]

    loads = [
        pltpu.make_async_copy(returned0_hbm, returned0_ref, load_sems.at[0]),
        pltpu.make_async_copy(returned1_hbm, returned1_ref, load_sems.at[1]),
    ]

    def start(copies):
        for item in copies:
            item.start()

    def wait(copies):
        for item in copies:
            item.wait()

    @pl.when(step == 0)
    def _():
        barrier = pltpu.get_barrier_semaphore()
        peers = [line * inner + row_peer(hop) for hop in range(1, inner)]
        peers += [flip(bit) * inner + row for bit in range(bits)]
        for peer in peers:
            pl.semaphore_signal(
                barrier,
                inc=1,
                device_id={"expert": peer},
                device_id_type=pl.DeviceIdType.MESH,
            )
        pl.semaphore_wait(barrier, len(peers))
        for chunk in range(chunks):
            start(reduce_lines(0, chunk))
        start(loads)
        wait(loads[:1])

    @pl.when(step == IMG_MB)
    def _():
        wait(loads[1:])

    column = lax.broadcasted_iota(jnp.int32, (seq, returned0_ref.shape[0]), 1)

    def mix(returned_ref):
        slots = slots_ref[0]
        gates = gates_ref[0]
        total = residual_ref[0]
        for choice in range(TOP):
            holds = slots[:, choice : choice + 1] == column
            picked = dot(holds.astype(f32).astype(bf16), returned_ref[...])
            total = total + gates[:, choice : choice + 1] * picked
        out_ref[0] = total.astype(bf16)

    @pl.when(step < IMG_MB)
    def _():
        mix(returned0_ref)

    @pl.when(step >= IMG_MB)
    def _():
        mix(returned1_ref)

    def reduced(bit, chunk):
        wait(reduce_lines(bit, chunk))
        add_lines(bit, chunk)
        if bit < bits - 1:
            start(reduce_lines(bit + 1, chunk))
        else:
            start(gather_lines(bit, chunk))

    def gathered(bit, chunk):
        wait(gather_lines(bit, chunk))
        if bit > 0:
            start(gather_lines(bit - 1, chunk))
        else:
            start(gather_rows(chunk))

    stages = [functools.partial(reduced, bit) for bit in range(bits)]
    stages += [functools.partial(gathered, bit) for bit in reversed(range(bits))]
    for place, stage in enumerate(stages):

        @pl.when(step == min(place + 1, 2 * IMG_MB - 1))
        def _():
            for chunk in range(chunks):
                stage(chunk)

    @pl.when(step == 2 * IMG_MB - 1)
    def _():
        for chunk in range(chunks):
            wait(gather_rows(chunk))
        for part in range(inner):
            for place in range(outer):
                block = part * outer + place
                din_ref[block] = full_ref[part, place, :, : 3 * features].astype(f32)
                dout_ref[block] = full_ref[part, place, :, 3 * features : 4 * features].astype(
                    f32
                )
                share = full_ref.shape[2]
                flat_ref[block * share : (block + 1) * share] = full_ref[
                    part, place, :, 4 * features :
                ].astype(f32)
        little_ref[...] = flat_ref[...].T[: little_ref.shape[0]]


def finish(slots, gates, residual, returned, part, parts, lines, collective):
    outer, share, width = part.shape
    inner = inner_size(parts)
    bits = outer.bit_length() - 1
    images, seq, features = residual.shape
    chunks = 4

    def whole(shape):
        return pl.BlockSpec(
            shape, lambda i: (0,) * len(shape), pipeline_mode=pl.Buffered(1)
        )

    def each(width):
        return pl.BlockSpec((1, seq, width), lambda i: (i, 0, 0))

    outs = [3 * features, features]
    little = (lines, parts * share)
    return pl.pallas_call(
        functools.partial(finish_kernel, inner, outer, bits),
        grid=(images,),
        in_specs=[
            each(TOP), each(TOP), each(features),
            HBM, HBM, whole(part.shape),
        ],
        out_specs=[each(features)] + [whole((parts, share, size)) for size in outs]
        + [whole(little)],
        out_shape=[jax.ShapeDtypeStruct((images, seq, features), bf16)]
        + [jax.ShapeDtypeStruct((parts, share, size), f32) for size in outs]
        + [jax.ShapeDtypeStruct(little, f32)],
        scratch_shapes=[
            *staged(*returned),
            pltpu.VMEM((parts * share, LANES), f32),
            pltpu.VMEM((outer, share, width), bf16),
            pltpu.VMEM((outer - 1, share, width), bf16),
            pltpu.VMEM((inner, outer, share, width), bf16),
            pltpu.SemaphoreType.DMA((2, chunks, outer - 1)),
            pltpu.SemaphoreType.DMA((2, chunks, outer - 1)),
            pltpu.SemaphoreType.DMA((2, chunks, inner - 1)),
        ],
        compiler_params=params(
            ("arbitrary",), collective_id=collective, has_side_effects=True
        ),
        cost_estimate=pl.CostEstimate(
            flops=4 * images * seq * returned[0].shape[0] * features,
            bytes_accessed=2 * features * (2 * returned[0].shape[0] + 3 * images * seq),
            transcendentals=0,
        ),
        name="finish",
    )(slots, gates, residual, *returned, part)


def attend_back_kernel(
    experts, add, rides, ranks, x_ref, top_ref, slots_ref, sent_hbm, proj_ref, mixed_ref, residual_ref,
    dense_hbm, small_ref, *refs
):
    if add:
        old_dense_ref, old_small_ref, drouter_ref, sums_b_hbm = refs[:4]
        refs = refs[4:]
    else:
        dweights_hbm, refs = refs[0], refs[1:]
    count = len(rides.arrays)
    outs = 4 if add else 5
    sources, refs = refs[:count], refs[len(rides.operands) :]
    grad_x_ref, ddense_ref = refs[:2]
    if add:
        grad_b_ref, bias_b_ref = refs[2:4]
    else:
        dsmall_ref, sums_b_hbm, grad_a_ref = refs[2:5]
    targets, refs = refs[outs : outs + count], refs[outs + count :]
    acc_in, acc_out, acc_small, dproj_ref, grad_mixed_ref = refs[:5]
    sent_ref, dense_ref, copy_sems = refs[5:8]
    refs = refs[8:]
    rank = lax.axis_index("dp")
    core = lax.rem(rank, 2)
    mine = rank // 2
    pairs = ranks // 2
    partner, *others = [{"dp": peer} for peer in dp_peers(ranks)]
    more = [partner] + others

    def remote(source, target, sems, index, peer):
        return pltpu.make_async_remote_copy(
            src_ref=source,
            dst_ref=target,
            send_sem=sems.at[0, index],
            recv_sem=sems.at[1, index],
            device_id=peer,
            device_id_type=pl.DeviceIdType.MESH,
        )

    if add:
        pack_ref, first_ref, second_ref, part_ref, third_ref = refs[:5]
        first_sems, second_sems, third_sems = refs[5:8]
        own_b_ref, other_b_ref, own_b_sem, other_b_sems = refs[8:12]
        refs = refs[12:]
    else:
        own_w_ref, other_w_ref, other_a_ref = refs[:3]
        own_w_sems, other_w_sems, other_a_sems, keep_b_sem = refs[3:7]
        refs = refs[7:]

    def core_swap(pair):
        rows = other_w_ref.shape[1]
        at = pl.multiple_of((2 * pair + 1 - core) * rows, rows)
        source = dweights_hbm.at[pl.ds(at, rows)]
        return remote(source, other_w_ref.at[pair], other_w_sems, pair, partner)

    def core_own(pair):
        rows = own_w_ref.shape[1]
        at = pl.multiple_of((2 * pair + core) * rows, rows)
        return pltpu.make_async_copy(
            dweights_hbm.at[pl.ds(at, rows)], own_w_ref.at[pair], own_w_sems.at[pair]
        )

    def send_a(hop):
        at = pl.ds(0, x_ref.shape[2])
        source = own_w_ref.at[lax.rem(mine + hop, pairs), :, at]
        return remote(source, other_a_ref.at[hop - 1], other_a_sems, hop - 1, others[hop - 1])

    def keep_b():
        at = pl.ds(x_ref.shape[2], sums_b_hbm.shape[2])
        return pltpu.make_async_copy(own_w_ref.at[:, :, at], sums_b_hbm, keep_b_sem.at[0])

    def send_b(hop):
        source = sums_b_hbm.at[lax.rem(mine + hop, pairs)]
        return remote(source, other_b_ref.at[hop - 1], other_b_sems, hop - 1, others[hop - 1])

    def own_b():
        return pltpu.make_async_copy(sums_b_hbm.at[mine], own_b_ref, own_b_sem.at[0])

    ride_refs = (sources, targets, refs)
    features = x_ref.shape[2]
    seq = x_ref.shape[1]
    step = pl.program_id(0)
    vectors = small_ref[...].astype(f32)
    loads = [
        pltpu.make_async_copy(sent_hbm, sent_ref, copy_sems.at[0]),
        pltpu.make_async_copy(dense_hbm, dense_ref, copy_sems.at[1]),
    ]
    sums_hbm = old_dense_ref if add else ddense_ref
    halves = [
        (acc_in, sums_hbm.at[:, pl.ds(0, 3 * features)], copy_sems.at[2]),
        (acc_out, sums_hbm.at[:, pl.ds(3 * features, features)], copy_sems.at[3]),
    ]
    if add:
        moves = [pltpu.make_async_copy(far, near, sem) for near, far, sem in halves]
    else:
        moves = [pltpu.make_async_copy(near, far, sem) for near, far, sem in halves]

    @pl.when(step == 0)
    def _():
        rides.start(ride_refs, more)
        for load in loads:
            load.start()
        if add:
            own_b().start()
            for hop in range(1, pairs):
                send_b(hop).start()
        else:
            for pair in range(pairs):
                core_swap(pair).start()
                core_own(pair).start()
        if add:
            for move in moves:
                move.start()
            acc_small[...] = old_small_ref[...]
        else:
            acc_in[...] = jnp.zeros(acc_in.shape, f32)
            acc_out[...] = jnp.zeros(acc_out.shape, f32)
            acc_small[...] = jnp.zeros(acc_small.shape, f32)
        for load in loads:
            load.wait()

    if not add:

        @pl.when(step == 1)
        def _():
            for pair in range(pairs):
                core_swap(pair).wait()
                core_own(pair).wait()
                total = own_w_ref[pair].astype(f32) + other_w_ref[pair].astype(f32)
                own_w_ref[pair] = total.astype(bf16)
            for hop in range(1, pairs):
                send_a(hop).start()
            keep_b().start()

    column = lax.broadcasted_iota(jnp.int32, (seq, sent_ref.shape[0]), 1)
    slots = slots_ref[0]
    holds = (slots[:, 0:1] == column) | (slots[:, 1:2] == column)
    grad_hidden = dot(holds.astype(f32).astype(bf16), sent_ref[...])
    normed_two, inverse_two = norm_forward(residual_ref[0])
    acc_small[2:3, :] += jnp.sum(grad_hidden * normed_two, axis=0, keepdims=True)
    acc_small[3:4, :] += jnp.sum(grad_hidden, axis=0, keepdims=True)
    grad_residual = top_ref[0].astype(f32) + norm_backward(
        grad_hidden * vectors[experts + 2 : experts + 3], normed_two, inverse_two
    )
    grad_branch = grad_residual.astype(bf16)
    grad_mixed_ref[...] = dot_t(grad_branch, dense_ref[:, 3 * features : 4 * features]).astype(
        bf16
    )
    low_half = lax.broadcasted_iota(jnp.int32, (1, LANES), 1) < HEAD_DIM
    scale = HEAD_DIM ** (-0.5)
    def head_pair(first):
        queries = proj_ref[0, :, pl.ds(first, LANES)]
        keys = proj_ref[0, :, pl.ds(features + first, LANES)]
        values = proj_ref[0, :, pl.ds(2 * features + first, LANES)]
        grad_out = grad_mixed_ref[:, pl.ds(first, LANES)]
        sums = [None, None, None]
        for half in range(2):
            keep = low_half if half == 0 else jnp.logical_not(low_half)
            head_queries = jnp.where(keep, queries * scale, 0).astype(bf16)
            head_keys = jnp.where(keep, keys, 0).astype(bf16)
            head_grad = jnp.where(keep, grad_out, 0).astype(bf16)
            scores = dot_t(keys, head_queries)
            top = jnp.max(scores, axis=0, keepdims=True)
            raised = jnp.exp(scores - top)
            probs = raised * (1.0 / jnp.sum(raised, axis=0, keepdims=True))
            grad_values = dot(probs.astype(bf16), head_grad)
            grad_weights = dot_t(values, head_grad)
            inner = jnp.sum(grad_weights * probs, axis=0, keepdims=True)
            grad_scores = (probs * (grad_weights - inner)).astype(bf16)
            grad_keys = dot(grad_scores, head_queries)
            grad_queries = t_dot(grad_scores, head_keys)
            for place, part in enumerate((grad_queries, grad_keys, grad_values)):
                sums[place] = part if half == 0 else sums[place] + part
        dproj_ref[:, pl.ds(first, LANES)] = (sums[0] * scale).astype(bf16)
        dproj_ref[:, pl.ds(features + first, LANES)] = sums[1].astype(bf16)
        dproj_ref[:, pl.ds(2 * features + first, LANES)] = sums[2].astype(bf16)
    for pair in range(features // LANES):
        head_pair(pair * LANES)
    normed_one, inverse_one = norm_forward(x_ref[0].astype(f32))
    attn_input = (
        normed_one * vectors[experts : experts + 1] + vectors[experts + 1 : experts + 2]
    ).astype(bf16)
    if add:

        @pl.when(step == 0)
        def _():
            for move in moves:
                move.wait()

    acc_out[...] += t_dot(mixed_ref[0], grad_branch)
    acc_in[...] += t_dot(attn_input, dproj_ref[...])
    grad_input = dot_t(dproj_ref[...], dense_ref[:, : 3 * features])
    acc_small[0:1, :] += jnp.sum(grad_input * normed_one, axis=0, keepdims=True)
    acc_small[1:2, :] += jnp.sum(grad_input, axis=0, keepdims=True)
    grad_x_ref[0] = grad_residual + norm_backward(
        grad_input * vectors[experts : experts + 1], normed_one, inverse_one
    )

    @pl.when(step == pl.num_programs(0) - 1)
    def _():
        if not add:
            for move in moves:
                move.start()
            dsmall_ref[...] = acc_small[...]
            total = own_w_ref[mine, :, :features].astype(f32)
            for hop in range(1, pairs):
                send_a(hop).wait()
                total = total + other_a_ref[hop - 1].astype(f32)
            grad_a_ref[...] = total
            keep_b().wait()
        else:
            used = acc_small.shape[0] + drouter_ref.shape[0]
            rest = jnp.zeros((LANES - used, features), f32)
            column = jnp.concatenate([acc_small[...], drouter_ref[...], rest], axis=0).T
            share = features // ranks
            for shard in range(ranks):
                at = slice(shard * share, (shard + 1) * share)
                place = (shard % 2, shard // 2)
                pack_ref[place[0], place[1], :, : 3 * features] = acc_in[at].astype(bf16)
                pack_ref[place[0], place[1], :, 3 * features : 4 * features] = acc_out[
                    at
                ].astype(bf16)
                pack_ref[place[0], place[1], :, 4 * features :] = column[at].astype(bf16)
            copy = remote(pack_ref.at[1 - core], first_ref, first_sems, 0, partner)
            copy.start()
            copy.wait()
            for pair in range(pairs):
                first_ref[pair] = (
                    first_ref[pair].astype(f32) + pack_ref[core, pair].astype(f32)
                ).astype(bf16)
            copies = [
                remote(
                    first_ref.at[lax.rem(mine + hop, pairs)], second_ref.at[hop - 1],
                    second_sems, hop - 1, others[hop - 1],
                )
                for hop in range(1, pairs)
            ]
            for copy in copies:
                copy.start()
            own_b().wait()
            total = own_b_ref[...].astype(f32)
            for hop in range(1, pairs):
                send_b(hop).wait()
                total = total + other_b_ref[hop - 1].astype(f32)
            grad_b_ref[...] = total[:, :features]
            bias_b_ref[...] = total[:, features:]
            total = first_ref[mine].astype(f32)
            for copy in copies:
                copy.wait()
            for hop in range(1, pairs):
                total = total + second_ref[hop - 1].astype(f32)
            total = total.astype(bf16)
            inner, outer, rows = part_ref.shape[:3]
            for block in range(inner * outer):
                part_ref[block // outer, block % outer] = total[block * rows : (block + 1) * rows]
            me = lax.axis_index("expert")
            row = lax.rem(me, inner)
            copies = []
            for hop in range(1, inner):
                peer = lax.rem(row + hop, inner)
                copies.append(
                    remote(
                        part_ref.at[peer], third_ref.at[hop - 1], third_sems, hop - 1,
                        {"expert": me - row + peer},
                    )
                )
            for copy in copies:
                copy.start()
            for copy in copies:
                copy.wait()
            total = part_ref[row].astype(f32)
            for hop in range(1, inner):
                total = total + third_ref[hop - 1].astype(f32)
            ddense_ref[...] = total.astype(bf16)
        rides.finish(ride_refs)
        if not add:
            for move in moves:
                move.wait()


def attend_back(
    images, out_grad, slots, sent, proj, mixed, residual, dense, small, experts, group, old,
    entries, collective, ranks, dweights=None, sums_b=None,
):
    seq, features = images.shape[1:]
    wide = 3 * features
    first = group * IMG_MB
    add = old is not None
    rides = Rides(entries)

    def rows(width):
        return pl.BlockSpec((1, seq, width), lambda i: (i, 0, 0))

    def source(width):
        return pl.BlockSpec((1, seq, width), lambda i: (first + i, 0, 0))

    def whole(shape):
        return pl.BlockSpec(shape, lambda i: (0, 0), pipeline_mode=pl.Buffered(1))

    small_grads = (8, features)
    in_specs = [
        source(features), source(features), source(TOP), HBM,
        source(wide), source(features), source(features),
        HBM, whole(small.shape),
    ]
    operands = [images, out_grad, slots, sent, proj, mixed, residual, dense, small]
    out_specs = [rows(features), HBM]
    out_shape = [
        jax.ShapeDtypeStruct((IMG_MB, seq, features), f32),
        jax.ShapeDtypeStruct((features, 4 * features), f32),
    ]
    if add:
        in_specs += [HBM] + [whole(array.shape) for array in old[1:]] + [HBM]
        operands += list(old) + [sums_b]
        out_specs += [whole((sums_b.shape[1], features)), whole((sums_b.shape[1], LANES))]
        out_shape += [
            jax.ShapeDtypeStruct((sums_b.shape[1], features), f32),
            jax.ShapeDtypeStruct((sums_b.shape[1], LANES), f32),
        ]
        shard = (features // ranks, 4 * features + LANES)
        inner = inner_size(experts)
        part = (experts // inner, shard[0] // experts, shard[1])
        out_specs[1] = pl.BlockSpec(
            part, lambda i: (0, 0, 0), pipeline_mode=pl.Buffered(1)
        )
        out_shape[1] = jax.ShapeDtypeStruct(part, bf16)
        reduce_scratch = [
            pltpu.VMEM((2, ranks // 2, *shard), bf16),
            pltpu.VMEM((ranks // 2, *shard), bf16),
            pltpu.VMEM((ranks // 2 - 1, *shard), bf16),
            pltpu.VMEM((inner, *part), bf16),
            pltpu.VMEM((inner - 1, *part), bf16),
            pltpu.SemaphoreType.DMA((2, 1)),
            pltpu.SemaphoreType.DMA((2, ranks // 2 - 1)),
            pltpu.SemaphoreType.DMA((2, inner - 1)),
            pltpu.VMEM(sums_b.shape[1:], bf16),
            pltpu.VMEM((ranks // 2 - 1, *sums_b.shape[1:]), bf16),
            pltpu.SemaphoreType.DMA((1,)),
            pltpu.SemaphoreType.DMA((2, ranks // 2 - 1)),
        ]
    else:
        out_specs.append(whole(small_grads))
        out_shape.append(jax.ShapeDtypeStruct(small_grads, f32))
        in_specs.append(HBM)
        operands.append(dweights)
        units = dweights.shape[0] // ranks
        rest = dweights.shape[1] - features
        out_specs += [HBM, whole((units, features))]
        out_shape += [
            jax.ShapeDtypeStruct((ranks // 2, units, rest), bf16),
            jax.ShapeDtypeStruct((units, features), f32),
        ]
        reduce_scratch = [
            pltpu.VMEM((ranks // 2, units, dweights.shape[1]), bf16),
            pltpu.VMEM((ranks // 2, units, dweights.shape[1]), bf16),
            pltpu.VMEM((ranks // 2 - 1, units, features), bf16),
            pltpu.SemaphoreType.DMA((ranks // 2,)),
            pltpu.SemaphoreType.DMA((2, ranks // 2)),
            pltpu.SemaphoreType.DMA((2, ranks // 2 - 1)),
            pltpu.SemaphoreType.DMA((1,)),
        ]
    return pl.pallas_call(
        functools.partial(attend_back_kernel, experts, add, rides, ranks),
        grid=(IMG_MB,),
        in_specs=in_specs + rides.in_specs,
        out_specs=out_specs + rides.out_specs,
        out_shape=out_shape + rides.out_shape,
        scratch_shapes=[
            pltpu.VMEM((features, 3 * features), f32),
            pltpu.VMEM((features, features), f32),
            pltpu.VMEM(small_grads, f32),
            pltpu.VMEM((seq, wide), bf16),
            pltpu.VMEM((seq, features), bf16),
            *staged(sent, dense),
        ]
        + reduce_scratch
        + rides.scratch,
        input_output_aliases=rides.aliases(len(operands), len(out_specs)),
        compiler_params=params(
            ("arbitrary",), collective_id=collective, has_side_effects=True
        ),
        cost_estimate=pl.CostEstimate(
            flops=IMG_MB * seq * 40 * features * features,
            bytes_accessed=8 * features * (4 * features + IMG_MB * seq * 4),
            transcendentals=IMG_MB * HEADS * seq * seq,
        ),
        name="attend_back",
    )(*operands, *rides.operands)


def per_device(
    images, first_gain, first_shift, attn_in, attn_out, second_gain, second_shift, router,
    expert_in, expert_bias, expert_out, routes, out_grad,
):
    features = images.shape[2]
    experts = router.shape[1]
    tok_mb = IMG_MB * SEQ
    capacity = max(2, (5 * TOP * tok_mb // (4 * experts) + 7) // 8 * 8)
    slot_rows = experts * capacity
    own = router.shape[0]
    ranks = features // own
    bias_rows = expert_bias.shape[1] // own
    used = experts + 4 + bias_rows
    small_rows = (used + 15) // 16 * 16
    line = lax.broadcasted_iota(jnp.int32, (4, own), 0)
    gains = jnp.where(
        line < 2,
        jnp.where(line == 0, first_gain[None], first_shift[None]),
        jnp.where(line == 2, second_gain[None], second_shift[None]),
    )

    def flat(blocks):
        return blocks.reshape(slot_rows, features)

    def blocks(rows):
        return rows.reshape(experts, capacity, features)

    (
        proj, mixed, residual, gates, slots, small, bias_row, dense, weight_in, weight_out,
        grad_rows_1, token_rows_1, grads_0, received_0,
    ) = front(
        images, routes.transpose(0, 2, 1), out_grad, router.T, gains, expert_bias, attn_in,
        attn_out, expert_in[0],
        expert_out[0], experts, capacity, ranks, small_rows, 5,
    )
    result_0, dx_0, *old, grads_1, received_1 = expert_block(
        flat(received_0), flat(grads_0), weight_in, weight_out, bias_row, small, experts, None,
        [(grad_rows_1, 0, capacity, None), (token_rows_1, 0, capacity, None)], 0,
    )
    early = max(8, capacity * 2 // 5 // 8 * 8)
    result_1, dx_1, dweights, drouter, sent_0, returned_0 = expert_block(
        flat(received_1), flat(grads_1), weight_in, weight_out, bias_row, small, experts, old,
        [(blocks(dx_0), 0, capacity, None), (blocks(result_0), 0, early, None)], 1,
    )
    grad_x_0, *old, sums_b, grad_expert_in, sent_1 = attend_back(
        images, out_grad, slots, flat(sent_0), proj, mixed, residual, dense, small,
        experts, 0, None, [(blocks(dx_1), 0, capacity, None)], 2, ranks, dweights,
    )
    grad_x_1, ddense, grad_expert_out, grad_bias, returned_0, returned_1 = attend_back(
        images, out_grad, slots, flat(sent_1), proj, mixed, residual, dense, small,
        experts, 1, old + [drouter],
        [(blocks(result_0), early, capacity, returned_0), (blocks(result_1), 0, capacity, None)],
        3, ranks, None, sums_b,
    )
    grad_blocks = [grad_x_0, grad_x_1]
    block_out, grad_attn_in, grad_attn_out, little = finish(
        slots, gates, residual, [flat(returned_0), flat(returned_1)], ddense, experts,
        8 + small_rows, 4,
    )
    return (
        block_out,
        jnp.concatenate(grad_blocks, axis=0),
        little[0],
        little[1],
        grad_attn_in.reshape(own, -1),
        grad_attn_out.reshape(own, -1),
        little[2],
        little[3],
        little[8 : 8 + experts].T,
        grad_expert_in[None],
        grad_bias[None, :, 0],
        grad_expert_out[None],
    )


def solution(mesh):
    return jax.shard_map(
        per_device,
        mesh=mesh,
        in_specs=(
            P(("dp", "expert"), None, None),
            P("dp"),
            P("dp"),
            P("dp", None),
            P("dp", None),
            P("dp"),
            P("dp"),
            P("dp", None),
            P("expert", "dp", None),
            P("expert", "dp"),
            P("expert", "dp", None),
            P(("dp", "expert"), None, None),
            P(("dp", "expert"), None, None),
        ),
        out_specs=(
            P(("dp", "expert"), None, None),
            P(("dp", "expert"), None, None),
            P("dp"),
            P("dp"),
            P("dp", None),
            P("dp", None),
            P("dp"),
            P("dp"),
            P("dp", None),
            P("expert", "dp", None),
            P("expert", "dp"),
            P("expert", "dp", None),
        ),
        check_vma=False,
    )
```

```python
import functools

import jax
import jax.numpy as jnp
from jax import lax
from jax.experimental import pallas as pl
from jax.experimental.pallas import tpu as pltpu
from jax.sharding import PartitionSpec as P

HEADS = 12
HEAD_DIM = 64
SEQ = 197
MICRO = 2
IMG_MB = 3
TOP = 2
LANES = 128
VMEM_LIMIT = 60 * 1024 * 1024

epsilon = 1e-06
f32 = jnp.float32
bf16 = jnp.bfloat16


def params(semantics, **more):
    return pltpu.CompilerParams(
        dimension_semantics=semantics, vmem_limit_bytes=VMEM_LIMIT, **more
    )


def dot(left, right):
    return lax.dot_general(
        left, right, (((1,), (0,)), ((), ())), preferred_element_type=f32
    )


def dot_t(left, right):
    return lax.dot_general(
        left, right, (((1,), (1,)), ((), ())), preferred_element_type=f32
    )


def t_dot(left, right):
    return lax.dot_general(
        left, right, (((0,), (0,)), ((), ())), preferred_element_type=f32
    )


def norm_forward(values):
    row_mean = jnp.mean(values, axis=-1, keepdims=True)
    centred = values - row_mean
    row_var = jnp.mean(centred * centred, axis=-1, keepdims=True)
    inverse = lax.rsqrt(row_var + epsilon)
    return centred * inverse, inverse


def norm_backward(grad_normed, normed, inverse):
    mean_grad = jnp.mean(grad_normed, axis=-1, keepdims=True)
    mean_cross = jnp.mean(grad_normed * normed, axis=-1, keepdims=True)
    return inverse * (grad_normed - mean_grad - normed * mean_cross)


def softmax_lanes(logits, count):
    lane = lax.broadcasted_iota(jnp.int32, logits.shape, 1)
    masked = jnp.where(lane < count, logits, -1e30)
    top = jnp.max(masked, axis=-1, keepdims=True)
    raised = jnp.where(lane < count, jnp.exp(masked - top), 0.0)
    return raised / jnp.sum(raised, axis=-1, keepdims=True)


def gelu_both(values):
    size = jnp.abs(values)
    bell = jnp.exp(values * values * -0.5)
    t = 1.0 / (1.0 + (0.3275911 * 0.7071067811865476) * size)
    tail = t * (
        0.5 * 0.254829592
        + t
        * (
            0.5 * -0.284496736
            + t * (0.5 * 1.421413741 + t * (0.5 * -1.453152027 + t * (0.5 * 1.061405429)))
        )
    )
    tail = tail * bell
    phi = jnp.where(values >= 0, 1.0 - tail, tail)
    return values * phi, phi + values * (0.3989422804014327 * bell)


class Rides:
    def __init__(self, entries):
        self.arrays = [entry[0] for entry in entries]
        self.rows = [pl.ds(entry[1], entry[2] - entry[1]) for entry in entries]
        self.before = [entry[3] for entry in entries if entry[3] is not None]
        self.filled = [index for index, entry in enumerate(entries) if entry[3] is not None]
        arrays = self.arrays
        self.parts = arrays[0].shape[0]
        self.operands = self.arrays + self.before
        self.in_specs = [pl.BlockSpec(memory_space=pl.ANY)] * len(self.operands)
        self.out_specs = [pl.BlockSpec(memory_space=pl.ANY)] * len(arrays)
        self.out_shape = [jax.ShapeDtypeStruct(a.shape, a.dtype) for a in arrays]
        self.scratch = [
            pltpu.SemaphoreType.DMA((self.parts,)),
            pltpu.SemaphoreType.DMA((self.parts,)),
            pltpu.SemaphoreType.DMA,
        ] * len(arrays)

    def aliases(self, inputs, outputs):
        first = inputs + len(self.arrays)
        return {first + place: outputs + index for place, index in enumerate(self.filled)}

    def copy(self, refs, index, offset):
        me = lax.axis_index("expert")
        peer = lax.rem(me + offset, self.parts)
        sources, targets, sems = refs
        return pltpu.make_async_remote_copy(
            src_ref=sources[index].at[peer, self.rows[index]],
            dst_ref=targets[index].at[me, self.rows[index]],
            send_sem=sems[3 * index].at[offset],
            recv_sem=sems[3 * index + 1].at[offset],
            device_id={"expert": peer},
            device_id_type=pl.DeviceIdType.MESH,
        )

    def own(self, refs):
        me = lax.axis_index("expert")
        sources, targets, sems = refs
        return [
            pltpu.make_async_copy(
                sources[index].at[me, self.rows[index]],
                targets[index].at[me, self.rows[index]],
                sems[3 * index + 2],
            )
            for index in range(len(sources))
        ]

    def start(self, refs, more=()):
        self.greet(more)
        self.send(refs)

    def greet(self, more):
        me = lax.axis_index("expert")
        barrier = pltpu.get_barrier_semaphore()
        for peer in more:
            pl.semaphore_signal(
                barrier, inc=1, device_id=peer, device_id_type=pl.DeviceIdType.MESH
            )

        @pl.loop(1, self.parts)
        def _(offset):
            pl.semaphore_signal(
                barrier,
                inc=1,
                device_id={"expert": lax.rem(me + offset, self.parts)},
                device_id_type=pl.DeviceIdType.MESH,
            )

        pl.semaphore_wait(barrier, self.parts - 1 + len(more))

    def send_hop(self, refs, hop):
        for index in range(len(self.rows)):
            self.copy(refs, index, hop).start()

    def send_own(self, refs):
        for copy in self.own(refs):
            copy.start()

    def send(self, refs):
        for index in range(len(self.rows)):

            @pl.loop(1, self.parts)
            def _(offset):
                self.copy(refs, index, offset).start()

        for copy in self.own(refs):
            copy.start()

    def finish(self, refs):
        for copy in self.own(refs):
            copy.wait()
        for index in range(len(self.rows)):

            @pl.loop(1, self.parts)
            def _(offset):
                self.copy(refs, index, offset).wait()


class Gather:
    def __init__(self, rows, ranks):
        self.rows = rows
        self.pairs = ranks // 2
        self.ranks = ranks
        sems = pltpu.SemaphoreType.DMA((2, self.pairs))
        self.scratch = [sems, sems, pltpu.SemaphoreType.DMA]

    def place(self, full, rank):
        return full.at[pl.ds(pl.multiple_of(rank * self.rows, self.rows), self.rows)]

    def copy(self, source, target, sems, hop, peer):
        return pltpu.make_async_remote_copy(
            src_ref=source,
            dst_ref=target,
            send_sem=sems.at[0, hop],
            recv_sem=sems.at[1, hop],
            device_id={"dp": peer},
            device_id_type=pl.DeviceIdType.MESH,
        )

    def first(self, refs, hop):
        shard, full, sems = refs
        target = self.place(full, lax.axis_index("dp"))
        source = target if shard is None else shard
        return self.copy(source, target, sems[0], hop, dp_peers(self.ranks)[hop])

    def second(self, refs, hop):
        _, full, sems = refs
        rank = lax.axis_index("dp")
        held = self.place(full, lax.rem(rank + self.ranks - 2 * hop, self.ranks))
        return self.copy(held, held, sems[1], hop, dp_peers(self.ranks)[0])

    def own(self, refs):
        shard, full, sems = refs
        target = self.place(full, lax.axis_index("dp"))
        return pltpu.make_async_copy(shard, target, sems[2])

    def start(self, refs):
        for hop in range(self.pairs):
            self.first(refs, hop).start()
        if refs[0] is not None:
            self.own(refs).start()

    def forward(self, refs):
        for hop in range(1, self.pairs):
            self.first(refs, hop).wait()
            self.second(refs, hop).start()

    def finish(self, refs):
        if refs[0] is not None:
            self.own(refs).wait()
        self.first(refs, 0).wait()
        for hop in range(1, self.pairs):
            self.second(refs, hop).wait()


def dp_peers(ranks):
    rank = lax.axis_index("dp")
    partner = rank + 1 - 2 * lax.rem(rank, 2)
    return [partner] + [lax.rem(rank + 2 * hop, ranks) for hop in range(1, ranks // 2)]


HBM = pl.BlockSpec(memory_space=pl.ANY)


def staged(*arrays):
    buffers = [pltpu.VMEM(array.shape, array.dtype) for array in arrays]
    return buffers + [pltpu.SemaphoreType.DMA((4,))]


def route_group(capacity, routes_ref, slots_ref, first):
    seq = routes_ref.shape[1]
    row = lax.broadcasted_iota(jnp.int32, (seq, seq), 0)
    col = lax.broadcasted_iota(jnp.int32, (seq, seq), 1)
    earlier = (col < row).astype(f32).astype(bf16)
    lane = lax.broadcasted_iota(jnp.int32, (seq, LANES), 1)
    base = jnp.zeros((1, LANES), f32)
    table = jnp.full((seq, LANES), -1.0, f32)
    for choice in range(TOP):
        for image in range(IMG_MB):
            named = routes_ref[first + image][:, choice : choice + 1]
            onehot = (lane == named).astype(f32)
            count = dot(earlier, onehot.astype(bf16)) + base
            position = jnp.sum(onehot * count, axis=1, keepdims=True).astype(jnp.int32)
            base = base + jnp.sum(onehot, axis=0, keepdims=True)
            slot = jnp.where(position < capacity, named * capacity + position, -1)
            slots_ref[first + image, :, choice : choice + 1] = slot
            table = jnp.where(lane == image * TOP + choice, slot.astype(f32), table)
    return table.T[:8].astype(jnp.int32)


def dispatch(lines, rows_ref, first, out_ref, send=None):
    experts, capacity = out_ref.shape[:2]
    seq = rows_ref.shape[1]
    slot = lax.broadcasted_iota(jnp.int32, (capacity, seq), 0)

    me = lax.axis_index("expert")

    def fill(hop):
        expert = lax.rem(me + hop, experts)
        here = slot + expert * capacity
        total = None
        for index in range(IMG_MB):
            at = index * TOP
            holds = (lines[at : at + 1] == here) | (lines[at + 1 : at + 2] == here)
            part = dot(holds.astype(f32).astype(bf16), rows_ref[first + index])
            total = part if total is None else total + part
        out_ref[expert] = total.astype(bf16)

    @pl.loop(1, experts)
    def _(hop):
        fill(hop)
        if send is not None:
            send(hop)

    fill(0)


def front_kernel(
    experts, capacity, ranks, rides, gathers,
    x_ref, named_ref, top_ref, router_ref, gains_ref, own_bias_ref, in_hbm, out_hbm, w1_hbm, w2_hbm,
    proj_ref, mixed_ref, residual_ref, gates_ref, slots_ref, small_ref, bias_ref,
    dense_hbm, w1_full, w2_full, grad_rows_hbm, token_rows_hbm, grads_hbm, received_hbm,
    dense_ref, rows_a, rows_b, hidden_ref, lines_ref, routes_ref, sems, *more,
):
    step = pl.program_id(0)
    features = x_ref.shape[2]
    ride_a = ([rows_a], [grads_hbm], more[:3])
    ride_b = ([rows_b], [received_hbm], more[3:6])
    dense_part = (None, dense_ref, more[6:9])
    w1_part = (w1_hbm, w1_full, more[9:12])
    w2_part = (w2_hbm, w2_full, more[12:15])
    gather_dense, gather_units = gathers
    keep_dense = pltpu.make_async_copy(dense_ref, dense_hbm, sems.at[0])
    keep_grads = pltpu.make_async_copy(rows_b, grad_rows_hbm, sems.at[1])
    keep_tokens = pltpu.make_async_copy(rows_a, token_rows_hbm, sems.at[2])

    @pl.when(step == 0)
    def _():
        own = features // ranks
        rank = lax.axis_index("dp")
        mine = pl.ds(pl.multiple_of(rank * own, own), own)
        fills = [
            pltpu.make_async_copy(
                in_hbm, dense_ref.at[mine, pl.ds(0, 3 * features)], sems.at[2]
            ),
            pltpu.make_async_copy(
                out_hbm, dense_ref.at[mine, pl.ds(3 * features, features)], sems.at[3]
            ),
        ]
        for fill in fills:
            fill.start()
        pieces = own_bias_ref.shape[1] // own
        own_bias = own_bias_ref[...].astype(f32)
        columns = jnp.concatenate(
            [router_ref[...].astype(f32), gains_ref[...].astype(f32)]
            + [own_bias[:, piece * own : (piece + 1) * own] for piece in range(pieces)]
            + [jnp.zeros((LANES - experts - 4 - pieces, own), f32)],
            axis=0,
        )
        dense_ref[mine, 4 * features :] = columns.T.astype(bf16)
        rides.greet([{"dp": peer} for peer in dp_peers(ranks)])
        for fill in fills:
            fill.wait()
        gather_dense.start(dense_part)
        images = named_ref.shape[0]
        named = [named_ref[index].astype(f32) for index in range(images)]
        rest = jnp.zeros((LANES - TOP * images, named_ref.shape[2]), f32)
        named = jnp.concatenate(named + [rest], axis=0).T.astype(jnp.int32)
        for index in range(images):
            routes_ref[index] = named[:, TOP * index : TOP * (index + 1)]
        lines = route_group(capacity, routes_ref, slots_ref, 0)
        lines_ref[0] = lines
        dispatch(lines, top_ref, 0, rows_a, lambda hop: rides.send_hop(ride_a, hop))
        rides.send_own(ride_a)
        lines = route_group(capacity, routes_ref, slots_ref, IMG_MB)
        lines_ref[1] = lines
        dispatch(lines, top_ref, IMG_MB, rows_b)
        keep_grads.start()
        gather_dense.forward(dense_part)
        gather_units.start(w1_part)
        gather_units.start(w2_part)
        gather_dense.finish(dense_part)
        keep_dense.start()
        small = dense_ref[:, 4 * features :].astype(f32).T
        small_ref[...] = small[: small_ref.shape[0]].astype(bf16)
        for line in range(pieces):
            at = experts + 4 + line
            for place in range(ranks):
                first = (place * pieces + line) * own
                bias_ref[:, first : first + own] = small[
                    at : at + 1, place * own : (place + 1) * own
                ].astype(bf16)
        keep_grads.wait()

    image = x_ref[0].astype(f32)
    vectors = small_ref[...].astype(f32)
    normed, _ = norm_forward(image)
    attn_input = (
        normed * vectors[experts : experts + 1] + vectors[experts + 1 : experts + 2]
    ).astype(bf16)
    proj_ref[0] = dot(attn_input, dense_ref[:, : 3 * features]).astype(bf16)
    low_half = lax.broadcasted_iota(jnp.int32, (1, LANES), 1) < HEAD_DIM
    for pair in range(features // LANES):
        first = pair * LANES
        queries = proj_ref[0, :, first : first + LANES]
        keys = proj_ref[0, :, features + first : features + first + LANES]
        values = proj_ref[0, :, 2 * features + first : 2 * features + first + LANES]
        out = None
        for half in range(2):
            keep = low_half if half == 0 else jnp.logical_not(low_half)
            scores = dot_t(
                jnp.where(keep, queries * HEAD_DIM ** (-0.5), 0).astype(bf16), keys
            )
            top = jnp.max(scores, axis=-1, keepdims=True)
            raised = jnp.exp(scores - top)
            share = 1.0 / jnp.sum(raised, axis=-1, keepdims=True)
            weights = (raised * share).astype(bf16)
            part = dot(weights, jnp.where(keep, values, 0).astype(bf16))
            out = part if out is None else out + part
        mixed_ref[0, :, first : first + LANES] = out.astype(bf16)
    residual = image + dot(mixed_ref[0], dense_ref[:, 3 * features : 4 * features])
    residual_ref[0] = residual
    normed, _ = norm_forward(residual)
    hidden = (
        normed * vectors[experts + 2 : experts + 3] + vectors[experts + 3 : experts + 4]
    ).astype(bf16)
    hidden_ref[lax.rem(step, IMG_MB)] = hidden
    probs = softmax_lanes(dot_t(hidden, small_ref[...]), experts)
    lane = lax.broadcasted_iota(jnp.int32, probs.shape, 1)
    routes = routes_ref[step]
    for choice in range(TOP):
        gates_ref[0, :, choice : choice + 1] = jnp.sum(
            jnp.where(lane == routes[:, choice : choice + 1], probs, 0.0),
            axis=1,
            keepdims=True,
        )

    @pl.when(step == IMG_MB - 1)
    def _():
        dispatch(lines_ref[0], hidden_ref, 0, rows_b, lambda hop: rides.send_hop(ride_b, hop))
        rides.send_own(ride_b)

    @pl.when(step == pl.num_programs(0) - 1)
    def _():
        rides.finish(ride_a)
        dispatch(lines_ref[1], hidden_ref, 0, rows_a)
        keep_tokens.start()
        gather_units.forward(w1_part)
        gather_units.forward(w2_part)
        gather_units.finish(w1_part)
        gather_units.finish(w2_part)
        keep_dense.wait()
        rides.finish(ride_b)
        keep_tokens.wait()


def front(
    images, named, out_grad, router, gains, bias, attn_in, attn_out, w1, w2, experts, capacity,
    ranks, small_rows, collective,
):
    count, seq, features = images.shape
    width = 4 * features + LANES
    slot_rows = jax.ShapeDtypeStruct((experts, capacity, features), bf16)
    rides = Rides([(slot_rows, 0, capacity, None)])
    gathers = (Gather(router.shape[1], ranks), Gather(w1.shape[0], ranks))

    def rows(width):
        return pl.BlockSpec((1, seq, width), lambda i: (i, 0, 0))

    def whole(shape):
        return pl.BlockSpec(
            shape, lambda i: (0,) * len(shape), pipeline_mode=pl.Buffered(1)
        )

    def out(width, dtype):
        return jax.ShapeDtypeStruct((count, seq, width), dtype)

    units = jax.ShapeDtypeStruct((ranks * w1.shape[0], features), bf16)
    return pl.pallas_call(
        functools.partial(front_kernel, experts, capacity, ranks, rides, gathers),
        grid=(count,),
        in_specs=[
            rows(features), whole(named.shape), whole(out_grad.shape), whole(router.shape),
            whole(gains.shape), whole(bias.shape), HBM, HBM, HBM, HBM,
        ],
        out_specs=[
            rows(3 * features), rows(features), rows(features), rows(TOP),
            whole((count, seq, TOP)), whole((small_rows, features)), whole((1, ranks * w1.shape[0])),
        ]
        + [HBM] * 7,
        out_shape=[
            out(3 * features, bf16),
            out(features, bf16),
            out(features, f32),
            out(TOP, f32),
            jax.ShapeDtypeStruct((count, seq, TOP), jnp.int32),
            jax.ShapeDtypeStruct((small_rows, features), bf16),
            jax.ShapeDtypeStruct((1, ranks * w1.shape[0]), bf16),
            jax.ShapeDtypeStruct((features, width), bf16),
            units,
            units,
            slot_rows,
            slot_rows,
            slot_rows,
            slot_rows,
        ],
        scratch_shapes=[
            pltpu.VMEM((features, width), bf16),
            pltpu.VMEM(slot_rows.shape, bf16),
            pltpu.VMEM(slot_rows.shape, bf16),
            pltpu.VMEM((IMG_MB, seq, features), bf16),
            pltpu.VMEM((count // IMG_MB, 8, seq), jnp.int32),
            pltpu.VMEM((count, seq, TOP), jnp.int32),
            pltpu.SemaphoreType.DMA((4,)),
        ]
        + rides.scratch
        + rides.scratch
        + gathers[0].scratch
        + gathers[1].scratch
        + gathers[1].scratch,
        compiler_params=params(
            ("arbitrary",), collective_id=collective, has_side_effects=True
        ),
        cost_estimate=pl.CostEstimate(
            flops=count * seq * 16 * features * features,
            bytes_accessed=4 * features * (4 * features + count * seq * 8),
            transcendentals=count * HEADS * seq * seq,
        ),
        name="front",
    )(images, named, out_grad, router, gains, bias, attn_in, attn_out, w1, w2)


def expert_kernel(
    experts, chunk, add, rides, x_hbm, g_hbm, w1_ref, w2_ref, bias_ref, small_ref, *refs
):
    if add:
        old_w_ref, old_router_ref = refs[:2]
        refs = refs[2:]
    count = len(rides.arrays)
    sources, refs = refs[:count], refs[len(rides.operands) :]
    ride_refs = (sources, refs[4 : count + 4], refs[count + 15 :])
    refs = refs[:4] + refs[count + 4 : count + 15]
    (
        result_hbm, dx_hbm, dw_ref, drouter_ref,
        result_acc, dx_acc, dr_ref, probs_ref, act_ref, pre_ref,
        x_ref, g_ref, result_ref, dx_ref, copy_sems,
    ) = refs
    loads = [
        pltpu.make_async_copy(x_hbm, x_ref, copy_sems.at[0]),
        pltpu.make_async_copy(g_hbm, g_ref, copy_sems.at[1]),
    ]
    stores = [
        pltpu.make_async_copy(result_ref, result_hbm, copy_sems.at[2]),
        pltpu.make_async_copy(dx_ref, dx_hbm, copy_sems.at[3]),
    ]
    step = pl.program_id(0)
    last = pl.num_programs(0) - 1
    rows = x_ref.shape[0]
    mine = lax.axis_index("expert")
    chunks = rows // chunk

    def each_chunk(body):
        for index in range(chunks):
            body(pl.ds(index * chunk, chunk))

    @pl.when(step == 0)
    def _():
        rides.start(ride_refs)
        for load in loads:
            load.start()
        for load in loads:
            load.wait()

        @each_chunk
        def _(at):
            probs = softmax_lanes(dot_t(x_ref[at, :], small_ref[...]), experts)
            lane = lax.broadcasted_iota(jnp.int32, probs.shape, 1)
            probs_ref[at, :] = probs
            gate = jnp.sum(jnp.where(lane == mine, probs, 0.0), axis=1, keepdims=True)
            dr_ref[at, :] = (gate * g_ref[at, :].astype(f32)).astype(bf16)
            result_acc[at, :] = jnp.zeros((chunk, x_ref.shape[1]), f32)
            dx_acc[at, :] = jnp.zeros((chunk, x_ref.shape[1]), f32)

    w1 = w1_ref[...]
    w2 = w2_ref[...]
    bias = bias_ref[...].astype(f32)

    def rows_step(index, dbias):
        at = pl.ds(index * chunk, chunk)
        act, slope = gelu_both(dot_t(x_ref[at, :], w1) + bias)
        act = act.astype(bf16)
        act_ref[at, :] = act
        result_acc[at, :] += dot(act, w2)
        grad_pre = (dot_t(dr_ref[at, :], w2) * slope).astype(bf16)
        pre_ref[at, :] = grad_pre
        dx_acc[at, :] += dot(grad_pre, w1)
        return dbias + jnp.sum(grad_pre.astype(f32), axis=0, keepdims=True)

    dbias = jnp.zeros(bias.shape, f32)
    for index in range(chunks):
        dbias = rows_step(index, dbias)
    dw1 = t_dot(pre_ref[...], x_ref[...])
    dw2 = t_dot(act_ref[...], dr_ref[...])
    dbias = jnp.broadcast_to(dbias, (LANES, dbias.shape[1])).T
    first = 0
    for part in (dw1, dw2, dbias):
        at = pl.ds(first, part.shape[1])
        if add:
            part = part + old_w_ref[:, at]
        dw_ref[:, at] = part.astype(dw_ref.dtype)
        first += part.shape[1]

    @pl.when(step == last)
    def _():
        if add:
            drouter_ref[...] = old_router_ref[...]
        else:
            drouter_ref[...] = jnp.zeros(drouter_ref.shape, f32)

        @each_chunk
        def _(at):
            result = result_acc[at, :].astype(bf16)
            result_ref[at, :] = result
            grad_gate = jnp.sum(
                g_ref[at, :].astype(f32) * result.astype(f32), axis=1, keepdims=True
            )
            probs = probs_ref[at, :]
            lane = lax.broadcasted_iota(jnp.int32, probs.shape, 1)
            chosen = lane == mine
            gate = jnp.sum(jnp.where(chosen, probs, 0.0), axis=1, keepdims=True)
            logits = (grad_gate * gate) * (chosen.astype(f32) - probs)
            high = logits.astype(bf16)
            low = (logits - high.astype(f32)).astype(bf16)
            dx_ref[at, :] = (
                dx_acc[at, :] + dot(high, small_ref[...]) + dot(low, small_ref[...])
            ).astype(bf16)
            drouter_ref[...] += t_dot(high, x_ref[at, :]) + t_dot(low, x_ref[at, :])

        for store in stores:
            store.start()
        rides.finish(ride_refs)
        for store in stores:
            store.wait()


def row_chunk(rows):
    best = rows
    for size in range(16, 513, 16):
        if rows % size == 0:
            best = size
    return best


def expert_block(x, g, w1, w2, bias, small, experts, old, entries, collective):
    rows, features = x.shape
    hidden_units = w1.shape[0]
    block = 512 if hidden_units % 512 == 0 else 256
    steps = hidden_units // block
    chunk = row_chunk(rows)
    add = old is not None
    out_type = bf16 if add else f32
    rides = Rides(entries)

    def whole(shape):
        return pl.BlockSpec(
            shape, lambda s: (0,) * len(shape), pipeline_mode=pl.Buffered(1)
        )

    packed = 2 * features + LANES
    unit_grads = pl.BlockSpec((block, packed), lambda s: (s, 0))
    units = pl.BlockSpec((block, features), lambda s: (s, 0))
    unit_row = pl.BlockSpec((1, block), lambda s: (0, s))
    in_specs = [
        HBM,
        HBM,
        units,
        units,
        unit_row,
        whole(small.shape),
    ]
    operands = [x, g, w1, w2, bias, small]
    if add:
        in_specs += [unit_grads, whole(small.shape)]
        operands += list(old)
    return pl.pallas_call(
        functools.partial(expert_kernel, experts, chunk, add, rides),
        grid=(steps,),
        in_specs=in_specs + rides.in_specs,
        out_specs=[
            HBM, HBM, unit_grads, whole(small.shape)
        ]
        + rides.out_specs,
        out_shape=[
            jax.ShapeDtypeStruct(x.shape, bf16),
            jax.ShapeDtypeStruct(x.shape, bf16),
            jax.ShapeDtypeStruct((hidden_units, packed), out_type),
            jax.ShapeDtypeStruct(small.shape, f32),
        ]
        + rides.out_shape,
        scratch_shapes=[
            pltpu.VMEM((rows, features), f32),
            pltpu.VMEM((rows, features), f32),
            pltpu.VMEM((rows, features), bf16),
            pltpu.VMEM((rows, small.shape[0]), f32),
            pltpu.VMEM((rows, block), bf16),
            pltpu.VMEM((rows, block), bf16),
            *staged(x, g, x, x),
        ]
        + rides.scratch,
        compiler_params=params(
            ("arbitrary",), collective_id=collective, has_side_effects=True
        ),
        cost_estimate=pl.CostEstimate(
            flops=12 * rows * features * hidden_units,
            bytes_accessed=(8 * rows + 12 * hidden_units) * features,
            transcendentals=rows * hidden_units,
        ),
        name="expert_block",
    )(*operands, *rides.operands)


def inner_size(parts):
    size = 1
    while parts % (2 * size) == 0 and 4 * size * size <= parts:
        size *= 2
    return size


def finish_kernel(
    inner, outer, bits, slots_ref, gates_ref, residual_ref,
    returned0_hbm, returned1_hbm, part_ref, out_ref, din_ref, dout_ref, little_ref,
    returned0_ref, returned1_ref, load_sems, flat_ref, sum_ref, second_ref, full_ref, sems2, sems3, sems4,
):
    step = pl.program_id(0)
    seq = slots_ref.shape[1]
    features = out_ref.shape[2]
    width = part_ref.shape[2]
    tiles = width // LANES
    chunks = 4
    edges = [LANES * (tiles * c // chunks) for c in range(chunks + 1)]
    cuts = [pl.ds(edges[c], edges[c + 1] - edges[c]) for c in range(chunks)]
    me = lax.axis_index("expert")
    row = lax.rem(me, inner)
    line = me // inner

    def row_peer(hop):
        return lax.rem(row + hop, inner)

    def copy(source, target, sems, chunk, hop, peer):
        return pltpu.make_async_remote_copy(
            src_ref=source,
            dst_ref=target,
            send_sem=sems.at[0, chunk, hop - 1],
            recv_sem=sems.at[1, chunk, hop - 1],
            device_id={"expert": peer},
            device_id_type=pl.DeviceIdType.MESH,
        )

    def flip(bit):
        size = 2**bit
        return line + size * (1 - 2 * lax.rem(line // size, 2))

    def held(bit, side):
        size = 2**bit
        mine = lax.rem(line // size, 2)
        first = lax.rem(line, size) + size * (mine if side else 1 - mine)
        return [first + 2 * size * place for place in range(outer // (2 * size))]

    def slot(bit, place):
        return sum(outer // 2 ** (lower + 1) for lower in range(bit)) + place

    def reduce_lines(bit, chunk):
        at = cuts[chunk]
        source = part_ref if bit == 0 else sum_ref
        return [
            copy(
                source.at[block, :, at], second_ref.at[slot(bit, place), :, at],
                sems2, chunk, 1 + slot(bit, place), flip(bit) * inner + row,
            )
            for place, block in enumerate(held(bit, False))
        ]

    def add_lines(bit, chunk):
        at = cuts[chunk]
        source = part_ref if bit == 0 else sum_ref
        for place, block in enumerate(held(bit, True)):
            total = source[block, :, at].astype(f32) + second_ref[
                slot(bit, place), :, at
            ].astype(f32)
            if bit == bits - 1:
                full_ref[row, block, :, at] = total.astype(bf16)
            else:
                sum_ref[block, :, at] = total.astype(bf16)

    def gather_lines(bit, chunk):
        at = cuts[chunk]
        return [
            copy(
                full_ref.at[row, block, :, at], full_ref.at[row, block, :, at],
                sems3, chunk, 1 + slot(bit, place), flip(bit) * inner + row,
            )
            for place, block in enumerate(held(bit, True))
        ]

    def gather_rows(chunk):
        at = cuts[chunk]
        return [
            copy(
                full_ref.at[row, :, :, at], full_ref.at[row, :, :, at],
                sems4, chunk, hop, line * inner + row_peer(hop),
            )
            for hop in range(1, inner)
        ]

    loads = [
        pltpu.make_async_copy(returned0_hbm, returned0_ref, load_sems.at[0]),
        pltpu.make_async_copy(returned1_hbm, returned1_ref, load_sems.at[1]),
    ]

    def start(copies):
        for item in copies:
            item.start()

    def wait(copies):
        for item in copies:
            item.wait()

    @pl.when(step == 0)
    def _():
        barrier = pltpu.get_barrier_semaphore()
        peers = [line * inner + row_peer(hop) for hop in range(1, inner)]
        peers += [flip(bit) * inner + row for bit in range(bits)]
        for peer in peers:
            pl.semaphore_signal(
                barrier,
                inc=1,
                device_id={"expert": peer},
                device_id_type=pl.DeviceIdType.MESH,
            )
        pl.semaphore_wait(barrier, len(peers))
        for chunk in range(chunks):
            start(reduce_lines(0, chunk))
        start(loads)
        wait(loads[:1])

    @pl.when(step == IMG_MB)
    def _():
        wait(loads[1:])

    column = lax.broadcasted_iota(jnp.int32, (seq, returned0_ref.shape[0]), 1)

    def mix(returned_ref):
        slots = slots_ref[0]
        gates = gates_ref[0]
        total = residual_ref[0]
        for choice in range(TOP):
            holds = slots[:, choice : choice + 1] == column
            picked = dot(holds.astype(f32).astype(bf16), returned_ref[...])
            total = total + gates[:, choice : choice + 1] * picked
        out_ref[0] = total.astype(bf16)

    @pl.when(step < IMG_MB)
    def _():
        mix(returned0_ref)

    @pl.when(step >= IMG_MB)
    def _():
        mix(returned1_ref)

    def reduced(bit, chunk):
        wait(reduce_lines(bit, chunk))
        add_lines(bit, chunk)
        if bit < bits - 1:
            start(reduce_lines(bit + 1, chunk))
        else:
            start(gather_lines(bit, chunk))

    def gathered(bit, chunk):
        wait(gather_lines(bit, chunk))
        if bit > 0:
            start(gather_lines(bit - 1, chunk))
        else:
            start(gather_rows(chunk))

    stages = [functools.partial(reduced, bit) for bit in range(bits)]
    stages += [functools.partial(gathered, bit) for bit in reversed(range(bits))]
    for place, stage in enumerate(stages):

        @pl.when(step == min(place + 1, 2 * IMG_MB - 1))
        def _():
            for chunk in range(chunks):
                stage(chunk)

    @pl.when(step == 2 * IMG_MB - 1)
    def _():
        for chunk in range(chunks):
            wait(gather_rows(chunk))
        for part in range(inner):
            for place in range(outer):
                block = part * outer + place
                din_ref[block] = full_ref[part, place, :, : 3 * features].astype(f32)
                dout_ref[block] = full_ref[part, place, :, 3 * features : 4 * features].astype(
                    f32
                )
                share = full_ref.shape[2]
                flat_ref[block * share : (block + 1) * share] = full_ref[
                    part, place, :, 4 * features :
                ].astype(f32)
        little_ref[...] = flat_ref[...].T[: little_ref.shape[0]]


def finish(slots, gates, residual, returned, part, parts, lines, collective):
    outer, share, width = part.shape
    inner = inner_size(parts)
    bits = outer.bit_length() - 1
    images, seq, features = residual.shape
    chunks = 4

    def whole(shape):
        return pl.BlockSpec(
            shape, lambda i: (0,) * len(shape), pipeline_mode=pl.Buffered(1)
        )

    def each(width):
        return pl.BlockSpec((1, seq, width), lambda i: (i, 0, 0))

    outs = [3 * features, features]
    little = (lines, parts * share)
    return pl.pallas_call(
        functools.partial(finish_kernel, inner, outer, bits),
        grid=(images,),
        in_specs=[
            each(TOP), each(TOP), each(features),
            HBM, HBM, whole(part.shape),
        ],
        out_specs=[each(features)] + [whole((parts, share, size)) for size in outs]
        + [whole(little)],
        out_shape=[jax.ShapeDtypeStruct((images, seq, features), bf16)]
        + [jax.ShapeDtypeStruct((parts, share, size), f32) for size in outs]
        + [jax.ShapeDtypeStruct(little, f32)],
        scratch_shapes=[
            *staged(*returned),
            pltpu.VMEM((parts * share, LANES), f32),
            pltpu.VMEM((outer, share, width), bf16),
            pltpu.VMEM((outer - 1, share, width), bf16),
            pltpu.VMEM((inner, outer, share, width), bf16),
            pltpu.SemaphoreType.DMA((2, chunks, outer - 1)),
            pltpu.SemaphoreType.DMA((2, chunks, outer - 1)),
            pltpu.SemaphoreType.DMA((2, chunks, inner - 1)),
        ],
        compiler_params=params(
            ("arbitrary",), collective_id=collective, has_side_effects=True
        ),
        cost_estimate=pl.CostEstimate(
            flops=4 * images * seq * returned[0].shape[0] * features,
            bytes_accessed=2 * features * (2 * returned[0].shape[0] + 3 * images * seq),
            transcendentals=0,
        ),
        name="finish",
    )(slots, gates, residual, *returned, part)


def attend_back_kernel(
    experts, add, rides, ranks, x_ref, top_ref, slots_ref, sent_hbm, proj_ref, mixed_ref, residual_ref,
    dense_hbm, small_ref, *refs
):
    if add:
        old_dense_ref, old_small_ref, drouter_ref, sums_b_hbm = refs[:4]
        refs = refs[4:]
    else:
        dweights_hbm, refs = refs[0], refs[1:]
    count = len(rides.arrays)
    outs = 4 if add else 5
    sources, refs = refs[:count], refs[len(rides.operands) :]
    grad_x_ref, ddense_ref = refs[:2]
    if add:
        grad_b_ref, bias_b_ref = refs[2:4]
    else:
        dsmall_ref, sums_b_hbm, grad_a_ref = refs[2:5]
    targets, refs = refs[outs : outs + count], refs[outs + count :]
    acc_in, acc_out, acc_small, dproj_ref, grad_mixed_ref = refs[:5]
    sent_ref, dense_ref, copy_sems = refs[5:8]
    refs = refs[8:]
    rank = lax.axis_index("dp")
    core = lax.rem(rank, 2)
    mine = rank // 2
    pairs = ranks // 2
    partner, *others = [{"dp": peer} for peer in dp_peers(ranks)]
    more = [partner] + others

    def remote(source, target, sems, index, peer):
        return pltpu.make_async_remote_copy(
            src_ref=source,
            dst_ref=target,
            send_sem=sems.at[0, index],
            recv_sem=sems.at[1, index],
            device_id=peer,
            device_id_type=pl.DeviceIdType.MESH,
        )

    if add:
        pack_ref, first_ref, second_ref, part_ref, third_ref = refs[:5]
        first_sems, second_sems, third_sems = refs[5:8]
        own_b_ref, other_b_ref, own_b_sem, other_b_sems = refs[8:12]
        refs = refs[12:]
    else:
        own_w_ref, other_w_ref, other_a_ref = refs[:3]
        own_w_sems, other_w_sems, other_a_sems, keep_b_sem = refs[3:7]
        refs = refs[7:]

    def core_swap(pair):
        rows = other_w_ref.shape[1]
        at = pl.multiple_of((2 * pair + 1 - core) * rows, rows)
        source = dweights_hbm.at[pl.ds(at, rows)]
        return remote(source, other_w_ref.at[pair], other_w_sems, pair, partner)

    def core_own(pair):
        rows = own_w_ref.shape[1]
        at = pl.multiple_of((2 * pair + core) * rows, rows)
        return pltpu.make_async_copy(
            dweights_hbm.at[pl.ds(at, rows)], own_w_ref.at[pair], own_w_sems.at[pair]
        )

    def send_a(hop):
        at = pl.ds(0, x_ref.shape[2])
        source = own_w_ref.at[lax.rem(mine + hop, pairs), :, at]
        return remote(source, other_a_ref.at[hop - 1], other_a_sems, hop - 1, others[hop - 1])

    def keep_b():
        at = pl.ds(x_ref.shape[2], sums_b_hbm.shape[2])
        return pltpu.make_async_copy(own_w_ref.at[:, :, at], sums_b_hbm, keep_b_sem.at[0])

    def send_b(hop):
        source = sums_b_hbm.at[lax.rem(mine + hop, pairs)]
        return remote(source, other_b_ref.at[hop - 1], other_b_sems, hop - 1, others[hop - 1])

    def own_b():
        return pltpu.make_async_copy(sums_b_hbm.at[mine], own_b_ref, own_b_sem.at[0])

    ride_refs = (sources, targets, refs)
    features = x_ref.shape[2]
    seq = x_ref.shape[1]
    step = pl.program_id(0)
    vectors = small_ref[...].astype(f32)
    loads = [
        pltpu.make_async_copy(sent_hbm, sent_ref, copy_sems.at[0]),
        pltpu.make_async_copy(dense_hbm, dense_ref, copy_sems.at[1]),
    ]
    sums_hbm = old_dense_ref if add else ddense_ref
    halves = [
        (acc_in, sums_hbm.at[:, pl.ds(0, 3 * features)], copy_sems.at[2]),
        (acc_out, sums_hbm.at[:, pl.ds(3 * features, features)], copy_sems.at[3]),
    ]
    if add:
        moves = [pltpu.make_async_copy(far, near, sem) for near, far, sem in halves]
    else:
        moves = [pltpu.make_async_copy(near, far, sem) for near, far, sem in halves]

    @pl.when(step == 0)
    def _():
        rides.start(ride_refs, more)
        for load in loads:
            load.start()
        if add:
            own_b().start()
            for hop in range(1, pairs):
                send_b(hop).start()
        else:
            for pair in range(pairs):
                core_swap(pair).start()
                core_own(pair).start()
        if add:
            for move in moves:
                move.start()
            acc_small[...] = old_small_ref[...]
        else:
            acc_in[...] = jnp.zeros(acc_in.shape, f32)
            acc_out[...] = jnp.zeros(acc_out.shape, f32)
            acc_small[...] = jnp.zeros(acc_small.shape, f32)
        for load in loads:
            load.wait()

    if not add:

        @pl.when(step == 1)
        def _():
            for pair in range(pairs):
                core_swap(pair).wait()
                core_own(pair).wait()
                total = own_w_ref[pair].astype(f32) + other_w_ref[pair].astype(f32)
                own_w_ref[pair] = total.astype(bf16)
            for hop in range(1, pairs):
                send_a(hop).start()
            keep_b().start()

    column = lax.broadcasted_iota(jnp.int32, (seq, sent_ref.shape[0]), 1)
    slots = slots_ref[0]
    holds = (slots[:, 0:1] == column) | (slots[:, 1:2] == column)
    grad_hidden = dot(holds.astype(f32).astype(bf16), sent_ref[...])
    normed_two, inverse_two = norm_forward(residual_ref[0])
    acc_small[2:3, :] += jnp.sum(grad_hidden * normed_two, axis=0, keepdims=True)
    acc_small[3:4, :] += jnp.sum(grad_hidden, axis=0, keepdims=True)
    grad_residual = top_ref[0].astype(f32) + norm_backward(
        grad_hidden * vectors[experts + 2 : experts + 3], normed_two, inverse_two
    )
    grad_branch = grad_residual.astype(bf16)
    grad_mixed_ref[...] = dot_t(grad_branch, dense_ref[:, 3 * features : 4 * features]).astype(
        bf16
    )
    low_half = lax.broadcasted_iota(jnp.int32, (1, LANES), 1) < HEAD_DIM
    scale = HEAD_DIM ** (-0.5)
    def head_pair(first):
        queries = proj_ref[0, :, pl.ds(first, LANES)]
        keys = proj_ref[0, :, pl.ds(features + first, LANES)]
        values = proj_ref[0, :, pl.ds(2 * features + first, LANES)]
        grad_out = grad_mixed_ref[:, pl.ds(first, LANES)]
        sums = [None, None, None]
        for half in range(2):
            keep = low_half if half == 0 else jnp.logical_not(low_half)
            head_queries = jnp.where(keep, queries * scale, 0).astype(bf16)
            head_keys = jnp.where(keep, keys, 0).astype(bf16)
            head_grad = jnp.where(keep, grad_out, 0).astype(bf16)
            scores = dot_t(keys, head_queries)
            top = jnp.max(scores, axis=0, keepdims=True)
            raised = jnp.exp(scores - top)
            probs = raised * (1.0 / jnp.sum(raised, axis=0, keepdims=True))
            grad_values = dot(probs.astype(bf16), head_grad)
            grad_weights = dot_t(values, head_grad)
            inner = jnp.sum(grad_weights * probs, axis=0, keepdims=True)
            grad_scores = (probs * (grad_weights - inner)).astype(bf16)
            grad_keys = dot(grad_scores, head_queries)
            grad_queries = t_dot(grad_scores, head_keys)
            for place, part in enumerate((grad_queries, grad_keys, grad_values)):
                sums[place] = part if half == 0 else sums[place] + part
        dproj_ref[:, pl.ds(first, LANES)] = (sums[0] * scale).astype(bf16)
        dproj_ref[:, pl.ds(features + first, LANES)] = sums[1].astype(bf16)
        dproj_ref[:, pl.ds(2 * features + first, LANES)] = sums[2].astype(bf16)
    for pair in range(features // LANES):
        head_pair(pair * LANES)
    normed_one, inverse_one = norm_forward(x_ref[0].astype(f32))
    attn_input = (
        normed_one * vectors[experts : experts + 1] + vectors[experts + 1 : experts + 2]
    ).astype(bf16)
    if add:

        @pl.when(step == 0)
        def _():
            for move in moves:
                move.wait()

    acc_out[...] += t_dot(mixed_ref[0], grad_branch)
    acc_in[...] += t_dot(attn_input, dproj_ref[...])
    grad_input = dot_t(dproj_ref[...], dense_ref[:, : 3 * features])
    acc_small[0:1, :] += jnp.sum(grad_input * normed_one, axis=0, keepdims=True)
    acc_small[1:2, :] += jnp.sum(grad_input, axis=0, keepdims=True)
    grad_x_ref[0] = grad_residual + norm_backward(
        grad_input * vectors[experts : experts + 1], normed_one, inverse_one
    )

    @pl.when(step == pl.num_programs(0) - 1)
    def _():
        if not add:
            for move in moves:
                move.start()
            dsmall_ref[...] = acc_small[...]
            total = own_w_ref[mine, :, :features].astype(f32)
            for hop in range(1, pairs):
                send_a(hop).wait()
                total = total + other_a_ref[hop - 1].astype(f32)
            grad_a_ref[...] = total
            keep_b().wait()
        else:
            used = acc_small.shape[0] + drouter_ref.shape[0]
            rest = jnp.zeros((LANES - used, features), f32)
            column = jnp.concatenate([acc_small[...], drouter_ref[...], rest], axis=0).T
            share = features // ranks
            for shard in range(ranks):
                at = slice(shard * share, (shard + 1) * share)
                place = (shard % 2, shard // 2)
                pack_ref[place[0], place[1], :, : 3 * features] = acc_in[at].astype(bf16)
                pack_ref[place[0], place[1], :, 3 * features : 4 * features] = acc_out[
                    at
                ].astype(bf16)
                pack_ref[place[0], place[1], :, 4 * features :] = column[at].astype(bf16)
            copy = remote(pack_ref.at[1 - core], first_ref, first_sems, 0, partner)
            copy.start()
            copy.wait()
            for pair in range(pairs):
                first_ref[pair] = (
                    first_ref[pair].astype(f32) + pack_ref[core, pair].astype(f32)
                ).astype(bf16)
            copies = [
                remote(
                    first_ref.at[lax.rem(mine + hop, pairs)], second_ref.at[hop - 1],
                    second_sems, hop - 1, others[hop - 1],
                )
                for hop in range(1, pairs)
            ]
            for copy in copies:
                copy.start()
            own_b().wait()
            total = own_b_ref[...].astype(f32)
            for hop in range(1, pairs):
                send_b(hop).wait()
                total = total + other_b_ref[hop - 1].astype(f32)
            grad_b_ref[...] = total[:, :features]
            bias_b_ref[...] = total[:, features:]
            total = first_ref[mine].astype(f32)
            for copy in copies:
                copy.wait()
            for hop in range(1, pairs):
                total = total + second_ref[hop - 1].astype(f32)
            total = total.astype(bf16)
            inner, outer, rows = part_ref.shape[:3]
            for block in range(inner * outer):
                part_ref[block // outer, block % outer] = total[block * rows : (block + 1) * rows]
            me = lax.axis_index("expert")
            row = lax.rem(me, inner)
            copies = []
            for hop in range(1, inner):
                peer = lax.rem(row + hop, inner)
                copies.append(
                    remote(
                        part_ref.at[peer], third_ref.at[hop - 1], third_sems, hop - 1,
                        {"expert": me - row + peer},
                    )
                )
            for copy in copies:
                copy.start()
            for copy in copies:
                copy.wait()
            total = part_ref[row].astype(f32)
            for hop in range(1, inner):
                total = total + third_ref[hop - 1].astype(f32)
            ddense_ref[...] = total.astype(bf16)
        rides.finish(ride_refs)
        if not add:
            for move in moves:
                move.wait()


def attend_back(
    images, out_grad, slots, sent, proj, mixed, residual, dense, small, experts, group, old,
    entries, collective, ranks, dweights=None, sums_b=None,
):
    seq, features = images.shape[1:]
    wide = 3 * features
    first = group * IMG_MB
    add = old is not None
    rides = Rides(entries)

    def rows(width):
        return pl.BlockSpec((1, seq, width), lambda i: (i, 0, 0))

    def source(width):
        return pl.BlockSpec((1, seq, width), lambda i: (first + i, 0, 0))

    def whole(shape):
        return pl.BlockSpec(shape, lambda i: (0, 0), pipeline_mode=pl.Buffered(1))

    small_grads = (8, features)
    in_specs = [
        source(features), source(features), source(TOP), HBM,
        source(wide), source(features), source(features),
        HBM, whole(small.shape),
    ]
    operands = [images, out_grad, slots, sent, proj, mixed, residual, dense, small]
    out_specs = [rows(features), HBM]
    out_shape = [
        jax.ShapeDtypeStruct((IMG_MB, seq, features), f32),
        jax.ShapeDtypeStruct((features, 4 * features), f32),
    ]
    if add:
        in_specs += [HBM] + [whole(array.shape) for array in old[1:]] + [HBM]
        operands += list(old) + [sums_b]
        out_specs += [whole((sums_b.shape[1], features)), whole((sums_b.shape[1], LANES))]
        out_shape += [
            jax.ShapeDtypeStruct((sums_b.shape[1], features), f32),
            jax.ShapeDtypeStruct((sums_b.shape[1], LANES), f32),
        ]
        shard = (features // ranks, 4 * features + LANES)
        inner = inner_size(experts)
        part = (experts // inner, shard[0] // experts, shard[1])
        out_specs[1] = pl.BlockSpec(
            part, lambda i: (0, 0, 0), pipeline_mode=pl.Buffered(1)
        )
        out_shape[1] = jax.ShapeDtypeStruct(part, bf16)
        reduce_scratch = [
            pltpu.VMEM((2, ranks // 2, *shard), bf16),
            pltpu.VMEM((ranks // 2, *shard), bf16),
            pltpu.VMEM((ranks // 2 - 1, *shard), bf16),
            pltpu.VMEM((inner, *part), bf16),
            pltpu.VMEM((inner - 1, *part), bf16),
            pltpu.SemaphoreType.DMA((2, 1)),
            pltpu.SemaphoreType.DMA((2, ranks // 2 - 1)),
            pltpu.SemaphoreType.DMA((2, inner - 1)),
            pltpu.VMEM(sums_b.shape[1:], bf16),
            pltpu.VMEM((ranks // 2 - 1, *sums_b.shape[1:]), bf16),
            pltpu.SemaphoreType.DMA((1,)),
            pltpu.SemaphoreType.DMA((2, ranks // 2 - 1)),
        ]
    else:
        out_specs.append(whole(small_grads))
        out_shape.append(jax.ShapeDtypeStruct(small_grads, f32))
        in_specs.append(HBM)
        operands.append(dweights)
        units = dweights.shape[0] // ranks
        rest = dweights.shape[1] - features
        out_specs += [HBM, whole((units, features))]
        out_shape += [
            jax.ShapeDtypeStruct((ranks // 2, units, rest), bf16),
            jax.ShapeDtypeStruct((units, features), f32),
        ]
        reduce_scratch = [
            pltpu.VMEM((ranks // 2, units, dweights.shape[1]), bf16),
            pltpu.VMEM((ranks // 2, units, dweights.shape[1]), bf16),
            pltpu.VMEM((ranks // 2 - 1, units, features), bf16),
            pltpu.SemaphoreType.DMA((ranks // 2,)),
            pltpu.SemaphoreType.DMA((2, ranks // 2)),
            pltpu.SemaphoreType.DMA((2, ranks // 2 - 1)),
            pltpu.SemaphoreType.DMA((1,)),
        ]
    return pl.pallas_call(
        functools.partial(attend_back_kernel, experts, add, rides, ranks),
        grid=(IMG_MB,),
        in_specs=in_specs + rides.in_specs,
        out_specs=out_specs + rides.out_specs,
        out_shape=out_shape + rides.out_shape,
        scratch_shapes=[
            pltpu.VMEM((features, 3 * features), f32),
            pltpu.VMEM((features, features), f32),
            pltpu.VMEM(small_grads, f32),
            pltpu.VMEM((seq, wide), bf16),
            pltpu.VMEM((seq, features), bf16),
            *staged(sent, dense),
        ]
        + reduce_scratch
        + rides.scratch,
        input_output_aliases=rides.aliases(len(operands), len(out_specs)),
        compiler_params=params(
            ("arbitrary",), collective_id=collective, has_side_effects=True
        ),
        cost_estimate=pl.CostEstimate(
            flops=IMG_MB * seq * 40 * features * features,
            bytes_accessed=8 * features * (4 * features + IMG_MB * seq * 4),
            transcendentals=IMG_MB * HEADS * seq * seq,
        ),
        name="attend_back",
    )(*operands, *rides.operands)


def per_device(
    images, first_gain, first_shift, attn_in, attn_out, second_gain, second_shift, router,
    expert_in, expert_bias, expert_out, routes, out_grad,
):
    features = images.shape[2]
    experts = router.shape[1]
    tok_mb = IMG_MB * SEQ
    capacity = max(2, (5 * TOP * tok_mb // (4 * experts) + 7) // 8 * 8)
    slot_rows = experts * capacity
    own = router.shape[0]
    ranks = features // own
    bias_rows = expert_bias.shape[1] // own
    used = experts + 4 + bias_rows
    small_rows = (used + 15) // 16 * 16
    line = lax.broadcasted_iota(jnp.int32, (4, own), 0)
    gains = jnp.where(
        line < 2,
        jnp.where(line == 0, first_gain[None], first_shift[None]),
        jnp.where(line == 2, second_gain[None], second_shift[None]),
    )

    def flat(blocks):
        return blocks.reshape(slot_rows, features)

    def blocks(rows):
        return rows.reshape(experts, capacity, features)

    (
        proj, mixed, residual, gates, slots, small, bias_row, dense, weight_in, weight_out,
        grad_rows_1, token_rows_1, grads_0, received_0,
    ) = front(
        images, routes.transpose(0, 2, 1), out_grad, router.T, gains, expert_bias, attn_in,
        attn_out, expert_in[0],
        expert_out[0], experts, capacity, ranks, small_rows, 5,
    )
    result_0, dx_0, *old, grads_1, received_1 = expert_block(
        flat(received_0), flat(grads_0), weight_in, weight_out, bias_row, small, experts, None,
        [(grad_rows_1, 0, capacity, None), (token_rows_1, 0, capacity, None)], 0,
    )
    early = max(8, capacity * 5 // 16 // 8 * 8)
    result_1, dx_1, dweights, drouter, sent_0, returned_0 = expert_block(
        flat(received_1), flat(grads_1), weight_in, weight_out, bias_row, small, experts, old,
        [(blocks(dx_0), 0, capacity, None), (blocks(result_0), 0, early, None)], 1,
    )
    grad_x_0, *old, sums_b, grad_expert_in, sent_1 = attend_back(
        images, out_grad, slots, flat(sent_0), proj, mixed, residual, dense, small,
        experts, 0, None, [(blocks(dx_1), 0, capacity, None)], 2, ranks, dweights,
    )
    grad_x_1, ddense, grad_expert_out, grad_bias, returned_0, returned_1 = attend_back(
        images, out_grad, slots, flat(sent_1), proj, mixed, residual, dense, small,
        experts, 1, old + [drouter],
        [(blocks(result_0), early, capacity, returned_0), (blocks(result_1), 0, capacity, None)],
        3, ranks, None, sums_b,
    )
    grad_blocks = [grad_x_0, grad_x_1]
    block_out, grad_attn_in, grad_attn_out, little = finish(
        slots, gates, residual, [flat(returned_0), flat(returned_1)], ddense, experts,
        8 + small_rows, 4,
    )
    return (
        block_out,
        jnp.concatenate(grad_blocks, axis=0),
        little[0],
        little[1],
        grad_attn_in.reshape(own, -1),
        grad_attn_out.reshape(own, -1),
        little[2],
        little[3],
        little[8 : 8 + experts].T,
        grad_expert_in[None],
        grad_bias[None, :, 0],
        grad_expert_out[None],
    )


def solution(mesh):
    return jax.shard_map(
        per_device,
        mesh=mesh,
        in_specs=(
            P(("dp", "expert"), None, None),
            P("dp"),
            P("dp"),
            P("dp", None),
            P("dp", None),
            P("dp"),
            P("dp"),
            P("dp", None),
            P("expert", "dp", None),
            P("expert", "dp"),
            P("expert", "dp", None),
            P(("dp", "expert"), None, None),
            P(("dp", "expert"), None, None),
        ),
        out_specs=(
            P(("dp", "expert"), None, None),
            P(("dp", "expert"), None, None),
            P("dp"),
            P("dp"),
            P("dp", None),
            P("dp", None),
            P("dp"),
            P("dp"),
            P("dp", None),
            P("expert", "dp", None),
            P("expert", "dp"),
            P("expert", "dp", None),
        ),
        check_vma=False,
    )
```
